32 devices in a mesh: dp: 8 (over z, x), tensor: 4 (over y, core).
Axes of the slice: x: 2, y: 2, z: 4, core: 2. Of those that a mesh axis runs over, the one named last changes fastest.
Arguments:
- tokens: bfloat16 [32768, 768], P(('dp', 'tensor')), may hold values from -6 to 6
- segment_ids: int32 [16, 2048], P('dp'), may hold values from 0 to 8, as said below
- memory_positions: int32 [16, 20], P('dp'), may hold values from 0 to 2047, as said below
- memory_rows: bfloat16 [20, 768], replicated, may hold values from -6 to 6
- qkv_weight: bfloat16 [768, 12, 192], P('dp', 'tensor'), may hold values from -0.21875 to 0.21875
- qv_bias: bfloat16 [12, 128], P('tensor'), may hold values from -3 to 3
- out_weight: bfloat16 [768, 12, 64], P('dp', 'tensor'), may hold values from -0.875 to 0.875
- out_bias: bfloat16 [768], replicated, may hold values from -1.75 to 1.75
- norm1_gain: bfloat16 [768], replicated, may hold values from 0.5 to 1.5
- norm1_bias: bfloat16 [768], replicated, may hold values from -1.75 to 1.75
- up_weight: bfloat16 [768, 3072], P('dp', 'tensor'), may hold values from -0.21875 to 0.21875
- up_bias: bfloat16 [3072], P('tensor'), may hold values from -3 to 3
- down_weight: bfloat16 [768, 3072], P('dp', 'tensor'), may hold values from -0.109375 to 0.109375
- down_bias: bfloat16 [768], replicated, may hold values from -1.75 to 1.75
- norm2_gain: bfloat16 [768], replicated, may hold values from 0.5 to 1.5
- norm2_bias: bfloat16 [768], replicated, may hold values from -1.75 to 1.75
- out_cotangent: bfloat16 [32768, 768], P(('dp', 'tensor')), may hold values from -6 to 6
Outputs:
- block_out: bfloat16 [32768, 768], P(('dp', 'tensor'))
- grad_tokens: float32 [32768, 768], P(('dp', 'tensor'))
- grad_memory_rows: float32 [20, 768], replicated
- grad_qkv_weight: float32 [768, 12, 192], P('dp', 'tensor')
- grad_qv_bias: float32 [12, 128], P('tensor')
- grad_out_weight: float32 [768, 12, 64], P('dp', 'tensor')
- grad_out_bias: float32 [768], replicated
- grad_norm1_gain: float32 [768], replicated
- grad_norm1_bias: float32 [768], replicated
- grad_up_weight: float32 [768, 3072], P('dp', 'tensor')
- grad_up_bias: float32 [3072], P('tensor')
- grad_down_weight: float32 [768, 3072], P('dp', 'tensor')
- grad_down_bias: float32 [768], replicated
- grad_norm2_gain: float32 [768], replicated
- grad_norm2_bias: float32 [768], replicated
The draws below stay inside these ranges and needn't reach their ends.
Inputs may be any that keep to these rules, and one draw needn't show every extreme that they name: `segment_ids`: never falling along a group; each group begins with segment 0 of at least 512 positions and holds every segment up to 8. `memory_positions`: within a group all positions differ; read rows lie among the first 512 positions, the first at 0, write rows among the last 512, the first at 2047.
All inputs are finite; a program needn't handle non-finite values.
Results may differ from the reference program's by a relative error of at most 0.015.
Values may be sent and summed in bfloat16 or wider, within the bound.
A program may use at most 192 MiB of HBM per device.

```python
import jax
import jax.numpy as jnp
from jax import lax

D = 768
H = 12
HD = 64
FF = 3072
READ = 10
WRITE = 10
MEM = 20
PROMPT = 1024
CONT = 8
GROUP = 2048
QBLOCK = 512
GROUPS_DP = 2
GROUPS = 16
TOKENS = 32768


def draw_segment_ids(key, part):
    first_key, second_key = jax.random.split(key)
    prompt_len = jax.random.randint(first_key, (GROUPS, 1), PROMPT // 2, PROMPT + 1)
    cont_span = (GROUP - prompt_len) // CONT
    jitter = jax.random.randint(second_key, (GROUPS, CONT), -1000000, 1000000)
    reach = cont_span // 4
    jitter = jitter % (2 * reach + 1) - reach
    steps_ahead = jnp.arange(CONT, dtype=jnp.int32)[None, :]
    bounds = prompt_len + steps_ahead * cont_span + jnp.where(steps_ahead == 0, 0, jitter)
    position = jnp.arange(GROUP, dtype=jnp.int32)[None, :, None]
    return jnp.sum((position >= bounds[:, None, :]).astype(jnp.int32), axis=-1).astype(jnp.int32)


def draw_memory_positions(key, part):
    group_keys = jax.random.split(key, GROUPS)

    def one_group(single):
        first_key, second_key = jax.random.split(single)
        reads = 1 + jax.random.permutation(first_key, PROMPT // 2 - 1)[:READ - 1]
        writes = 1 + jax.random.permutation(second_key, PROMPT // 2 - 1)[:WRITE - 1]
        reads = jnp.concatenate([jnp.zeros((1,), jnp.int32), reads.astype(jnp.int32)])
        writes = GROUP - 1 - jnp.concatenate([jnp.zeros((1,), jnp.int32), writes.astype(jnp.int32)])
        return jnp.concatenate([reads, writes]).astype(jnp.int32)
    return jax.vmap(one_group)(group_keys)


def strengthened(result, stream_key, source, target, blocks, factor):
    def block_of(dim):
        return (jnp.arange(result.shape[dim]) // (result.shape[dim] // blocks)).reshape((-1,) + (1,) * (result.ndim - 1 - dim))

    one_side = jax.random.permutation(stream_key, blocks)[block_of(target)]
    second = (block_of(target) + blocks // 2) % blocks
    return jnp.where((block_of(source) == one_side) | (block_of(source) == second), factor * result, result)


def steps_of(stream_key, extent, pieces, smallest, largest):
    def one(dim, parts):
        steps = jax.random.uniform(jax.random.fold_in(jax.random.fold_in(stream_key, 6), dim), (parts,), jnp.float32, smallest / len(pieces), largest / len(pieces))
        return jnp.repeat(jnp.exp(steps), extent[dim] // parts).reshape((-1,) + (1,) * (len(extent) - dim - 1))

    level = one(*pieces[0])
    for cut in pieces[1:]:
        level = level * one(*cut)
    return level


def centred(key, extent, scale, limit, cuts=(), kind=jnp.bfloat16):
    loudness = steps_of(key, extent, cuts, -0.22, 0.18) if cuts else 1.0
    entries = jax.random.normal(key, extent, jnp.float32) * scale * loudness
    return jnp.minimum(jnp.maximum(entries, -limit), limit).astype(kind)


def gaussian_with(stream_key, extent, deviation, most, pieces, heavy, held_as=jnp.bfloat16):
    entries = deviation * jax.random.normal(stream_key, extent, jnp.float32)
    if pieces:
        entries = entries * steps_of(stream_key, extent, pieces, -0.22, 0.18)
    return jnp.clip(strengthened(entries, jax.random.fold_in(stream_key, 3), *heavy), -most, most).astype(held_as)


def setup_inputs(seed: int = 0) -> dict:
    arg_keys = jax.random.split(jax.random.key(seed), 18)
    tokens = gaussian_with(arg_keys[0], (TOKENS, D), 1.0, 6.0, ((0, 32),), (0, 1, 32, 2.75))
    segment_ids = draw_segment_ids(jax.random.fold_in(arg_keys[17], 71), 0)
    memory_positions = draw_memory_positions(jax.random.fold_in(arg_keys[17], 71), 0)
    memory_rows = centred(arg_keys[3], (MEM, D), 1.0, 6.0)
    qkv_weight = centred(arg_keys[4], (D, H, 3 * HD), D ** -0.5, 0.21875, ((0, 8), (1, 4)))
    qv_bias = centred(arg_keys[5], (H, 2 * HD), 0.5, 3.0, ((0, 4),))
    out_weight = centred(arg_keys[6], (D, H, HD), (D // 16) ** -0.5, 0.875, ((0, 8), (1, 4)))
    out_bias = centred(arg_keys[7], (D,), 0.3, 1.75)
    norm1_gain = jnp.clip(1.0 + 0.1 * jax.random.normal(arg_keys[8], (D,), jnp.float32), 0.5, 1.5).astype(jnp.bfloat16)
    norm1_bias = centred(arg_keys[9], (D,), 0.3, 1.75)
    up_weight = centred(arg_keys[10], (D, FF), D ** -0.5, 0.21875, ((0, 8), (1, 4)))
    up_bias = centred(arg_keys[11], (FF,), 0.5, 3.0, ((0, 4),))
    down_weight = centred(arg_keys[12], (D, FF), FF ** -0.5, 0.109375, ((0, 8), (1, 4)))
    down_bias = centred(arg_keys[13], (D,), 0.3, 1.75)
    norm2_gain = jnp.clip(1.0 + 0.1 * jax.random.normal(arg_keys[14], (D,), jnp.float32), 0.5, 1.5).astype(jnp.bfloat16)
    norm2_bias = centred(arg_keys[15], (D,), 0.3, 1.75)
    out_cotangent = gaussian_with(arg_keys[16], (TOKENS, D), 1.0, 6.0, ((0, 32),), (0, 1, 32, 2.75))
    return {"tokens": tokens, "segment_ids": segment_ids, "memory_positions": memory_positions, "memory_rows": memory_rows, "qkv_weight": qkv_weight, "qv_bias": qv_bias, "out_weight": out_weight, "out_bias": out_bias, "norm1_gain": norm1_gain, "norm1_bias": norm1_bias, "up_weight": up_weight, "up_bias": up_bias, "down_weight": down_weight, "down_bias": down_bias, "norm2_gain": norm2_gain, "norm2_bias": norm2_bias, "out_cotangent": out_cotangent}


EPSILON = 1e-12
MASKED = -1e+30

@jax.custom_vjp
def low(v):
    return lax.optimization_barrier(v.astype(jnp.bfloat16)).astype(jnp.float32)

@jax.custom_vjp
def low_back(v):
    return v

def low_keep(v):
    return (low(v), None)

def low_pass(kept, grad):
    return (grad,)

def back_keep(v):
    return (v, None)

def back_low(kept, grad):
    return (low(grad),)
low.defvjp(low_keep, low_pass)
low_back.defvjp(back_keep, back_low)

def layer_norm(values, norm_gain, norm_shift):
    centre = values - lax.optimization_barrier(jnp.mean(values, axis=-1, keepdims=True))
    spread = lax.optimization_barrier(jnp.mean(centre * centre, axis=-1, keepdims=True))
    return centre * lax.rsqrt(spread + EPSILON) * norm_gain + norm_shift

def attention(query_all, key_all, value_all, segments):
    group_count = segments.shape[0]
    block_count = GROUP // QBLOCK

    def one_block(block_index):
        group_index = block_index // block_count
        within = block_index % block_count * QBLOCK
        first_row = group_index * GROUP + within
        query_rows = lax.dynamic_slice_in_dim(query_all, first_row, QBLOCK, 0)
        key_rows = lax.dynamic_slice_in_dim(key_all, group_index * GROUP, GROUP, 0)
        value_rows = lax.dynamic_slice_in_dim(value_all, group_index * GROUP, GROUP, 0)
        group_segments = lax.dynamic_index_in_dim(segments, group_index, 0, keepdims=False)
        query_segments = lax.dynamic_slice_in_dim(group_segments, within, QBLOCK, 0)
        visible = (group_segments[None, :] == 0) | (group_segments[None, :] == query_segments[:, None])
        scores = jnp.einsum('bhe,ghe->hbg', query_rows, key_rows, precision=lax.Precision.HIGHEST) * HD ** (-0.5)
        scores = low_back(jnp.where(visible[None], scores, MASKED))
        weights = low(jax.nn.softmax(scores, axis=-1))
        return jnp.einsum('hbg,ghe->bhe', weights, value_rows, precision=lax.Precision.HIGHEST)
    mixed = lax.map(jax.checkpoint(one_block), jnp.arange(group_count * block_count, dtype=jnp.int32))
    return mixed.reshape(-1, H, HD)

def forward_stretch(inputs, segments, positions, params):
    memory_rows, qkv_weight, qv_bias, out_weight, out_bias, norm1_gain, norm1_bias, up_weight, up_bias, down_weight, down_bias, norm2_gain, norm2_bias = params
    row_count = inputs.shape[0]
    group_count = segments.shape[0]
    targets = (positions + GROUP * jnp.arange(group_count, dtype=jnp.int32)[:, None]).reshape(-1)
    memory_picks = (jnp.arange(row_count, dtype=jnp.int32)[:, None] == targets[None, :]).astype(jnp.float32)
    memory_table = jnp.tile(memory_rows, (group_count, 1))
    start_rows = inputs + jnp.dot(memory_picks, memory_table, precision=lax.Precision.HIGHEST)
    inputs_low = low(start_rows)
    qkv_bias = jnp.concatenate([qv_bias[:, :HD], jnp.zeros((H, HD), jnp.float32), qv_bias[:, HD:]], axis=-1)
    projected = jnp.einsum('td,dhe->the', inputs_low, qkv_weight, precision=lax.Precision.HIGHEST) + qkv_bias
    projected = low(low_back(projected))
    head_mixed = attention(projected[..., :HD], projected[..., HD:2 * HD], projected[..., 2 * HD:], segments)
    head_mixed = low(low_back(head_mixed))
    attended = jnp.einsum('the,dhe->td', head_mixed, out_weight, precision=lax.Precision.HIGHEST) + out_bias
    attended = low_back(attended)
    hidden = layer_norm(start_rows + attended, norm1_gain, norm1_bias)
    pre_act = jnp.dot(low(hidden), up_weight, precision=lax.Precision.HIGHEST) + up_bias
    pre_act = low_back(pre_act)
    activated = low(jax.nn.gelu(pre_act, approximate=False))
    branch = jnp.einsum('tf,df->td', activated, down_weight, precision=lax.Precision.HIGHEST) + down_bias
    branch = low_back(branch)
    return layer_norm(hidden + branch, norm2_gain, norm2_bias)

def reference(tokens, segment_ids, memory_positions, memory_rows, qkv_weight, qv_bias, out_weight, out_bias, norm1_gain, norm1_bias, up_weight, up_bias, down_weight, down_bias, norm2_gain, norm2_bias, out_cotangent):
    params = tuple((item.astype(jnp.float32) for item in (memory_rows, qkv_weight, qv_bias, out_weight, out_bias, norm1_gain, norm1_bias, up_weight, up_bias, down_weight, down_bias, norm2_gain, norm2_bias)))
    stretch_rows = GROUPS_DP * GROUP
    stretch_count = TOKENS // stretch_rows
    token_stretches = tokens.astype(jnp.float32).reshape(stretch_count, stretch_rows, D)
    cotangent_stretches = out_cotangent.astype(jnp.float32).reshape(stretch_count, stretch_rows, D)
    segment_stretches = segment_ids.reshape(stretch_count, GROUPS_DP, GROUP)
    position_stretches = memory_positions.reshape(stretch_count, GROUPS_DP, MEM)
    zero_grads = jax.tree.map(jnp.zeros_like, params)

    def one_stretch(totals, items):
        stretch_inputs, stretch_cotangent, segments, positions = items

        def apply(inputs, weights):
            return forward_stretch(inputs, segments, positions, weights)
        outputs, pullback = jax.vjp(apply, stretch_inputs, params)
        grad_inputs, grad_params = pullback(stretch_cotangent)
        totals = jax.tree.map(jnp.add, totals, grad_params)
        return (totals, (outputs.astype(jnp.bfloat16), grad_inputs))
    totals, (outputs, grad_inputs) = lax.scan(one_stretch, zero_grads, (token_stretches, cotangent_stretches, segment_stretches, position_stretches))
    return (outputs.reshape(TOKENS, D), grad_inputs.reshape(TOKENS, D), totals[0], totals[1], totals[2], totals[3], totals[4], totals[5], totals[6], totals[7], totals[8], totals[9], totals[10], totals[11], totals[12])
```

```python
import jax
import jax.numpy as jnp
from jax import lax
from jax.experimental import pallas as pl
from jax.experimental.pallas import tpu as pltpu
from jax.sharding import PartitionSpec as P

EPSILON = 1e-12
TILE = 256
MASKED = -1e30
VMEM_MAX = 64 * 1024 * 1024 - 128 * 1024
NT = (((1,), (1,)), ((), ()))
NN = (((1,), (0,)), ((), ()))


def mm(a, b, dims=NN):
    return lax.dot_general(a, b, dims, preferred_element_type=jnp.float32)


def fold8(x):
    r = x.shape[0]
    return x.reshape(r // 8, 8, x.shape[1])


def head_masks(block):
    lane = lax.broadcasted_iota(jnp.int32, block.shape, 1)
    zero = jnp.zeros_like(block)
    return jnp.where(lane < 64, block, zero), jnp.where(lane < 64, zero, block)


def tile_visible(first_ref, last_ref, i, t):
    return (first_ref[t] == 0) | ((first_ref[t] <= last_ref[i]) & (last_ref[t] >= first_ref[i]))


def forward_kernel(first_ref, last_ref, q_ref, k_ref, v_ref, kseg_ref, qseg_ref, o_ref, lse_ref,
                   vt_ref, qm_ref, s_ref, m_ref, l_ref, acc_ref):
    i = pl.program_id(0)
    tiles = pl.num_programs(0)
    pairs = q_ref.shape[1] // 128
    heads = 2 * pairs

    @pl.when(i == 0)
    def _():
        def turn(t, c):
            rows = pl.ds(pl.multiple_of(t * TILE, TILE), TILE)
            vt_ref[t] = v_ref[rows, :].T
            return c
        lax.fori_loop(0, tiles, turn, 0)

    for g in range(pairs):
        a, b = head_masks(q_ref[:, 128 * g:128 * g + 128])
        qm_ref[2 * g] = a
        qm_ref[2 * g + 1] = b
    m_ref[...] = jnp.full_like(m_ref, MASKED)
    l_ref[...] = jnp.zeros_like(l_ref)
    acc_ref[...] = jnp.zeros_like(acc_ref)
    qseg = qseg_ref[0:1, :]

    def scores(t, c):
        @pl.when(tile_visible(first_ref, last_ref, i, t))
        def _():
            rows = pl.ds(pl.multiple_of(t * TILE, TILE), TILE)
            kseg = kseg_ref[rows, 0:1]
            seen = (kseg == 0) | (kseg == qseg)
            for h in range(heads):
                kp = k_ref[rows, 128 * (h // 2):128 * (h // 2) + 128]
                s = mm(kp, qm_ref[h], NT)
                s = jnp.where(seen, s, MASKED)
                s_ref[h, t] = s
                m_ref[h] = jnp.maximum(m_ref[h], jnp.max(fold8(s), axis=0))
        return c
    lax.fori_loop(0, tiles, scores, 0)
    for h in range(heads):
        m_ref[h] = jnp.broadcast_to(jnp.max(m_ref[h], axis=0, keepdims=True), (8, TILE))

    def mix(t, c):
        @pl.when(tile_visible(first_ref, last_ref, i, t))
        def _():
            for h in range(heads):
                p = jnp.exp(s_ref[h, t] - m_ref[h, 0:1, :])
                l_ref[h] = l_ref[h] + jnp.sum(fold8(p), axis=0)
                acc_ref[h] = acc_ref[h] + mm(vt_ref[t, 64 * h:64 * h + 64, :], p.astype(jnp.bfloat16))
        return c
    lax.fori_loop(0, tiles, mix, 0)
    for h in range(heads):
        total = jnp.sum(l_ref[h], axis=0, keepdims=True)
        lse_ref[h:h + 1, :] = m_ref[h, 0:1, :] + jnp.log(total)
        acc_ref[h] = acc_ref[h] / total
    for g in range(pairs):
        pair = jnp.concatenate([acc_ref[2 * g], acc_ref[2 * g + 1]], axis=0)
        o_ref[:, 128 * g:128 * g + 128] = pair.T.astype(jnp.bfloat16)


def attend_forward(q, k, v, seg):
    n, width = q.shape
    tiles = n // TILE
    heads = width // 64
    first = seg[::TILE]
    last = seg[TILE - 1::TILE]
    kseg = jnp.broadcast_to(seg[:, None], (n, 128))
    qseg = jnp.broadcast_to(seg[None, :], (8, n))
    whole = lambda shape: pl.BlockSpec(shape, lambda i, *_: (0,) * len(shape))
    return pl.pallas_call(
        forward_kernel,
        out_shape=(jax.ShapeDtypeStruct((n, width), jnp.bfloat16), jax.ShapeDtypeStruct((8, n), jnp.float32)),
        grid_spec=pltpu.PrefetchScalarGridSpec(
            num_scalar_prefetch=2, grid=(tiles,),
            in_specs=[pl.BlockSpec((TILE, width), lambda i, *_: (i, 0)), whole((n, width)), whole((n, width)),
                      whole((n, 128)), pl.BlockSpec((8, TILE), lambda i, *_: (0, i))],
            out_specs=[pl.BlockSpec((TILE, width), lambda i, *_: (i, 0)), pl.BlockSpec((8, TILE), lambda i, *_: (0, i))],
            scratch_shapes=[
                pltpu.VMEM((tiles, width, TILE), jnp.bfloat16),
                pltpu.VMEM((heads, TILE, 128), jnp.bfloat16),
                pltpu.VMEM((heads, tiles, TILE, TILE), jnp.float32),
                pltpu.VMEM((heads, 8, TILE), jnp.float32),
                pltpu.VMEM((heads, 8, TILE), jnp.float32),
                pltpu.VMEM((heads, 64, TILE), jnp.float32),
            ]),
        compiler_params=pltpu.CompilerParams(dimension_semantics=("arbitrary",), vmem_limit_bytes=VMEM_MAX),
        cost_estimate=pl.CostEstimate(flops=4 * n * n * width, bytes_accessed=8 * n * width, transcendentals=n * n * heads),
        name="attend_forward",
    )(first, last, q, k, v, kseg, qseg)


def backward_kernel(first_ref, last_ref, q_ref, do_ref, k_ref, v_ref, kseg_ref, qseg_ref, lse_ref,
                    dq_ref, dk_ref, dv_ref, kt_ref, qm_ref, dom_ref, p_ref, g_ref, delta_ref, dqt_ref, dka_ref, dva_ref):
    i = pl.program_id(0)
    tiles = pl.num_programs(0)
    pairs = q_ref.shape[1] // 128
    heads = 2 * pairs

    @pl.when(i == 0)
    def _():
        def turn(t, c):
            rows = pl.ds(pl.multiple_of(t * TILE, TILE), TILE)
            kt_ref[t] = k_ref[rows, :].T
            dka_ref[rows, :] = jnp.zeros((TILE, 128 * pairs), jnp.float32)
            dva_ref[rows, :] = jnp.zeros((TILE, 128 * pairs), jnp.float32)
            return c
        lax.fori_loop(0, tiles, turn, 0)

    for g in range(pairs):
        a, b = head_masks(q_ref[:, 128 * g:128 * g + 128])
        qm_ref[2 * g] = a
        qm_ref[2 * g + 1] = b
        a, b = head_masks(do_ref[:, 128 * g:128 * g + 128])
        dom_ref[2 * g] = a
        dom_ref[2 * g + 1] = b
    delta_ref[...] = jnp.zeros_like(delta_ref)
    dqt_ref[...] = jnp.zeros_like(dqt_ref)
    qseg = qseg_ref[0:1, :]

    def first_pass(t, c):
        @pl.when(tile_visible(first_ref, last_ref, i, t))
        def _():
            rows = pl.ds(pl.multiple_of(t * TILE, TILE), TILE)
            kseg = kseg_ref[rows, 0:1]
            seen = (kseg == 0) | (kseg == qseg)
            for g in range(pairs):
                cols = slice(128 * g, 128 * g + 128)
                kp = k_ref[rows, cols]
                vp = v_ref[rows, cols]
                part = None
                for h in (2 * g, 2 * g + 1):
                    s = mm(kp, qm_ref[h], NT)
                    p = jnp.where(seen, jnp.exp(s - lse_ref[h:h + 1, :]), 0.0)
                    d = mm(vp, dom_ref[h], NT)
                    p_ref[h, t] = p
                    g_ref[h, t] = d
                    delta_ref[h] = delta_ref[h] + jnp.sum(fold8(p * d), axis=0)
                    one = mm(p.astype(jnp.bfloat16), dom_ref[h])
                    part = one if part is None else part + one
                dva_ref[rows, cols] = dva_ref[rows, cols] + part
        return c
    lax.fori_loop(0, tiles, first_pass, 0)
    for h in range(heads):
        delta_ref[h] = jnp.broadcast_to(jnp.sum(delta_ref[h], axis=0, keepdims=True), (8, TILE))

    def second_pass(t, c):
        @pl.when(tile_visible(first_ref, last_ref, i, t))
        def _():
            rows = pl.ds(pl.multiple_of(t * TILE, TILE), TILE)
            for g in range(pairs):
                cols = slice(128 * g, 128 * g + 128)
                part = None
                for h in (2 * g, 2 * g + 1):
                    ds = (p_ref[h, t] * (g_ref[h, t] - delta_ref[h, 0:1, :])).astype(jnp.bfloat16)
                    one = mm(ds, qm_ref[h])
                    part = one if part is None else part + one
                    dqt_ref[h] = dqt_ref[h] + mm(kt_ref[t, 64 * h:64 * h + 64, :], ds)
                dka_ref[rows, cols] = dka_ref[rows, cols] + part
        return c
    lax.fori_loop(0, tiles, second_pass, 0)
    for g in range(pairs):
        pair = jnp.concatenate([dqt_ref[2 * g], dqt_ref[2 * g + 1]], axis=0)
        dq_ref[:, 128 * g:128 * g + 128] = (pair.T * 0.125).astype(jnp.bfloat16)

    @pl.when(i == tiles - 1)
    def _():
        dk_ref[...] = dka_ref[...].astype(jnp.bfloat16)
        dv_ref[...] = dva_ref[...].astype(jnp.bfloat16)


def attend_backward(q, k, v, do, lse, seg):
    n, width = q.shape
    tiles = n // TILE
    heads = width // 64
    first = seg[::TILE]
    last = seg[TILE - 1::TILE]
    kseg = jnp.broadcast_to(seg[:, None], (n, 128))
    qseg = jnp.broadcast_to(seg[None, :], (8, n))
    whole = lambda shape: pl.BlockSpec(shape, lambda i, *_: (0,) * len(shape))
    rows = pl.BlockSpec((TILE, width), lambda i, *_: (i, 0))
    stat = pl.BlockSpec((8, TILE), lambda i, *_: (0, i))
    out = jax.ShapeDtypeStruct((n, width), jnp.bfloat16)
    return pl.pallas_call(
        backward_kernel,
        out_shape=(out, out, out),
        grid_spec=pltpu.PrefetchScalarGridSpec(
            num_scalar_prefetch=2, grid=(tiles,),
            in_specs=[rows, rows, whole((n, width)), whole((n, width)), whole((n, 128)), stat, stat],
            out_specs=[rows, whole((n, width)), whole((n, width))],
            scratch_shapes=[
                pltpu.VMEM((tiles, width, TILE), jnp.bfloat16),
                pltpu.VMEM((heads, TILE, 128), jnp.bfloat16),
                pltpu.VMEM((heads, TILE, 128), jnp.bfloat16),
                pltpu.VMEM((heads, tiles, TILE, TILE), jnp.float32),
                pltpu.VMEM((heads, tiles, TILE, TILE), jnp.float32),
                pltpu.VMEM((heads, 8, TILE), jnp.float32),
                pltpu.VMEM((heads, 64, TILE), jnp.float32),
                pltpu.VMEM((n, width), jnp.float32),
                pltpu.VMEM((n, width), jnp.float32),
            ]),
        compiler_params=pltpu.CompilerParams(dimension_semantics=("arbitrary",), vmem_limit_bytes=VMEM_MAX),
        cost_estimate=pl.CostEstimate(flops=10 * n * n * width, bytes_accessed=14 * n * width, transcendentals=n * n * heads),
        name="attend_backward",
    )(first, last, q, do, k, v, kseg, qseg, lse)


def layer_norm(values, norm_gain, norm_shift):
    centre = values - jnp.mean(values, axis=-1, keepdims=True)
    spread = jnp.mean(centre * centre, axis=-1, keepdims=True)
    return centre * lax.rsqrt(spread + EPSILON) * norm_gain + norm_shift


def gelu_exact(values):
    return jax.nn.gelu(values, approximate=False)


AXES = ("dp", "tensor")


class Grid:
    def __init__(self, dp, tensor):
        self.dp, self.tensor = dp, tensor
        factors, rest = [2], dp // 2
        while rest > 8:
            factors.insert(0, 4)
            rest //= 4
        if rest > 1:
            factors.insert(0, rest)
        self.factors = factors

    def digit(self, j):
        stride = 1
        for f in self.factors[j + 1:]:
            stride *= f
        return stride, self.factors[j]

    def my_digit(self, j):
        stride, f = self.digit(j)
        return lax.axis_index("dp") // stride % f

    def turn(self, value, j, k):
        stride, f = self.digit(j)
        pairs = []
        for d in range(self.dp):
            g = d // stride % f
            to = d + ((g + k) % f - g) * stride
            for t in range(self.tensor):
                pairs.append((d * self.tensor + t, to * self.tensor + t))
        return lax.ppermute(value, AXES, pairs)

    def swap_dp(self, value, bit):
        pairs = [(d * self.tensor + t, (d ^ bit) * self.tensor + t) for d in range(self.dp) for t in range(self.tensor)]
        return lax.ppermute(value, AXES, pairs)

    def swap(self, value, bit):
        pairs = [(d * self.tensor + t, d * self.tensor + (t ^ bit)) for d in range(self.dp) for t in range(self.tensor)]
        return lax.ppermute(value, AXES, pairs)

    def gather_stage(self, value, j, axis):
        _, f = self.digit(j)
        g = self.my_digit(j)
        got = [value] + [self.turn(value, j, k) for k in range(1, f)]
        if f == 2:
            lower = jnp.where(g == 0, got[0], got[1])
            upper = jnp.where(g == 0, got[1], got[0])
            return jnp.stack([lower, upper], axis=axis)
        ring = got[::-1]
        return lax.dynamic_slice_in_dim(jnp.stack(ring + ring[:-1], axis=axis), f - 1 - g, f, axis)

    def gather(self, shard, outer_first=False):
        count = len(self.factors)
        value = shard
        for j in range(count - 1):
            value = self.gather_stage(value, j, j)
        if outer_first:
            value = jnp.stack([value, self.swap(value, 2)])
            value = self.gather_stage(value, count - 1, count)
            return value.reshape(2, -1, shard.shape[-1])
        value = self.gather_stage(value, count - 1, count - 1)
        value = value.reshape(-1, shard.shape[-1])
        return jnp.stack([value, self.swap(value, 2)])

    def reduce_stage(self, value, j, axis):
        _, f = self.digit(j)
        g = self.my_digit(j)
        total = lax.dynamic_index_in_dim(value, g, axis, keepdims=False).astype(jnp.float32)
        for k in range(1, f):
            part = lax.dynamic_index_in_dim(value, (g + k) % f, axis, keepdims=False)
            total = total + self.turn(part.astype(jnp.bfloat16), j, k).astype(jnp.float32)
        return total

    def reduce(self, parts, outer_first=True):
        count = len(self.factors)
        columns = parts.shape[-1]
        value = parts
        if outer_first:
            value = value[0].astype(jnp.float32) + self.swap(value[1].astype(jnp.bfloat16), 2).astype(jnp.float32)
            value = value.reshape(*self.factors, -1, columns)
            value = self.reduce_stage(value, count - 1, count - 1)
        else:
            value = value.reshape(2, *self.factors, -1, columns)
            value = self.reduce_stage(value, count - 1, count)
            value = value[0] + self.swap(value[1].astype(jnp.bfloat16), 2).astype(jnp.float32)
        for j in reversed(range(count - 1)):
            value = self.reduce_stage(value, j, j)
        return value

    def total(self, vector):
        for bit in (1, 2):
            vector = vector + self.swap(vector, bit)
        bit = 1
        while bit < self.dp:
            vector = vector + self.swap_dp(vector, bit)
            bit *= 2
        return vector


def shards(grid, tokens, segment_ids, memory_positions, memory_rows, qkv_weight, qv_bias, out_weight, out_bias,
           norm1_gain, norm1_bias, up_weight, up_bias, down_weight, down_bias, norm2_gain, norm2_bias, out_cotangent):
    f32, bf16 = jnp.float32, jnp.bfloat16
    rows, width = tokens.shape
    group_len = segment_ids.shape[1]
    tensor = lax.axis_index("tensor")
    inner, outer = tensor % 2, tensor // 2
    slice_rows = qkv_weight.shape[0]
    heads = qkv_weight.shape[1]
    hd = 64
    hw = heads * hd
    units = up_weight.shape[1]

    segments = lax.dynamic_index_in_dim(segment_ids, outer, 0, keepdims=False)
    positions = lax.dynamic_index_in_dim(memory_positions, outer, 0, keepdims=False)
    row_place = inner * rows + jnp.arange(rows, dtype=jnp.int32)
    picks = (row_place[:, None] == positions[None, :])
    x0 = tokens.astype(f32) + jnp.dot(picks.astype(bf16), memory_rows, preferred_element_type=f32)
    xl = x0.astype(bf16)

    shard_qkv = qkv_weight.reshape(slice_rows, heads, 3, hd).transpose(0, 2, 1, 3).reshape(slice_rows, 3 * hw)
    w_qkv = grid.gather(shard_qkv)
    w_qkv = w_qkv.reshape(2, width, 3, hw).transpose(1, 2, 0, 3).reshape(width, 6 * hw)
    other = grid.swap(xl, 1)
    x_all = jnp.concatenate([jnp.where(inner == 0, xl, other), jnp.where(inner == 0, other, xl)])
    w_out = grid.gather(out_weight.reshape(slice_rows, hw), True)
    w_up = grid.gather(up_weight)
    w_down = grid.gather(down_weight, True)

    small = jnp.concatenate([qv_bias.reshape(-1), up_bias])
    small_other = grid.swap(small, 2)
    qv = jnp.stack([small[:2 * hw], small_other[:2 * hw]]).reshape(2, heads, 2, hd).astype(f32)
    b_up = jnp.concatenate([small[2 * hw:], small_other[2 * hw:]])
    b_up = jnp.stack([b_up, grid.swap(b_up, 1)]).astype(f32)
    b_qkv = jnp.stack([qv[:, :, 0], jnp.zeros_like(qv[:, :, 0]), qv[:, :, 1]], 0).reshape(6 * hw)

    joined = lambda w: w.transpose(1, 0, 2).reshape(width, -1)
    w_out, w_up, w_down = joined(w_out), joined(w_up), joined(w_down)
    w_out = (w_out, grid.swap(w_out, 1))
    w_up = (w_up, grid.swap(w_up, 1))
    w_down = (w_down, grid.swap(w_down, 1))

    qkv = (jnp.dot(x_all, w_qkv, preferred_element_type=f32) + b_qkv).astype(bf16)
    q = qkv[:, :2 * hw] * jnp.asarray(0.125, bf16)
    k = qkv[:, 2 * hw:4 * hw]
    v = qkv[:, 4 * hw:]
    mixed, lse = attend_forward(q, k, v, segments)
    halves = mixed.reshape(2, rows, 2 * hw)
    o_own = lax.dynamic_index_in_dim(halves, inner, 0, keepdims=False)
    o_got = grid.swap(lax.dynamic_index_in_dim(halves, 1 - inner, 0, keepdims=False), 1)
    o = (o_own, o_got)

    attended = out_bias.astype(f32)
    for side in range(2):
        attended = attended + mm(o[side], w_out[side], NT)
    r1 = x0 + attended
    g1, s1 = norm1_gain.astype(f32), norm1_bias.astype(f32)
    g2, s2 = norm2_gain.astype(f32), norm2_bias.astype(f32)
    h1 = layer_norm(r1, g1, s1)
    hl = h1.astype(bf16)
    u = [mm(hl, w_up[side]) + b_up[side] for side in range(2)]
    z = [gelu_exact(one).astype(bf16) for one in u]
    r2 = h1 + down_bias.astype(f32)
    for side in range(2):
        r2 = r2 + mm(z[side], w_down[side], NT)
    block_out = layer_norm(r2, g2, s2).astype(bf16)
    cot = out_cotangent.astype(f32)
    dr2, dg2, ds2 = jax.vjp(layer_norm, r2, g2, s2)[1](cot)
    dfl = dr2.astype(bf16)
    d_down_bias = jnp.sum(dfl.astype(f32), axis=0)
    TN = (((0,), (0,)), ((), ()))
    g_down = [mm(dfl, z[side], TN) for side in range(2)]
    dul = [jax.vjp(gelu_exact, u[side])[1](mm(dfl, w_down[side]))[0].astype(bf16) for side in range(2)]
    g_up = [mm(hl, dul[side], TN) for side in range(2)]
    d_up_bias = [jnp.sum(dul[side].astype(f32), axis=0) for side in range(2)]
    dh1 = dr2
    for side in range(2):
        dh1 = dh1 + mm(dul[side], w_up[side], NT)
    dr1, dg1, ds1 = jax.vjp(layer_norm, r1, g1, s1)[1](dh1)
    dal = dr1.astype(bf16)
    d_out_bias = jnp.sum(dal.astype(f32), axis=0)
    g_out = [mm(dal, o[side], TN) for side in range(2)]
    dol = [mm(dal, w_out[side]).astype(bf16) for side in range(2)]
    got = grid.swap(dol[1], 1)
    do_all = jnp.concatenate([jnp.where(inner == 0, dol[0], got), jnp.where(inner == 0, got, dol[0])])

    def spread(pair, outer_first):
        own = pair[0] + grid.swap(pair[1].astype(bf16), 1).astype(f32)
        own = own.reshape(width, 2, -1).transpose(1, 0, 2)
        return grid.reduce(own, outer_first)

    grad_down = spread(g_down, True)
    grad_up = spread(g_up, False)
    grad_out = spread(g_out, True)

    dq, dk, dv = attend_backward(q, k, v, do_all, lse, segments)
    d_qkv = jnp.concatenate([dq, dk, dv], axis=-1)
    g_qkv = mm(x_all, d_qkv, TN)
    d_bias = jnp.sum(d_qkv.astype(f32), axis=0).reshape(3, 2, hw)
    part = mm(d_qkv, w_qkv, NT).reshape(2, rows, width)
    mine = lax.dynamic_index_in_dim(part, inner, 0, keepdims=False)
    theirs = lax.dynamic_index_in_dim(part, 1 - inner, 0, keepdims=False).astype(bf16)
    grad_tokens = mine + grid.swap(theirs, 1).astype(f32) + dr1
    grad_qkv = grid.reduce(g_qkv.reshape(width, 3, 2, hw).transpose(2, 0, 1, 3).reshape(2, width, 3 * hw), True)
    grad_qkv = grad_qkv.reshape(slice_rows, 3, heads, hd).transpose(0, 2, 1, 3).reshape(slice_rows, heads, 3 * hd)
    grad_memory = jnp.dot(picks.astype(f32).T, grad_tokens, precision=lax.Precision.HIGHEST)

    order = jnp.arange(4, dtype=jnp.int32) ^ tensor
    up_parts = jnp.concatenate(d_up_bias).reshape(2, 2, units).transpose(0, 1, 2)
    up_parts = jnp.stack([up_parts[0, 0], up_parts[1, 0], up_parts[0, 1], up_parts[1, 1]])[order]
    nothing = jnp.zeros_like(d_bias[0, 0])
    take = lambda o_: jnp.stack([d_bias[0, o_].reshape(heads, hd), d_bias[2, o_].reshape(heads, hd)], 1).reshape(-1)
    blank = jnp.zeros((2 * hw,), f32)
    qv_parts = jnp.stack([take(0), blank, take(1), blank])[order]
    pieces = [grad_memory.reshape(-1), d_out_bias, dg1, ds1, d_down_bias, dg2, ds2, up_parts.reshape(-1), qv_parts.reshape(-1)]
    summed = grid.total(jnp.concatenate(pieces))
    outs, at = [], 0
    for piece in pieces:
        outs.append(lax.slice_in_dim(summed, at, at + piece.size))
        at += piece.size
    t_memory, t_out_bias, t_g1, t_s1, t_down_bias, t_g2, t_s2, t_up, t_qv = outs
    grad_up_bias = lax.dynamic_index_in_dim(t_up.reshape(4, units), tensor, 0, keepdims=False)
    grad_qv = lax.dynamic_index_in_dim(t_qv.reshape(4, heads, 2 * hd), tensor, 0, keepdims=False)
    return (block_out, grad_tokens, t_memory.reshape(-1, width), grad_qkv, grad_qv,
            grad_out.reshape(slice_rows, heads, hd), t_out_bias, t_g1, t_s1, grad_up, grad_up_bias, grad_down,
            t_down_bias, t_g2, t_s2)


def solution(mesh):
    grid = Grid(mesh.shape["dp"], mesh.shape["tensor"])
    tokens, dp, none = P(AXES, None), P("dp", None), P()
    heads, matrix = P("dp", "tensor", None), P("dp", "tensor")
    in_specs = (tokens, dp, dp, none, heads, P("tensor", None), heads, none, none, none, matrix, P("tensor"), matrix,
                none, none, none, tokens)
    out_specs = (tokens, tokens, none, heads, P("tensor", None), heads, none, none, none, matrix, P("tensor"), matrix,
                 none, none, none)

    def run(*args):
        return shards(grid, *args)

    return jax.shard_map(run, mesh=mesh, in_specs=in_specs, out_specs=out_specs, check_vma=False)
```

```python
import functools

import jax
import jax.numpy as jnp
from jax import lax
from jax.experimental import pallas as pl
from jax.experimental.pallas import tpu as pltpu
from jax.sharding import PartitionSpec as P

EPSILON = 1e-12
TILE = 256
MASKED = -1e30
VMEM_MAX = 64 * 1024 * 1024 - 128 * 1024
NT = (((1,), (1,)), ((), ()))
NN = (((1,), (0,)), ((), ()))


def mm(a, b, dims=NN):
    return lax.dot_general(a, b, dims, preferred_element_type=jnp.float32)


def fold8(x):
    r = x.shape[0]
    return x.reshape(r // 8, 8, x.shape[1])


def head_masks(block):
    lane = lax.broadcasted_iota(jnp.int32, block.shape, 1)
    zero = jnp.zeros_like(block)
    return jnp.where(lane < 64, block, zero), jnp.where(lane < 64, zero, block)


def tile_visible(first_ref, last_ref, i, t):
    return (first_ref[t] == 0) | ((first_ref[t] <= last_ref[i]) & (last_ref[t] >= first_ref[i]))


def forward_kernel(first_ref, last_ref, q_ref, k_ref, v_ref, kseg_ref, qseg_ref, o_ref, lse_ref,
                   vt_ref, qm_ref, s_ref, m_ref, l_ref, acc_ref):
    i = pl.program_id(0)
    tiles = pl.num_programs(0)
    pairs = q_ref.shape[1] // 128
    heads = 2 * pairs

    @pl.when(i == 0)
    def _():
        def turn(t, c):
            rows = pl.ds(pl.multiple_of(t * TILE, TILE), TILE)
            vt_ref[t] = v_ref[rows, :].T
            return c
        lax.fori_loop(0, tiles, turn, 0)

    for g in range(pairs):
        a, b = head_masks(q_ref[:, 128 * g:128 * g + 128])
        qm_ref[2 * g] = a
        qm_ref[2 * g + 1] = b
    m_ref[...] = jnp.full_like(m_ref, MASKED)
    l_ref[...] = jnp.zeros_like(l_ref)
    acc_ref[...] = jnp.zeros_like(acc_ref)
    qseg = qseg_ref[0:1, :]

    def scores(t, c):
        @pl.when(tile_visible(first_ref, last_ref, i, t))
        def _():
            rows = pl.ds(pl.multiple_of(t * TILE, TILE), TILE)
            kseg = kseg_ref[rows, 0:1]
            seen = (kseg == 0) | (kseg == qseg)
            for h in range(heads):
                kp = k_ref[rows, 128 * (h // 2):128 * (h // 2) + 128]
                s = mm(kp, qm_ref[h], NT)
                s = jnp.where(seen, s, MASKED)
                s_ref[h, t] = s
                m_ref[h] = jnp.maximum(m_ref[h], jnp.max(fold8(s), axis=0))
        return c
    lax.fori_loop(0, tiles, scores, 0)
    for h in range(heads):
        m_ref[h] = jnp.broadcast_to(jnp.max(m_ref[h], axis=0, keepdims=True), (8, TILE))

    def mix(t, c):
        @pl.when(tile_visible(first_ref, last_ref, i, t))
        def _():
            for h in range(heads):
                p = jnp.exp(s_ref[h, t] - m_ref[h, 0:1, :])
                l_ref[h] = l_ref[h] + jnp.sum(fold8(p), axis=0)
                acc_ref[h] = acc_ref[h] + mm(vt_ref[t, 64 * h:64 * h + 64, :], p.astype(jnp.bfloat16))
        return c
    lax.fori_loop(0, tiles, mix, 0)
    for h in range(heads):
        total = jnp.sum(l_ref[h], axis=0, keepdims=True)
        lse_ref[h:h + 1, :] = m_ref[h, 0:1, :] + jnp.log(total)
        acc_ref[h] = acc_ref[h] / total
    for g in range(pairs):
        pair = jnp.concatenate([acc_ref[2 * g], acc_ref[2 * g + 1]], axis=0)
        o_ref[:, 128 * g:128 * g + 128] = pair.T.astype(jnp.bfloat16)


def attend_forward(q, k, v, seg):
    n, width = q.shape
    tiles = n // TILE
    heads = width // 64
    first = seg[::TILE]
    last = seg[TILE - 1::TILE]
    kseg = jnp.broadcast_to(seg[:, None], (n, 128))
    qseg = jnp.broadcast_to(seg[None, :], (8, n))
    whole = lambda shape: pl.BlockSpec(shape, lambda i, *_: (0,) * len(shape))
    return pl.pallas_call(
        forward_kernel,
        out_shape=(jax.ShapeDtypeStruct((n, width), jnp.bfloat16), jax.ShapeDtypeStruct((8, n), jnp.float32)),
        grid_spec=pltpu.PrefetchScalarGridSpec(
            num_scalar_prefetch=2, grid=(tiles,),
            in_specs=[pl.BlockSpec((TILE, width), lambda i, *_: (i, 0)), whole((n, width)), whole((n, width)),
                      whole((n, 128)), pl.BlockSpec((8, TILE), lambda i, *_: (0, i))],
            out_specs=[pl.BlockSpec((TILE, width), lambda i, *_: (i, 0)), pl.BlockSpec((8, TILE), lambda i, *_: (0, i))],
            scratch_shapes=[
                pltpu.VMEM((tiles, width, TILE), jnp.bfloat16),
                pltpu.VMEM((heads, TILE, 128), jnp.bfloat16),
                pltpu.VMEM((heads, tiles, TILE, TILE), jnp.float32),
                pltpu.VMEM((heads, 8, TILE), jnp.float32),
                pltpu.VMEM((heads, 8, TILE), jnp.float32),
                pltpu.VMEM((heads, 64, TILE), jnp.float32),
            ]),
        compiler_params=pltpu.CompilerParams(dimension_semantics=("arbitrary",), vmem_limit_bytes=VMEM_MAX),
        cost_estimate=pl.CostEstimate(flops=4 * n * n * width, bytes_accessed=8 * n * width, transcendentals=n * n * heads),
        name="attend_forward",
    )(first, last, q, k, v, kseg, qseg)


def backward_kernel(base, first_ref, last_ref, q_ref, do_ref, k_ref, v_ref, kseg_ref, qseg_ref, lse_ref,
                    d_ref, kt_ref, qm_ref, dom_ref, p_ref, g_ref, delta_ref, dqt_ref, dka_ref, dva_ref):
    i = pl.program_id(0)
    tiles = pl.num_programs(0)
    pairs = q_ref.shape[1] // 128
    heads = 2 * pairs

    @pl.when(i == 0)
    def _():
        def turn(t, c):
            rows = pl.ds(pl.multiple_of(t * TILE, TILE), TILE)
            kt_ref[t] = k_ref[rows, :].T
            dka_ref[rows, :] = jnp.zeros((TILE, 128 * pairs), jnp.float32)
            dva_ref[rows, :] = jnp.zeros((TILE, 128 * pairs), jnp.float32)
            return c
        lax.fori_loop(0, tiles, turn, 0)

    for g in range(pairs):
        a, b = head_masks(q_ref[:, 128 * g:128 * g + 128])
        qm_ref[2 * g] = a
        qm_ref[2 * g + 1] = b
        a, b = head_masks(do_ref[:, 128 * g:128 * g + 128])
        dom_ref[2 * g] = a
        dom_ref[2 * g + 1] = b
    delta_ref[...] = jnp.zeros_like(delta_ref)
    dqt_ref[...] = jnp.zeros_like(dqt_ref)
    qseg = qseg_ref[0:1, :]

    def first_pass(t, c):
        @pl.when(tile_visible(first_ref, last_ref, i, t))
        def _():
            rows = pl.ds(pl.multiple_of(t * TILE, TILE), TILE)
            kseg = kseg_ref[rows, 0:1]
            seen = (kseg == 0) | (kseg == qseg)
            for g in range(pairs):
                cols = slice(128 * g, 128 * g + 128)
                kp = k_ref[rows, cols]
                vp = v_ref[rows, cols]
                part = None
                for h in (2 * g, 2 * g + 1):
                    s = mm(kp, qm_ref[h], NT)
                    p = jnp.where(seen, jnp.exp(s - lse_ref[base + h:base + h + 1, :]), 0.0)
                    d = mm(vp, dom_ref[h], NT)
                    p_ref[h, t] = p
                    g_ref[h, t] = d
                    delta_ref[h] = delta_ref[h] + jnp.sum(fold8(p * d), axis=0)
                    one = mm(p.astype(jnp.bfloat16), dom_ref[h])
                    part = one if part is None else part + one
                dva_ref[rows, cols] = dva_ref[rows, cols] + part
        return c
    lax.fori_loop(0, tiles, first_pass, 0)
    for h in range(heads):
        delta_ref[h] = jnp.broadcast_to(jnp.sum(delta_ref[h], axis=0, keepdims=True), (8, TILE))

    def second_pass(t, c):
        @pl.when(tile_visible(first_ref, last_ref, i, t))
        def _():
            rows = pl.ds(pl.multiple_of(t * TILE, TILE), TILE)
            for g in range(pairs):
                cols = slice(128 * g, 128 * g + 128)
                part = None
                for h in (2 * g, 2 * g + 1):
                    ds = (p_ref[h, t] * (g_ref[h, t] - delta_ref[h, 0:1, :])).astype(jnp.bfloat16)
                    one = mm(ds, qm_ref[h])
                    part = one if part is None else part + one
                    dqt_ref[h] = dqt_ref[h] + mm(kt_ref[t, 64 * h:64 * h + 64, :], ds)
                dka_ref[rows, cols] = dka_ref[rows, cols] + part
        return c
    lax.fori_loop(0, tiles, second_pass, 0)
    for g in range(pairs):
        pair = jnp.concatenate([dqt_ref[2 * g], dqt_ref[2 * g + 1]], axis=0)
        own = pl.ds(pl.multiple_of(i * TILE, TILE), TILE)
        d_ref[own, 128 * g:128 * g + 128] = (pair.T * 0.125).astype(jnp.bfloat16)

    @pl.when(i == tiles - 1)
    def _():
        d_ref[:, 128 * pairs:256 * pairs] = dka_ref[...].astype(jnp.bfloat16)
        d_ref[:, 256 * pairs:384 * pairs] = dva_ref[...].astype(jnp.bfloat16)


def attend_backward(g, q, k, v, do, lse, seg):
    n, width = q.shape[0], 128
    tiles = n // TILE
    heads = width // 64
    first = seg[::TILE]
    last = seg[TILE - 1::TILE]
    kseg = jnp.broadcast_to(seg[:, None], (n, 128))
    qseg = jnp.broadcast_to(seg[None, :], (8, n))
    whole = lambda shape: pl.BlockSpec(shape, lambda i, *_: (0,) * len(shape))
    rows = pl.BlockSpec((TILE, width), lambda i, *_: (i, g))
    column = pl.BlockSpec((n, width), lambda i, *_: (0, g))
    stat = pl.BlockSpec((8, TILE), lambda i, *_: (0, i))
    return pl.pallas_call(
        functools.partial(backward_kernel, 2 * g),
        out_shape=jax.ShapeDtypeStruct((n, 3 * width), jnp.bfloat16),
        grid_spec=pltpu.PrefetchScalarGridSpec(
            num_scalar_prefetch=2, grid=(tiles,),
            in_specs=[rows, rows, column, column, whole((n, 128)), stat, stat],
            out_specs=whole((n, 3 * width)),
            scratch_shapes=[
                pltpu.VMEM((tiles, width, TILE), jnp.bfloat16),
                pltpu.VMEM((heads, TILE, 128), jnp.bfloat16),
                pltpu.VMEM((heads, TILE, 128), jnp.bfloat16),
                pltpu.VMEM((heads, tiles, TILE, TILE), jnp.float32),
                pltpu.VMEM((heads, tiles, TILE, TILE), jnp.float32),
                pltpu.VMEM((heads, 8, TILE), jnp.float32),
                pltpu.VMEM((heads, 64, TILE), jnp.float32),
                pltpu.VMEM((n, width), jnp.float32),
                pltpu.VMEM((n, width), jnp.float32),
            ]),
        compiler_params=pltpu.CompilerParams(dimension_semantics=("arbitrary",), vmem_limit_bytes=VMEM_MAX),
        cost_estimate=pl.CostEstimate(flops=10 * n * n * width, bytes_accessed=14 * n * width, transcendentals=n * n * heads),
        name="attend_backward",
    )(first, last, q, do, k, v, kseg, qseg, lse)


BLOCK = 256
STRIP = 64


def normal_cdf_parts(u):
    v = u * 0.7071067811865476
    c = jnp.clip(v, -3.832506856900711, 3.832506856900711)
    c2 = c * c
    top = 0.00022905065861350646
    for a in (0.0034082910107109506, 0.050955695062380861, 0.18520832239976145, 1.128379143519084):
        top = top * c2 + a
    low = -1.1791602954361697e-7
    for b in (0.000023547966471313185, 0.0010179625278914885, 0.014070470171167667, 0.11098505178285362,
              0.49746925110067538, 1.0):
        low = low * c2 + b
    cdf = 0.5 + 0.5 * (c * top / low)
    slope = jnp.exp(-(v * v)) * (u * 0.3989422804014327)
    return u * cdf, cdf + slope


def middle_kernel(pieces, o_all, x0, outs, ups, downs, cot, vec_ref, bup_ref,
                  block_out, dr1, do_all, g_down, g_up, g_out, sums_ref, upsum_ref,
                  o_ref, raw_ref, wo_ref, wu_ref, wd_ref, hat_ref, inv_ref, acc_ref, hl_ref, hlt_ref, gp_ref, z_ref, c_ref,
                  df_ref, dft_ref, y_ref, st_ref, su_ref, ru_ref, rd_ref, go_ref, rgo_ref, u0_ref, u1_ref,
                  sem, osem, send, recv):
    f32, bf16 = jnp.float32, jnp.bfloat16
    rows, width = hat_ref.shape
    blocks = rows // BLOCK
    part = wu_ref.shape[2]
    bf = lambda a: a.astype(bf16)
    dp, tensor = lax.axis_index("dp"), lax.axis_index("tensor")
    inner = tensor % 2
    partner = (dp, tensor + 1 - 2 * inner)
    mine = pl.multiple_of(inner * rows, 1024)
    theirs = pl.multiple_of((1 - inner) * rows, 1024)
    greet([partner])

    def remote(n, src, dst):
        return pltpu.make_async_remote_copy(src, dst, send.at[n], recv.at[n], device_id=partner,
                                            device_id_type=pl.DeviceIdType.MESH)

    swap_o = remote(0, o_all.at[pl.ds(theirs, rows), :], o_ref.at[1])
    swap_o.start()
    count = [0]

    def load(src, dst):
        copy = pltpu.make_async_copy(src, dst, sem.at[count[0]])
        count[0] += 1
        copy.start()
        return copy

    def weight(sources, dst):
        if not pieces:
            return [load(sources[0].at[o], dst.at[o]) for o in range(2)]
        digit = dp % 2
        made = []
        for o in range(2):
            for zi in range(sources[0].shape[1]):
                for n in range(2):
                    place = 2 * zi + (digit if n == 0 else 1 - digit)
                    r = sources[n].shape[2]
                    made.append(load(sources[n].at[o, zi], dst.at[o, pl.ds(pl.multiple_of(place * r, r), r), :]))
        return made

    first = [load(o_all.at[pl.ds(mine, rows), :], o_ref.at[0]), load(x0, hat_ref)] + weight(outs, raw_ref.at[0])
    if pieces:
        second = [load(ups[o], wu_ref.at[o]) for o in range(2)]
    else:
        second = [load(ups[0].at[o], wu_ref.at[o]) for o in range(2)]
    second = second + weight(downs, wd_ref)
    late = load(cot, c_ref)
    vec = lambda n: vec_ref[n:n + 1, :]
    sums_ref[...] = jnp.zeros_like(sums_ref)
    upsum_ref[...] = jnp.zeros_like(upsum_ref)
    for copy in first:
        copy.wait()
    swaps = [remote(1, raw_ref.at[0], raw_ref.at[1])]
    swaps[0].start()
    for copy in second:
        copy.wait()
    for o in range(2):
        swaps.append(remote(2 + 2 * o, wu_ref.at[o], wu_ref.at[2 + o]))
        swaps.append(remote(3 + 2 * o, wd_ref.at[o], wd_ref.at[2 + o]))
    for copy in swaps[1:]:
        copy.start()
    lane = lax.broadcasted_iota(jnp.int32, (width, 128), 1)

    def order_heads(side):
        wo_ref[side, :, 0:128] = raw_ref[side, 0, :, 0:128]
        wo_ref[side, :, 128:256] = raw_ref[side, 1, :, 0:128]
        upper = pltpu.roll(raw_ref[side, 1, :, 128:256].astype(f32), 64, 1)
        wo_ref[side, :, 256:384] = bf(jnp.where(lane < 64, raw_ref[side, 0, :, 128:256].astype(f32), upper))
    order_heads(0)
    swaps[0].wait()
    order_heads(1)
    swap_o.wait()

    def strips(body):
        def run(s, carry):
            body(pl.ds(pl.multiple_of(s * STRIP, STRIP), STRIP))
            return carry
        lax.fori_loop(0, rows // STRIP, run, 0)

    def add_sum(n, value):
        sums_ref[n] = sums_ref[n] + jnp.sum(fold(value), axis=0)

    def fold(value):
        return value.reshape(value.shape[0] // 8, 8, value.shape[1])

    def mean(value):
        return jnp.sum(value, axis=-1, keepdims=True) * (1.0 / width)

    def project(b, carry):
        r = pl.ds(pl.multiple_of(b * BLOCK, BLOCK), BLOCK)
        acc_ref[r, :] = mm(o_ref[0, r, :], wo_ref[0], NT) + mm(o_ref[1, r, :], wo_ref[1], NT)
        return carry
    lax.fori_loop(0, blocks, project, 0)

    def first_norm(r):
        r1 = hat_ref[r, :] + (acc_ref[r, :] + vec(0))
        centre = r1 - mean(r1)
        inv = lax.rsqrt(mean(centre * centre) + EPSILON)
        hat = centre * inv
        hat_ref[r, :] = hat
        inv_ref[r, :] = inv
        hl_ref[r, :] = bf(hat * vec(1) + vec(2))
    strips(first_norm)
    for b in range(blocks):
        hlt_ref[:, BLOCK * b:BLOCK * b + BLOCK] = hl_ref[BLOCK * b:BLOCK * b + BLOCK, :].T
    acc_ref[...] = jnp.zeros_like(acc_ref)

    bufs = (u0_ref, u1_ref)

    def forward(j, carry):
        for o in range(2):
            @pl.when(j == 2 + o)
            def _(o=o):
                swaps[1 + 2 * o].wait()
                swaps[2 + 2 * o].wait()

        def lift(b):
            bufs[b % 2][...] = mm(hl_ref[BLOCK * b:BLOCK * b + BLOCK, :], wu_ref[j]) + bup_ref[j]
        lift(0)
        for b in range(blocks):
            if b + 1 < blocks:
                lift(b + 1)
            r = slice(BLOCK * b, BLOCK * b + BLOCK)
            for i in range(0, BLOCK, 32):
                for w in range(0, part, 256):
                    z, gp = normal_cdf_parts(bufs[b % 2][i:i + 32, w:w + 256])
                    z_ref[j, BLOCK * b + i:BLOCK * b + i + 32, w:w + 256] = bf(z)
                    gp_ref[j, BLOCK * b + i:BLOCK * b + i + 32, w:w + 256] = gp
            acc_ref[r, :] = acc_ref[r, :] + mm(z_ref[j, r, :], wd_ref[j], NT)
        return carry
    lax.fori_loop(0, 4, forward, 0)
    late.wait()

    def second_norm(r):
        h1 = hat_ref[r, :] * vec(1) + vec(2)
        r2 = h1 + (acc_ref[r, :] + vec(3))
        centre = r2 - mean(r2)
        inv = lax.rsqrt(mean(centre * centre) + EPSILON)
        hat = centre * inv
        y_ref[r, :] = bf(hat * vec(4) + vec(5))
        c = c_ref[r, :].astype(f32)
        add_sum(0, c * hat)
        add_sum(1, c)
        w = c * vec(4)
        dr2 = (w - mean(w) - hat * mean(w * hat)) * inv
        acc_ref[r, :] = dr2
        low = bf(dr2)
        df_ref[r, :] = low
        add_sum(2, low.astype(f32))
    strips(second_norm)
    stores = [pltpu.make_async_copy(y_ref, block_out, osem.at[0])]
    stores[0].start()
    for b in range(blocks):
        dft_ref[:, BLOCK * b:BLOCK * b + BLOCK] = df_ref[BLOCK * b:BLOCK * b + BLOCK, :].T

    def backward(n, carry):
        j = 3 - n

        def lower(b):
            bufs[b % 2][...] = mm(df_ref[BLOCK * b:BLOCK * b + BLOCK, :], wd_ref[j])
        slot = n % 2
        away = [remote(6 + slot, st_ref.at[slot], rd_ref.at[slot]), remote(8 + slot, su_ref.at[slot], ru_ref.at[slot])]
        lower(0)
        for b in range(blocks):
            if b + 1 < blocks:
                lower(b + 1)
            r = slice(BLOCK * b, BLOCK * b + BLOCK)
            for i in range(0, BLOCK, 64):
                q = slice(BLOCK * b + i, BLOCK * b + i + 64)
                dul = bf(bufs[b % 2][i:i + 64, :] * gp_ref[j, q, :])
                upsum_ref[j] = upsum_ref[j] + jnp.sum(fold(dul.astype(f32)), axis=0)
                hat2_ref[q, :] = dul
            acc_ref[r, :] = acc_ref[r, :] + mm(hat2_ref[r, :], wu_ref[j], NT)

        @pl.when(n < 2)
        def _():
            for m in range(0, width, BLOCK):
                st_ref[slot, m:m + BLOCK, :] = bf(mm(dft_ref[m:m + BLOCK, :], z_ref[j]))
            away[0].start()
            for m in range(0, width, BLOCK):
                su_ref[slot, m:m + BLOCK, :] = bf(mm(hlt_ref[m:m + BLOCK, :], hat2_ref[...]))
            away[1].start()

        @pl.when(n >= 2)
        def _():
            away[0].wait()
            for m in range(0, width, BLOCK):
                got = rd_ref[slot, m:m + BLOCK, :].astype(f32)
                st_ref[slot, m:m + BLOCK, :] = bf(mm(dft_ref[m:m + BLOCK, :], z_ref[j]) + got)
            pltpu.make_async_copy(st_ref.at[slot], g_down.at[j], osem.at[1 + slot]).start()
            away[1].wait()
            for m in range(0, width, BLOCK):
                got = ru_ref[slot, m:m + BLOCK, :].astype(f32)
                su_ref[slot, m:m + BLOCK, :] = bf(mm(hlt_ref[m:m + BLOCK, :], hat2_ref[...]) + got)
            pltpu.make_async_copy(su_ref.at[slot], g_up.at[j], osem.at[3 + slot]).start()
        return carry
    hat2_ref = y_ref
    stores[0].wait()
    lax.fori_loop(0, 4, backward, 0)

    def first_back(r):
        dh1 = acc_ref[r, :]
        hat = hat_ref[r, :]
        add_sum(3, dh1 * hat)
        add_sum(4, dh1)
        w = dh1 * vec(1)
        grad = (w - mean(w) - hat * mean(w * hat)) * inv_ref[r, :]
        acc_ref[r, :] = grad
        low = bf(grad)
        df_ref[r, :] = low
        add_sum(5, low.astype(f32))
    strips(first_back)
    out = pltpu.make_async_copy(acc_ref, dr1, osem.at[0])
    out.start()
    stores = [out]
    for b in range(blocks):
        dft_ref[:, BLOCK * b:BLOCK * b + BLOCK] = df_ref[BLOCK * b:BLOCK * b + BLOCK, :].T
    lane = lax.broadcasted_iota(jnp.int32, (BLOCK, 128), 1)

    def out_grad(side, m):
        tiles = [mm(dft_ref[m:m + BLOCK, :], o_ref[side, :, 128 * g:128 * g + 128]) for g in range(3)]
        third = [jnp.where(lane < 64, tiles[2], 0.0), jnp.where(lane < 64, pltpu.roll(tiles[2], 64, 1), 0.0)]
        return [jnp.concatenate([tiles[o], third[o]], axis=1) for o in range(2)]
    for m in range(0, width, BLOCK):
        for o, value in enumerate(out_grad(1, m)):
            go_ref[o, m:m + BLOCK, :] = bf(value)
    swap_go = remote(10, go_ref, rgo_ref)
    swap_go.start()
    ow = wo_ref.shape[2]
    for side in (1, 0):
        def push(b, carry):
            r = pl.ds(pl.multiple_of(b * BLOCK, BLOCK), BLOCK)
            y_ref[r, ow * side:ow * side + ow] = bf(mm(df_ref[r, :], wo_ref[side]))
            return carry
        lax.fori_loop(0, blocks, push, 0)
        if side == 1:
            swap_do = remote(11, y_ref.at[:, pl.ds(ow, ow)], do_all.at[pl.ds(mine, rows), :])
            swap_do.start()
        else:
            copy = pltpu.make_async_copy(y_ref.at[:, pl.ds(0, ow)], do_all.at[pl.ds(mine, rows), :], osem.at[5])
            copy.start()
            stores.append(copy)
    swap_go.wait()
    for m in range(0, width, BLOCK):
        for o, value in enumerate(out_grad(0, m)):
            go_ref[o, m:m + BLOCK, :] = bf(value + rgo_ref[o, m:m + BLOCK, :].astype(f32))
    copy = pltpu.make_async_copy(go_ref, g_out, osem.at[6])
    copy.start()
    stores.append(copy)
    for slot in range(2):
        pltpu.make_async_copy(st_ref.at[slot], g_down.at[0], osem.at[1 + slot]).wait()
        pltpu.make_async_copy(su_ref.at[slot], g_up.at[0], osem.at[3 + slot]).wait()
    swap_do.wait()
    for copy in stores:
        copy.wait()


def middle(o_all, x0, outs, ups, downs, cot, vec, bup):
    f32, bf16 = jnp.float32, jnp.bfloat16
    rows, width = x0.shape
    ow = o_all.shape[1]
    part = bup.shape[-1]
    pieces = len(ups) == 2
    shape = jax.ShapeDtypeStruct
    hbm = pl.BlockSpec(memory_space=pl.ANY)
    vmem = pl.BlockSpec(memory_space=pltpu.VMEM)
    v = pltpu.VMEM
    n = len(ups)

    def kernel(o_all, x0, *refs):
        weights = refs[:3 * n]
        middle_kernel(pieces, o_all, x0, weights[:n], weights[n:2 * n], weights[2 * n:], *refs[3 * n:])

    return pl.pallas_call(
        kernel,
        out_shape=(shape((rows, width), bf16), shape((rows, width), f32), shape((2 * rows, ow), bf16),
                   shape((2, width, part), bf16), shape((2, width, part), bf16), shape((2, width, 256), bf16),
                   shape((6, 8, width), f32), shape((4, 8, part), f32)),
        in_specs=[hbm] * (3 + 3 * n) + [vmem] * 2,
        out_specs=[hbm] * 6 + [vmem] * 2,
        scratch_shapes=[
            v((2, rows, ow), bf16), v((2, 2, width, 256), bf16), v((2, width, ow), bf16), v((4, width, part), bf16),
            v((4, width, part), bf16),
            v((rows, width), f32), v((rows, 1), f32), v((rows, width), f32), v((rows, width), bf16), v((width, rows), bf16),
            v((4, rows, part), f32), v((4, rows, part), bf16), v((rows, width), bf16), v((rows, width), bf16),
            v((width, rows), bf16), v((rows, width), bf16), v((2, width, part), bf16),
            v((2, width, part), bf16), v((2, width, part), bf16), v((2, width, part), bf16), v((2, width, 256), bf16),
            v((2, width, 256), bf16), v((BLOCK, part), f32), v((BLOCK, part), f32),
            pltpu.SemaphoreType.DMA((40,)), pltpu.SemaphoreType.DMA((7,)),
            pltpu.SemaphoreType.DMA((12,)), pltpu.SemaphoreType.DMA((12,)),
        ],
        compiler_params=pltpu.CompilerParams(vmem_limit_bytes=VMEM_MAX, collective_id=1, has_side_effects=True),
        cost_estimate=pl.CostEstimate(flops=6 * rows * width * 9 * width, bytes_accessed=60_000_000, transcendentals=2 * rows * 4 * part),
        name="middle",
    )(o_all, x0, *outs, *ups, *downs, cot, vec, bup)


class Exchange:
    def __init__(self, send, recv):
        self.send, self.recv, self.used = send, recv, 0

    def copy(self, src, dst, device):
        n = self.used
        self.used += 1
        return pltpu.make_async_remote_copy(src, dst, self.send.at[n], self.recv.at[n], device_id=device,
                                            device_id_type=pl.DeviceIdType.MESH)


def greet(devices):
    barrier = pltpu.get_barrier_semaphore()
    for device in devices:
        pl.semaphore_signal(barrier, inc=1, device_id=device, device_id_type=pl.DeviceIdType.MESH)
    pl.semaphore_wait(barrier, len(devices))


def entry_kernel(tokens, pos_ref, mem_ref, wq_ref, bq_ref, wu_ref, wd_ref, wo_ref,
                 x0_out, x_out, q_out, k_out, v_out, w_out, up_g, down_g, out_g,
                 x0_ref, x_ref, g_ref, b_ref, y_ref, q_ref, k_ref, v_ref, send, recv, sem):
    f32, bf16 = jnp.float32, jnp.bfloat16
    rows, width = x0_ref.shape
    dp, tensor = lax.axis_index("dp"), lax.axis_index("tensor")
    z, x = dp // 2, dp % 2
    inner = tensor % 2
    zs = [(z + 4 - k) % 4 for k in range(4)]
    at = [2 * zs[k] + x for k in range(4)]
    far = [2 * zs[k] + 1 - x for k in range(4)]
    to_z = [None] + [(2 * ((z + k) % 4) + x, tensor) for k in range(1, 4)]
    to_x = (2 * z + 1 - x, tensor)
    to_y = (dp, (tensor + 2) % 4)
    to_core = (dp, tensor + 1 - 2 * inner)
    greet(to_z[1:] + [to_x, to_y, to_core])
    ex = Exchange(send, recv)
    started = []

    def go(src, dst, device):
        copy = ex.copy(src, dst, device)
        copy.start()
        started.append(copy)
        return copy

    local = []

    def keep(src, dst):
        copy = pltpu.make_async_copy(src, dst, sem.at[len(local)])
        copy.start()
        local.append(copy)
        return copy

    own = keep(wq_ref, g_ref.at[0, at[0]])
    own_bias = keep(bq_ref, b_ref.at[0])
    z_q = [None] + [go(wq_ref, g_ref.at[0, at[0]], to_z[k]) for k in range(1, 4)]
    x_q = [go(wq_ref, g_ref.at[0, at[0]], to_x)]
    y_q = [go(wq_ref, g_ref.at[1, at[0]], to_y)]
    bias = go(bq_ref, b_ref.at[1], to_y)

    mine = pl.multiple_of(inner * rows, 1024)
    positions = pos_ref[0:1, :]
    strip = 128

    def start(s, carry):
        r = pl.multiple_of(s * strip, strip)
        place = lax.broadcasted_iota(jnp.int32, (strip, positions.shape[1]), 0) + (inner * rows + r)
        picks = jnp.where(place == positions, 1.0, 0.0).astype(bf16)
        value = tokens[pl.ds(r, strip), :].astype(f32) + mm(picks, mem_ref[...])
        x0_ref[pl.ds(r, strip), :] = value
        x_ref[pl.ds(mine + r, strip), :] = value.astype(bf16)
        return carry
    lax.fori_loop(0, rows // strip, start, 0)
    keep(x0_ref, x0_out)
    core = go(x_ref.at[pl.ds(mine, rows), :], x_ref.at[pl.ds(mine, rows), :], to_core)

    for k in range(1, 4):
        z_q[k].wait_recv()
        x_q.append(go(g_ref.at[0, at[k]], g_ref.at[0, at[k]], to_x))
        y_q.append(go(g_ref.at[0, at[k]], g_ref.at[1, at[k]], to_y))
    z_u = [None] + [go(wu_ref, up_g.at[at[0]], to_z[k]) for k in range(1, 4)]
    z_d = [None] + [go(wd_ref, down_g.at[0, z], to_z[k]) for k in range(1, 4)]
    z_o = [None] + [go(wo_ref, out_g.at[0, z], to_z[k]) for k in range(1, 4)]
    keep(wu_ref, up_g.at[at[0]])
    keep(wd_ref, down_g.at[0, z])
    keep(wo_ref, out_g.at[0, z])
    last = []
    for k in range(2):
        x_q[k].wait_recv()
        last.append(go(g_ref.at[0, far[k]], g_ref.at[1, far[k]], to_y))
    for k in range(2, 4):
        y_q[k].wait_recv()
        last.append(go(g_ref.at[1, at[k]], g_ref.at[1, at[k]], to_x))
    rest = [go(wu_ref, up_g.at[at[0]], to_x), go(wd_ref, down_g.at[1, z], to_y), go(wo_ref, out_g.at[1, z], to_y)]
    for copy in x_q[2:] + y_q[:2] + last + [bias, core]:
        copy.wait_recv()
    own.wait()
    own_bias.wait()
    keep(g_ref, w_out)
    keep(x_ref, x_out)

    lane = lax.broadcasted_iota(jnp.int32, (BLOCK, 128), 1)
    y_ref[...] = jnp.zeros_like(y_ref)

    def project(b, carry):
        r = pl.ds(pl.multiple_of(b * BLOCK, BLOCK), BLOCK)
        for o in range(2):
            y_ref[o, :, 0:576] = mm(x_ref[r, :], g_ref[o].reshape(width, 576)) + b_ref[o, 0:1, 0:576].astype(f32)
        tile = lambda o, n: y_ref[o, :, 128 * n:128 * n + 128]
        turn = lambda value: pltpu.roll(value, 64, 1)
        third = (jnp.where(lane < 64, tile(0, 3), turn(tile(1, 3))), jnp.where(lane < 64, turn(tile(0, 3)), tile(1, 3)),
                 jnp.where(lane < 64, tile(0, 4), turn(tile(1, 4))))
        for n, ref in enumerate((q_ref, k_ref, v_ref)):
            for g, value in enumerate((tile(0, n), tile(1, n), third[n])):
                value = value.astype(bf16)
                if n == 0:
                    value = value * jnp.asarray(0.125, bf16)
                ref[r, 128 * g:128 * g + 128] = value
        return carry
    lax.fori_loop(0, 2 * rows // BLOCK, project, 0)
    for src, dst in ((q_ref, q_out), (k_ref, k_out), (v_ref, v_out)):
        keep(src, dst)
    for k in range(1, 4):
        z_u[k].wait_recv()
        rest.append(go(up_g.at[at[k]], up_g.at[at[k]], to_x))
        z_d[k].wait_recv()
        rest.append(go(down_g.at[0, zs[k]], down_g.at[1, zs[k]], to_y))
        z_o[k].wait_recv()
        rest.append(go(out_g.at[0, zs[k]], out_g.at[1, zs[k]], to_y))
    for copy in rest:
        copy.wait_recv()
    for copy in started:
        copy.wait_send()
    for copy in local[2:]:
        copy.wait()


def entry(tokens, positions, memory_rows, shard_qkv, biases, up, down, out):
    f32, bf16 = jnp.float32, jnp.bfloat16
    rows, width = tokens.shape
    r = up.shape[0]
    shape, v = jax.ShapeDtypeStruct, pltpu.VMEM
    hbm, vmem = pl.BlockSpec(memory_space=pl.ANY), pl.BlockSpec(memory_space=pltpu.VMEM)
    qkv = shape((2 * rows, 384), bf16)
    return pl.pallas_call(
        entry_kernel,
        out_shape=(shape((rows, width), f32), shape((2 * rows, width), bf16), qkv, qkv, qkv,
                   shape((2, 8, r, 576), bf16), shape((8, r, up.shape[1]), bf16), shape((2, 4, r, down.shape[1]), bf16),
                   shape((2, 4, r, out.shape[1]), bf16)),
        in_specs=[vmem] * 8,
        out_specs=[hbm] * 9,
        scratch_shapes=[
            v((rows, width), f32), v((2 * rows, width), bf16), v((2, 8, r, 576), bf16), v((2, 16, 640), bf16),
            v((2, BLOCK, 640), f32), v((2 * rows, 384), bf16), v((2 * rows, 384), bf16), v((2 * rows, 384), bf16),
            pltpu.SemaphoreType.DMA((48,)), pltpu.SemaphoreType.DMA((48,)), pltpu.SemaphoreType.DMA((16,)),
        ],
        compiler_params=pltpu.CompilerParams(vmem_limit_bytes=VMEM_MAX, collective_id=0, has_side_effects=True),
        cost_estimate=pl.CostEstimate(flops=4 * rows * width * 1152, bytes_accessed=20_000_000, transcendentals=0),
        name="entry",
    )(tokens, positions, memory_rows, shard_qkv, biases, up, down, out)


def layer_norm(values, norm_gain, norm_shift):
    centre = values - jnp.mean(values, axis=-1, keepdims=True)
    spread = jnp.mean(centre * centre, axis=-1, keepdims=True)
    return centre * lax.rsqrt(spread + EPSILON) * norm_gain + norm_shift


def gelu_exact(values):
    return jax.nn.gelu(values, approximate=False)


AXES = ("dp", "tensor")


class Grid:
    def __init__(self, dp, tensor):
        self.dp, self.tensor = dp, tensor
        factors, rest = [2], dp // 2
        while rest > 8:
            factors.insert(0, 4)
            rest //= 4
        if rest > 1:
            factors.insert(0, rest)
        self.factors = factors

    def digit(self, j):
        stride = 1
        for f in self.factors[j + 1:]:
            stride *= f
        return stride, self.factors[j]

    def my_digit(self, j):
        stride, f = self.digit(j)
        return lax.axis_index("dp") // stride % f

    def turn(self, value, j, k):
        stride, f = self.digit(j)
        pairs = []
        for d in range(self.dp):
            g = d // stride % f
            to = d + ((g + k) % f - g) * stride
            for t in range(self.tensor):
                pairs.append((d * self.tensor + t, to * self.tensor + t))
        return lax.ppermute(value, AXES, pairs)

    def swap_dp(self, value, bit):
        pairs = [(d * self.tensor + t, (d ^ bit) * self.tensor + t) for d in range(self.dp) for t in range(self.tensor)]
        return lax.ppermute(value, AXES, pairs)

    def swap(self, value, bit):
        pairs = [(d * self.tensor + t, d * self.tensor + (t ^ bit)) for d in range(self.dp) for t in range(self.tensor)]
        return lax.ppermute(value, AXES, pairs)

    def gather_stage(self, value, j, axis):
        _, f = self.digit(j)
        g = self.my_digit(j)
        got = [value] + [self.turn(value, j, k) for k in range(1, f)]
        if f == 2:
            lower = jnp.where(g == 0, got[0], got[1])
            upper = jnp.where(g == 0, got[1], got[0])
            return jnp.stack([lower, upper], axis=axis)
        ring = got[::-1]
        return lax.dynamic_slice_in_dim(jnp.stack(ring + ring[:-1], axis=axis), f - 1 - g, f, axis)

    def gather(self, shard, outer_first=False):
        count = len(self.factors)
        value = shard
        for j in range(count - 1):
            value = self.gather_stage(value, j, j)
        if outer_first:
            value = jnp.stack([value, self.swap(value, 2)])
            value = self.gather_stage(value, count - 1, count)
            return value.reshape(2, -1, shard.shape[-1])
        value = self.gather_stage(value, count - 1, count - 1)
        value = value.reshape(-1, shard.shape[-1])
        return jnp.stack([value, self.swap(value, 2)])

    def reduce_stage(self, value, j, axis):
        _, f = self.digit(j)
        g = self.my_digit(j)
        total = lax.dynamic_index_in_dim(value, g, axis, keepdims=False).astype(jnp.float32)
        for k in range(1, f):
            part = lax.dynamic_index_in_dim(value, (g + k) % f, axis, keepdims=False)
            total = total + self.turn(part.astype(jnp.bfloat16), j, k).astype(jnp.float32)
        return total

    def reduce(self, parts, outer_first=True):
        count = len(self.factors)
        columns = parts.shape[-1]
        value = parts
        if outer_first:
            value = value[0].astype(jnp.float32) + self.swap(value[1].astype(jnp.bfloat16), 2).astype(jnp.float32)
            value = value.reshape(*self.factors, -1, columns)
            value = self.reduce_stage(value, count - 1, count - 1)
        else:
            value = value.reshape(2, *self.factors, -1, columns)
            value = self.reduce_stage(value, count - 1, count)
            value = value[0] + self.swap(value[1].astype(jnp.bfloat16), 2).astype(jnp.float32)
        for j in reversed(range(count - 1)):
            value = self.reduce_stage(value, j, j)
        return value

    @property
    def stages(self):
        return len(self.factors) + 1

    def open(self, parts, outer_first):
        columns = parts.shape[-1]
        return parts if outer_first else parts.reshape(2, *self.factors, -1, columns)

    def stage(self, value, outer_first, n):
        count = len(self.factors)
        if n == (0 if outer_first else 1):
            value = value[0].astype(jnp.float32) + self.swap(value[1].astype(jnp.bfloat16), 2).astype(jnp.float32)
            return value.reshape(*self.factors, -1, value.shape[-1]) if outer_first else value
        if n == 0:
            return self.reduce_stage(value, count - 1, count)
        return self.reduce_stage(value, count - n, count - n)

    def total(self, vector):
        for bit in (1, 2):
            vector = vector + self.swap(vector, bit)
        bit = 1
        while bit < self.dp:
            vector = vector + self.swap_dp(vector, bit)
            bit *= 2
        return vector


def shards(grid, tokens, segment_ids, memory_positions, memory_rows, qkv_weight, qv_bias, out_weight, out_bias,
           norm1_gain, norm1_bias, up_weight, up_bias, down_weight, down_bias, norm2_gain, norm2_bias, out_cotangent):
    f32, bf16 = jnp.float32, jnp.bfloat16
    rows, width = tokens.shape
    group_len = segment_ids.shape[1]
    tensor = lax.axis_index("tensor")
    inner, outer = tensor % 2, tensor // 2
    slice_rows = qkv_weight.shape[0]
    heads = qkv_weight.shape[1]
    hd = 64
    hw = heads * hd
    units = up_weight.shape[1]

    segments = lax.dynamic_index_in_dim(segment_ids, outer, 0, keepdims=False)
    positions = lax.dynamic_index_in_dim(memory_positions, outer, 0, keepdims=False)
    row_place = inner * rows + jnp.arange(rows, dtype=jnp.int32)
    picks = (row_place[:, None] == positions[None, :])
    joined = lambda w: w.transpose(1, 0, 2).reshape(width, -1)

    parts = qkv_weight.reshape(slice_rows, heads, 3, hd)
    order_columns = lambda p: jnp.concatenate([p[..., :2, n, :].reshape(*p.shape[:-3], 2 * hd) for n in range(3)]
                                              + [p[..., 2, n, :] for n in range(3)], axis=-1)
    shard_qkv = order_columns(parts)
    shard_out = jnp.pad(out_weight.reshape(slice_rows, hw), ((0, 0), (0, 256 - hw)))
    bias_parts = qv_bias.reshape(heads, 2, hd)
    bias_qkv = order_columns(jnp.stack([bias_parts[:, 0], jnp.zeros_like(bias_parts[:, 0]), bias_parts[:, 1]], 1))
    bias_qkv = jnp.pad(bias_qkv[None], ((0, 15), (0, 64)))
    if grid.dp == 8 and grid.tensor == 4:
        memory = memory_positions.shape[1]
        place = jnp.pad(positions[None], ((0, 7), (0, 32 - memory)), constant_values=-1)
        table = jnp.pad(memory_rows, ((0, 32 - memory), (0, 0)))
        x0, x_all, q, k, v, w_qkv, up_g, down_g, out_g = entry(tokens, place, table, shard_qkv, bias_qkv, up_weight, down_weight, shard_out)
        w_qkv = w_qkv.reshape(2, width, 9 * hd)
        up_all = up_g.reshape(width, units)
        ups = (up_all, grid.swap(up_all, 2))
        downs = (down_g, grid.turn(down_g, 1, 1))
        outs = (out_g, grid.turn(out_g, 1, 1))
    else:
        x0 = tokens.astype(f32) + jnp.dot(picks.astype(bf16), memory_rows, preferred_element_type=f32)
        xl = x0.astype(bf16)
        w_qkv = grid.gather(shard_qkv)
        other = grid.swap(xl, 1)
        x_all = jnp.concatenate([jnp.where(inner == 0, xl, other), jnp.where(inner == 0, other, xl)])
        b_two = jnp.stack([bias_qkv[0], grid.swap(bias_qkv[0], 2)]).astype(f32)
        y = [(mm(x_all, w_qkv[o]) + b_two[o, :9 * hd]).astype(bf16) for o in range(2)]
        third = lambda n: [one[:, (6 + n) * hd:(7 + n) * hd] for one in y]
        q, k, v = [jnp.concatenate([y[0][:, 2 * n * hd:2 * (n + 1) * hd], y[1][:, 2 * n * hd:2 * (n + 1) * hd]] + third(n), 1)
                   for n in range(3)]
        q = q * jnp.asarray(0.125, bf16)
        outs, ups, downs = (grid.gather(shard_out, True),), (grid.gather(up_weight),), (grid.gather(down_weight, True),)
    b_up = jnp.concatenate([up_bias, grid.swap(up_bias, 2)])
    b_up = jnp.stack([b_up, grid.swap(b_up, 1)]).astype(f32)
    mixed, lse = attend_forward(q, k, v, segments)
    vec = jnp.stack([out_bias, norm1_gain, norm1_bias, down_bias, norm2_gain, norm2_bias, norm2_bias, norm2_bias]).astype(f32)
    (block_out, dr1, do_all, g_down, g_up, g_out, sums, up_sums) = middle(
        mixed, x0, outs, ups, downs, out_cotangent, vec, b_up.reshape(4, 1, units))
    TN = (((0,), (0,)), ((), ()))

    tie = lax.optimization_barrier
    kinds = (True, False, True)
    state = [grid.open(parts, kind) for parts, kind in zip((g_down, g_up, g_out), kinds)]
    step = lambda n, state: [grid.stage(value, kind, n) for value, kind in zip(state, kinds)]
    late = [(1, 0, 2)[n] for n in range(3)]
    d = [None] * 3
    state, d[1] = step(0, state), attend_backward(1, q, k, v, do_all, lse, segments)
    state, d[1], q = tie((state, d[1], q))
    g_one = mm(x_all, d[1], TN).astype(bf16)
    state, d[0] = step(1, state), attend_backward(0, q, k, v, do_all, lse, segments)
    state, d[0], q, g_one = tie((state, d[0], q, g_one))
    g_zero = mm(x_all, d[0], TN)
    first = g_zero + grid.swap(g_one, 2).astype(f32)
    state, d[2] = step(2, state), attend_backward(2, q, k, v, do_all, lse, segments)
    state, d[2], first = tie((state, d[2], first))
    for n in range(3, grid.stages):
        state = step(n, state)
    grad_down, grad_up, grad_out = state
    grad_out = grad_out[:, :hw]

    g_two = mm(x_all, d[2], TN)
    side = lambda m, o: jnp.concatenate([m[:, (2 * n + o) * hd:(2 * n + o + 1) * hd] for n in range(3)], 1)
    second = side(g_two, 0) + grid.swap(side(g_two, 1).astype(bf16), 2).astype(f32)
    both = jnp.concatenate([first, second], 1).reshape(*grid.factors, slice_rows, 9 * hd)
    for j in reversed(range(len(grid.factors))):
        both = grid.reduce_stage(both, j, j)
    restore = lambda p: jnp.stack([jnp.concatenate([p[..., 2 * n * hd:2 * (n + 1) * hd].reshape(*p.shape[:-1], 2, hd),
                                                    p[..., None, (6 + n) * hd:(7 + n) * hd]], -2) for n in range(3)], -2)
    grad_qkv = restore(both).reshape(slice_rows, heads, 3 * hd)
    third = jnp.concatenate([w_qkv[o][:, (6 + n) * hd:(7 + n) * hd] for n in range(3) for o in range(2)], 1)
    part = (mm(d[0], w_qkv[0][:, :6 * hd], NT) + mm(d[1], w_qkv[1][:, :6 * hd], NT) + mm(d[2], third, NT)).reshape(2, rows, width)
    mine = lax.dynamic_index_in_dim(part, inner, 0, keepdims=False)
    theirs = lax.dynamic_index_in_dim(part, 1 - inner, 0, keepdims=False).astype(bf16)
    grad_tokens = mine + grid.swap(theirs, 1).astype(f32) + dr1
    d_sum = [jnp.sum(one.astype(f32), axis=0) for one in d]
    d_bias = [jnp.concatenate([d_sum[o]] + [d_sum[2][(2 * n + o) * hd:(2 * n + o + 1) * hd] for n in range(3)]) for o in range(2)]
    dg2, ds2, d_down_bias, dg1, ds1, d_out_bias = jnp.sum(sums, axis=1)
    d_up_bias = jnp.sum(up_sums, axis=1).reshape(2, 2 * units)
    grad_memory = jnp.dot(picks.astype(f32).T, grad_tokens, precision=lax.Precision.HIGHEST)

    order = jnp.arange(4, dtype=jnp.int32) ^ tensor
    up_parts = d_up_bias.reshape(2, 2, units)
    up_parts = jnp.stack([up_parts[0, 0], up_parts[1, 0], up_parts[0, 1], up_parts[1, 1]])[order]
    take = lambda o: restore(d_bias[o])[:, 0::2].reshape(-1)
    blank = jnp.zeros((2 * hw,), f32)
    qv_parts = jnp.stack([take(0), blank, take(1), blank])[order]
    pieces = [grad_memory.reshape(-1), d_out_bias, dg1, ds1, d_down_bias, dg2, ds2, up_parts.reshape(-1), qv_parts.reshape(-1)]
    summed = grid.total(jnp.concatenate(pieces))
    outs, at = [], 0
    for piece in pieces:
        outs.append(lax.slice_in_dim(summed, at, at + piece.size))
        at += piece.size
    t_memory, t_out_bias, t_g1, t_s1, t_down_bias, t_g2, t_s2, t_up, t_qv = outs
    grad_up_bias = lax.dynamic_index_in_dim(t_up.reshape(4, units), tensor, 0, keepdims=False)
    grad_qv = lax.dynamic_index_in_dim(t_qv.reshape(4, heads, 2 * hd), tensor, 0, keepdims=False)
    return (block_out, grad_tokens, t_memory.reshape(-1, width), grad_qkv, grad_qv,
            grad_out.reshape(slice_rows, heads, hd), t_out_bias, t_g1, t_s1, grad_up, grad_up_bias, grad_down,
            t_down_bias, t_g2, t_s2)


def solution(mesh):
    grid = Grid(mesh.shape["dp"], mesh.shape["tensor"])
    tokens, dp, none = P(AXES, None), P("dp", None), P()
    heads, matrix = P("dp", "tensor", None), P("dp", "tensor")
    in_specs = (tokens, dp, dp, none, heads, P("tensor", None), heads, none, none, none, matrix, P("tensor"), matrix,
                none, none, none, tokens)
    out_specs = (tokens, tokens, none, heads, P("tensor", None), heads, none, none, none, matrix, P("tensor"), matrix,
                 none, none, none)

    def run(*args):
        return shards(grid, *args)

    return jax.shard_map(run, mesh=mesh, in_specs=in_specs, out_specs=out_specs, check_vma=False)
```

```python
import functools

import jax
import jax.numpy as jnp
from jax import lax
from jax.experimental import pallas as pl
from jax.experimental.pallas import tpu as pltpu
from jax.sharding import PartitionSpec as P

EPSILON = 1e-12
TILE = 256
MASKED = -1e30
VMEM_MAX = 64 * 1024 * 1024 - 128 * 1024
NT = (((1,), (1,)), ((), ()))
NN = (((1,), (0,)), ((), ()))


def mm(a, b, dims=NN):
    return lax.dot_general(a, b, dims, preferred_element_type=jnp.float32)


def fold8(x):
    r = x.shape[0]
    return x.reshape(r // 8, 8, x.shape[1])


def head_masks(block):
    lane = lax.broadcasted_iota(jnp.int32, block.shape, 1)
    zero = jnp.zeros_like(block)
    return jnp.where(lane < 64, block, zero), jnp.where(lane < 64, zero, block)


def tile_visible(first_ref, last_ref, i, t):
    return (first_ref[t] == 0) | ((first_ref[t] <= last_ref[i]) & (last_ref[t] >= first_ref[i]))


def forward_kernel(first_ref, last_ref, q_ref, k_ref, v_ref, kseg_ref, qseg_ref, o_ref, lse_ref,
                   vt_ref, qm_ref, s_ref, m_ref, l_ref, acc_ref):
    i = pl.program_id(0)
    tiles = pl.num_programs(0)
    pairs = q_ref.shape[1] // 128
    heads = 2 * pairs

    @pl.when(i == 0)
    def _():
        def turn(t, c):
            rows = pl.ds(pl.multiple_of(t * TILE, TILE), TILE)
            vt_ref[t] = v_ref[rows, :].T
            return c
        lax.fori_loop(0, tiles, turn, 0)

    for g in range(pairs):
        a, b = head_masks(q_ref[:, 128 * g:128 * g + 128])
        qm_ref[2 * g] = a
        qm_ref[2 * g + 1] = b
    m_ref[...] = jnp.full_like(m_ref, MASKED)
    l_ref[...] = jnp.zeros_like(l_ref)
    acc_ref[...] = jnp.zeros_like(acc_ref)
    qseg = qseg_ref[0:1, :]

    def scores(t, c):
        @pl.when(tile_visible(first_ref, last_ref, i, t))
        def _():
            rows = pl.ds(pl.multiple_of(t * TILE, TILE), TILE)
            kseg = kseg_ref[rows, 0:1]
            seen = (kseg == 0) | (kseg == qseg)
            for h in range(heads):
                kp = k_ref[rows, 128 * (h // 2):128 * (h // 2) + 128]
                s = mm(kp, qm_ref[h], NT)
                s = jnp.where(seen, s, MASKED)
                s_ref[h, t] = s
                m_ref[h] = jnp.maximum(m_ref[h], jnp.max(fold8(s), axis=0))
        return c
    lax.fori_loop(0, tiles, scores, 0)
    for h in range(heads):
        m_ref[h] = jnp.broadcast_to(jnp.max(m_ref[h], axis=0, keepdims=True), (8, TILE))

    def mix(t, c):
        @pl.when(tile_visible(first_ref, last_ref, i, t))
        def _():
            for h in range(heads):
                p = jnp.exp(s_ref[h, t] - m_ref[h, 0:1, :])
                l_ref[h] = l_ref[h] + jnp.sum(fold8(p), axis=0)
                acc_ref[h] = acc_ref[h] + mm(vt_ref[t, 64 * h:64 * h + 64, :], p.astype(jnp.bfloat16))
        return c
    lax.fori_loop(0, tiles, mix, 0)
    for h in range(heads):
        total = jnp.sum(l_ref[h], axis=0, keepdims=True)
        lse_ref[h:h + 1, :] = m_ref[h, 0:1, :] + jnp.log(total)
        acc_ref[h] = acc_ref[h] / total
    for g in range(pairs):
        pair = jnp.concatenate([acc_ref[2 * g], acc_ref[2 * g + 1]], axis=0)
        o_ref[:, 128 * g:128 * g + 128] = pair.T.astype(jnp.bfloat16)


def attend_forward(q, k, v, seg):
    n, width = q.shape
    tiles = n // TILE
    heads = width // 64
    first = seg[::TILE]
    last = seg[TILE - 1::TILE]
    kseg = jnp.broadcast_to(seg[:, None], (n, 128))
    qseg = jnp.broadcast_to(seg[None, :], (8, n))
    whole = lambda shape: pl.BlockSpec(shape, lambda i, *_: (0,) * len(shape))
    return pl.pallas_call(
        forward_kernel,
        out_shape=(jax.ShapeDtypeStruct((n, width), jnp.bfloat16), jax.ShapeDtypeStruct((8, n), jnp.float32)),
        grid_spec=pltpu.PrefetchScalarGridSpec(
            num_scalar_prefetch=2, grid=(tiles,),
            in_specs=[pl.BlockSpec((TILE, width), lambda i, *_: (i, 0)), whole((n, width)), whole((n, width)),
                      whole((n, 128)), pl.BlockSpec((8, TILE), lambda i, *_: (0, i))],
            out_specs=[pl.BlockSpec((TILE, width), lambda i, *_: (i, 0)), pl.BlockSpec((8, TILE), lambda i, *_: (0, i))],
            scratch_shapes=[
                pltpu.VMEM((tiles, width, TILE), jnp.bfloat16),
                pltpu.VMEM((heads, TILE, 128), jnp.bfloat16),
                pltpu.VMEM((heads, tiles, TILE, TILE), jnp.float32),
                pltpu.VMEM((heads, 8, TILE), jnp.float32),
                pltpu.VMEM((heads, 8, TILE), jnp.float32),
                pltpu.VMEM((heads, 64, TILE), jnp.float32),
            ]),
        compiler_params=pltpu.CompilerParams(dimension_semantics=("arbitrary",), vmem_limit_bytes=VMEM_MAX),
        cost_estimate=pl.CostEstimate(flops=4 * n * n * width, bytes_accessed=8 * n * width, transcendentals=n * n * heads),
        name="attend_forward",
    )(first, last, q, k, v, kseg, qseg)


def backward_kernel(base, first_ref, last_ref, q_ref, do_ref, k_ref, v_ref, kseg_ref, qseg_ref, lse_ref,
                    d_ref, kt_ref, qm_ref, dom_ref, p_ref, g_ref, delta_ref, dqt_ref, dka_ref, dva_ref):
    i = pl.program_id(0)
    tiles = pl.num_programs(0)
    pairs = q_ref.shape[1] // 128
    heads = 2 * pairs

    @pl.when(i == 0)
    def _():
        def turn(t, c):
            rows = pl.ds(pl.multiple_of(t * TILE, TILE), TILE)
            kt_ref[t] = k_ref[rows, :].T
            dka_ref[rows, :] = jnp.zeros((TILE, 128 * pairs), jnp.float32)
            dva_ref[rows, :] = jnp.zeros((TILE, 128 * pairs), jnp.float32)
            return c
        lax.fori_loop(0, tiles, turn, 0)

    for g in range(pairs):
        a, b = head_masks(q_ref[:, 128 * g:128 * g + 128])
        qm_ref[2 * g] = a
        qm_ref[2 * g + 1] = b
        a, b = head_masks(do_ref[:, 128 * g:128 * g + 128])
        dom_ref[2 * g] = a
        dom_ref[2 * g + 1] = b
    delta_ref[...] = jnp.zeros_like(delta_ref)
    dqt_ref[...] = jnp.zeros_like(dqt_ref)
    qseg = qseg_ref[0:1, :]

    def first_pass(t, c):
        @pl.when(tile_visible(first_ref, last_ref, i, t))
        def _():
            rows = pl.ds(pl.multiple_of(t * TILE, TILE), TILE)
            kseg = kseg_ref[rows, 0:1]
            seen = (kseg == 0) | (kseg == qseg)
            for g in range(pairs):
                cols = slice(128 * g, 128 * g + 128)
                kp = k_ref[rows, cols]
                vp = v_ref[rows, cols]
                part = None
                for h in (2 * g, 2 * g + 1):
                    s = mm(kp, qm_ref[h], NT)
                    p = jnp.where(seen, jnp.exp(s - lse_ref[base + h:base + h + 1, :]), 0.0)
                    d = mm(vp, dom_ref[h], NT)
                    p_ref[h, t] = p
                    g_ref[h, t] = d
                    delta_ref[h] = delta_ref[h] + jnp.sum(fold8(p * d), axis=0)
                    one = mm(p.astype(jnp.bfloat16), dom_ref[h])
                    part = one if part is None else part + one
                dva_ref[rows, cols] = dva_ref[rows, cols] + part
        return c
    lax.fori_loop(0, tiles, first_pass, 0)
    for h in range(heads):
        delta_ref[h] = jnp.broadcast_to(jnp.sum(delta_ref[h], axis=0, keepdims=True), (8, TILE))

    def second_pass(t, c):
        @pl.when(tile_visible(first_ref, last_ref, i, t))
        def _():
            rows = pl.ds(pl.multiple_of(t * TILE, TILE), TILE)
            for g in range(pairs):
                cols = slice(128 * g, 128 * g + 128)
                part = None
                for h in (2 * g, 2 * g + 1):
                    ds = (p_ref[h, t] * (g_ref[h, t] - delta_ref[h, 0:1, :])).astype(jnp.bfloat16)
                    one = mm(ds, qm_ref[h])
                    part = one if part is None else part + one
                    dqt_ref[h] = dqt_ref[h] + mm(kt_ref[t, 64 * h:64 * h + 64, :], ds)
                dka_ref[rows, cols] = dka_ref[rows, cols] + part
        return c
    lax.fori_loop(0, tiles, second_pass, 0)
    for g in range(pairs):
        pair = jnp.concatenate([dqt_ref[2 * g], dqt_ref[2 * g + 1]], axis=0)
        own = pl.ds(pl.multiple_of(i * TILE, TILE), TILE)
        d_ref[own, 128 * g:128 * g + 128] = (pair.T * 0.125).astype(jnp.bfloat16)

    @pl.when(i == tiles - 1)
    def _():
        d_ref[:, 128 * pairs:256 * pairs] = dka_ref[...].astype(jnp.bfloat16)
        d_ref[:, 256 * pairs:384 * pairs] = dva_ref[...].astype(jnp.bfloat16)


def attend_backward(g, q, k, v, do, lse, seg):
    n, width = q.shape[0], 128
    tiles = n // TILE
    heads = width // 64
    first = seg[::TILE]
    last = seg[TILE - 1::TILE]
    kseg = jnp.broadcast_to(seg[:, None], (n, 128))
    qseg = jnp.broadcast_to(seg[None, :], (8, n))
    whole = lambda shape: pl.BlockSpec(shape, lambda i, *_: (0,) * len(shape))
    rows = pl.BlockSpec((TILE, width), lambda i, *_: (i, g))
    column = pl.BlockSpec((n, width), lambda i, *_: (0, g))
    stat = pl.BlockSpec((8, TILE), lambda i, *_: (0, i))
    return pl.pallas_call(
        functools.partial(backward_kernel, 2 * g),
        out_shape=jax.ShapeDtypeStruct((n, 3 * width), jnp.bfloat16),
        grid_spec=pltpu.PrefetchScalarGridSpec(
            num_scalar_prefetch=2, grid=(tiles,),
            in_specs=[rows, rows, column, column, whole((n, 128)), stat, stat],
            out_specs=whole((n, 3 * width)),
            scratch_shapes=[
                pltpu.VMEM((tiles, width, TILE), jnp.bfloat16),
                pltpu.VMEM((heads, TILE, 128), jnp.bfloat16),
                pltpu.VMEM((heads, TILE, 128), jnp.bfloat16),
                pltpu.VMEM((heads, tiles, TILE, TILE), jnp.float32),
                pltpu.VMEM((heads, tiles, TILE, TILE), jnp.float32),
                pltpu.VMEM((heads, 8, TILE), jnp.float32),
                pltpu.VMEM((heads, 64, TILE), jnp.float32),
                pltpu.VMEM((n, width), jnp.float32),
                pltpu.VMEM((n, width), jnp.float32),
            ]),
        compiler_params=pltpu.CompilerParams(dimension_semantics=("arbitrary",), vmem_limit_bytes=VMEM_MAX),
        cost_estimate=pl.CostEstimate(flops=10 * n * n * width, bytes_accessed=14 * n * width, transcendentals=n * n * heads),
        name="attend_backward",
    )(first, last, q, do, k, v, kseg, qseg, lse)


BLOCK = 256
STRIP = 64


def normal_cdf_parts(u):
    v = u * 0.7071067811865476
    c = jnp.clip(v, -3.832506856900711, 3.832506856900711)
    c2 = c * c
    top = 0.00022905065861350646
    for a in (0.0034082910107109506, 0.050955695062380861, 0.18520832239976145, 1.128379143519084):
        top = top * c2 + a
    low = -1.1791602954361697e-7
    for b in (0.000023547966471313185, 0.0010179625278914885, 0.014070470171167667, 0.11098505178285362,
              0.49746925110067538, 1.0):
        low = low * c2 + b
    cdf = 0.5 + 0.5 * (c * top / low)
    slope = jnp.exp(-(v * v)) * (u * 0.3989422804014327)
    return u * cdf, cdf + slope


def middle_kernel(pieces, o_all, x0, outs, ups, downs, cot, vec_ref, bup_ref,
                  block_out, dr1, do_all, g_down, g_up, g_out, sums_ref, upsum_ref,
                  o_ref, raw_ref, wo_ref, wu_ref, wd_ref, hat_ref, inv_ref, acc_ref, hl_ref, hlt_ref, gp_ref, z_ref, c_ref,
                  df_ref, dft_ref, y_ref, st_ref, su_ref, ru_ref, rd_ref, go_ref, rgo_ref, u0_ref, u1_ref,
                  sem, osem, send, recv):
    f32, bf16 = jnp.float32, jnp.bfloat16
    rows, width = hat_ref.shape
    blocks = rows // BLOCK
    part = wu_ref.shape[2]
    bf = lambda a: a.astype(bf16)
    dp, tensor = lax.axis_index("dp"), lax.axis_index("tensor")
    inner = tensor % 2
    partner = (dp, tensor + 1 - 2 * inner)
    mine = pl.multiple_of(inner * rows, 1024)
    theirs = pl.multiple_of((1 - inner) * rows, 1024)
    greet([partner])

    def remote(n, src, dst):
        return pltpu.make_async_remote_copy(src, dst, send.at[n], recv.at[n], device_id=partner,
                                            device_id_type=pl.DeviceIdType.MESH)

    swap_o = remote(0, o_all.at[pl.ds(theirs, rows), :], o_ref.at[1])
    swap_o.start()
    count = [0]

    def load(src, dst):
        copy = pltpu.make_async_copy(src, dst, sem.at[count[0]])
        count[0] += 1
        copy.start()
        return copy

    def weight(sources, dst):
        if not pieces:
            return [load(sources[0].at[o], dst.at[o]) for o in range(2)]
        digit = dp % 2
        made = []
        for o in range(2):
            for zi in range(sources[0].shape[1]):
                for n in range(2):
                    place = 2 * zi + (digit if n == 0 else 1 - digit)
                    r = sources[n].shape[2]
                    made.append(load(sources[n].at[o, zi], dst.at[o, pl.ds(pl.multiple_of(place * r, r), r), :]))
        return made

    first = [load(o_all.at[pl.ds(mine, rows), :], o_ref.at[0]), load(x0, hat_ref)] + weight(outs, raw_ref.at[0])
    if pieces:
        second = [load(ups[o], wu_ref.at[o]) for o in range(2)]
    else:
        second = [load(ups[0].at[o], wu_ref.at[o]) for o in range(2)]
    second = second + weight(downs, wd_ref)
    late = load(cot, c_ref)
    vec = lambda n: vec_ref[n:n + 1, :]
    sums_ref[...] = jnp.zeros_like(sums_ref)
    upsum_ref[...] = jnp.zeros_like(upsum_ref)
    for copy in first:
        copy.wait()
    swaps = [remote(1, raw_ref.at[0], raw_ref.at[1])]
    swaps[0].start()
    for copy in second:
        copy.wait()
    for o in range(2):
        swaps.append(remote(2 + 2 * o, wu_ref.at[o], wu_ref.at[2 + o]))
        swaps.append(remote(3 + 2 * o, wd_ref.at[o], wd_ref.at[2 + o]))
    for copy in swaps[1:]:
        copy.start()
    lane = lax.broadcasted_iota(jnp.int32, (width, 128), 1)

    def order_heads(side):
        wo_ref[side, :, 0:128] = raw_ref[side, 0, :, 0:128]
        wo_ref[side, :, 128:256] = raw_ref[side, 1, :, 0:128]
        upper = pltpu.roll(raw_ref[side, 1, :, 128:256].astype(f32), 64, 1)
        wo_ref[side, :, 256:384] = bf(jnp.where(lane < 64, raw_ref[side, 0, :, 128:256].astype(f32), upper))
    order_heads(0)
    swaps[0].wait()
    order_heads(1)
    swap_o.wait()

    def strips(body):
        def run(s, carry):
            body(pl.ds(pl.multiple_of(s * STRIP, STRIP), STRIP))
            return carry
        lax.fori_loop(0, rows // STRIP, run, 0)

    def add_sum(n, value):
        sums_ref[n] = sums_ref[n] + jnp.sum(fold(value), axis=0)

    def fold(value):
        return value.reshape(value.shape[0] // 8, 8, value.shape[1])

    def mean(value):
        return jnp.sum(value, axis=-1, keepdims=True) * (1.0 / width)

    def project(b, carry):
        r = pl.ds(pl.multiple_of(b * BLOCK, BLOCK), BLOCK)
        acc_ref[r, :] = mm(o_ref[0, r, :], wo_ref[0], NT) + mm(o_ref[1, r, :], wo_ref[1], NT)
        return carry
    lax.fori_loop(0, blocks, project, 0)

    def first_norm(r):
        r1 = hat_ref[r, :] + (acc_ref[r, :] + vec(0))
        centre = r1 - mean(r1)
        inv = lax.rsqrt(mean(centre * centre) + EPSILON)
        hat = centre * inv
        hat_ref[r, :] = hat
        inv_ref[r, :] = inv
        hl_ref[r, :] = bf(hat * vec(1) + vec(2))
    strips(first_norm)
    for b in range(blocks):
        hlt_ref[:, BLOCK * b:BLOCK * b + BLOCK] = hl_ref[BLOCK * b:BLOCK * b + BLOCK, :].T
    acc_ref[...] = jnp.zeros_like(acc_ref)

    bufs = (u0_ref, u1_ref)

    def forward(j, carry):
        for o in range(2):
            @pl.when(j == 2 + o)
            def _(o=o):
                swaps[1 + 2 * o].wait()
                swaps[2 + 2 * o].wait()

        def lift(b):
            bufs[b % 2][...] = mm(hl_ref[BLOCK * b:BLOCK * b + BLOCK, :], wu_ref[j]) + bup_ref[j]
        lift(0)
        for b in range(blocks):
            if b + 1 < blocks:
                lift(b + 1)
            r = slice(BLOCK * b, BLOCK * b + BLOCK)
            for i in range(0, BLOCK, 32):
                for w in range(0, part, 256):
                    z, gp = normal_cdf_parts(bufs[b % 2][i:i + 32, w:w + 256])
                    z_ref[j, BLOCK * b + i:BLOCK * b + i + 32, w:w + 256] = bf(z)
                    gp_ref[j, BLOCK * b + i:BLOCK * b + i + 32, w:w + 256] = gp
            acc_ref[r, :] = acc_ref[r, :] + mm(z_ref[j, r, :], wd_ref[j], NT)
        return carry
    lax.fori_loop(0, 4, forward, 0)
    late.wait()

    def second_norm(r):
        h1 = hat_ref[r, :] * vec(1) + vec(2)
        r2 = h1 + (acc_ref[r, :] + vec(3))
        centre = r2 - mean(r2)
        inv = lax.rsqrt(mean(centre * centre) + EPSILON)
        hat = centre * inv
        y_ref[r, :] = bf(hat * vec(4) + vec(5))
        c = c_ref[r, :].astype(f32)
        add_sum(0, c * hat)
        add_sum(1, c)
        w = c * vec(4)
        dr2 = (w - mean(w) - hat * mean(w * hat)) * inv
        acc_ref[r, :] = dr2
        low = bf(dr2)
        df_ref[r, :] = low
        add_sum(2, low.astype(f32))
    strips(second_norm)
    stores = [pltpu.make_async_copy(y_ref, block_out, osem.at[0])]
    stores[0].start()
    for b in range(blocks):
        dft_ref[:, BLOCK * b:BLOCK * b + BLOCK] = df_ref[BLOCK * b:BLOCK * b + BLOCK, :].T

    def backward(n, carry):
        j = 3 - n

        def lower(b):
            bufs[b % 2][...] = mm(df_ref[BLOCK * b:BLOCK * b + BLOCK, :], wd_ref[j])
        slot = n % 2
        away = [remote(6 + slot, st_ref.at[slot], rd_ref.at[slot]), remote(8 + slot, su_ref.at[slot], ru_ref.at[slot])]
        lower(0)
        for b in range(blocks):
            if b + 1 < blocks:
                lower(b + 1)
            r = slice(BLOCK * b, BLOCK * b + BLOCK)
            for i in range(0, BLOCK, 64):
                q = slice(BLOCK * b + i, BLOCK * b + i + 64)
                dul = bf(bufs[b % 2][i:i + 64, :] * gp_ref[j, q, :])
                upsum_ref[j] = upsum_ref[j] + jnp.sum(fold(dul.astype(f32)), axis=0)
                hat2_ref[q, :] = dul
            acc_ref[r, :] = acc_ref[r, :] + mm(hat2_ref[r, :], wu_ref[j], NT)

        @pl.when(n < 2)
        def _():
            for m in range(0, width, BLOCK):
                st_ref[slot, m:m + BLOCK, :] = bf(mm(dft_ref[m:m + BLOCK, :], z_ref[j]))
            away[0].start()
            for m in range(0, width, BLOCK):
                su_ref[slot, m:m + BLOCK, :] = bf(mm(hlt_ref[m:m + BLOCK, :], hat2_ref[...]))
            away[1].start()

        @pl.when(n >= 2)
        def _():
            away[0].wait()
            for m in range(0, width, BLOCK):
                got = rd_ref[slot, m:m + BLOCK, :].astype(f32)
                st_ref[slot, m:m + BLOCK, :] = bf(mm(dft_ref[m:m + BLOCK, :], z_ref[j]) + got)
            pltpu.make_async_copy(st_ref.at[slot], g_down.at[j], osem.at[1 + slot]).start()
            away[1].wait()
            for m in range(0, width, BLOCK):
                got = ru_ref[slot, m:m + BLOCK, :].astype(f32)
                su_ref[slot, m:m + BLOCK, :] = bf(mm(hlt_ref[m:m + BLOCK, :], hat2_ref[...]) + got)
            pltpu.make_async_copy(su_ref.at[slot], g_up.at[j], osem.at[3 + slot]).start()
        return carry
    hat2_ref = y_ref
    stores[0].wait()
    lax.fori_loop(0, 4, backward, 0)

    def first_back(r):
        dh1 = acc_ref[r, :]
        hat = hat_ref[r, :]
        add_sum(3, dh1 * hat)
        add_sum(4, dh1)
        w = dh1 * vec(1)
        grad = (w - mean(w) - hat * mean(w * hat)) * inv_ref[r, :]
        acc_ref[r, :] = grad
        low = bf(grad)
        df_ref[r, :] = low
        add_sum(5, low.astype(f32))
    strips(first_back)
    out = pltpu.make_async_copy(acc_ref, dr1, osem.at[0])
    out.start()
    stores = [out]
    for b in range(blocks):
        dft_ref[:, BLOCK * b:BLOCK * b + BLOCK] = df_ref[BLOCK * b:BLOCK * b + BLOCK, :].T
    lane = lax.broadcasted_iota(jnp.int32, (BLOCK, 128), 1)

    def out_grad(side, m):
        tiles = [mm(dft_ref[m:m + BLOCK, :], o_ref[side, :, 128 * g:128 * g + 128]) for g in range(3)]
        third = [jnp.where(lane < 64, tiles[2], 0.0), jnp.where(lane < 64, pltpu.roll(tiles[2], 64, 1), 0.0)]
        return [jnp.concatenate([tiles[o], third[o]], axis=1) for o in range(2)]
    for m in range(0, width, BLOCK):
        for o, value in enumerate(out_grad(1, m)):
            go_ref[o, m:m + BLOCK, :] = bf(value)
    swap_go = remote(10, go_ref, rgo_ref)
    swap_go.start()
    ow = wo_ref.shape[2]
    for side in (1, 0):
        def push(b, carry):
            r = pl.ds(pl.multiple_of(b * BLOCK, BLOCK), BLOCK)
            y_ref[r, ow * side:ow * side + ow] = bf(mm(df_ref[r, :], wo_ref[side]))
            return carry
        lax.fori_loop(0, blocks, push, 0)
        if side == 1:
            swap_do = remote(11, y_ref.at[:, pl.ds(ow, ow)], do_all.at[pl.ds(mine, rows), :])
            swap_do.start()
        else:
            copy = pltpu.make_async_copy(y_ref.at[:, pl.ds(0, ow)], do_all.at[pl.ds(mine, rows), :], osem.at[5])
            copy.start()
            stores.append(copy)
    swap_go.wait()
    for m in range(0, width, BLOCK):
        for o, value in enumerate(out_grad(0, m)):
            go_ref[o, m:m + BLOCK, :] = bf(value + rgo_ref[o, m:m + BLOCK, :].astype(f32))
    copy = pltpu.make_async_copy(go_ref, g_out, osem.at[6])
    copy.start()
    stores.append(copy)
    for slot in range(2):
        pltpu.make_async_copy(st_ref.at[slot], g_down.at[0], osem.at[1 + slot]).wait()
        pltpu.make_async_copy(su_ref.at[slot], g_up.at[0], osem.at[3 + slot]).wait()
    swap_do.wait()
    for copy in stores:
        copy.wait()


def middle(o_all, x0, outs, ups, downs, cot, vec, bup):
    f32, bf16 = jnp.float32, jnp.bfloat16
    rows, width = x0.shape
    ow = o_all.shape[1]
    part = bup.shape[-1]
    pieces = len(ups) == 2
    shape = jax.ShapeDtypeStruct
    hbm = pl.BlockSpec(memory_space=pl.ANY)
    vmem = pl.BlockSpec(memory_space=pltpu.VMEM)
    v = pltpu.VMEM
    n = len(ups)

    def kernel(o_all, x0, *refs):
        weights = refs[:3 * n]
        middle_kernel(pieces, o_all, x0, weights[:n], weights[n:2 * n], weights[2 * n:], *refs[3 * n:])

    return pl.pallas_call(
        kernel,
        out_shape=(shape((rows, width), bf16), shape((rows, width), f32), shape((2 * rows, ow), bf16),
                   shape((2, width, part), bf16), shape((2, width, part), bf16), shape((2, width, 256), bf16),
                   shape((6, 8, width), f32), shape((4, 8, part), f32)),
        in_specs=[hbm] * (3 + 3 * n) + [vmem] * 2,
        out_specs=[hbm] * 6 + [vmem] * 2,
        scratch_shapes=[
            v((2, rows, ow), bf16), v((2, 2, width, 256), bf16), v((2, width, ow), bf16), v((4, width, part), bf16),
            v((4, width, part), bf16),
            v((rows, width), f32), v((rows, 1), f32), v((rows, width), f32), v((rows, width), bf16), v((width, rows), bf16),
            v((4, rows, part), f32), v((4, rows, part), bf16), v((rows, width), bf16), v((rows, width), bf16),
            v((width, rows), bf16), v((rows, width), bf16), v((2, width, part), bf16),
            v((2, width, part), bf16), v((2, width, part), bf16), v((2, width, part), bf16), v((2, width, 256), bf16),
            v((2, width, 256), bf16), v((BLOCK, part), f32), v((BLOCK, part), f32),
            pltpu.SemaphoreType.DMA((40,)), pltpu.SemaphoreType.DMA((7,)),
            pltpu.SemaphoreType.DMA((12,)), pltpu.SemaphoreType.DMA((12,)),
        ],
        compiler_params=pltpu.CompilerParams(vmem_limit_bytes=VMEM_MAX, collective_id=1, has_side_effects=True),
        cost_estimate=pl.CostEstimate(flops=6 * rows * width * 9 * width, bytes_accessed=60_000_000, transcendentals=2 * rows * 4 * part),
        name="middle",
    )(o_all, x0, *outs, *ups, *downs, cot, vec, bup)


class Exchange:
    def __init__(self, send, recv):
        self.send, self.recv, self.used = send, recv, 0

    def copy(self, src, dst, device):
        n = self.used
        self.used += 1
        return pltpu.make_async_remote_copy(src, dst, self.send.at[n], self.recv.at[n], device_id=device,
                                            device_id_type=pl.DeviceIdType.MESH)


def greet(devices):
    barrier = pltpu.get_barrier_semaphore()
    for device in devices:
        pl.semaphore_signal(barrier, inc=1, device_id=device, device_id_type=pl.DeviceIdType.MESH)
    pl.semaphore_wait(barrier, len(devices))


def entry_kernel(tokens, pos_ref, mem_ref, wq_ref, bq_ref, wu_ref, wd_ref, wo_ref,
                 x0_out, x_out, q_out, k_out, v_out, w_out, up_g, down_g, out_g,
                 x0_ref, x_ref, g_ref, b_ref, y_ref, q_ref, k_ref, v_ref, send, recv, sem):
    f32, bf16 = jnp.float32, jnp.bfloat16
    rows, width = x0_ref.shape
    dp, tensor = lax.axis_index("dp"), lax.axis_index("tensor")
    z, x = dp // 2, dp % 2
    inner = tensor % 2
    zs = [(z + 4 - k) % 4 for k in range(4)]
    at = [2 * zs[k] + x for k in range(4)]
    far = [2 * zs[k] + 1 - x for k in range(4)]
    to_z = [None] + [(2 * ((z + k) % 4) + x, tensor) for k in range(1, 4)]
    to_x = (2 * z + 1 - x, tensor)
    to_y = (dp, (tensor + 2) % 4)
    to_core = (dp, tensor + 1 - 2 * inner)
    greet(to_z[1:] + [to_x, to_y, to_core])
    ex = Exchange(send, recv)
    started = []

    def go(src, dst, device):
        copy = ex.copy(src, dst, device)
        copy.start()
        started.append(copy)
        return copy

    local = []

    def keep(src, dst):
        copy = pltpu.make_async_copy(src, dst, sem.at[len(local)])
        copy.start()
        local.append(copy)
        return copy

    own = keep(wq_ref, g_ref.at[0, at[0]])
    own_bias = keep(bq_ref, b_ref.at[0])
    z_q = [None] + [go(wq_ref, g_ref.at[0, at[0]], to_z[k]) for k in range(1, 4)]
    x_q = [go(wq_ref, g_ref.at[0, at[0]], to_x)]
    y_q = [go(wq_ref, g_ref.at[1, at[0]], to_y)]
    bias = go(bq_ref, b_ref.at[1], to_y)

    mine = pl.multiple_of(inner * rows, 1024)
    positions = pos_ref[0:1, :]
    strip = 128

    def start(s, carry):
        r = pl.multiple_of(s * strip, strip)
        place = lax.broadcasted_iota(jnp.int32, (strip, positions.shape[1]), 0) + (inner * rows + r)
        picks = jnp.where(place == positions, 1.0, 0.0).astype(bf16)
        value = tokens[pl.ds(r, strip), :].astype(f32) + mm(picks, mem_ref[...])
        x0_ref[pl.ds(r, strip), :] = value
        x_ref[pl.ds(mine + r, strip), :] = value.astype(bf16)
        return carry
    lax.fori_loop(0, rows // strip, start, 0)
    keep(x0_ref, x0_out)
    core = go(x_ref.at[pl.ds(mine, rows), :], x_ref.at[pl.ds(mine, rows), :], to_core)

    for k in range(1, 4):
        z_q[k].wait_recv()
        x_q.append(go(g_ref.at[0, at[k]], g_ref.at[0, at[k]], to_x))
        y_q.append(go(g_ref.at[0, at[k]], g_ref.at[1, at[k]], to_y))
    z_u = [None] + [go(wu_ref, up_g.at[at[0]], to_z[k]) for k in range(1, 4)]
    z_d = [None] + [go(wd_ref, down_g.at[0, z], to_z[k]) for k in range(1, 4)]
    z_o = [None] + [go(wo_ref, out_g.at[0, z], to_z[k]) for k in range(1, 4)]
    keep(wu_ref, up_g.at[at[0]])
    keep(wd_ref, down_g.at[0, z])
    keep(wo_ref, out_g.at[0, z])
    last = []
    for k in range(2):
        x_q[k].wait_recv()
        last.append(go(g_ref.at[0, far[k]], g_ref.at[1, far[k]], to_y))
    for k in range(2, 4):
        y_q[k].wait_recv()
        last.append(go(g_ref.at[1, at[k]], g_ref.at[1, at[k]], to_x))
    rest = [go(wu_ref, up_g.at[at[0]], to_x), go(wd_ref, down_g.at[1, z], to_y), go(wo_ref, out_g.at[1, z], to_y)]
    for copy in x_q[2:] + y_q[:2] + last + [bias, core]:
        copy.wait_recv()
    own.wait()
    own_bias.wait()
    keep(g_ref, w_out)
    keep(x_ref, x_out)

    lane = lax.broadcasted_iota(jnp.int32, (BLOCK, 128), 1)
    y_ref[...] = jnp.zeros_like(y_ref)

    def project(b, carry):
        r = pl.ds(pl.multiple_of(b * BLOCK, BLOCK), BLOCK)
        for o in range(2):
            y_ref[o, :, 0:576] = mm(x_ref[r, :], g_ref[o].reshape(width, 576)) + b_ref[o, 0:1, 0:576].astype(f32)
        tile = lambda o, n: y_ref[o, :, 128 * n:128 * n + 128]
        turn = lambda value: pltpu.roll(value, 64, 1)
        third = (jnp.where(lane < 64, tile(0, 3), turn(tile(1, 3))), jnp.where(lane < 64, turn(tile(0, 3)), tile(1, 3)),
                 jnp.where(lane < 64, tile(0, 4), turn(tile(1, 4))))
        for n, ref in enumerate((q_ref, k_ref, v_ref)):
            for g, value in enumerate((tile(0, n), tile(1, n), third[n])):
                value = value.astype(bf16)
                if n == 0:
                    value = value * jnp.asarray(0.125, bf16)
                ref[r, 128 * g:128 * g + 128] = value
        return carry
    lax.fori_loop(0, 2 * rows // BLOCK, project, 0)
    for src, dst in ((q_ref, q_out), (k_ref, k_out), (v_ref, v_out)):
        keep(src, dst)
    for k in range(1, 4):
        z_u[k].wait_recv()
        rest.append(go(up_g.at[at[k]], up_g.at[at[k]], to_x))
        z_d[k].wait_recv()
        rest.append(go(down_g.at[0, zs[k]], down_g.at[1, zs[k]], to_y))
        z_o[k].wait_recv()
        rest.append(go(out_g.at[0, zs[k]], out_g.at[1, zs[k]], to_y))
    for copy in rest:
        copy.wait_recv()
    for copy in started:
        copy.wait_send()
    for copy in local[2:]:
        copy.wait()


def entry(tokens, positions, memory_rows, shard_qkv, biases, up, down, out):
    f32, bf16 = jnp.float32, jnp.bfloat16
    rows, width = tokens.shape
    r = up.shape[0]
    shape, v = jax.ShapeDtypeStruct, pltpu.VMEM
    hbm, vmem = pl.BlockSpec(memory_space=pl.ANY), pl.BlockSpec(memory_space=pltpu.VMEM)
    qkv = shape((2 * rows, 384), bf16)
    return pl.pallas_call(
        entry_kernel,
        out_shape=(shape((rows, width), f32), shape((2 * rows, width), bf16), qkv, qkv, qkv,
                   shape((2, 8, r, 576), bf16), shape((8, r, up.shape[1]), bf16), shape((2, 4, r, down.shape[1]), bf16),
                   shape((2, 4, r, out.shape[1]), bf16)),
        in_specs=[vmem] * 8,
        out_specs=[hbm] * 9,
        scratch_shapes=[
            v((rows, width), f32), v((2 * rows, width), bf16), v((2, 8, r, 576), bf16), v((2, 16, 640), bf16),
            v((2, BLOCK, 640), f32), v((2 * rows, 384), bf16), v((2 * rows, 384), bf16), v((2 * rows, 384), bf16),
            pltpu.SemaphoreType.DMA((48,)), pltpu.SemaphoreType.DMA((48,)), pltpu.SemaphoreType.DMA((16,)),
        ],
        compiler_params=pltpu.CompilerParams(vmem_limit_bytes=VMEM_MAX, collective_id=0, has_side_effects=True),
        cost_estimate=pl.CostEstimate(flops=4 * rows * width * 1152, bytes_accessed=20_000_000, transcendentals=0),
        name="entry",
    )(tokens, positions, memory_rows, shard_qkv, biases, up, down, out)


def exit_kernel(x_all, d0, d1, d2, w_all, third, first_ref, dr1, pos_ref, sums_in, up_in,
                tok_out, first_out, second_out, small_out,
                x_ref, xt_ref, d_ref, w_ref, dr_ref, g_ref, own_ref, oth_ref, yb_ref, xs_ref, xb_ref, zt_ref, zs_ref, zb_ref,
                fs_ref, fb_ref, their_ref, got_ref, tok_ref, s_ref, t_ref, r_ref, send, recv, sem):
    f32, bf16 = jnp.float32, jnp.bfloat16
    rows, width = dr_ref.shape
    dp, tensor = lax.axis_index("dp"), lax.axis_index("tensor")
    z, x = dp // 2, dp % 2
    inner, outer = tensor % 2, tensor // 2
    up_z = [None] + [(z + k) % 4 for k in range(1, 4)]
    to_z = [None] + [(2 * up_z[k] + x, tensor) for k in range(1, 4)]
    to_x = (2 * z + 1 - x, tensor)
    to_y = (dp, (tensor + 2) % 4)
    to_core = (dp, tensor + 1 - 2 * inner)
    near_z = (2 * (z + 1 - 2 * (z % 2)) + x, tensor)
    far_z = to_z[2]
    loads = []
    for src, dst in ((d2, d_ref.at[2]), (x_all, x_ref), (d0, d_ref.at[0]), (d1, d_ref.at[1]),
                     (w_all.at[0, :, pl.ds(0, 384)], w_ref.at[0]), (w_all.at[1, :, pl.ds(0, 384)], w_ref.at[1]),
                     (third, w_ref.at[2]), (dr1, dr_ref)):
        copy = pltpu.make_async_copy(src, dst, sem.at[len(loads)])
        copy.start()
        loads.append(copy)
    greet(to_z[1:] + [to_x, to_y, to_core])
    ex = Exchange(send, recv)
    started = []

    def go(src, dst, device):
        copy = ex.copy(src, dst, device)
        copy.start()
        started.append(copy)
        return copy

    for k in range(1, 4):
        fs_ref[k - 1] = first_ref[up_z[k]].astype(bf16)
    z_first = [go(fs_ref.at[k - 1], fb_ref.at[k - 1], to_z[k]) for k in range(1, 4)]

    loads[0].wait()
    loads[1].wait()
    for b in range(2 * rows // BLOCK):
        xt_ref[:, BLOCK * b:BLOCK * b + BLOCK] = x_ref[BLOCK * b:BLOCK * b + BLOCK, :].T
    for m in range(0, width, BLOCK):
        g_ref[m:m + BLOCK, :] = mm(xt_ref[m:m + BLOCK, :], d_ref[2])
    half = own_ref.shape[3]
    lane = lax.broadcasted_iota(jnp.int32, (half, 128), 1)
    for p in range(8):
        for n in range(3):
            low = g_ref[2 * half * p:2 * half * p + half, 128 * n:128 * n + 128]
            high = g_ref[2 * half * p + half:2 * half * (p + 1), 128 * n:128 * n + 128]
            own_ref[p % 2, p // 2, n] = jnp.where(lane < 64, low, pltpu.roll(high, 64, 1))
            oth_ref[p % 2, p // 2, n] = jnp.where(lane < 64, pltpu.roll(low, 64, 1), high).astype(bf16)
    y_far = go(oth_ref.at[1 - x], yb_ref.at[0], to_y)
    y_near = go(oth_ref.at[x], yb_ref.at[1], to_y)

    for copy in loads[2:]:
        copy.wait()
    place = lax.broadcasted_iota(jnp.int32, (32, 2 * rows), 1)
    which = lax.broadcasted_iota(jnp.int32, (32, 2 * rows), 0)
    picks = jnp.where((place == pos_ref[:, 0:1]) | (which == 24), 1.0, 0.0).astype(bf16)
    picked = [mm(picks, d_ref[n]) for n in range(3)]
    own_place = lax.broadcasted_iota(jnp.int32, (32, rows), 1) + inner * rows
    own_picks = jnp.where(own_place == pos_ref[:, 0:1], 1.0, 0.0)
    memory = lax.dot_general(own_picks, dr_ref[...], NN, precision=lax.Precision.HIGHEST, preferred_element_type=f32)
    for n in range(3):
        memory = memory + mm(picked[n].astype(bf16), w_ref[n], NT)
    hw = s_ref.shape[2]

    def put(row, value):
        for h in range(2):
            s_ref[h, row:row + 1, :] = value[:, hw * h:hw * h + hw]
    for h in range(2):
        s_ref[h, 0:24, :] = memory[0:24, hw * h:hw * h + hw]
        s_ref[h, 38:40, :] = jnp.zeros((2, hw), f32)
    for n in range(6):
        put(24 + n, jnp.sum(sums_in[n], axis=0, keepdims=True))
    ups = [jnp.sum(up_in[n], axis=0, keepdims=True) for n in (0, 2, 1, 3)]
    total = [value[24:25, :] for value in picked]
    turned = jnp.concatenate([pltpu.roll(picked[2][24:32, 128 * n:128 * n + 128], 64, 1) for n in range(3)], axis=1)[0:1, :]
    for t in range(4):
        n = (t % 2 + inner) % 2 + 2 * ((t // 2 + outer) % 2)
        value = jnp.zeros_like(ups[0])
        for other in range(4):
            value = value + jnp.where(n == other, ups[other], 0.0)
        put(30 + t, value)
        s_ref[0, 34 + t:35 + t, :] = jnp.where(n == 0, total[0], 0.0) + jnp.where(n == 2, total[1], 0.0)
        s_ref[1, 34 + t:35 + t, :] = jnp.where(n == 0, total[2], 0.0) + jnp.where(n == 2, turned, 0.0)
    small = [go(s_ref.at[1 - inner], r_ref.at[0], to_core)]
    hops = [to_y, to_x, near_z, far_z]

    def hop(n):
        small[n].wait_recv()
        t_ref[n] = (s_ref[inner] if n == 0 else t_ref[n - 1]) + r_ref[n]
        if n < 4:
            small.append(go(t_ref.at[n], r_ref.at[n + 1], hops[n]))
        else:
            small.append(go(t_ref.at[n], r_ref.at[5], to_core))
            small_out[inner] = t_ref[n]

    mine = pl.multiple_of(inner * rows, 1024)
    theirs = pl.multiple_of((1 - inner) * rows, 1024)

    def block(start):
        r = pl.ds(pl.multiple_of(start, BLOCK), BLOCK)
        return mm(d_ref[0, r, :], w_ref[0], NT) + mm(d_ref[1, r, :], w_ref[1], NT) + mm(d_ref[2, r, :], w_ref[2], NT)

    def away(b, carry):
        their_ref[pl.ds(pl.multiple_of(b * BLOCK, BLOCK), BLOCK), :] = block(theirs + b * BLOCK).astype(bf16)
        return carry
    lax.fori_loop(0, rows // BLOCK, away, 0)
    tokens = go(their_ref, got_ref, to_core)
    hop(0)
    y_far.wait_recv()
    for k in range(4):
        xs_ref[k] = (own_ref[1 - x, k] + yb_ref[0, k].astype(f32)).astype(bf16)
    x_sum = go(xs_ref, xb_ref, to_x)

    def stay(b, carry):
        tok_ref[pl.ds(pl.multiple_of(b * BLOCK, BLOCK), BLOCK), :] = block(mine + b * BLOCK)
        return carry
    lax.fori_loop(0, rows // BLOCK, stay, 0)
    hop(1)
    y_near.wait_recv()
    x_sum.wait_recv()
    for k in range(4):
        zt_ref[k] = own_ref[x, k] + yb_ref[1, k].astype(f32) + xb_ref[k].astype(f32)
    for k in range(1, 4):
        zs_ref[k - 1] = zt_ref[up_z[k]].astype(bf16)
    z_second = [go(zs_ref.at[k - 1], zb_ref.at[k - 1], to_z[k]) for k in range(1, 4)]
    hop(2)
    tokens.wait_recv()

    def finish(s, carry):
        r = pl.ds(pl.multiple_of(s * STRIP, STRIP), STRIP)
        tok_ref[r, :] = tok_ref[r, :] + got_ref[r, :].astype(f32) + dr_ref[r, :]
        return carry
    lax.fori_loop(0, rows // STRIP, finish, 0)
    out = pltpu.make_async_copy(tok_ref, tok_out, sem.at[8])
    out.start()
    hop(3)
    for copy in z_first:
        copy.wait_recv()
    first_out[...] = first_ref[z] + fb_ref[0].astype(f32) + fb_ref[1].astype(f32) + fb_ref[2].astype(f32)
    for copy in z_second:
        copy.wait_recv()
    second_out[...] = zt_ref[z] + zb_ref[0].astype(f32) + zb_ref[1].astype(f32) + zb_ref[2].astype(f32)
    hop(4)
    small[5].wait_recv()
    small_out[1 - inner] = r_ref[5]
    for copy in started:
        copy.wait_send()
    out.wait()


def leave(x_all, d, w_qkv, third, first, dr1, place, sums, up_sums):
    f32, bf16 = jnp.float32, jnp.bfloat16
    rows, width = dr1.shape
    r, half = first.shape[1], first.shape[1] // 2
    shape, v = jax.ShapeDtypeStruct, pltpu.VMEM
    hbm, vmem = pl.BlockSpec(memory_space=pl.ANY), pl.BlockSpec(memory_space=pltpu.VMEM)
    return pl.pallas_call(
        exit_kernel,
        out_shape=(shape((rows, width), f32), shape((r, 384), f32), shape((3, half, 128), f32), shape((2, 40, width // 2), f32)),
        in_specs=[hbm] * 6 + [vmem, hbm] + [vmem] * 3,
        out_specs=[hbm] + [vmem] * 3,
        scratch_shapes=[
            v((2 * rows, width), bf16), v((width, 2 * rows), bf16), v((3, 2 * rows, 384), bf16), v((3, width, 384), bf16),
            v((rows, width), f32), v((width, 384), f32), v((2, 4, 3, half, 128), f32), v((2, 4, 3, half, 128), bf16),
            v((2, 4, 3, half, 128), bf16), v((4, 3, half, 128), bf16), v((4, 3, half, 128), bf16), v((4, 3, half, 128), f32),
            v((3, 3, half, 128), bf16), v((3, 3, half, 128), bf16), v((3, r, 384), bf16), v((3, r, 384), bf16),
            v((rows, width), bf16), v((rows, width), bf16), v((rows, width), f32), v((2, 40, width // 2), f32),
            v((5, 40, width // 2), f32), v((6, 40, width // 2), f32),
            pltpu.SemaphoreType.DMA((16,)), pltpu.SemaphoreType.DMA((16,)), pltpu.SemaphoreType.DMA((9,)),
        ],
        compiler_params=pltpu.CompilerParams(vmem_limit_bytes=VMEM_MAX, collective_id=2, has_side_effects=True),
        cost_estimate=pl.CostEstimate(flops=2 * rows * width * 384 * 8, bytes_accessed=20_000_000, transcendentals=0),
        name="leave",
    )(x_all, *d, w_qkv, third, first, dr1, place, sums, up_sums)


def layer_norm(values, norm_gain, norm_shift):
    centre = values - jnp.mean(values, axis=-1, keepdims=True)
    spread = jnp.mean(centre * centre, axis=-1, keepdims=True)
    return centre * lax.rsqrt(spread + EPSILON) * norm_gain + norm_shift


def gelu_exact(values):
    return jax.nn.gelu(values, approximate=False)


AXES = ("dp", "tensor")


class Grid:
    def __init__(self, dp, tensor):
        self.dp, self.tensor = dp, tensor
        factors, rest = [2], dp // 2
        while rest > 8:
            factors.insert(0, 4)
            rest //= 4
        if rest > 1:
            factors.insert(0, rest)
        self.factors = factors

    def digit(self, j):
        stride = 1
        for f in self.factors[j + 1:]:
            stride *= f
        return stride, self.factors[j]

    def my_digit(self, j):
        stride, f = self.digit(j)
        return lax.axis_index("dp") // stride % f

    def turn(self, value, j, k):
        stride, f = self.digit(j)
        pairs = []
        for d in range(self.dp):
            g = d // stride % f
            to = d + ((g + k) % f - g) * stride
            for t in range(self.tensor):
                pairs.append((d * self.tensor + t, to * self.tensor + t))
        return lax.ppermute(value, AXES, pairs)

    def swap_dp(self, value, bit):
        pairs = [(d * self.tensor + t, (d ^ bit) * self.tensor + t) for d in range(self.dp) for t in range(self.tensor)]
        return lax.ppermute(value, AXES, pairs)

    def swap(self, value, bit):
        pairs = [(d * self.tensor + t, d * self.tensor + (t ^ bit)) for d in range(self.dp) for t in range(self.tensor)]
        return lax.ppermute(value, AXES, pairs)

    def gather_stage(self, value, j, axis):
        _, f = self.digit(j)
        g = self.my_digit(j)
        got = [value] + [self.turn(value, j, k) for k in range(1, f)]
        if f == 2:
            lower = jnp.where(g == 0, got[0], got[1])
            upper = jnp.where(g == 0, got[1], got[0])
            return jnp.stack([lower, upper], axis=axis)
        ring = got[::-1]
        return lax.dynamic_slice_in_dim(jnp.stack(ring + ring[:-1], axis=axis), f - 1 - g, f, axis)

    def gather(self, shard, outer_first=False):
        count = len(self.factors)
        value = shard
        for j in range(count - 1):
            value = self.gather_stage(value, j, j)
        if outer_first:
            value = jnp.stack([value, self.swap(value, 2)])
            value = self.gather_stage(value, count - 1, count)
            return value.reshape(2, -1, shard.shape[-1])
        value = self.gather_stage(value, count - 1, count - 1)
        value = value.reshape(-1, shard.shape[-1])
        return jnp.stack([value, self.swap(value, 2)])

    def reduce_stage(self, value, j, axis):
        _, f = self.digit(j)
        g = self.my_digit(j)
        total = lax.dynamic_index_in_dim(value, g, axis, keepdims=False).astype(jnp.float32)
        for k in range(1, f):
            part = lax.dynamic_index_in_dim(value, (g + k) % f, axis, keepdims=False)
            total = total + self.turn(part.astype(jnp.bfloat16), j, k).astype(jnp.float32)
        return total

    def reduce(self, parts, outer_first=True):
        count = len(self.factors)
        columns = parts.shape[-1]
        value = parts
        if outer_first:
            value = value[0].astype(jnp.float32) + self.swap(value[1].astype(jnp.bfloat16), 2).astype(jnp.float32)
            value = value.reshape(*self.factors, -1, columns)
            value = self.reduce_stage(value, count - 1, count - 1)
        else:
            value = value.reshape(2, *self.factors, -1, columns)
            value = self.reduce_stage(value, count - 1, count)
            value = value[0] + self.swap(value[1].astype(jnp.bfloat16), 2).astype(jnp.float32)
        for j in reversed(range(count - 1)):
            value = self.reduce_stage(value, j, j)
        return value

    @property
    def stages(self):
        return len(self.factors) + 1

    def open(self, parts, outer_first):
        columns = parts.shape[-1]
        return parts if outer_first else parts.reshape(2, *self.factors, -1, columns)

    def stage(self, value, outer_first, n):
        count = len(self.factors)
        if n == (0 if outer_first else 1):
            value = value[0].astype(jnp.float32) + self.swap(value[1].astype(jnp.bfloat16), 2).astype(jnp.float32)
            return value.reshape(*self.factors, -1, value.shape[-1]) if outer_first else value
        if n == 0:
            return self.reduce_stage(value, count - 1, count)
        return self.reduce_stage(value, count - n, count - n)

    def sends(self, value, outer_first, n):
        count = len(self.factors)
        if n == (0 if outer_first else 1):
            return value[0], [value[1].astype(jnp.bfloat16)]
        j = count - 1 if n == 0 else count - n
        return self.digit_sends(value, j, count if n == 0 else j)

    def digit_sends(self, value, j, axis):
        _, f = self.digit(j)
        g = self.my_digit(j)
        take = lambda k: lax.dynamic_index_in_dim(value, (g + k) % f, axis, keepdims=False)
        return take(0), [take(k).astype(jnp.bfloat16) for k in range(1, f)]

    def moves(self, parts, outer_first, n):
        count = len(self.factors)
        if n == (0 if outer_first else 1):
            return [self.swap(parts[0], 2)]
        j = count - 1 if n == 0 else count - n
        return [self.turn(part, j, k + 1) for k, part in enumerate(parts)]

    def sums(self, kept, parts, outer_first, n):
        value = kept.astype(jnp.float32)
        for part in parts:
            value = value + part.astype(jnp.float32)
        return value.reshape(*self.factors, -1, value.shape[-1]) if n == 0 and outer_first else value

    def total(self, vector):
        for bit in (1, 2):
            vector = vector + self.swap(vector, bit)
        bit = 1
        while bit < self.dp:
            vector = vector + self.swap_dp(vector, bit)
            bit *= 2
        return vector


def shards(grid, tokens, segment_ids, memory_positions, memory_rows, qkv_weight, qv_bias, out_weight, out_bias,
           norm1_gain, norm1_bias, up_weight, up_bias, down_weight, down_bias, norm2_gain, norm2_bias, out_cotangent):
    f32, bf16 = jnp.float32, jnp.bfloat16
    rows, width = tokens.shape
    group_len = segment_ids.shape[1]
    tensor = lax.axis_index("tensor")
    inner, outer = tensor % 2, tensor // 2
    slice_rows = qkv_weight.shape[0]
    heads = qkv_weight.shape[1]
    hd = 64
    hw = heads * hd
    units = up_weight.shape[1]

    segments = lax.dynamic_index_in_dim(segment_ids, outer, 0, keepdims=False)
    positions = lax.dynamic_index_in_dim(memory_positions, outer, 0, keepdims=False)
    row_place = inner * rows + jnp.arange(rows, dtype=jnp.int32)
    picks = (row_place[:, None] == positions[None, :])
    joined = lambda w: w.transpose(1, 0, 2).reshape(width, -1)

    parts = qkv_weight.reshape(slice_rows, heads, 3, hd)
    order_columns = lambda p: jnp.concatenate([p[..., :2, n, :].reshape(*p.shape[:-3], 2 * hd) for n in range(3)]
                                              + [p[..., 2, n, :] for n in range(3)], axis=-1)
    shard_qkv = order_columns(parts)
    shard_out = jnp.pad(out_weight.reshape(slice_rows, hw), ((0, 0), (0, 256 - hw)))
    bias_parts = qv_bias.reshape(heads, 2, hd)
    bias_qkv = order_columns(jnp.stack([bias_parts[:, 0], jnp.zeros_like(bias_parts[:, 0]), bias_parts[:, 1]], 1))
    bias_qkv = jnp.pad(bias_qkv[None], ((0, 15), (0, 64)))
    fused = grid.dp == 8 and grid.tensor == 4
    if fused:
        memory = memory_positions.shape[1]
        place = jnp.pad(positions[None], ((0, 7), (0, 32 - memory)), constant_values=-1)
        table = jnp.pad(memory_rows, ((0, 32 - memory), (0, 0)))
        x0, x_all, q, k, v, w_qkv, up_g, down_g, out_g = entry(tokens, place, table, shard_qkv, bias_qkv, up_weight, down_weight, shard_out)
        column = jnp.pad(jnp.broadcast_to(positions[:, None], (memory, 128)), ((0, 32 - memory), (0, 0)), constant_values=-1)
        w_qkv = w_qkv.reshape(2, width, 9 * hd)
        third = jnp.concatenate([w_qkv[o][:, (6 + n) * hd:(7 + n) * hd] for n in range(3) for o in range(2)], 1)
        up_all = up_g.reshape(width, units)
        ups = (up_all, grid.swap(up_all, 2))
        downs = (down_g, grid.turn(down_g, 1, 1))
        outs = (out_g, grid.turn(out_g, 1, 1))
    else:
        x0 = tokens.astype(f32) + jnp.dot(picks.astype(bf16), memory_rows, preferred_element_type=f32)
        xl = x0.astype(bf16)
        w_qkv = grid.gather(shard_qkv)
        other = grid.swap(xl, 1)
        x_all = jnp.concatenate([jnp.where(inner == 0, xl, other), jnp.where(inner == 0, other, xl)])
        b_two = jnp.stack([bias_qkv[0], grid.swap(bias_qkv[0], 2)]).astype(f32)
        y = [(mm(x_all, w_qkv[o]) + b_two[o, :9 * hd]).astype(bf16) for o in range(2)]
        third = lambda n: [one[:, (6 + n) * hd:(7 + n) * hd] for one in y]
        q, k, v = [jnp.concatenate([y[0][:, 2 * n * hd:2 * (n + 1) * hd], y[1][:, 2 * n * hd:2 * (n + 1) * hd]] + third(n), 1)
                   for n in range(3)]
        q = q * jnp.asarray(0.125, bf16)
        outs, ups, downs = (grid.gather(shard_out, True),), (grid.gather(up_weight),), (grid.gather(down_weight, True),)
    b_up = jnp.concatenate([up_bias, grid.swap(up_bias, 2)])
    b_up = jnp.stack([b_up, grid.swap(b_up, 1)]).astype(f32)
    mixed, lse = attend_forward(q, k, v, segments)
    vec = jnp.stack([out_bias, norm1_gain, norm1_bias, down_bias, norm2_gain, norm2_bias, norm2_bias, norm2_bias]).astype(f32)
    (block_out, dr1, do_all, g_down, g_up, g_out, sums, up_sums) = middle(
        mixed, x0, outs, ups, downs, out_cotangent, vec, b_up.reshape(4, 1, units))
    if fused:
        return finish_small(grid, tensor, x_all, q, k, v, do_all, lse, segments, w_qkv, third, dr1, column, sums, up_sums, block_out,
                            (g_down, g_up, g_out), hw)

    TN = (((0,), (0,)), ((), ()))
    tie = lax.optimization_barrier
    kinds = (True, False, True)
    state = [grid.open(parts, kind) for parts, kind in zip((g_down, g_up, g_out), kinds)]
    step = lambda n, state: [grid.stage(value, kind, n) for value, kind in zip(state, kinds)]
    late = [(1, 0, 2)[n] for n in range(3)]
    d = [None] * 3
    state, d[1] = step(0, state), attend_backward(1, q, k, v, do_all, lse, segments)
    state, d[1], q = tie((state, d[1], q))
    g_one = mm(x_all, d[1], TN).astype(bf16)
    state, d[0] = step(1, state), attend_backward(0, q, k, v, do_all, lse, segments)
    state, d[0], q, g_one = tie((state, d[0], q, g_one))
    g_zero = mm(x_all, d[0], TN)
    first = g_zero + grid.swap(g_one, 2).astype(f32)
    state, d[2] = step(2, state), attend_backward(2, q, k, v, do_all, lse, segments)
    state, d[2], first = tie((state, d[2], first))
    for n in range(3, grid.stages):
        state = step(n, state)
    grad_down, grad_up, grad_out = state
    grad_out = grad_out[:, :hw]

    g_two = mm(x_all, d[2], TN)
    side = lambda m, o: jnp.concatenate([m[:, (2 * n + o) * hd:(2 * n + o + 1) * hd] for n in range(3)], 1)
    second = side(g_two, 0) + grid.swap(side(g_two, 1).astype(bf16), 2).astype(f32)
    both = jnp.concatenate([first, second], 1).reshape(*grid.factors, slice_rows, 9 * hd)
    for j in reversed(range(len(grid.factors))):
        both = grid.reduce_stage(both, j, j)
    restore = lambda p: jnp.stack([jnp.concatenate([p[..., 2 * n * hd:2 * (n + 1) * hd].reshape(*p.shape[:-1], 2, hd),
                                                    p[..., None, (6 + n) * hd:(7 + n) * hd]], -2) for n in range(3)], -2)
    grad_qkv = restore(both).reshape(slice_rows, heads, 3 * hd)
    third = jnp.concatenate([w_qkv[o][:, (6 + n) * hd:(7 + n) * hd] for n in range(3) for o in range(2)], 1)
    part = (mm(d[0], w_qkv[0][:, :6 * hd], NT) + mm(d[1], w_qkv[1][:, :6 * hd], NT) + mm(d[2], third, NT)).reshape(2, rows, width)
    mine = lax.dynamic_index_in_dim(part, inner, 0, keepdims=False)
    theirs = lax.dynamic_index_in_dim(part, 1 - inner, 0, keepdims=False).astype(bf16)
    grad_tokens = mine + grid.swap(theirs, 1).astype(f32) + dr1
    d_sum = [jnp.sum(one.astype(f32), axis=0) for one in d]
    d_bias = [jnp.concatenate([d_sum[o]] + [d_sum[2][(2 * n + o) * hd:(2 * n + o + 1) * hd] for n in range(3)]) for o in range(2)]
    dg2, ds2, d_down_bias, dg1, ds1, d_out_bias = jnp.sum(sums, axis=1)
    d_up_bias = jnp.sum(up_sums, axis=1).reshape(2, 2 * units)
    grad_memory = jnp.dot(picks.astype(f32).T, grad_tokens, precision=lax.Precision.HIGHEST)

    order = jnp.arange(4, dtype=jnp.int32) ^ tensor
    up_parts = d_up_bias.reshape(2, 2, units)
    up_parts = jnp.stack([up_parts[0, 0], up_parts[1, 0], up_parts[0, 1], up_parts[1, 1]])[order]
    take = lambda o: restore(d_bias[o])[:, 0::2].reshape(-1)
    blank = jnp.zeros((2 * hw,), f32)
    qv_parts = jnp.stack([take(0), blank, take(1), blank])[order]
    pieces = [grad_memory.reshape(-1), d_out_bias, dg1, ds1, d_down_bias, dg2, ds2, up_parts.reshape(-1), qv_parts.reshape(-1)]
    summed = grid.total(jnp.concatenate(pieces))
    outs, at = [], 0
    for piece in pieces:
        outs.append(lax.slice_in_dim(summed, at, at + piece.size))
        at += piece.size
    t_memory, t_out_bias, t_g1, t_s1, t_down_bias, t_g2, t_s2, t_up, t_qv = outs
    grad_up_bias = lax.dynamic_index_in_dim(t_up.reshape(4, units), tensor, 0, keepdims=False)
    grad_qv = lax.dynamic_index_in_dim(t_qv.reshape(4, heads, 2 * hd), tensor, 0, keepdims=False)
    return (block_out, grad_tokens, t_memory.reshape(-1, width), grad_qkv, grad_qv,
            grad_out.reshape(slice_rows, heads, hd), t_out_bias, t_g1, t_s1, grad_up, grad_up_bias, grad_down,
            t_down_bias, t_g2, t_s2)


def finish_small(grid, tensor, x_all, q, k, v, do_all, lse, segments, w_qkv, third, dr1, column, sums, up_sums, block_out, grads, hw):
    f32, bf16 = jnp.float32, jnp.bfloat16
    tie = lax.optimization_barrier
    TN = (((0,), (0,)), ((), ()))
    kinds = (True, False, True)
    width = dr1.shape[1]
    state = [grid.open(parts, kind) for parts, kind in zip(grads, kinds)]

    def beside(n, state, pair, q, extra, move):
        split = [grid.sends(value, kind, n) for value, kind in zip(state, kinds)]
        parts, extra, q = tie(([s[1] for s in split], extra, q))
        moved = [grid.moves(part, kind, n) for part, kind in zip(parts, kinds)]
        extra = [move(e) for e in extra]
        d = attend_backward(pair, q, k, v, do_all, lse, segments)
        moved, extra, d, q = tie((moved, extra, d, q))
        return [grid.sums(s[0], part, kind, n) for s, part, kind in zip(split, moved, kinds)], d, q, extra

    state, d_one, q, _ = beside(0, state, 1, q, [], None)
    g_one = mm(x_all, d_one, TN).astype(bf16)
    state, d_zero, q, got = beside(1, state, 0, q, [g_one], lambda e: grid.swap(e, 2))
    first = mm(x_all, d_zero, TN) + got[0].astype(f32)
    kept, parts = grid.digit_sends(first.reshape(*grid.factors, -1, first.shape[-1]), 1, 1)
    state, d_two, q, got = beside(2, state, 2, q, parts, lambda e: grid.turn(e, 1, 1))
    first = kept + got[0].astype(f32)
    grad_down, grad_up, grad_out = state
    grad_tokens, one, two, small = leave(x_all, (d_zero, d_one, d_two), w_qkv, third, first, dr1, column, sums, up_sums)
    hd = 64
    slice_rows = one.shape[0]
    two = two.reshape(3, slice_rows // 2, 2, hd).transpose(2, 1, 0, 3).reshape(slice_rows, 1, 3, hd)
    grad_qkv = jnp.concatenate([one.reshape(slice_rows, 3, 2, hd).transpose(0, 2, 1, 3), two], 1).reshape(slice_rows, 3, 3 * hd)
    row = lambda at: lax.dynamic_index_in_dim(small, at, 1, keepdims=False)
    full = lambda at: small[:, at].reshape(width)
    qv = row(34 + tensor)
    part = lambda n: jnp.concatenate([qv[0, 128 * n:128 * n + 128].reshape(2, hd), qv[1:2, 128 * n:128 * n + hd]])
    grad_qv = jnp.concatenate([part(0), part(2)], 1)
    t_out_bias, t_g1, t_s1, t_down_bias, t_g2, t_s2 = [full(24 + n) for n in (5, 3, 4, 2, 0, 1)]
    return (block_out, grad_tokens, small[:, :20].transpose(1, 0, 2).reshape(20, width), grad_qkv, grad_qv,
            grad_out[:, :hw].reshape(slice_rows, 3, hd), t_out_bias, t_g1, t_s1, grad_up, row(30 + tensor).reshape(width), grad_down,
            t_down_bias, t_g2, t_s2)


def solution(mesh):
    grid = Grid(mesh.shape["dp"], mesh.shape["tensor"])
    tokens, dp, none = P(AXES, None), P("dp", None), P()
    heads, matrix = P("dp", "tensor", None), P("dp", "tensor")
    in_specs = (tokens, dp, dp, none, heads, P("tensor", None), heads, none, none, none, matrix, P("tensor"), matrix,
                none, none, none, tokens)
    out_specs = (tokens, tokens, none, heads, P("tensor", None), heads, none, none, none, matrix, P("tensor"), matrix,
                 none, none, none)

    def run(*args):
        return shards(grid, *args)

    return jax.shard_map(run, mesh=mesh, in_specs=in_specs, out_specs=out_specs, check_vma=False)
```

```python
import functools

import jax
import jax.numpy as jnp
from jax import lax
from jax.experimental import pallas as pl
from jax.experimental.pallas import tpu as pltpu
from jax.sharding import PartitionSpec as P

EPSILON = 1e-12
TILE = 256
MASKED = -1e30
VMEM_MAX = 64 * 1024 * 1024 - 128 * 1024
NT = (((1,), (1,)), ((), ()))
NN = (((1,), (0,)), ((), ()))


def mm(a, b, dims=NN):
    return lax.dot_general(a, b, dims, preferred_element_type=jnp.float32)


def fold8(x):
    r = x.shape[0]
    return x.reshape(r // 8, 8, x.shape[1])


def head_masks(block):
    lane = lax.broadcasted_iota(jnp.int32, block.shape, 1)
    zero = jnp.zeros_like(block)
    return jnp.where(lane < 64, block, zero), jnp.where(lane < 64, zero, block)


def tile_visible(first_ref, last_ref, i, t):
    return (first_ref[t] == 0) | ((first_ref[t] <= last_ref[i]) & (last_ref[t] >= first_ref[i]))


def forward_kernel(first_ref, last_ref, q_ref, k_ref, v_ref, kseg_ref, qseg_ref, o_ref, lse_ref,
                   vt_ref, qm_ref, s_ref, m_ref, l_ref, acc_ref):
    i = pl.program_id(0)
    tiles = pl.num_programs(0)
    pairs = q_ref.shape[1] // 128
    heads = 2 * pairs

    @pl.when(i == 0)
    def _():
        def turn(t, c):
            rows = pl.ds(pl.multiple_of(t * TILE, TILE), TILE)
            vt_ref[t] = v_ref[rows, :].T
            return c
        lax.fori_loop(0, tiles, turn, 0)

    for g in range(pairs):
        a, b = head_masks(q_ref[:, 128 * g:128 * g + 128])
        qm_ref[2 * g] = a
        qm_ref[2 * g + 1] = b
    m_ref[...] = jnp.full_like(m_ref, MASKED)
    l_ref[...] = jnp.zeros_like(l_ref)
    acc_ref[...] = jnp.zeros_like(acc_ref)
    qseg = qseg_ref[0:1, :]

    def scores(t, c):
        @pl.when(tile_visible(first_ref, last_ref, i, t))
        def _():
            rows = pl.ds(pl.multiple_of(t * TILE, TILE), TILE)
            kseg = kseg_ref[rows, :]
            kseg = jnp.concatenate([kseg, kseg], axis=1)
            seen = (kseg == 0) | (kseg == qseg)
            for h in range(heads):
                kp = k_ref[rows, 128 * (h // 2):128 * (h // 2) + 128]
                s = mm(kp, qm_ref[h], NT)
                s = jnp.where(seen, s, MASKED)
                s_ref[h, t] = s
                m_ref[h] = jnp.maximum(m_ref[h], jnp.max(fold8(s), axis=0))
        return c
    lax.fori_loop(0, tiles, scores, 0)
    for h in range(heads):
        m_ref[h] = jnp.broadcast_to(jnp.max(m_ref[h], axis=0, keepdims=True), (8, TILE))

    def mix(t, c):
        @pl.when(tile_visible(first_ref, last_ref, i, t))
        def _():
            for h in range(heads):
                p = jnp.exp(s_ref[h, t] - m_ref[h, 0:1, :])
                l_ref[h] = l_ref[h] + jnp.sum(fold8(p), axis=0)
                acc_ref[h] = acc_ref[h] + mm(vt_ref[t, 64 * h:64 * h + 64, :], p.astype(jnp.bfloat16))
        return c
    lax.fori_loop(0, tiles, mix, 0)
    for h in range(heads):
        total = jnp.sum(l_ref[h], axis=0, keepdims=True)
        lse_ref[h:h + 1, :] = m_ref[h, 0:1, :] + jnp.log(total)
        acc_ref[h] = acc_ref[h] / total
    for g in range(pairs):
        pair = jnp.concatenate([acc_ref[2 * g], acc_ref[2 * g + 1]], axis=0)
        o_ref[:, 128 * g:128 * g + 128] = pair.T.astype(jnp.bfloat16)


def attend_forward(q, k, v, seg):
    n, width = q.shape
    tiles = n // TILE
    heads = width // 64
    first = seg[::TILE]
    last = seg[TILE - 1::TILE]
    kseg = jnp.broadcast_to(seg[:, None], (n, 128))
    qseg = jnp.broadcast_to(seg[None, :], (8, n))
    whole = lambda shape: pl.BlockSpec(shape, lambda i, *_: (0,) * len(shape))
    return pl.pallas_call(
        forward_kernel,
        out_shape=(jax.ShapeDtypeStruct((n, width), jnp.bfloat16), jax.ShapeDtypeStruct((8, n), jnp.float32)),
        grid_spec=pltpu.PrefetchScalarGridSpec(
            num_scalar_prefetch=2, grid=(tiles,),
            in_specs=[pl.BlockSpec((TILE, width), lambda i, *_: (i, 0)), whole((n, width)), whole((n, width)),
                      whole((n, 128)), pl.BlockSpec((8, TILE), lambda i, *_: (0, i))],
            out_specs=[pl.BlockSpec((TILE, width), lambda i, *_: (i, 0)), pl.BlockSpec((8, TILE), lambda i, *_: (0, i))],
            scratch_shapes=[
                pltpu.VMEM((tiles, width, TILE), jnp.bfloat16),
                pltpu.VMEM((heads, TILE, 128), jnp.bfloat16),
                pltpu.VMEM((heads, tiles, TILE, TILE), jnp.float32),
                pltpu.VMEM((heads, 8, TILE), jnp.float32),
                pltpu.VMEM((heads, 8, TILE), jnp.float32),
                pltpu.VMEM((heads, 64, TILE), jnp.float32),
            ]),
        compiler_params=pltpu.CompilerParams(dimension_semantics=("arbitrary",), vmem_limit_bytes=VMEM_MAX),
        cost_estimate=pl.CostEstimate(flops=4 * n * n * width, bytes_accessed=8 * n * width, transcendentals=n * n * heads),
        name="attend_forward",
    )(first, last, q, k, v, kseg, qseg)


def backward_kernel(base, first_ref, last_ref, q_ref, do_ref, o_ref, k_ref, v_ref, kseg_ref, qseg_ref, lse_ref,
                    d_ref, kt_ref, qm_ref, dom_ref, delta_ref, dqt_ref, dka_ref, dva_ref):
    i = pl.program_id(0)
    tiles = pl.num_programs(0)

    @pl.when(i == 0)
    def _():
        def turn(t, c):
            rows = pl.ds(pl.multiple_of(t * TILE, TILE), TILE)
            kt_ref[t] = k_ref[rows, :].T
            dka_ref[rows, :] = jnp.zeros((TILE, 128), jnp.float32)
            dva_ref[rows, :] = jnp.zeros((TILE, 128), jnp.float32)
            return c
        lax.fori_loop(0, tiles, turn, 0)

    for ref, masked in ((q_ref, qm_ref), (do_ref, dom_ref)):
        masked[0], masked[1] = head_masks(ref[...])
    inner = (do_ref[...].astype(jnp.float32) * o_ref[...].astype(jnp.float32)).T
    for h in range(2):
        delta_ref[h] = jnp.broadcast_to(jnp.sum(inner[64 * h:64 * h + 64], axis=0, keepdims=True), (8, TILE))
    dqt_ref[...] = jnp.zeros_like(dqt_ref)
    qseg = qseg_ref[0:1, :]

    def count(t, c):
        prompt, before, upto = c
        return (prompt + (first_ref[t] == 0).astype(jnp.int32), before + (last_ref[t] < first_ref[i]).astype(jnp.int32),
                upto + (first_ref[t] <= last_ref[i]).astype(jnp.int32))
    zero = jnp.int32(0)
    prompt, before, upto = lax.fori_loop(0, tiles, count, (zero, zero, zero))
    start = jnp.maximum(prompt, before)
    visible = prompt + jnp.maximum(upto - start, 0)

    def one_tile(n):
        t = jnp.where(n < prompt, n, start + n - prompt)
        rows = pl.ds(pl.multiple_of(t * TILE, TILE), TILE)
        kseg = kseg_ref[rows, :]
        kseg = jnp.concatenate([kseg, kseg], axis=1)
        seen = (kseg == 0) | (kseg == qseg)
        kp = k_ref[rows, :]
        vp = v_ref[rows, :]
        s = [mm(kp, qm_ref[h], NT) for h in range(2)]
        d = [mm(vp, dom_ref[h], NT) for h in range(2)]
        p = [jnp.where(seen, jnp.exp(s[h] - lse_ref[base + h:base + h + 1, :]), 0.0) for h in range(2)]
        ds = [(p[h] * (d[h] - delta_ref[h, 0:1, :])).astype(jnp.bfloat16) for h in range(2)]
        p = [value.astype(jnp.bfloat16) for value in p]
        dva_ref[rows, :] = dva_ref[rows, :] + (mm(p[0], dom_ref[0]) + mm(p[1], dom_ref[1]))
        dka_ref[rows, :] = dka_ref[rows, :] + (mm(ds[0], qm_ref[0]) + mm(ds[1], qm_ref[1]))
        return [mm(kt_ref[t, 64 * h:64 * h + 64, :], ds[h]) for h in range(2)]

    def two_tiles(n, c):
        one, two = one_tile(2 * n), one_tile(2 * n + 1)
        for h in range(2):
            dqt_ref[h] = dqt_ref[h] + (one[h] + two[h])
        return c
    lax.fori_loop(0, visible // 2, two_tiles, 0)

    @pl.when(visible % 2 == 1)
    def _():
        for h, value in enumerate(one_tile(visible - 1)):
            dqt_ref[h] = dqt_ref[h] + value
    pair = jnp.concatenate([dqt_ref[0], dqt_ref[1]], axis=0)
    own = pl.ds(pl.multiple_of(i * TILE, TILE), TILE)
    d_ref[own, 0:128] = (pair.T * 0.125).astype(jnp.bfloat16)

    @pl.when(i == tiles - 1)
    def _():
        d_ref[:, 128:256] = dka_ref[...].astype(jnp.bfloat16)
        d_ref[:, 256:384] = dva_ref[...].astype(jnp.bfloat16)


def attend_backward(g, q, k, v, do, o, lse, seg):
    n, width = q.shape[0], 128
    tiles = n // TILE
    heads = width // 64
    first = seg[::TILE]
    last = seg[TILE - 1::TILE]
    kseg = jnp.broadcast_to(seg[:, None], (n, 128))
    qseg = jnp.broadcast_to(seg[None, :], (8, n))
    whole = lambda shape: pl.BlockSpec(shape, lambda i, *_: (0,) * len(shape))
    rows = pl.BlockSpec((TILE, width), lambda i, *_: (i, g))
    column = pl.BlockSpec((n, width), lambda i, *_: (0, g))
    stat = pl.BlockSpec((8, TILE), lambda i, *_: (0, i))
    return pl.pallas_call(
        functools.partial(backward_kernel, 2 * g),
        out_shape=jax.ShapeDtypeStruct((n, 3 * width), jnp.bfloat16),
        grid_spec=pltpu.PrefetchScalarGridSpec(
            num_scalar_prefetch=2, grid=(tiles,),
            in_specs=[rows, rows, rows, column, column, whole((n, 128)), stat, stat],
            out_specs=whole((n, 3 * width)),
            scratch_shapes=[
                pltpu.VMEM((tiles, width, TILE), jnp.bfloat16),
                pltpu.VMEM((heads, TILE, 128), jnp.bfloat16),
                pltpu.VMEM((heads, TILE, 128), jnp.bfloat16),
                pltpu.VMEM((heads, 8, TILE), jnp.float32),
                pltpu.VMEM((heads, 64, TILE), jnp.float32),
                pltpu.VMEM((n, width), jnp.float32),
                pltpu.VMEM((n, width), jnp.float32),
            ]),
        compiler_params=pltpu.CompilerParams(dimension_semantics=("arbitrary",), vmem_limit_bytes=VMEM_MAX),
        cost_estimate=pl.CostEstimate(flops=10 * n * n * width, bytes_accessed=14 * n * width, transcendentals=n * n * heads),
        name="attend_backward",
    )(first, last, q, do, o, k, v, kseg, qseg, lse)


BLOCK = 256
STRIP = 64


def normal_cdf_parts(u):
    v = u * 0.7071067811865476
    c = jnp.clip(v, -3.832506856900711, 3.832506856900711)
    c2 = c * c
    top = 0.00022905065861350646
    for a in (0.0034082910107109506, 0.050955695062380861, 0.18520832239976145, 1.128379143519084):
        top = top * c2 + a
    low = -1.1791602954361697e-7
    for b in (0.000023547966471313185, 0.0010179625278914885, 0.014070470171167667, 0.11098505178285362,
              0.49746925110067538, 1.0):
        low = low * c2 + b
    cdf = 0.5 + 0.5 * (c * top / low)
    slope = jnp.exp(-(v * v)) * (u * 0.3989422804014327)
    return u * cdf, cdf + slope


def middle_kernel(pieces, o_all, x0, outs, ups, downs, cot, vec_ref, bup_ref,
                  block_out, dr1, do_all, g_down, g_up, g_out, sums_ref, upsum_ref,
                  o_ref, raw_ref, wo_ref, wu_ref, wd_ref, hat_ref, inv_ref, acc_ref, hl_ref, hlt_ref, gp_ref, z_ref, c_ref,
                  df_ref, dft_ref, y_ref, st_ref, su_ref, ru_ref, rd_ref, go_ref, rgo_ref, u0_ref, u1_ref,
                  sem, osem, send, recv):
    f32, bf16 = jnp.float32, jnp.bfloat16
    rows, width = hat_ref.shape
    blocks = rows // BLOCK
    part = wu_ref.shape[2]
    bf = lambda a: a.astype(bf16)
    dp, tensor = lax.axis_index("dp"), lax.axis_index("tensor")
    inner = tensor % 2
    partner = (dp, tensor + 1 - 2 * inner)
    mine = pl.multiple_of(inner * rows, 1024)
    theirs = pl.multiple_of((1 - inner) * rows, 1024)
    greet([partner])

    def remote(n, src, dst):
        return pltpu.make_async_remote_copy(src, dst, send.at[n], recv.at[n], device_id=partner,
                                            device_id_type=pl.DeviceIdType.MESH)

    swap_o = remote(0, o_all.at[pl.ds(theirs, rows), :], o_ref.at[1])
    swap_o.start()
    count = [0]

    def load(src, dst):
        copy = pltpu.make_async_copy(src, dst, sem.at[count[0]])
        count[0] += 1
        copy.start()
        return copy

    def weight(sources, dst):
        if not pieces:
            return [load(sources[0].at[o], dst.at[o]) for o in range(2)]
        digit = dp % 2
        made = []
        for o in range(2):
            for zi in range(sources[0].shape[1]):
                for n in range(2):
                    place = 2 * zi + (digit if n == 0 else 1 - digit)
                    r = sources[n].shape[2]
                    made.append(load(sources[n].at[o, zi], dst.at[o, pl.ds(pl.multiple_of(place * r, r), r), :]))
        return made

    first = [load(o_all.at[pl.ds(mine, rows), :], o_ref.at[0]), load(x0, hat_ref)] + weight(outs, raw_ref.at[0])
    if pieces:
        second = [load(ups[o], wu_ref.at[o]) for o in range(2)]
    else:
        second = [load(ups[0].at[o], wu_ref.at[o]) for o in range(2)]
    second = second + weight(downs, wd_ref)
    late = load(cot, c_ref)
    vec = lambda n: vec_ref[n:n + 1, :]
    sums_ref[...] = jnp.zeros_like(sums_ref)
    upsum_ref[...] = jnp.zeros_like(upsum_ref)
    for copy in first:
        copy.wait()
    swaps = [remote(1, raw_ref.at[0], raw_ref.at[1])]
    swaps[0].start()
    for copy in second:
        copy.wait()
    for o in range(2):
        swaps.append(remote(2 + 2 * o, wu_ref.at[o], wu_ref.at[2 + o]))
        swaps.append(remote(3 + 2 * o, wd_ref.at[o], wd_ref.at[2 + o]))
    for copy in swaps[1:]:
        copy.start()
    lane = lax.broadcasted_iota(jnp.int32, (width, 128), 1)

    def order_heads(side):
        wo_ref[side, :, 0:128] = raw_ref[side, 0, :, 0:128]
        wo_ref[side, :, 128:256] = raw_ref[side, 1, :, 0:128]
        upper = pltpu.roll(raw_ref[side, 1, :, 128:256].astype(f32), 64, 1)
        wo_ref[side, :, 256:384] = bf(jnp.where(lane < 64, raw_ref[side, 0, :, 128:256].astype(f32), upper))
    order_heads(0)
    swaps[0].wait()
    order_heads(1)
    swap_o.wait()

    def strips(body):
        def run(s, carry):
            body(pl.ds(pl.multiple_of(s * STRIP, STRIP), STRIP))
            return carry
        lax.fori_loop(0, rows // STRIP, run, 0)

    def add_sum(n, value):
        sums_ref[n] = sums_ref[n] + jnp.sum(fold(value), axis=0)

    def fold(value):
        return value.reshape(value.shape[0] // 8, 8, value.shape[1])

    def mean(value):
        return jnp.sum(value, axis=-1, keepdims=True) * (1.0 / width)

    def project(b, carry):
        r = pl.ds(pl.multiple_of(b * BLOCK, BLOCK), BLOCK)
        acc_ref[r, :] = mm(o_ref[0, r, :], wo_ref[0], NT) + mm(o_ref[1, r, :], wo_ref[1], NT)
        return carry
    lax.fori_loop(0, blocks, project, 0)

    def first_norm(r):
        r1 = hat_ref[r, :] + (acc_ref[r, :] + vec(0))
        centre = r1 - mean(r1)
        inv = lax.rsqrt(mean(centre * centre) + EPSILON)
        hat = centre * inv
        hat_ref[r, :] = hat
        inv_ref[r, :] = inv
        hl_ref[r, :] = bf(hat * vec(1) + vec(2))
    strips(first_norm)
    for b in range(blocks):
        hlt_ref[:, BLOCK * b:BLOCK * b + BLOCK] = hl_ref[BLOCK * b:BLOCK * b + BLOCK, :].T
    acc_ref[...] = jnp.zeros_like(acc_ref)

    bufs = (u0_ref, u1_ref)

    def forward(j, carry):
        for o in range(2):
            @pl.when(j == 2 + o)
            def _(o=o):
                swaps[1 + 2 * o].wait()
                swaps[2 + 2 * o].wait()

        def lift(b):
            bufs[b % 2][...] = mm(hl_ref[BLOCK * b:BLOCK * b + BLOCK, :], wu_ref[j]) + bup_ref[j, 0:1, :].astype(f32)
        lift(0)
        for b in range(blocks):
            if b + 1 < blocks:
                lift(b + 1)
            r = slice(BLOCK * b, BLOCK * b + BLOCK)
            for i in range(0, BLOCK, 32):
                for w in range(0, part, 256):
                    z, gp = normal_cdf_parts(bufs[b % 2][i:i + 32, w:w + 256])
                    z_ref[j, BLOCK * b + i:BLOCK * b + i + 32, w:w + 256] = bf(z)
                    gp_ref[j, BLOCK * b + i:BLOCK * b + i + 32, w:w + 256] = gp
            acc_ref[r, :] = acc_ref[r, :] + mm(z_ref[j, r, :], wd_ref[j], NT)
        return carry
    lax.fori_loop(0, 4, forward, 0)
    late.wait()

    def second_norm(r):
        h1 = hat_ref[r, :] * vec(1) + vec(2)
        r2 = h1 + (acc_ref[r, :] + vec(3))
        centre = r2 - mean(r2)
        inv = lax.rsqrt(mean(centre * centre) + EPSILON)
        hat = centre * inv
        y_ref[r, :] = bf(hat * vec(4) + vec(5))
        c = c_ref[r, :].astype(f32)
        add_sum(0, c * hat)
        add_sum(1, c)
        w = c * vec(4)
        dr2 = (w - mean(w) - hat * mean(w * hat)) * inv
        acc_ref[r, :] = dr2
        low = bf(dr2)
        df_ref[r, :] = low
        add_sum(2, low.astype(f32))
    strips(second_norm)
    stores = [pltpu.make_async_copy(y_ref, block_out, osem.at[0])]
    stores[0].start()
    for b in range(blocks):
        dft_ref[:, BLOCK * b:BLOCK * b + BLOCK] = df_ref[BLOCK * b:BLOCK * b + BLOCK, :].T

    def backward(n, carry):
        j = 3 - n

        def lower(b):
            bufs[b % 2][...] = mm(df_ref[BLOCK * b:BLOCK * b + BLOCK, :], wd_ref[j])
        slot = n % 2
        away = [remote(6 + slot, st_ref.at[slot], rd_ref.at[slot]), remote(8 + slot, su_ref.at[slot], ru_ref.at[slot])]
        lower(0)
        for b in range(blocks):
            if b + 1 < blocks:
                lower(b + 1)
            r = slice(BLOCK * b, BLOCK * b + BLOCK)
            for i in range(0, BLOCK, 64):
                q = slice(BLOCK * b + i, BLOCK * b + i + 64)
                dul = bf(bufs[b % 2][i:i + 64, :] * gp_ref[j, q, :])
                upsum_ref[j] = upsum_ref[j] + jnp.sum(fold(dul.astype(f32)), axis=0)
                hat2_ref[q, :] = dul
            acc_ref[r, :] = acc_ref[r, :] + mm(hat2_ref[r, :], wu_ref[j], NT)

        @pl.when(n < 2)
        def _():
            for m in range(0, width, BLOCK):
                st_ref[slot, m:m + BLOCK, :] = bf(mm(dft_ref[m:m + BLOCK, :], z_ref[j]))
            away[0].start()
            for m in range(0, width, BLOCK):
                su_ref[slot, m:m + BLOCK, :] = bf(mm(hlt_ref[m:m + BLOCK, :], hat2_ref[...]))
            away[1].start()

        @pl.when(n >= 2)
        def _():
            away[0].wait()
            for m in range(0, width, BLOCK):
                got = rd_ref[slot, m:m + BLOCK, :].astype(f32)
                st_ref[slot, m:m + BLOCK, :] = bf(mm(dft_ref[m:m + BLOCK, :], z_ref[j]) + got)
            pltpu.make_async_copy(st_ref.at[slot], g_down.at[j], osem.at[1 + slot]).start()
            away[1].wait()
            for m in range(0, width, BLOCK):
                got = ru_ref[slot, m:m + BLOCK, :].astype(f32)
                su_ref[slot, m:m + BLOCK, :] = bf(mm(hlt_ref[m:m + BLOCK, :], hat2_ref[...]) + got)
            pltpu.make_async_copy(su_ref.at[slot], g_up.at[j], osem.at[3 + slot]).start()
        return carry
    hat2_ref = y_ref
    stores[0].wait()
    lax.fori_loop(0, 4, backward, 0)

    def first_back(r):
        dh1 = acc_ref[r, :]
        hat = hat_ref[r, :]
        add_sum(3, dh1 * hat)
        add_sum(4, dh1)
        w = dh1 * vec(1)
        grad = (w - mean(w) - hat * mean(w * hat)) * inv_ref[r, :]
        acc_ref[r, :] = grad
        low = bf(grad)
        df_ref[r, :] = low
        add_sum(5, low.astype(f32))
    strips(first_back)
    out = pltpu.make_async_copy(acc_ref, dr1, osem.at[0])
    out.start()
    stores = [out]
    for b in range(blocks):
        dft_ref[:, BLOCK * b:BLOCK * b + BLOCK] = df_ref[BLOCK * b:BLOCK * b + BLOCK, :].T
    lane = lax.broadcasted_iota(jnp.int32, (BLOCK, 128), 1)

    def out_grad(side, m):
        tiles = [mm(dft_ref[m:m + BLOCK, :], o_ref[side, :, 128 * g:128 * g + 128]) for g in range(3)]
        third = [jnp.where(lane < 64, tiles[2], 0.0), jnp.where(lane < 64, pltpu.roll(tiles[2], 64, 1), 0.0)]
        return [jnp.concatenate([tiles[o], third[o]], axis=1) for o in range(2)]
    for m in range(0, width, BLOCK):
        for o, value in enumerate(out_grad(1, m)):
            go_ref[o, m:m + BLOCK, :] = bf(value)
    swap_go = remote(10, go_ref, rgo_ref)
    swap_go.start()
    ow = wo_ref.shape[2]
    for side in (1, 0):
        def push(b, carry):
            r = pl.ds(pl.multiple_of(b * BLOCK, BLOCK), BLOCK)
            y_ref[r, ow * side:ow * side + ow] = bf(mm(df_ref[r, :], wo_ref[side]))
            return carry
        lax.fori_loop(0, blocks, push, 0)
        if side == 1:
            swap_do = remote(11, y_ref.at[:, pl.ds(ow, ow)], do_all.at[pl.ds(mine, rows), :])
            swap_do.start()
        else:
            copy = pltpu.make_async_copy(y_ref.at[:, pl.ds(0, ow)], do_all.at[pl.ds(mine, rows), :], osem.at[5])
            copy.start()
            stores.append(copy)
    swap_go.wait()
    for m in range(0, width, BLOCK):
        for o, value in enumerate(out_grad(0, m)):
            go_ref[o, m:m + BLOCK, :] = bf(value + rgo_ref[o, m:m + BLOCK, :].astype(f32))
    copy = pltpu.make_async_copy(go_ref, g_out, osem.at[6])
    copy.start()
    stores.append(copy)
    for slot in range(2):
        pltpu.make_async_copy(st_ref.at[slot], g_down.at[0], osem.at[1 + slot]).wait()
        pltpu.make_async_copy(su_ref.at[slot], g_up.at[0], osem.at[3 + slot]).wait()
    swap_do.wait()
    for copy in stores:
        copy.wait()


def middle(o_all, x0, outs, ups, downs, cot, vec, bup):
    f32, bf16 = jnp.float32, jnp.bfloat16
    rows, width = x0.shape
    ow = o_all.shape[1]
    part = bup.shape[-1]
    pieces = len(ups) == 2
    shape = jax.ShapeDtypeStruct
    hbm = pl.BlockSpec(memory_space=pl.ANY)
    vmem = pl.BlockSpec(memory_space=pltpu.VMEM)
    v = pltpu.VMEM
    n = len(ups)

    def kernel(o_all, x0, *refs):
        weights = refs[:3 * n]
        middle_kernel(pieces, o_all, x0, weights[:n], weights[n:2 * n], weights[2 * n:], *refs[3 * n:])

    return pl.pallas_call(
        kernel,
        out_shape=(shape((rows, width), bf16), shape((rows, width), f32), shape((2 * rows, ow), bf16),
                   shape((2, width, part), bf16), shape((2, width, part), bf16), shape((2, width, 256), bf16),
                   shape((6, 8, width), f32), shape((4, 8, part), f32)),
        in_specs=[hbm] * (3 + 3 * n) + [vmem] * 2,
        out_specs=[hbm] * 6 + [vmem] * 2,
        scratch_shapes=[
            v((2, rows, ow), bf16), v((2, 2, width, 256), bf16), v((2, width, ow), bf16), v((4, width, part), bf16),
            v((4, width, part), bf16),
            v((rows, width), f32), v((rows, 1), f32), v((rows, width), f32), v((rows, width), bf16), v((width, rows), bf16),
            v((4, rows, part), f32), v((4, rows, part), bf16), v((rows, width), bf16), v((rows, width), bf16),
            v((width, rows), bf16), v((rows, width), bf16), v((2, width, part), bf16),
            v((2, width, part), bf16), v((2, width, part), bf16), v((2, width, part), bf16), v((2, width, 256), bf16),
            v((2, width, 256), bf16), v((BLOCK, part), f32), v((BLOCK, part), f32),
            pltpu.SemaphoreType.DMA((40,)), pltpu.SemaphoreType.DMA((7,)),
            pltpu.SemaphoreType.DMA((12,)), pltpu.SemaphoreType.DMA((12,)),
        ],
        compiler_params=pltpu.CompilerParams(vmem_limit_bytes=VMEM_MAX, collective_id=1, has_side_effects=True),
        cost_estimate=pl.CostEstimate(flops=6 * rows * width * 9 * width, bytes_accessed=60_000_000, transcendentals=2 * rows * 4 * part),
        name="middle",
    )(o_all, x0, *outs, *ups, *downs, cot, vec, bup)


class Exchange:
    def __init__(self, send, recv):
        self.send, self.recv, self.used = send, recv, 0

    def copy(self, src, dst, device):
        n = self.used
        self.used += 1
        return pltpu.make_async_remote_copy(src, dst, self.send.at[n], self.recv.at[n], device_id=device,
                                            device_id_type=pl.DeviceIdType.MESH)


def greet(devices):
    barrier = pltpu.get_barrier_semaphore()
    for device in devices:
        pl.semaphore_signal(barrier, inc=1, device_id=device, device_id_type=pl.DeviceIdType.MESH)
    pl.semaphore_wait(barrier, len(devices))


def entry_kernel(tokens, pos_ref, mem_ref, wq_ref, bq_ref, bu_ref, wu_ref, wd_ref, wo_ref,
                 x0_out, x_out, q_out, k_out, v_out, w_out, up_g, down_g, out_g, bu_out,
                 x0_ref, x_ref, g_ref, b_ref, y_ref, q_ref, k_ref, v_ref, ub_ref, send, recv, sem):
    f32, bf16 = jnp.float32, jnp.bfloat16
    rows, width = x0_ref.shape
    dp, tensor = lax.axis_index("dp"), lax.axis_index("tensor")
    z, x = dp // 2, dp % 2
    inner = tensor % 2
    zs = [(z + 4 - k) % 4 for k in range(4)]
    at = [2 * zs[k] + x for k in range(4)]
    far = [2 * zs[k] + 1 - x for k in range(4)]
    to_z = [None] + [(2 * ((z + k) % 4) + x, tensor) for k in range(1, 4)]
    to_x = (2 * z + 1 - x, tensor)
    to_y = (dp, (tensor + 2) % 4)
    to_core = (dp, tensor + 1 - 2 * inner)
    to_both = (dp, 3 - tensor)
    greet(to_z[1:] + [to_x, to_y, to_core, to_both])
    ex = Exchange(send, recv)
    started = []

    def go(src, dst, device):
        copy = ex.copy(src, dst, device)
        copy.start()
        started.append(copy)
        return copy

    local = []

    def keep(src, dst):
        copy = pltpu.make_async_copy(src, dst, sem.at[len(local)])
        copy.start()
        local.append(copy)
        return copy

    own = keep(wq_ref, g_ref.at[0, at[0]])
    own_bias = keep(bq_ref, b_ref.at[0])
    z_q = [None] + [go(wq_ref, g_ref.at[0, at[0]], to_z[k]) for k in range(1, 4)]
    x_q = [go(wq_ref, g_ref.at[0, at[0]], to_x)]
    y_q = [go(wq_ref, g_ref.at[1, at[0]], to_y)]
    bias = go(bq_ref, b_ref.at[1], to_y)
    up_bias = [go(bu_ref, ub_ref.at[n - 1], to) for n, to in ((1, to_y), (2, to_core), (3, to_both))]

    mine = pl.multiple_of(inner * rows, 1024)
    positions = pos_ref[0:1, :]
    strip = 128

    def start(s, carry):
        r = pl.multiple_of(s * strip, strip)
        place = lax.broadcasted_iota(jnp.int32, (strip, positions.shape[1]), 0) + (inner * rows + r)
        picks = jnp.where(place == positions, 1.0, 0.0).astype(bf16)
        value = tokens[pl.ds(r, strip), :].astype(f32) + mm(picks, mem_ref[...])
        x0_ref[pl.ds(r, strip), :] = value
        x_ref[pl.ds(mine + r, strip), :] = value.astype(bf16)
        return carry
    lax.fori_loop(0, rows // strip, start, 0)
    keep(x0_ref, x0_out)
    core = go(x_ref.at[pl.ds(mine, rows), :], x_ref.at[pl.ds(mine, rows), :], to_core)

    for k in range(1, 4):
        z_q[k].wait_recv()
        x_q.append(go(g_ref.at[0, at[k]], g_ref.at[0, at[k]], to_x))
        y_q.append(go(g_ref.at[0, at[k]], g_ref.at[1, at[k]], to_y))
    z_u = [None] + [go(wu_ref, up_g.at[at[0]], to_z[k]) for k in range(1, 4)]
    z_d = [None] + [go(wd_ref, down_g.at[0, z], to_z[k]) for k in range(1, 4)]
    z_o = [None] + [go(wo_ref, out_g.at[0, z], to_z[k]) for k in range(1, 4)]
    keep(wu_ref, up_g.at[at[0]])
    keep(wd_ref, down_g.at[0, z])
    keep(wo_ref, out_g.at[0, z])
    last = []
    for k in range(2):
        x_q[k].wait_recv()
        last.append(go(g_ref.at[0, far[k]], g_ref.at[1, far[k]], to_y))
    for k in range(2, 4):
        y_q[k].wait_recv()
        last.append(go(g_ref.at[1, at[k]], g_ref.at[1, at[k]], to_x))
    rest = [go(wu_ref, up_g.at[at[0]], to_x), go(wd_ref, down_g.at[1, z], to_y), go(wo_ref, out_g.at[1, z], to_y)]
    for copy in x_q[2:] + y_q[:2] + last + [bias, core]:
        copy.wait_recv()
    own.wait()
    own_bias.wait()
    keep(g_ref, w_out)
    keep(x_ref, x_out)

    lane = lax.broadcasted_iota(jnp.int32, (BLOCK, 128), 1)
    y_ref[...] = jnp.zeros_like(y_ref)

    def project(b, carry):
        r = pl.ds(pl.multiple_of(b * BLOCK, BLOCK), BLOCK)
        for o in range(2):
            y_ref[o, :, 0:576] = mm(x_ref[r, :], g_ref[o].reshape(width, 576)) + b_ref[o, 0:1, 0:576].astype(f32)
        tile = lambda o, n: y_ref[o, :, 128 * n:128 * n + 128]
        turn = lambda value: pltpu.roll(value, 64, 1)
        third = (jnp.where(lane < 64, tile(0, 3), turn(tile(1, 3))), jnp.where(lane < 64, turn(tile(0, 3)), tile(1, 3)),
                 jnp.where(lane < 64, tile(0, 4), turn(tile(1, 4))))
        for n, ref in enumerate((q_ref, k_ref, v_ref)):
            for g, value in enumerate((tile(0, n), tile(1, n), third[n])):
                value = value.astype(bf16)
                if n == 0:
                    value = value * jnp.asarray(0.125, bf16)
                ref[r, 128 * g:128 * g + 128] = value
        return carry
    lax.fori_loop(0, 2 * rows // BLOCK, project, 0)
    for src, dst in ((q_ref, q_out), (k_ref, k_out), (v_ref, v_out)):
        keep(src, dst)
    for k in range(1, 4):
        z_u[k].wait_recv()
        rest.append(go(up_g.at[at[k]], up_g.at[at[k]], to_x))
        z_d[k].wait_recv()
        rest.append(go(down_g.at[0, zs[k]], down_g.at[1, zs[k]], to_y))
        z_o[k].wait_recv()
        rest.append(go(out_g.at[0, zs[k]], out_g.at[1, zs[k]], to_y))
    for copy in rest + up_bias:
        copy.wait_recv()
    bu_out[0] = bu_ref[...]
    for n in range(3):
        bu_out[n + 1] = ub_ref[n]
    for copy in started:
        copy.wait_send()
    for copy in local[2:]:
        copy.wait()


def entry(tokens, positions, memory_rows, shard_qkv, biases, up_bias, up, down, out):
    f32, bf16 = jnp.float32, jnp.bfloat16
    rows, width = tokens.shape
    r = up.shape[0]
    shape, v = jax.ShapeDtypeStruct, pltpu.VMEM
    hbm, vmem = pl.BlockSpec(memory_space=pl.ANY), pl.BlockSpec(memory_space=pltpu.VMEM)
    qkv = shape((2 * rows, 384), bf16)
    return pl.pallas_call(
        entry_kernel,
        out_shape=(shape((rows, width), f32), shape((2 * rows, width), bf16), qkv, qkv, qkv,
                   shape((2, 8, r, 576), bf16), shape((8, r, up.shape[1]), bf16), shape((2, 4, r, down.shape[1]), bf16),
                   shape((2, 4, r, out.shape[1]), bf16), shape((4, 16, up.shape[1]), bf16)),
        in_specs=[vmem] * 9,
        out_specs=[hbm] * 9 + [vmem],
        scratch_shapes=[
            v((rows, width), f32), v((2 * rows, width), bf16), v((2, 8, r, 576), bf16), v((2, 16, 640), bf16),
            v((2, BLOCK, 640), f32), v((2 * rows, 384), bf16), v((2 * rows, 384), bf16), v((2 * rows, 384), bf16),
            v((3, 16, up.shape[1]), bf16),
            pltpu.SemaphoreType.DMA((48,)), pltpu.SemaphoreType.DMA((48,)), pltpu.SemaphoreType.DMA((16,)),
        ],
        compiler_params=pltpu.CompilerParams(vmem_limit_bytes=VMEM_MAX, collective_id=0, has_side_effects=True),
        cost_estimate=pl.CostEstimate(flops=4 * rows * width * 1152, bytes_accessed=20_000_000, transcendentals=0),
        name="entry",
    )(tokens, positions, memory_rows, shard_qkv, biases, up_bias, up, down, out)


def exit_kernel(x_all, d0, d1, d2, w_all, third, first_ref, dr1, pos_ref, sums_in, up_in,
                tok_out, first_out, second_out, small_out,
                x_ref, xt_ref, d_ref, w_ref, dr_ref, g_ref, own_ref, oth_ref, yb_ref, xs_ref, xb_ref, zt_ref, zs_ref, zb_ref,
                fs_ref, fb_ref, their_ref, got_ref, tok_ref, s_ref, t_ref, r_ref, send, recv, sem):
    f32, bf16 = jnp.float32, jnp.bfloat16
    rows, width = dr_ref.shape
    dp, tensor = lax.axis_index("dp"), lax.axis_index("tensor")
    z, x = dp // 2, dp % 2
    inner, outer = tensor % 2, tensor // 2
    up_z = [None] + [(z + k) % 4 for k in range(1, 4)]
    to_z = [None] + [(2 * up_z[k] + x, tensor) for k in range(1, 4)]
    to_x = (2 * z + 1 - x, tensor)
    to_y = (dp, (tensor + 2) % 4)
    to_core = (dp, tensor + 1 - 2 * inner)
    near_z = (2 * (z + 1 - 2 * (z % 2)) + x, tensor)
    far_z = to_z[2]
    loads = []
    for src, dst in ((d2, d_ref.at[2]), (x_all, x_ref), (d0, d_ref.at[0]), (d1, d_ref.at[1]),
                     (w_all.at[0, :, pl.ds(0, 384)], w_ref.at[0]), (w_all.at[1, :, pl.ds(0, 384)], w_ref.at[1]),
                     (third, w_ref.at[2]), (dr1, dr_ref)):
        copy = pltpu.make_async_copy(src, dst, sem.at[len(loads)])
        copy.start()
        loads.append(copy)
    greet(to_z[1:] + [to_x, to_y, to_core])
    ex = Exchange(send, recv)
    started = []

    def go(src, dst, device):
        copy = ex.copy(src, dst, device)
        copy.start()
        started.append(copy)
        return copy

    for k in range(1, 4):
        fs_ref[k - 1] = first_ref[up_z[k]].astype(bf16)
    z_first = [go(fs_ref.at[k - 1], fb_ref.at[k - 1], to_z[k]) for k in range(1, 4)]

    loads[0].wait()
    loads[1].wait()
    for b in range(2 * rows // BLOCK):
        xt_ref[:, BLOCK * b:BLOCK * b + BLOCK] = x_ref[BLOCK * b:BLOCK * b + BLOCK, :].T
    for m in range(0, width, BLOCK):
        g_ref[m:m + BLOCK, :] = mm(xt_ref[m:m + BLOCK, :], d_ref[2])
    half = own_ref.shape[3]
    lane = lax.broadcasted_iota(jnp.int32, (half, 128), 1)
    for p in range(8):
        for n in range(3):
            low = g_ref[2 * half * p:2 * half * p + half, 128 * n:128 * n + 128]
            high = g_ref[2 * half * p + half:2 * half * (p + 1), 128 * n:128 * n + 128]
            own_ref[p % 2, p // 2, n] = jnp.where(lane < 64, low, pltpu.roll(high, 64, 1))
            oth_ref[p % 2, p // 2, n] = jnp.where(lane < 64, pltpu.roll(low, 64, 1), high).astype(bf16)
    y_far = go(oth_ref.at[1 - x], yb_ref.at[0], to_y)
    y_near = go(oth_ref.at[x], yb_ref.at[1], to_y)

    for copy in loads[2:]:
        copy.wait()
    place = lax.broadcasted_iota(jnp.int32, (32, 2 * rows), 1)
    which = lax.broadcasted_iota(jnp.int32, (32, 2 * rows), 0)
    picks = jnp.where((place == pos_ref[:, 0:1]) | (which == 24), 1.0, 0.0).astype(bf16)
    picked = [mm(picks, d_ref[n]) for n in range(3)]
    own_place = lax.broadcasted_iota(jnp.int32, (32, rows), 1) + inner * rows
    own_picks = jnp.where(own_place == pos_ref[:, 0:1], 1.0, 0.0)
    memory = lax.dot_general(own_picks, dr_ref[...], NN, precision=lax.Precision.HIGHEST, preferred_element_type=f32)
    for n in range(3):
        memory = memory + mm(picked[n].astype(bf16), w_ref[n], NT)
    hw = s_ref.shape[2]

    def put(row, value):
        for h in range(2):
            s_ref[h, row:row + 1, :] = value[:, hw * h:hw * h + hw]
    for h in range(2):
        s_ref[h, 0:24, :] = memory[0:24, hw * h:hw * h + hw]
        s_ref[h, 38:40, :] = jnp.zeros((2, hw), f32)
    for n in range(6):
        put(24 + n, jnp.sum(sums_in[n], axis=0, keepdims=True))
    ups = [jnp.sum(up_in[n], axis=0, keepdims=True) for n in (0, 2, 1, 3)]
    total = [value[24:25, :] for value in picked]
    turned = jnp.concatenate([pltpu.roll(picked[2][24:32, 128 * n:128 * n + 128], 64, 1) for n in range(3)], axis=1)[0:1, :]
    for t in range(4):
        n = (t % 2 + inner) % 2 + 2 * ((t // 2 + outer) % 2)
        value = jnp.zeros_like(ups[0])
        for other in range(4):
            value = value + jnp.where(n == other, ups[other], 0.0)
        put(30 + t, value)
        s_ref[0, 34 + t:35 + t, :] = jnp.where(n == 0, total[0], 0.0) + jnp.where(n == 2, total[1], 0.0)
        s_ref[1, 34 + t:35 + t, :] = jnp.where(n == 0, total[2], 0.0) + jnp.where(n == 2, turned, 0.0)
    small = [go(s_ref.at[1 - inner], r_ref.at[0], to_core)]
    hops = [to_y, to_x, near_z, far_z]

    def hop(n):
        small[n].wait_recv()
        t_ref[n] = (s_ref[inner] if n == 0 else t_ref[n - 1]) + r_ref[n]
        if n < 4:
            small.append(go(t_ref.at[n], r_ref.at[n + 1], hops[n]))
        else:
            small.append(go(t_ref.at[n], r_ref.at[5], to_core))
            small_out[inner] = t_ref[n]

    mine = pl.multiple_of(inner * rows, 1024)
    theirs = pl.multiple_of((1 - inner) * rows, 1024)

    def block(start):
        r = pl.ds(pl.multiple_of(start, BLOCK), BLOCK)
        return mm(d_ref[0, r, :], w_ref[0], NT) + mm(d_ref[1, r, :], w_ref[1], NT) + mm(d_ref[2, r, :], w_ref[2], NT)

    def away(b, carry):
        their_ref[pl.ds(pl.multiple_of(b * BLOCK, BLOCK), BLOCK), :] = block(theirs + b * BLOCK).astype(bf16)
        return carry
    lax.fori_loop(0, rows // BLOCK, away, 0)
    tokens = go(their_ref, got_ref, to_core)
    hop(0)
    y_far.wait_recv()
    for k in range(4):
        xs_ref[k] = (own_ref[1 - x, k] + yb_ref[0, k].astype(f32)).astype(bf16)
    x_sum = go(xs_ref, xb_ref, to_x)

    def stay(b, carry):
        tok_ref[pl.ds(pl.multiple_of(b * BLOCK, BLOCK), BLOCK), :] = block(mine + b * BLOCK)
        return carry
    lax.fori_loop(0, rows // BLOCK, stay, 0)
    hop(1)
    y_near.wait_recv()
    x_sum.wait_recv()
    for k in range(4):
        zt_ref[k] = own_ref[x, k] + yb_ref[1, k].astype(f32) + xb_ref[k].astype(f32)
    for k in range(1, 4):
        zs_ref[k - 1] = zt_ref[up_z[k]].astype(bf16)
    z_second = [go(zs_ref.at[k - 1], zb_ref.at[k - 1], to_z[k]) for k in range(1, 4)]
    hop(2)
    tokens.wait_recv()

    def finish(s, carry):
        r = pl.ds(pl.multiple_of(s * STRIP, STRIP), STRIP)
        tok_ref[r, :] = tok_ref[r, :] + got_ref[r, :].astype(f32) + dr_ref[r, :]
        return carry
    lax.fori_loop(0, rows // STRIP, finish, 0)
    out = pltpu.make_async_copy(tok_ref, tok_out, sem.at[8])
    out.start()
    hop(3)
    for copy in z_first:
        copy.wait_recv()
    first_out[...] = first_ref[z] + fb_ref[0].astype(f32) + fb_ref[1].astype(f32) + fb_ref[2].astype(f32)
    for copy in z_second:
        copy.wait_recv()
    second_out[...] = zt_ref[z] + zb_ref[0].astype(f32) + zb_ref[1].astype(f32) + zb_ref[2].astype(f32)
    hop(4)
    small[5].wait_recv()
    small_out[1 - inner] = r_ref[5]
    for copy in started:
        copy.wait_send()
    out.wait()


def leave(x_all, d, w_qkv, third, first, dr1, place, sums, up_sums):
    f32, bf16 = jnp.float32, jnp.bfloat16
    rows, width = dr1.shape
    r, half = first.shape[1], first.shape[1] // 2
    shape, v = jax.ShapeDtypeStruct, pltpu.VMEM
    hbm, vmem = pl.BlockSpec(memory_space=pl.ANY), pl.BlockSpec(memory_space=pltpu.VMEM)
    return pl.pallas_call(
        exit_kernel,
        out_shape=(shape((rows, width), f32), shape((r, 384), f32), shape((3, half, 128), f32), shape((2, 40, width // 2), f32)),
        in_specs=[hbm] * 6 + [vmem, hbm] + [vmem] * 3,
        out_specs=[hbm] + [vmem] * 3,
        scratch_shapes=[
            v((2 * rows, width), bf16), v((width, 2 * rows), bf16), v((3, 2 * rows, 384), bf16), v((3, width, 384), bf16),
            v((rows, width), f32), v((width, 384), f32), v((2, 4, 3, half, 128), f32), v((2, 4, 3, half, 128), bf16),
            v((2, 4, 3, half, 128), bf16), v((4, 3, half, 128), bf16), v((4, 3, half, 128), bf16), v((4, 3, half, 128), f32),
            v((3, 3, half, 128), bf16), v((3, 3, half, 128), bf16), v((3, r, 384), bf16), v((3, r, 384), bf16),
            v((rows, width), bf16), v((rows, width), bf16), v((rows, width), f32), v((2, 40, width // 2), f32),
            v((5, 40, width // 2), f32), v((6, 40, width // 2), f32),
            pltpu.SemaphoreType.DMA((16,)), pltpu.SemaphoreType.DMA((16,)), pltpu.SemaphoreType.DMA((9,)),
        ],
        compiler_params=pltpu.CompilerParams(vmem_limit_bytes=VMEM_MAX, collective_id=2, has_side_effects=True),
        cost_estimate=pl.CostEstimate(flops=2 * rows * width * 384 * 8, bytes_accessed=20_000_000, transcendentals=0),
        name="leave",
    )(x_all, *d, w_qkv, third, first, dr1, place, sums, up_sums)


def layer_norm(values, norm_gain, norm_shift):
    centre = values - jnp.mean(values, axis=-1, keepdims=True)
    spread = jnp.mean(centre * centre, axis=-1, keepdims=True)
    return centre * lax.rsqrt(spread + EPSILON) * norm_gain + norm_shift


def gelu_exact(values):
    return jax.nn.gelu(values, approximate=False)


AXES = ("dp", "tensor")


class Grid:
    def __init__(self, dp, tensor):
        self.dp, self.tensor = dp, tensor
        factors, rest = [2], dp // 2
        while rest > 8:
            factors.insert(0, 4)
            rest //= 4
        if rest > 1:
            factors.insert(0, rest)
        self.factors = factors

    def digit(self, j):
        stride = 1
        for f in self.factors[j + 1:]:
            stride *= f
        return stride, self.factors[j]

    def my_digit(self, j):
        stride, f = self.digit(j)
        return lax.axis_index("dp") // stride % f

    def turn(self, value, j, k):
        stride, f = self.digit(j)
        pairs = []
        for d in range(self.dp):
            g = d // stride % f
            to = d + ((g + k) % f - g) * stride
            for t in range(self.tensor):
                pairs.append((d * self.tensor + t, to * self.tensor + t))
        return lax.ppermute(value, AXES, pairs)

    def swap_dp(self, value, bit):
        pairs = [(d * self.tensor + t, (d ^ bit) * self.tensor + t) for d in range(self.dp) for t in range(self.tensor)]
        return lax.ppermute(value, AXES, pairs)

    def swap(self, value, bit):
        pairs = [(d * self.tensor + t, d * self.tensor + (t ^ bit)) for d in range(self.dp) for t in range(self.tensor)]
        return lax.ppermute(value, AXES, pairs)

    def gather_stage(self, value, j, axis):
        _, f = self.digit(j)
        g = self.my_digit(j)
        got = [value] + [self.turn(value, j, k) for k in range(1, f)]
        if f == 2:
            lower = jnp.where(g == 0, got[0], got[1])
            upper = jnp.where(g == 0, got[1], got[0])
            return jnp.stack([lower, upper], axis=axis)
        ring = got[::-1]
        return lax.dynamic_slice_in_dim(jnp.stack(ring + ring[:-1], axis=axis), f - 1 - g, f, axis)

    def gather(self, shard, outer_first=False):
        count = len(self.factors)
        value = shard
        for j in range(count - 1):
            value = self.gather_stage(value, j, j)
        if outer_first:
            value = jnp.stack([value, self.swap(value, 2)])
            value = self.gather_stage(value, count - 1, count)
            return value.reshape(2, -1, shard.shape[-1])
        value = self.gather_stage(value, count - 1, count - 1)
        value = value.reshape(-1, shard.shape[-1])
        return jnp.stack([value, self.swap(value, 2)])

    def reduce_stage(self, value, j, axis):
        _, f = self.digit(j)
        g = self.my_digit(j)
        total = lax.dynamic_index_in_dim(value, g, axis, keepdims=False).astype(jnp.float32)
        for k in range(1, f):
            part = lax.dynamic_index_in_dim(value, (g + k) % f, axis, keepdims=False)
            total = total + self.turn(part.astype(jnp.bfloat16), j, k).astype(jnp.float32)
        return total

    def reduce(self, parts, outer_first=True):
        count = len(self.factors)
        columns = parts.shape[-1]
        value = parts
        if outer_first:
            value = value[0].astype(jnp.float32) + self.swap(value[1].astype(jnp.bfloat16), 2).astype(jnp.float32)
            value = value.reshape(*self.factors, -1, columns)
            value = self.reduce_stage(value, count - 1, count - 1)
        else:
            value = value.reshape(2, *self.factors, -1, columns)
            value = self.reduce_stage(value, count - 1, count)
            value = value[0] + self.swap(value[1].astype(jnp.bfloat16), 2).astype(jnp.float32)
        for j in reversed(range(count - 1)):
            value = self.reduce_stage(value, j, j)
        return value

    @property
    def stages(self):
        return len(self.factors) + 1

    def open(self, parts, outer_first):
        columns = parts.shape[-1]
        return parts if outer_first else parts.reshape(2, *self.factors, -1, columns)

    def stage(self, value, outer_first, n):
        count = len(self.factors)
        if n == (0 if outer_first else 1):
            value = value[0].astype(jnp.float32) + self.swap(value[1].astype(jnp.bfloat16), 2).astype(jnp.float32)
            return value.reshape(*self.factors, -1, value.shape[-1]) if outer_first else value
        if n == 0:
            return self.reduce_stage(value, count - 1, count)
        return self.reduce_stage(value, count - n, count - n)

    def sends(self, value, outer_first, n):
        count = len(self.factors)
        if n == (0 if outer_first else 1):
            return value[0], [value[1].astype(jnp.bfloat16)]
        j = count - 1 if n == 0 else count - n
        return self.digit_sends(value, j, count if n == 0 else j)

    def digit_sends(self, value, j, axis):
        _, f = self.digit(j)
        g = self.my_digit(j)
        take = lambda k: lax.dynamic_index_in_dim(value, (g + k) % f, axis, keepdims=False)
        return take(0), [take(k).astype(jnp.bfloat16) for k in range(1, f)]

    def moves(self, parts, outer_first, n):
        count = len(self.factors)
        if n == (0 if outer_first else 1):
            return [self.swap(parts[0], 2)]
        j = count - 1 if n == 0 else count - n
        return [self.turn(part, j, k + 1) for k, part in enumerate(parts)]

    def sums(self, kept, parts, outer_first, n):
        value = kept.astype(jnp.float32)
        for part in parts:
            value = value + part.astype(jnp.float32)
        return value.reshape(*self.factors, -1, value.shape[-1]) if n == 0 and outer_first else value

    def total(self, vector):
        for bit in (1, 2):
            vector = vector + self.swap(vector, bit)
        bit = 1
        while bit < self.dp:
            vector = vector + self.swap_dp(vector, bit)
            bit *= 2
        return vector


def shards(grid, tokens, segment_ids, memory_positions, memory_rows, qkv_weight, qv_bias, out_weight, out_bias,
           norm1_gain, norm1_bias, up_weight, up_bias, down_weight, down_bias, norm2_gain, norm2_bias, out_cotangent):
    f32, bf16 = jnp.float32, jnp.bfloat16
    rows, width = tokens.shape
    group_len = segment_ids.shape[1]
    tensor = lax.axis_index("tensor")
    inner, outer = tensor % 2, tensor // 2
    slice_rows = qkv_weight.shape[0]
    heads = qkv_weight.shape[1]
    hd = 64
    hw = heads * hd
    units = up_weight.shape[1]

    segments = lax.dynamic_index_in_dim(segment_ids, outer, 0, keepdims=False)
    positions = lax.dynamic_index_in_dim(memory_positions, outer, 0, keepdims=False)
    row_place = inner * rows + jnp.arange(rows, dtype=jnp.int32)
    picks = (row_place[:, None] == positions[None, :])
    joined = lambda w: w.transpose(1, 0, 2).reshape(width, -1)

    parts = qkv_weight.reshape(slice_rows, heads, 3, hd)
    order_columns = lambda p: jnp.concatenate([p[..., :2, n, :].reshape(*p.shape[:-3], 2 * hd) for n in range(3)]
                                              + [p[..., 2, n, :] for n in range(3)], axis=-1)
    shard_qkv = order_columns(parts)
    shard_out = jnp.pad(out_weight.reshape(slice_rows, hw), ((0, 0), (0, 256 - hw)))
    bias_parts = qv_bias.reshape(heads, 2, hd)
    bias_qkv = order_columns(jnp.stack([bias_parts[:, 0], jnp.zeros_like(bias_parts[:, 0]), bias_parts[:, 1]], 1))
    bias_qkv = jnp.pad(bias_qkv[None], ((0, 15), (0, 64)))
    own_up_bias = jnp.broadcast_to(up_bias[None], (16, units))
    fused = grid.dp == 8 and grid.tensor == 4
    if fused:
        memory = memory_positions.shape[1]
        place = jnp.pad(positions[None], ((0, 7), (0, 32 - memory)), constant_values=-1)
        table = jnp.pad(memory_rows, ((0, 32 - memory), (0, 0)))
        x0, x_all, q, k, v, w_qkv, up_g, down_g, out_g, b_up = entry(tokens, place, table, shard_qkv, bias_qkv, own_up_bias, up_weight, down_weight, shard_out)
        column = jnp.pad(jnp.broadcast_to(positions[:, None], (memory, 128)), ((0, 32 - memory), (0, 0)), constant_values=-1)
        w_qkv = w_qkv.reshape(2, width, 9 * hd)
        third = jnp.concatenate([w_qkv[o][:, (6 + n) * hd:(7 + n) * hd] for n in range(3) for o in range(2)], 1)
        up_all = up_g.reshape(width, units)
        ups = (up_all, grid.swap(up_all, 2))
        downs = (down_g, grid.turn(down_g, 1, 1))
        outs = (out_g, grid.turn(out_g, 1, 1))
    else:
        x0 = tokens.astype(f32) + jnp.dot(picks.astype(bf16), memory_rows, preferred_element_type=f32)
        xl = x0.astype(bf16)
        w_qkv = grid.gather(shard_qkv)
        other = grid.swap(xl, 1)
        x_all = jnp.concatenate([jnp.where(inner == 0, xl, other), jnp.where(inner == 0, other, xl)])
        b_two = jnp.stack([bias_qkv[0], grid.swap(bias_qkv[0], 2)]).astype(f32)
        y = [(mm(x_all, w_qkv[o]) + b_two[o, :9 * hd]).astype(bf16) for o in range(2)]
        third = lambda n: [one[:, (6 + n) * hd:(7 + n) * hd] for one in y]
        q, k, v = [jnp.concatenate([y[0][:, 2 * n * hd:2 * (n + 1) * hd], y[1][:, 2 * n * hd:2 * (n + 1) * hd]] + third(n), 1)
                   for n in range(3)]
        q = q * jnp.asarray(0.125, bf16)
        b_up = jnp.stack([own_up_bias, grid.swap(own_up_bias, 2)])
        b_up = jnp.concatenate([b_up, grid.swap(b_up, 1)])
        outs, ups, downs = (grid.gather(shard_out, True),), (grid.gather(up_weight),), (grid.gather(down_weight, True),)
    mixed, lse = attend_forward(q, k, v, segments)
    vec = jnp.stack([out_bias, norm1_gain, norm1_bias, down_bias, norm2_gain, norm2_bias, norm2_bias, norm2_bias]).astype(f32)
    (block_out, dr1, do_all, g_down, g_up, g_out, sums, up_sums) = middle(
        mixed, x0, outs, ups, downs, out_cotangent, vec, b_up)
    if fused:
        return finish_small(grid, tensor, x_all, q, k, v, do_all, mixed, lse, segments, w_qkv, third, dr1, column, sums, up_sums, block_out,
                            (g_down, g_up, g_out), hw)

    TN = (((0,), (0,)), ((), ()))
    tie = lax.optimization_barrier
    kinds = (True, False, True)
    state = [grid.open(parts, kind) for parts, kind in zip((g_down, g_up, g_out), kinds)]
    step = lambda n, state: [grid.stage(value, kind, n) for value, kind in zip(state, kinds)]
    late = [(1, 0, 2)[n] for n in range(3)]
    d = [None] * 3
    state, d[1] = step(0, state), attend_backward(1, q, k, v, do_all, mixed, lse, segments)
    state, d[1], q = tie((state, d[1], q))
    g_one = mm(x_all, d[1], TN).astype(bf16)
    state, d[0] = step(1, state), attend_backward(0, q, k, v, do_all, mixed, lse, segments)
    state, d[0], q, g_one = tie((state, d[0], q, g_one))
    g_zero = mm(x_all, d[0], TN)
    first = g_zero + grid.swap(g_one, 2).astype(f32)
    state, d[2] = step(2, state), attend_backward(2, q, k, v, do_all, mixed, lse, segments)
    state, d[2], first = tie((state, d[2], first))
    for n in range(3, grid.stages):
        state = step(n, state)
    grad_down, grad_up, grad_out = state
    grad_out = grad_out[:, :hw]

    g_two = mm(x_all, d[2], TN)
    side = lambda m, o: jnp.concatenate([m[:, (2 * n + o) * hd:(2 * n + o + 1) * hd] for n in range(3)], 1)
    second = side(g_two, 0) + grid.swap(side(g_two, 1).astype(bf16), 2).astype(f32)
    both = jnp.concatenate([first, second], 1).reshape(*grid.factors, slice_rows, 9 * hd)
    for j in reversed(range(len(grid.factors))):
        both = grid.reduce_stage(both, j, j)
    restore = lambda p: jnp.stack([jnp.concatenate([p[..., 2 * n * hd:2 * (n + 1) * hd].reshape(*p.shape[:-1], 2, hd),
                                                    p[..., None, (6 + n) * hd:(7 + n) * hd]], -2) for n in range(3)], -2)
    grad_qkv = restore(both).reshape(slice_rows, heads, 3 * hd)
    third = jnp.concatenate([w_qkv[o][:, (6 + n) * hd:(7 + n) * hd] for n in range(3) for o in range(2)], 1)
    part = (mm(d[0], w_qkv[0][:, :6 * hd], NT) + mm(d[1], w_qkv[1][:, :6 * hd], NT) + mm(d[2], third, NT)).reshape(2, rows, width)
    mine = lax.dynamic_index_in_dim(part, inner, 0, keepdims=False)
    theirs = lax.dynamic_index_in_dim(part, 1 - inner, 0, keepdims=False).astype(bf16)
    grad_tokens = mine + grid.swap(theirs, 1).astype(f32) + dr1
    d_sum = [jnp.sum(one.astype(f32), axis=0) for one in d]
    d_bias = [jnp.concatenate([d_sum[o]] + [d_sum[2][(2 * n + o) * hd:(2 * n + o + 1) * hd] for n in range(3)]) for o in range(2)]
    dg2, ds2, d_down_bias, dg1, ds1, d_out_bias = jnp.sum(sums, axis=1)
    d_up_bias = jnp.sum(up_sums, axis=1).reshape(2, 2 * units)
    grad_memory = jnp.dot(picks.astype(f32).T, grad_tokens, precision=lax.Precision.HIGHEST)

    order = jnp.arange(4, dtype=jnp.int32) ^ tensor
    up_parts = d_up_bias.reshape(2, 2, units)
    up_parts = jnp.stack([up_parts[0, 0], up_parts[1, 0], up_parts[0, 1], up_parts[1, 1]])[order]
    take = lambda o: restore(d_bias[o])[:, 0::2].reshape(-1)
    blank = jnp.zeros((2 * hw,), f32)
    qv_parts = jnp.stack([take(0), blank, take(1), blank])[order]
    pieces = [grad_memory.reshape(-1), d_out_bias, dg1, ds1, d_down_bias, dg2, ds2, up_parts.reshape(-1), qv_parts.reshape(-1)]
    summed = grid.total(jnp.concatenate(pieces))
    outs, at = [], 0
    for piece in pieces:
        outs.append(lax.slice_in_dim(summed, at, at + piece.size))
        at += piece.size
    t_memory, t_out_bias, t_g1, t_s1, t_down_bias, t_g2, t_s2, t_up, t_qv = outs
    grad_up_bias = lax.dynamic_index_in_dim(t_up.reshape(4, units), tensor, 0, keepdims=False)
    grad_qv = lax.dynamic_index_in_dim(t_qv.reshape(4, heads, 2 * hd), tensor, 0, keepdims=False)
    return (block_out, grad_tokens, t_memory.reshape(-1, width), grad_qkv, grad_qv,
            grad_out.reshape(slice_rows, heads, hd), t_out_bias, t_g1, t_s1, grad_up, grad_up_bias, grad_down,
            t_down_bias, t_g2, t_s2)


def finish_small(grid, tensor, x_all, q, k, v, do_all, mixed, lse, segments, w_qkv, third, dr1, column, sums, up_sums, block_out, grads, hw):
    f32, bf16 = jnp.float32, jnp.bfloat16
    tie = lax.optimization_barrier
    TN = (((0,), (0,)), ((), ()))
    kinds = (True, False, True)
    width = dr1.shape[1]
    state = [grid.open(parts, kind) for parts, kind in zip(grads, kinds)]

    def beside(n, state, pair, q, extra, move):
        split = [grid.sends(value, kind, n) for value, kind in zip(state, kinds)]
        parts, extra, q = tie(([s[1] for s in split], extra, q))
        moved = [grid.moves(part, kind, n) for part, kind in zip(parts, kinds)]
        extra = [move(e) for e in extra]
        d = attend_backward(pair, q, k, v, do_all, mixed, lse, segments)
        moved, extra, d, q = tie((moved, extra, d, q))
        return [grid.sums(s[0], part, kind, n) for s, part, kind in zip(split, moved, kinds)], d, q, extra

    state, d_one, q, _ = beside(0, state, 1, q, [], None)
    g_one = mm(x_all, d_one, TN).astype(bf16)
    state, d_zero, q, got = beside(1, state, 0, q, [g_one], lambda e: grid.swap(e, 2))
    first = mm(x_all, d_zero, TN) + got[0].astype(f32)
    kept, parts = grid.digit_sends(first.reshape(*grid.factors, -1, first.shape[-1]), 1, 1)
    state, d_two, q, got = beside(2, state, 2, q, parts, lambda e: grid.turn(e, 1, 1))
    first = kept + got[0].astype(f32)
    grad_down, grad_up, grad_out = state
    grad_tokens, one, two, small = leave(x_all, (d_zero, d_one, d_two), w_qkv, third, first, dr1, column, sums, up_sums)
    hd = 64
    slice_rows = one.shape[0]
    two = two.reshape(3, slice_rows // 2, 2, hd).transpose(2, 1, 0, 3).reshape(slice_rows, 1, 3, hd)
    grad_qkv = jnp.concatenate([one.reshape(slice_rows, 3, 2, hd).transpose(0, 2, 1, 3), two], 1).reshape(slice_rows, 3, 3 * hd)
    row = lambda at: lax.dynamic_index_in_dim(small, at, 1, keepdims=False)
    full = lambda at: small[:, at].reshape(width)
    qv = row(34 + tensor)
    part = lambda n: jnp.concatenate([qv[0, 128 * n:128 * n + 128].reshape(2, hd), qv[1:2, 128 * n:128 * n + hd]])
    grad_qv = jnp.concatenate([part(0), part(2)], 1)
    t_out_bias, t_g1, t_s1, t_down_bias, t_g2, t_s2 = [full(24 + n) for n in (5, 3, 4, 2, 0, 1)]
    return (block_out, grad_tokens, small[:, :20].transpose(1, 0, 2).reshape(20, width), grad_qkv, grad_qv,
            grad_out[:, :hw].reshape(slice_rows, 3, hd), t_out_bias, t_g1, t_s1, grad_up, row(30 + tensor).reshape(width), grad_down,
            t_down_bias, t_g2, t_s2)


def solution(mesh):
    grid = Grid(mesh.shape["dp"], mesh.shape["tensor"])
    tokens, dp, none = P(AXES, None), P("dp", None), P()
    heads, matrix = P("dp", "tensor", None), P("dp", "tensor")
    in_specs = (tokens, dp, dp, none, heads, P("tensor", None), heads, none, none, none, matrix, P("tensor"), matrix,
                none, none, none, tokens)
    out_specs = (tokens, tokens, none, heads, P("tensor", None), heads, none, none, none, matrix, P("tensor"), matrix,
                 none, none, none)

    def run(*args):
        return shards(grid, *args)

    return jax.shard_map(run, mesh=mesh, in_specs=in_specs, out_specs=out_specs, check_vma=False)
```

```python
import functools

import jax
import jax.numpy as jnp
from jax import lax
from jax.experimental import pallas as pl
from jax.experimental.pallas import tpu as pltpu
from jax.sharding import PartitionSpec as P

EPSILON = 1e-12
TILE = 256
MASKED = -1e30
VMEM_MAX = 64 * 1024 * 1024 - 128 * 1024
NT = (((1,), (1,)), ((), ()))
NN = (((1,), (0,)), ((), ()))


def mm(a, b, dims=NN):
    return lax.dot_general(a, b, dims, preferred_element_type=jnp.float32)


def fold8(x):
    r = x.shape[0]
    return x.reshape(r // 8, 8, x.shape[1])


def head_masks(block):
    lane = lax.broadcasted_iota(jnp.int32, block.shape, 1)
    zero = jnp.zeros_like(block)
    return jnp.where(lane < 64, block, zero), jnp.where(lane < 64, zero, block)


def tile_visible(first_ref, last_ref, i, t):
    return (first_ref[t] == 0) | ((first_ref[t] <= last_ref[i]) & (last_ref[t] >= first_ref[i]))


def forward_kernel(first_ref, last_ref, q_ref, k_ref, v_ref, kseg_ref, qseg_ref, o_ref, lse_ref,
                   vt_ref, qm_ref, s_ref, m_ref, l_ref, acc_ref):
    i = pl.program_id(0)
    tiles = pl.num_programs(0)
    pairs = q_ref.shape[1] // 128
    heads = 2 * pairs

    @pl.when(i == 0)
    def _():
        def turn(t, c):
            rows = pl.ds(pl.multiple_of(t * TILE, TILE), TILE)
            vt_ref[t] = v_ref[rows, :].T
            return c
        lax.fori_loop(0, tiles, turn, 0)

    for g in range(pairs):
        a, b = head_masks(q_ref[:, 128 * g:128 * g + 128])
        qm_ref[2 * g] = a
        qm_ref[2 * g + 1] = b
    m_ref[...] = jnp.full_like(m_ref, MASKED)
    l_ref[...] = jnp.zeros_like(l_ref)
    acc_ref[...] = jnp.zeros_like(acc_ref)
    qseg = qseg_ref[0:1, :]

    def scores(t, c):
        @pl.when(tile_visible(first_ref, last_ref, i, t))
        def _():
            rows = pl.ds(pl.multiple_of(t * TILE, TILE), TILE)
            kseg = kseg_ref[rows, :]
            kseg = jnp.concatenate([kseg, kseg], axis=1)
            seen = (kseg == 0) | (kseg == qseg)
            for h in range(heads):
                kp = k_ref[rows, 128 * (h // 2):128 * (h // 2) + 128]
                s = mm(kp, qm_ref[h], NT)
                s = jnp.where(seen, s, MASKED)
                s_ref[h, t] = s
                m_ref[h] = jnp.maximum(m_ref[h], jnp.max(fold8(s), axis=0))
        return c
    lax.fori_loop(0, tiles, scores, 0)
    for h in range(heads):
        m_ref[h] = jnp.broadcast_to(jnp.max(m_ref[h], axis=0, keepdims=True), (8, TILE))

    def mix(t, c):
        @pl.when(tile_visible(first_ref, last_ref, i, t))
        def _():
            for h in range(heads):
                p = jnp.exp(s_ref[h, t] - m_ref[h, 0:1, :])
                l_ref[h] = l_ref[h] + jnp.sum(fold8(p), axis=0)
                acc_ref[h] = acc_ref[h] + mm(vt_ref[t, 64 * h:64 * h + 64, :], p.astype(jnp.bfloat16))
        return c
    lax.fori_loop(0, tiles, mix, 0)
    for h in range(heads):
        total = jnp.sum(l_ref[h], axis=0, keepdims=True)
        lse_ref[h:h + 1, :] = m_ref[h, 0:1, :] + jnp.log(total)
        acc_ref[h] = acc_ref[h] / total
    for g in range(pairs):
        pair = jnp.concatenate([acc_ref[2 * g], acc_ref[2 * g + 1]], axis=0)
        o_ref[:, 128 * g:128 * g + 128] = pair.T.astype(jnp.bfloat16)


def attend_forward(q, k, v, seg):
    n, width = q.shape
    tiles = n // TILE
    heads = width // 64
    first = seg[::TILE]
    last = seg[TILE - 1::TILE]
    kseg = jnp.broadcast_to(seg[:, None], (n, 128))
    qseg = jnp.broadcast_to(seg[None, :], (8, n))
    whole = lambda shape: pl.BlockSpec(shape, lambda i, *_: (0,) * len(shape))
    return pl.pallas_call(
        forward_kernel,
        out_shape=(jax.ShapeDtypeStruct((n, width), jnp.bfloat16), jax.ShapeDtypeStruct((8, n), jnp.float32)),
        grid_spec=pltpu.PrefetchScalarGridSpec(
            num_scalar_prefetch=2, grid=(tiles,),
            in_specs=[pl.BlockSpec((TILE, width), lambda i, *_: (i, 0)), whole((n, width)), whole((n, width)),
                      whole((n, 128)), pl.BlockSpec((8, TILE), lambda i, *_: (0, i))],
            out_specs=[pl.BlockSpec((TILE, width), lambda i, *_: (i, 0)), pl.BlockSpec((8, TILE), lambda i, *_: (0, i))],
            scratch_shapes=[
                pltpu.VMEM((tiles, width, TILE), jnp.bfloat16),
                pltpu.VMEM((heads, TILE, 128), jnp.bfloat16),
                pltpu.VMEM((heads, tiles, TILE, TILE), jnp.float32),
                pltpu.VMEM((heads, 8, TILE), jnp.float32),
                pltpu.VMEM((heads, 8, TILE), jnp.float32),
                pltpu.VMEM((heads, 64, TILE), jnp.float32),
            ]),
        compiler_params=pltpu.CompilerParams(dimension_semantics=("arbitrary",), vmem_limit_bytes=VMEM_MAX),
        cost_estimate=pl.CostEstimate(flops=4 * n * n * width, bytes_accessed=8 * n * width, transcendentals=n * n * heads),
        name="attend_forward",
    )(first, last, q, k, v, kseg, qseg)


def backward_kernel(base, first_ref, last_ref, q_ref, do_ref, o_ref, k_ref, v_ref, kseg_ref, qseg_ref, lse_ref,
                    d_ref, kt_ref, qm_ref, dom_ref, delta_ref, dqt_ref, dka_ref, dva_ref):
    i = pl.program_id(0)
    tiles = pl.num_programs(0)

    @pl.when(i == 0)
    def _():
        def turn(t, c):
            rows = pl.ds(pl.multiple_of(t * TILE, TILE), TILE)
            kt_ref[t] = k_ref[rows, :].T
            dka_ref[rows, :] = jnp.zeros((TILE, 128), jnp.float32)
            dva_ref[rows, :] = jnp.zeros((TILE, 128), jnp.float32)
            return c
        lax.fori_loop(0, tiles, turn, 0)

    for ref, masked in ((q_ref, qm_ref), (do_ref, dom_ref)):
        masked[0], masked[1] = head_masks(ref[...])
    inner = (do_ref[...].astype(jnp.float32) * o_ref[...].astype(jnp.float32)).T
    for h in range(2):
        delta_ref[h] = jnp.broadcast_to(jnp.sum(inner[64 * h:64 * h + 64], axis=0, keepdims=True), (8, TILE))
    dqt_ref[...] = jnp.zeros_like(dqt_ref)
    qseg = qseg_ref[0:1, :]

    def count(t, c):
        prompt, before, upto = c
        return (prompt + (first_ref[t] == 0).astype(jnp.int32), before + (last_ref[t] < first_ref[i]).astype(jnp.int32),
                upto + (first_ref[t] <= last_ref[i]).astype(jnp.int32))
    zero = jnp.int32(0)
    prompt, before, upto = lax.fori_loop(0, tiles, count, (zero, zero, zero))
    start = jnp.maximum(prompt, before)
    visible = prompt + jnp.maximum(upto - start, 0)

    def one_tile(n):
        t = jnp.where(n < prompt, n, start + n - prompt)
        rows = pl.ds(pl.multiple_of(t * TILE, TILE), TILE)
        kseg = kseg_ref[rows, :]
        kseg = jnp.concatenate([kseg, kseg], axis=1)
        seen = (kseg == 0) | (kseg == qseg)
        kp = k_ref[rows, :]
        vp = v_ref[rows, :]
        s = [mm(kp, qm_ref[h], NT) for h in range(2)]
        d = [mm(vp, dom_ref[h], NT) for h in range(2)]
        p = [jnp.where(seen, jnp.exp(s[h] - lse_ref[base + h:base + h + 1, :]), 0.0) for h in range(2)]
        ds = [(p[h] * (d[h] - delta_ref[h, 0:1, :])).astype(jnp.bfloat16) for h in range(2)]
        p = [value.astype(jnp.bfloat16) for value in p]
        dva_ref[rows, :] = dva_ref[rows, :] + (mm(p[0], dom_ref[0]) + mm(p[1], dom_ref[1]))
        dka_ref[rows, :] = dka_ref[rows, :] + (mm(ds[0], qm_ref[0]) + mm(ds[1], qm_ref[1]))
        return [mm(kt_ref[t, 64 * h:64 * h + 64, :], ds[h]) for h in range(2)]

    def two_tiles(n, c):
        one, two = one_tile(2 * n), one_tile(2 * n + 1)
        for h in range(2):
            dqt_ref[h] = dqt_ref[h] + (one[h] + two[h])
        return c
    lax.fori_loop(0, visible // 2, two_tiles, 0)

    @pl.when(visible % 2 == 1)
    def _():
        for h, value in enumerate(one_tile(visible - 1)):
            dqt_ref[h] = dqt_ref[h] + value
    pair = jnp.concatenate([dqt_ref[0], dqt_ref[1]], axis=0)
    own = pl.ds(pl.multiple_of(i * TILE, TILE), TILE)
    d_ref[own, 0:128] = (pair.T * 0.125).astype(jnp.bfloat16)

    @pl.when(i == tiles - 1)
    def _():
        d_ref[:, 128:256] = dka_ref[...].astype(jnp.bfloat16)
        d_ref[:, 256:384] = dva_ref[...].astype(jnp.bfloat16)


def attend_backward(g, q, k, v, do, o, lse, seg):
    n, width = q.shape[0], 128
    tiles = n // TILE
    heads = width // 64
    first = seg[::TILE]
    last = seg[TILE - 1::TILE]
    kseg = jnp.broadcast_to(seg[:, None], (n, 128))
    qseg = jnp.broadcast_to(seg[None, :], (8, n))
    whole = lambda shape: pl.BlockSpec(shape, lambda i, *_: (0,) * len(shape))
    rows = pl.BlockSpec((TILE, width), lambda i, *_: (i, g))
    column = pl.BlockSpec((n, width), lambda i, *_: (0, g))
    stat = pl.BlockSpec((8, TILE), lambda i, *_: (0, i))
    return pl.pallas_call(
        functools.partial(backward_kernel, 2 * g),
        out_shape=jax.ShapeDtypeStruct((n, 3 * width), jnp.bfloat16),
        grid_spec=pltpu.PrefetchScalarGridSpec(
            num_scalar_prefetch=2, grid=(tiles,),
            in_specs=[rows, rows, rows, column, column, whole((n, 128)), stat, stat],
            out_specs=whole((n, 3 * width)),
            scratch_shapes=[
                pltpu.VMEM((tiles, width, TILE), jnp.bfloat16),
                pltpu.VMEM((heads, TILE, 128), jnp.bfloat16),
                pltpu.VMEM((heads, TILE, 128), jnp.bfloat16),
                pltpu.VMEM((heads, 8, TILE), jnp.float32),
                pltpu.VMEM((heads, 64, TILE), jnp.float32),
                pltpu.VMEM((n, width), jnp.float32),
                pltpu.VMEM((n, width), jnp.float32),
            ]),
        compiler_params=pltpu.CompilerParams(dimension_semantics=("arbitrary",), vmem_limit_bytes=VMEM_MAX),
        cost_estimate=pl.CostEstimate(flops=10 * n * n * width, bytes_accessed=14 * n * width, transcendentals=n * n * heads),
        name="attend_backward",
    )(first, last, q, do, o, k, v, kseg, qseg, lse)


BLOCK = 256
STRIP = 64


def normal_cdf_parts(u):
    v = u * 0.7071067811865476
    c = jnp.clip(v, -3.832506856900711, 3.832506856900711)
    c2 = c * c
    top = 0.00022905065861350646
    for a in (0.0034082910107109506, 0.050955695062380861, 0.18520832239976145, 1.128379143519084):
        top = top * c2 + a
    low = -1.1791602954361697e-7
    for b in (0.000023547966471313185, 0.0010179625278914885, 0.014070470171167667, 0.11098505178285362,
              0.49746925110067538, 1.0):
        low = low * c2 + b
    cdf = 0.5 + 0.5 * (c * top / low)
    slope = jnp.exp(-(v * v)) * (u * 0.3989422804014327)
    return u * cdf, cdf + slope


def middle_kernel(pieces, o_all, x0, outs, ups, downs, cot, vec_ref, bup_ref,
                  block_out, dr1, do_all, g_down, g_up, g_out, sums_ref, upsum_ref,
                  o_ref, raw_ref, wo_ref, wu_ref, wd_ref, hat_ref, inv_ref, acc_ref, hl_ref, hlt_ref, gp_ref, z_ref, c_ref,
                  df_ref, dft_ref, y_ref, st_ref, su_ref, ru_ref, rd_ref, go_ref, rgo_ref, u0_ref, u1_ref,
                  sem, osem, send, recv):
    f32, bf16 = jnp.float32, jnp.bfloat16
    rows, width = hat_ref.shape
    blocks = rows // BLOCK
    part = wu_ref.shape[2]
    bf = lambda a: a.astype(bf16)
    dp, tensor = lax.axis_index("dp"), lax.axis_index("tensor")
    inner = tensor % 2
    partner = (dp, tensor + 1 - 2 * inner)
    mine = pl.multiple_of(inner * rows, 1024)
    theirs = pl.multiple_of((1 - inner) * rows, 1024)
    greet([partner])

    def remote(n, src, dst):
        return pltpu.make_async_remote_copy(src, dst, send.at[n], recv.at[n], device_id=partner,
                                            device_id_type=pl.DeviceIdType.MESH)

    swap_o = remote(0, o_all.at[pl.ds(theirs, rows), :], o_ref.at[1])
    swap_o.start()
    count = [0]

    def load(src, dst):
        copy = pltpu.make_async_copy(src, dst, sem.at[count[0]])
        count[0] += 1
        copy.start()
        return copy

    def weight(sources, dst):
        if not pieces:
            return [load(sources[0].at[o], dst.at[o]) for o in range(2)]
        digit = dp % 2
        made = []
        for o in range(2):
            for zi in range(sources[0].shape[1]):
                for n in range(2):
                    place = 2 * zi + (digit if n == 0 else 1 - digit)
                    r = sources[n].shape[2]
                    made.append(load(sources[n].at[o, zi], dst.at[o, pl.ds(pl.multiple_of(place * r, r), r), :]))
        return made

    first = [load(o_all.at[pl.ds(mine, rows), :], o_ref.at[0]), load(x0, hat_ref)] + weight(outs, raw_ref.at[0])
    if pieces:
        second = [load(ups[o], wu_ref.at[o]) for o in range(2)]
    else:
        second = [load(ups[0].at[o], wu_ref.at[o]) for o in range(2)]
    second = second + weight(downs, wd_ref)
    late = load(cot, c_ref)
    vec = lambda n: vec_ref[n:n + 1, :]
    sums_ref[...] = jnp.zeros_like(sums_ref)
    upsum_ref[...] = jnp.zeros_like(upsum_ref)
    for copy in first:
        copy.wait()
    swaps = [remote(1, raw_ref.at[0], raw_ref.at[1])]
    swaps[0].start()
    for copy in second:
        copy.wait()
    for o in range(2):
        swaps.append(remote(2 + 2 * o, wu_ref.at[o], wu_ref.at[2 + o]))
        swaps.append(remote(3 + 2 * o, wd_ref.at[o], wd_ref.at[2 + o]))
    for copy in swaps[1:]:
        copy.start()
    lane = lax.broadcasted_iota(jnp.int32, (width, 128), 1)

    def order_heads(side):
        wo_ref[side, :, 0:128] = raw_ref[side, 0, :, 0:128]
        wo_ref[side, :, 128:256] = raw_ref[side, 1, :, 0:128]
        upper = pltpu.roll(raw_ref[side, 1, :, 128:256].astype(f32), 64, 1)
        wo_ref[side, :, 256:384] = bf(jnp.where(lane < 64, raw_ref[side, 0, :, 128:256].astype(f32), upper))
    order_heads(0)
    swaps[0].wait()
    order_heads(1)
    swap_o.wait()

    def strips(body):
        def run(s, carry):
            body(pl.ds(pl.multiple_of(s * STRIP, STRIP), STRIP))
            return carry
        lax.fori_loop(0, rows // STRIP, run, 0)

    def add_sum(n, value):
        sums_ref[n] = sums_ref[n] + jnp.sum(fold(value), axis=0)

    def fold(value):
        return value.reshape(value.shape[0] // 8, 8, value.shape[1])

    def mean(value):
        return jnp.sum(value, axis=-1, keepdims=True) * (1.0 / width)

    def project(b, carry):
        r = pl.ds(pl.multiple_of(b * BLOCK, BLOCK), BLOCK)
        acc_ref[r, :] = mm(o_ref[0, r, :], wo_ref[0], NT) + mm(o_ref[1, r, :], wo_ref[1], NT)
        return carry
    lax.fori_loop(0, blocks, project, 0)

    def first_norm(r):
        r1 = hat_ref[r, :] + (acc_ref[r, :] + vec(0))
        centre = r1 - mean(r1)
        inv = lax.rsqrt(mean(centre * centre) + EPSILON)
        hat = centre * inv
        hat_ref[r, :] = hat
        inv_ref[r, :] = inv
        hl_ref[r, :] = bf(hat * vec(1) + vec(2))
    strips(first_norm)
    for b in range(blocks):
        hlt_ref[:, BLOCK * b:BLOCK * b + BLOCK] = hl_ref[BLOCK * b:BLOCK * b + BLOCK, :].T
    acc_ref[...] = jnp.zeros_like(acc_ref)

    bufs = (u0_ref, u1_ref)

    def forward(j, carry):
        for o in range(2):
            @pl.when(j == 2 + o)
            def _(o=o):
                swaps[1 + 2 * o].wait()
                swaps[2 + 2 * o].wait()

        def lift(b):
            bufs[b % 2][...] = mm(hl_ref[BLOCK * b:BLOCK * b + BLOCK, :], wu_ref[j]) + bup_ref[j, 0:1, :].astype(f32)
        lift(0)
        for b in range(blocks):
            if b + 1 < blocks:
                lift(b + 1)
            r = slice(BLOCK * b, BLOCK * b + BLOCK)
            for i in range(0, BLOCK, 32):
                for w in range(0, part, 256):
                    z, gp = normal_cdf_parts(bufs[b % 2][i:i + 32, w:w + 256])
                    z_ref[j, BLOCK * b + i:BLOCK * b + i + 32, w:w + 256] = bf(z)
                    gp_ref[j, BLOCK * b + i:BLOCK * b + i + 32, w:w + 256] = gp
            acc_ref[r, :] = acc_ref[r, :] + mm(z_ref[j, r, :], wd_ref[j], NT)
        return carry
    lax.fori_loop(0, 4, forward, 0)
    late.wait()

    def second_norm(r):
        h1 = hat_ref[r, :] * vec(1) + vec(2)
        r2 = h1 + (acc_ref[r, :] + vec(3))
        centre = r2 - mean(r2)
        inv = lax.rsqrt(mean(centre * centre) + EPSILON)
        hat = centre * inv
        y_ref[r, :] = bf(hat * vec(4) + vec(5))
        c = c_ref[r, :].astype(f32)
        add_sum(0, c * hat)
        add_sum(1, c)
        w = c * vec(4)
        dr2 = (w - mean(w) - hat * mean(w * hat)) * inv
        acc_ref[r, :] = dr2
        low = bf(dr2)
        df_ref[r, :] = low
        add_sum(2, low.astype(f32))
    strips(second_norm)
    stores = [pltpu.make_async_copy(y_ref, block_out, osem.at[0])]
    stores[0].start()
    for b in range(blocks):
        dft_ref[:, BLOCK * b:BLOCK * b + BLOCK] = df_ref[BLOCK * b:BLOCK * b + BLOCK, :].T

    def backward(n, carry):
        j = 3 - n

        def lower(b):
            bufs[b % 2][...] = mm(df_ref[BLOCK * b:BLOCK * b + BLOCK, :], wd_ref[j])
        slot = n % 2
        away = [remote(6 + slot, st_ref.at[slot], rd_ref.at[slot]), remote(8 + slot, su_ref.at[slot], ru_ref.at[slot])]
        lower(0)
        for b in range(blocks):
            if b + 1 < blocks:
                lower(b + 1)
            r = slice(BLOCK * b, BLOCK * b + BLOCK)
            for i in range(0, BLOCK, 64):
                q = slice(BLOCK * b + i, BLOCK * b + i + 64)
                dul = bf(bufs[b % 2][i:i + 64, :] * gp_ref[j, q, :])
                upsum_ref[j] = upsum_ref[j] + jnp.sum(fold(dul.astype(f32)), axis=0)
                hat2_ref[q, :] = dul
            acc_ref[r, :] = acc_ref[r, :] + mm(hat2_ref[r, :], wu_ref[j], NT)

        @pl.when(n < 2)
        def _():
            for m in range(0, width, BLOCK):
                st_ref[slot, m:m + BLOCK, :] = bf(mm(dft_ref[m:m + BLOCK, :], z_ref[j]))
            away[0].start()
            for m in range(0, width, BLOCK):
                su_ref[slot, m:m + BLOCK, :] = bf(mm(hlt_ref[m:m + BLOCK, :], hat2_ref[...]))
            away[1].start()

        @pl.when(n >= 2)
        def _():
            away[0].wait()
            for m in range(0, width, BLOCK):
                got = rd_ref[slot, m:m + BLOCK, :].astype(f32)
                st_ref[slot, m:m + BLOCK, :] = bf(mm(dft_ref[m:m + BLOCK, :], z_ref[j]) + got)
            if pieces:
                for o in range(2):
                    @pl.when(j == o)
                    def _(o=o):
                        pltpu.make_async_copy(st_ref.at[slot], g_down[o], osem.at[1 + slot]).start()
            else:
                pltpu.make_async_copy(st_ref.at[slot], g_down.at[j], osem.at[1 + slot]).start()
            away[1].wait()
            for m in range(0, width, BLOCK):
                got = ru_ref[slot, m:m + BLOCK, :].astype(f32)
                su_ref[slot, m:m + BLOCK, :] = bf(mm(hlt_ref[m:m + BLOCK, :], hat2_ref[...]) + got)
            if pieces:
                r = g_up[0].shape[2]
                for zi in range(g_up[0].shape[1]):
                    for o in range(2):
                        at = pl.multiple_of((2 * zi + (dp + o) % 2) * r, r)
                        pltpu.make_async_copy(su_ref.at[slot, pl.ds(at, r), :], g_up[o].at[j, zi], osem.at[3 + slot]).start()
            else:
                pltpu.make_async_copy(su_ref.at[slot], g_up.at[j], osem.at[3 + slot]).start()
        return carry
    hat2_ref = y_ref
    stores[0].wait()
    lax.fori_loop(0, 4, backward, 0)

    def first_back(r):
        dh1 = acc_ref[r, :]
        hat = hat_ref[r, :]
        add_sum(3, dh1 * hat)
        add_sum(4, dh1)
        w = dh1 * vec(1)
        grad = (w - mean(w) - hat * mean(w * hat)) * inv_ref[r, :]
        acc_ref[r, :] = grad
        low = bf(grad)
        df_ref[r, :] = low
        add_sum(5, low.astype(f32))
    strips(first_back)
    out = pltpu.make_async_copy(acc_ref, dr1, osem.at[0])
    out.start()
    stores = [out]
    for b in range(blocks):
        dft_ref[:, BLOCK * b:BLOCK * b + BLOCK] = df_ref[BLOCK * b:BLOCK * b + BLOCK, :].T
    lane = lax.broadcasted_iota(jnp.int32, (BLOCK, 128), 1)

    def out_grad(side, m):
        tiles = [mm(dft_ref[m:m + BLOCK, :], o_ref[side, :, 128 * g:128 * g + 128]) for g in range(3)]
        third = [jnp.where(lane < 64, tiles[2], 0.0), jnp.where(lane < 64, pltpu.roll(tiles[2], 64, 1), 0.0)]
        return [jnp.concatenate([tiles[o], third[o]], axis=1) for o in range(2)]
    for m in range(0, width, BLOCK):
        for o, value in enumerate(out_grad(1, m)):
            go_ref[o, m:m + BLOCK, :] = bf(value)
    swap_go = remote(10, go_ref, rgo_ref)
    swap_go.start()
    ow = wo_ref.shape[2]
    for side in (1, 0):
        def push(b, carry):
            r = pl.ds(pl.multiple_of(b * BLOCK, BLOCK), BLOCK)
            y_ref[r, ow * side:ow * side + ow] = bf(mm(df_ref[r, :], wo_ref[side]))
            return carry
        lax.fori_loop(0, blocks, push, 0)
        if side == 1:
            swap_do = remote(11, y_ref.at[:, pl.ds(ow, ow)], do_all.at[pl.ds(mine, rows), :])
            swap_do.start()
        else:
            copy = pltpu.make_async_copy(y_ref.at[:, pl.ds(0, ow)], do_all.at[pl.ds(mine, rows), :], osem.at[5])
            copy.start()
            stores.append(copy)
    swap_go.wait()
    for m in range(0, width, BLOCK):
        for o, value in enumerate(out_grad(0, m)):
            go_ref[o, m:m + BLOCK, :] = bf(value + rgo_ref[o, m:m + BLOCK, :].astype(f32))
    for o in range(2 if pieces else 1):
        copy = pltpu.make_async_copy(go_ref.at[o] if pieces else go_ref, g_out[o] if pieces else g_out, osem.at[6 + o])
        copy.start()
        stores.append(copy)
    whole = g_down[0] if pieces else g_down.at[0]
    for slot in range(2):
        pltpu.make_async_copy(st_ref.at[slot], whole, osem.at[1 + slot]).wait()
        pltpu.make_async_copy(su_ref.at[slot], whole, osem.at[3 + slot]).wait()
    swap_do.wait()
    for copy in stores:
        copy.wait()


def middle(o_all, x0, outs, ups, downs, cot, vec, bup):
    f32, bf16 = jnp.float32, jnp.bfloat16
    rows, width = x0.shape
    ow = o_all.shape[1]
    part = bup.shape[-1]
    pieces = len(ups) == 2
    shape = jax.ShapeDtypeStruct
    hbm = pl.BlockSpec(memory_space=pl.ANY)
    vmem = pl.BlockSpec(memory_space=pltpu.VMEM)
    v = pltpu.VMEM
    n = len(ups)

    def kernel(o_all, x0, *refs):
        weights, rest = refs[:3 * n], refs[3 * n:]
        if pieces:
            rest = rest[:6] + (rest[6:8], rest[8:10], rest[10:12]) + rest[12:]
        middle_kernel(pieces, o_all, x0, weights[:n], weights[n:2 * n], weights[2 * n:], *rest)

    if pieces:
        parts = (2, *downs[0].shape[1:2], downs[0].shape[2], part)
        grads = [shape((width, part), bf16)] * 2 + [shape(parts, bf16)] * 2 + [shape((width, 256), bf16)] * 2
    else:
        grads = [shape((2, width, part), bf16), shape((2, width, part), bf16), shape((2, width, 256), bf16)]
    return pl.pallas_call(
        kernel,
        out_shape=(shape((rows, width), bf16), shape((rows, width), f32), shape((2 * rows, ow), bf16),
                   *grads, shape((6, 8, width), f32), shape((4, 8, part), f32)),
        in_specs=[hbm] * (3 + 3 * n) + [vmem] * 2,
        out_specs=[hbm] * (3 + len(grads)) + [vmem] * 2,
        scratch_shapes=[
            v((2, rows, ow), bf16), v((2, 2, width, 256), bf16), v((2, width, ow), bf16), v((4, width, part), bf16),
            v((4, width, part), bf16),
            v((rows, width), f32), v((rows, 1), f32), v((rows, width), f32), v((rows, width), bf16), v((width, rows), bf16),
            v((4, rows, part), f32), v((4, rows, part), bf16), v((rows, width), bf16), v((rows, width), bf16),
            v((width, rows), bf16), v((rows, width), bf16), v((2, width, part), bf16),
            v((2, width, part), bf16), v((2, width, part), bf16), v((2, width, part), bf16), v((2, width, 256), bf16),
            v((2, width, 256), bf16), v((BLOCK, part), f32), v((BLOCK, part), f32),
            pltpu.SemaphoreType.DMA((40,)), pltpu.SemaphoreType.DMA((8,)),
            pltpu.SemaphoreType.DMA((12,)), pltpu.SemaphoreType.DMA((12,)),
        ],
        compiler_params=pltpu.CompilerParams(vmem_limit_bytes=VMEM_MAX, collective_id=1, has_side_effects=True),
        cost_estimate=pl.CostEstimate(flops=6 * rows * width * 9 * width, bytes_accessed=60_000_000, transcendentals=2 * rows * 4 * part),
        name="middle",
    )(o_all, x0, *outs, *ups, *downs, cot, vec, bup)


class Exchange:
    def __init__(self, send, recv):
        self.send, self.recv, self.used = send, recv, 0

    def copy(self, src, dst, device):
        n = self.used
        self.used += 1
        return pltpu.make_async_remote_copy(src, dst, self.send.at[n], self.recv.at[n], device_id=device,
                                            device_id_type=pl.DeviceIdType.MESH)


def greet(devices):
    barrier = pltpu.get_barrier_semaphore()
    for device in devices:
        pl.semaphore_signal(barrier, inc=1, device_id=device, device_id_type=pl.DeviceIdType.MESH)
    pl.semaphore_wait(barrier, len(devices))


def entry_kernel(tokens, pos_ref, mem_ref, wq_ref, bq_ref, bu_ref, wu_ref, wd_ref, wo_ref,
                 x0_out, x_out, q_out, k_out, v_out, w_out, up_g, down_g, out_g, bu_out,
                 x0_ref, x_ref, g_ref, b_ref, y_ref, q_ref, k_ref, v_ref, ub_ref, send, recv, sem):
    f32, bf16 = jnp.float32, jnp.bfloat16
    rows, width = x0_ref.shape
    dp, tensor = lax.axis_index("dp"), lax.axis_index("tensor")
    z, x = dp // 2, dp % 2
    inner = tensor % 2
    zs = [(z + 4 - k) % 4 for k in range(4)]
    at = [2 * zs[k] + x for k in range(4)]
    far = [2 * zs[k] + 1 - x for k in range(4)]
    to_z = [None] + [(2 * ((z + k) % 4) + x, tensor) for k in range(1, 4)]
    to_x = (2 * z + 1 - x, tensor)
    to_y = (dp, (tensor + 2) % 4)
    to_core = (dp, tensor + 1 - 2 * inner)
    to_both = (dp, 3 - tensor)
    greet(to_z[1:] + [to_x, to_y, to_core, to_both])
    ex = Exchange(send, recv)
    started = []

    def go(src, dst, device):
        copy = ex.copy(src, dst, device)
        copy.start()
        started.append(copy)
        return copy

    local = []

    def keep(src, dst):
        copy = pltpu.make_async_copy(src, dst, sem.at[len(local)])
        copy.start()
        local.append(copy)
        return copy

    own = keep(wq_ref, g_ref.at[0, at[0]])
    own_bias = keep(bq_ref, b_ref.at[0])
    z_q = [None] + [go(wq_ref, g_ref.at[0, at[0]], to_z[k]) for k in range(1, 4)]
    x_q = [go(wq_ref, g_ref.at[0, at[0]], to_x)]
    y_q = [go(wq_ref, g_ref.at[1, at[0]], to_y)]
    bias = go(bq_ref, b_ref.at[1], to_y)
    up_bias = [go(bu_ref, ub_ref.at[n - 1], to) for n, to in ((1, to_y), (2, to_core), (3, to_both))]

    mine = pl.multiple_of(inner * rows, 1024)
    positions = pos_ref[0:1, :]
    strip = 128

    def start(s, carry):
        r = pl.multiple_of(s * strip, strip)
        place = lax.broadcasted_iota(jnp.int32, (strip, positions.shape[1]), 0) + (inner * rows + r)
        picks = jnp.where(place == positions, 1.0, 0.0).astype(bf16)
        value = tokens[pl.ds(r, strip), :].astype(f32) + mm(picks, mem_ref[...])
        x0_ref[pl.ds(r, strip), :] = value
        x_ref[pl.ds(mine + r, strip), :] = value.astype(bf16)
        return carry
    lax.fori_loop(0, rows // strip, start, 0)
    keep(x0_ref, x0_out)
    core = go(x_ref.at[pl.ds(mine, rows), :], x_ref.at[pl.ds(mine, rows), :], to_core)

    for k in range(1, 4):
        z_q[k].wait_recv()
        x_q.append(go(g_ref.at[0, at[k]], g_ref.at[0, at[k]], to_x))
        y_q.append(go(g_ref.at[0, at[k]], g_ref.at[1, at[k]], to_y))
    z_u = [None] + [go(wu_ref, up_g.at[at[0]], to_z[k]) for k in range(1, 4)]
    z_d = [None] + [go(wd_ref, down_g.at[0, z], to_z[k]) for k in range(1, 4)]
    z_o = [None] + [go(wo_ref, out_g.at[0, z], to_z[k]) for k in range(1, 4)]
    keep(wu_ref, up_g.at[at[0]])
    keep(wd_ref, down_g.at[0, z])
    keep(wo_ref, out_g.at[0, z])
    last = []
    for k in range(2):
        x_q[k].wait_recv()
        last.append(go(g_ref.at[0, far[k]], g_ref.at[1, far[k]], to_y))
    for k in range(2, 4):
        y_q[k].wait_recv()
        last.append(go(g_ref.at[1, at[k]], g_ref.at[1, at[k]], to_x))
    rest = [go(wu_ref, up_g.at[at[0]], to_x), go(wd_ref, down_g.at[1, z], to_y), go(wo_ref, out_g.at[1, z], to_y)]
    for copy in x_q[2:] + y_q[:2] + last + [bias, core]:
        copy.wait_recv()
    own.wait()
    own_bias.wait()
    keep(g_ref, w_out)
    keep(x_ref, x_out)

    lane = lax.broadcasted_iota(jnp.int32, (BLOCK, 128), 1)
    y_ref[...] = jnp.zeros_like(y_ref)

    def project(b, carry):
        r = pl.ds(pl.multiple_of(b * BLOCK, BLOCK), BLOCK)
        for o in range(2):
            y_ref[o, :, 0:576] = mm(x_ref[r, :], g_ref[o].reshape(width, 576)) + b_ref[o, 0:1, 0:576].astype(f32)
        tile = lambda o, n: y_ref[o, :, 128 * n:128 * n + 128]
        turn = lambda value: pltpu.roll(value, 64, 1)
        third = (jnp.where(lane < 64, tile(0, 3), turn(tile(1, 3))), jnp.where(lane < 64, turn(tile(0, 3)), tile(1, 3)),
                 jnp.where(lane < 64, tile(0, 4), turn(tile(1, 4))))
        for n, ref in enumerate((q_ref, k_ref, v_ref)):
            for g, value in enumerate((tile(0, n), tile(1, n), third[n])):
                value = value.astype(bf16)
                if n == 0:
                    value = value * jnp.asarray(0.125, bf16)
                ref[r, 128 * g:128 * g + 128] = value
        return carry
    lax.fori_loop(0, 2 * rows // BLOCK, project, 0)
    for src, dst in ((q_ref, q_out), (k_ref, k_out), (v_ref, v_out)):
        keep(src, dst)
    for k in range(1, 4):
        z_u[k].wait_recv()
        rest.append(go(up_g.at[at[k]], up_g.at[at[k]], to_x))
        z_d[k].wait_recv()
        rest.append(go(down_g.at[0, zs[k]], down_g.at[1, zs[k]], to_y))
        z_o[k].wait_recv()
        rest.append(go(out_g.at[0, zs[k]], out_g.at[1, zs[k]], to_y))
    for copy in rest + up_bias:
        copy.wait_recv()
    bu_out[0] = bu_ref[...]
    for n in range(3):
        bu_out[n + 1] = ub_ref[n]
    for copy in started:
        copy.wait_send()
    for copy in local[2:]:
        copy.wait()


def entry(tokens, positions, memory_rows, shard_qkv, biases, up_bias, up, down, out):
    f32, bf16 = jnp.float32, jnp.bfloat16
    rows, width = tokens.shape
    r = up.shape[0]
    shape, v = jax.ShapeDtypeStruct, pltpu.VMEM
    hbm, vmem = pl.BlockSpec(memory_space=pl.ANY), pl.BlockSpec(memory_space=pltpu.VMEM)
    qkv = shape((2 * rows, 384), bf16)
    return pl.pallas_call(
        entry_kernel,
        out_shape=(shape((rows, width), f32), shape((2 * rows, width), bf16), qkv, qkv, qkv,
                   shape((2, 8, r, 576), bf16), shape((8, r, up.shape[1]), bf16), shape((2, 4, r, down.shape[1]), bf16),
                   shape((2, 4, r, out.shape[1]), bf16), shape((4, 16, up.shape[1]), bf16)),
        in_specs=[vmem] * 9,
        out_specs=[hbm] * 9 + [vmem],
        scratch_shapes=[
            v((rows, width), f32), v((2 * rows, width), bf16), v((2, 8, r, 576), bf16), v((2, 16, 640), bf16),
            v((2, BLOCK, 640), f32), v((2 * rows, 384), bf16), v((2 * rows, 384), bf16), v((2 * rows, 384), bf16),
            v((3, 16, up.shape[1]), bf16),
            pltpu.SemaphoreType.DMA((48,)), pltpu.SemaphoreType.DMA((48,)), pltpu.SemaphoreType.DMA((16,)),
        ],
        compiler_params=pltpu.CompilerParams(vmem_limit_bytes=VMEM_MAX, collective_id=0, has_side_effects=True),
        cost_estimate=pl.CostEstimate(flops=4 * rows * width * 1152, bytes_accessed=20_000_000, transcendentals=0),
        name="entry",
    )(tokens, positions, memory_rows, shard_qkv, biases, up_bias, up, down, out)


def exit_kernel(x_all, d0, d1, d2, w_all, third, kept_ref, came_ref, dr1, pos_ref, sums_in, up_in,
                tok_out, first_out, second_out, small_out,
                x_ref, xt_ref, d_ref, w_ref, dr_ref, g_ref, own_ref, oth_ref, yb_ref, xs_ref, xb_ref, zt_ref, zs_ref, zb_ref,
                fs_ref, fb_ref, their_ref, got_ref, tok_ref, s_ref, t_ref, r_ref, first_ref, send, recv, sem):
    f32, bf16 = jnp.float32, jnp.bfloat16
    rows, width = dr_ref.shape
    dp, tensor = lax.axis_index("dp"), lax.axis_index("tensor")
    z, x = dp // 2, dp % 2
    inner, outer = tensor % 2, tensor // 2
    up_z = [None] + [(z + k) % 4 for k in range(1, 4)]
    to_z = [None] + [(2 * up_z[k] + x, tensor) for k in range(1, 4)]
    to_x = (2 * z + 1 - x, tensor)
    to_y = (dp, (tensor + 2) % 4)
    to_core = (dp, tensor + 1 - 2 * inner)
    near_z = (2 * (z + 1 - 2 * (z % 2)) + x, tensor)
    far_z = to_z[2]
    loads = []
    for src, dst in ((d2, d_ref.at[2]), (x_all, x_ref), (d0, d_ref.at[0]), (d1, d_ref.at[1]),
                     (w_all.at[0, :, pl.ds(0, 384)], w_ref.at[0]), (w_all.at[1, :, pl.ds(0, 384)], w_ref.at[1]),
                     (third, w_ref.at[2]), (dr1, dr_ref)):
        copy = pltpu.make_async_copy(src, dst, sem.at[len(loads)])
        copy.start()
        loads.append(copy)
    greet(to_z[1:] + [to_x, to_y, to_core])
    ex = Exchange(send, recv)
    started = []

    def go(src, dst, device):
        copy = ex.copy(src, dst, device)
        copy.start()
        started.append(copy)
        return copy

    for k in range(4):
        first_ref[k] = kept_ref[k] + came_ref[k].astype(f32)
    for k in range(1, 4):
        fs_ref[k - 1] = first_ref[up_z[k]].astype(bf16)
    z_first = [go(fs_ref.at[k - 1], fb_ref.at[k - 1], to_z[k]) for k in range(1, 4)]

    loads[0].wait()
    loads[1].wait()
    for b in range(2 * rows // BLOCK):
        xt_ref[:, BLOCK * b:BLOCK * b + BLOCK] = x_ref[BLOCK * b:BLOCK * b + BLOCK, :].T
    for m in range(0, width, BLOCK):
        g_ref[m:m + BLOCK, :] = mm(xt_ref[m:m + BLOCK, :], d_ref[2])
    half = own_ref.shape[3]
    lane = lax.broadcasted_iota(jnp.int32, (half, 128), 1)
    for p in range(8):
        for n in range(3):
            low = g_ref[2 * half * p:2 * half * p + half, 128 * n:128 * n + 128]
            high = g_ref[2 * half * p + half:2 * half * (p + 1), 128 * n:128 * n + 128]
            own_ref[p % 2, p // 2, n] = jnp.where(lane < 64, low, pltpu.roll(high, 64, 1))
            oth_ref[p % 2, p // 2, n] = jnp.where(lane < 64, pltpu.roll(low, 64, 1), high).astype(bf16)
    y_far = go(oth_ref.at[1 - x], yb_ref.at[0], to_y)
    y_near = go(oth_ref.at[x], yb_ref.at[1], to_y)

    for copy in loads[2:]:
        copy.wait()
    place = lax.broadcasted_iota(jnp.int32, (32, 2 * rows), 1)
    which = lax.broadcasted_iota(jnp.int32, (32, 2 * rows), 0)
    picks = jnp.where((place == pos_ref[:, 0:1]) | (which == 24), 1.0, 0.0).astype(bf16)
    picked = [mm(picks, d_ref[n]) for n in range(3)]
    own_place = lax.broadcasted_iota(jnp.int32, (32, rows), 1) + inner * rows
    own_picks = jnp.where(own_place == pos_ref[:, 0:1], 1.0, 0.0)
    memory = lax.dot_general(own_picks, dr_ref[...], NN, precision=lax.Precision.HIGHEST, preferred_element_type=f32)
    for n in range(3):
        memory = memory + mm(picked[n].astype(bf16), w_ref[n], NT)
    hw = s_ref.shape[2]

    def put(row, value):
        for h in range(2):
            s_ref[h, row:row + 1, :] = value[:, hw * h:hw * h + hw]
    for h in range(2):
        s_ref[h, 0:24, :] = memory[0:24, hw * h:hw * h + hw]
        s_ref[h, 38:40, :] = jnp.zeros((2, hw), f32)
    for n in range(6):
        put(24 + n, jnp.sum(sums_in[n], axis=0, keepdims=True))
    ups = [jnp.sum(up_in[n], axis=0, keepdims=True) for n in (0, 2, 1, 3)]
    total = [value[24:25, :] for value in picked]
    turned = jnp.concatenate([pltpu.roll(picked[2][24:32, 128 * n:128 * n + 128], 64, 1) for n in range(3)], axis=1)[0:1, :]
    for t in range(4):
        n = (t % 2 + inner) % 2 + 2 * ((t // 2 + outer) % 2)
        value = jnp.zeros_like(ups[0])
        for other in range(4):
            value = value + jnp.where(n == other, ups[other], 0.0)
        put(30 + t, value)
        s_ref[0, 34 + t:35 + t, :] = jnp.where(n == 0, total[0], 0.0) + jnp.where(n == 2, total[1], 0.0)
        s_ref[1, 34 + t:35 + t, :] = jnp.where(n == 0, total[2], 0.0) + jnp.where(n == 2, turned, 0.0)
    small = [go(s_ref.at[1 - inner], r_ref.at[0], to_core)]
    hops = [to_y, to_x, near_z, far_z]

    def hop(n):
        small[n].wait_recv()
        t_ref[n] = (s_ref[inner] if n == 0 else t_ref[n - 1]) + r_ref[n]
        if n < 4:
            small.append(go(t_ref.at[n], r_ref.at[n + 1], hops[n]))
        else:
            small.append(go(t_ref.at[n], r_ref.at[5], to_core))
            small_out[inner] = t_ref[n]

    mine = pl.multiple_of(inner * rows, 1024)
    theirs = pl.multiple_of((1 - inner) * rows, 1024)

    def block(start):
        r = pl.ds(pl.multiple_of(start, BLOCK), BLOCK)
        return mm(d_ref[0, r, :], w_ref[0], NT) + mm(d_ref[1, r, :], w_ref[1], NT) + mm(d_ref[2, r, :], w_ref[2], NT)

    def away(b, carry):
        their_ref[pl.ds(pl.multiple_of(b * BLOCK, BLOCK), BLOCK), :] = block(theirs + b * BLOCK).astype(bf16)
        return carry
    lax.fori_loop(0, rows // BLOCK, away, 0)
    tokens = go(their_ref, got_ref, to_core)
    hop(0)
    y_far.wait_recv()
    for k in range(4):
        xs_ref[k] = (own_ref[1 - x, k] + yb_ref[0, k].astype(f32)).astype(bf16)
    x_sum = go(xs_ref, xb_ref, to_x)

    def stay(b, carry):
        tok_ref[pl.ds(pl.multiple_of(b * BLOCK, BLOCK), BLOCK), :] = block(mine + b * BLOCK)
        return carry
    lax.fori_loop(0, rows // BLOCK, stay, 0)
    hop(1)
    y_near.wait_recv()
    x_sum.wait_recv()
    for k in range(4):
        zt_ref[k] = own_ref[x, k] + yb_ref[1, k].astype(f32) + xb_ref[k].astype(f32)
    for k in range(1, 4):
        zs_ref[k - 1] = zt_ref[up_z[k]].astype(bf16)
    z_second = [go(zs_ref.at[k - 1], zb_ref.at[k - 1], to_z[k]) for k in range(1, 4)]
    hop(2)
    tokens.wait_recv()

    def finish(s, carry):
        r = pl.ds(pl.multiple_of(s * STRIP, STRIP), STRIP)
        tok_ref[r, :] = tok_ref[r, :] + got_ref[r, :].astype(f32) + dr_ref[r, :]
        return carry
    lax.fori_loop(0, rows // STRIP, finish, 0)
    out = pltpu.make_async_copy(tok_ref, tok_out, sem.at[8])
    out.start()
    hop(3)
    for copy in z_first:
        copy.wait_recv()
    first_out[...] = first_ref[z] + fb_ref[0].astype(f32) + fb_ref[1].astype(f32) + fb_ref[2].astype(f32)
    for copy in z_second:
        copy.wait_recv()
    second_out[...] = zt_ref[z] + zb_ref[0].astype(f32) + zb_ref[1].astype(f32) + zb_ref[2].astype(f32)
    hop(4)
    small[5].wait_recv()
    small_out[1 - inner] = r_ref[5]
    for copy in started:
        copy.wait_send()
    out.wait()


def leave(x_all, d, w_qkv, third, first, came, dr1, place, sums, up_sums):
    f32, bf16 = jnp.float32, jnp.bfloat16
    rows, width = dr1.shape
    r, half = first.shape[1], first.shape[1] // 2
    shape, v = jax.ShapeDtypeStruct, pltpu.VMEM
    hbm, vmem = pl.BlockSpec(memory_space=pl.ANY), pl.BlockSpec(memory_space=pltpu.VMEM)
    return pl.pallas_call(
        exit_kernel,
        out_shape=(shape((rows, width), f32), shape((r, 384), f32), shape((3, half, 128), f32), shape((2, 40, width // 2), f32)),
        in_specs=[hbm] * 6 + [vmem] * 2 + [hbm] + [vmem] * 3,
        out_specs=[hbm] + [vmem] * 3,
        scratch_shapes=[
            v((2 * rows, width), bf16), v((width, 2 * rows), bf16), v((3, 2 * rows, 384), bf16), v((3, width, 384), bf16),
            v((rows, width), f32), v((width, 384), f32), v((2, 4, 3, half, 128), f32), v((2, 4, 3, half, 128), bf16),
            v((2, 4, 3, half, 128), bf16), v((4, 3, half, 128), bf16), v((4, 3, half, 128), bf16), v((4, 3, half, 128), f32),
            v((3, 3, half, 128), bf16), v((3, 3, half, 128), bf16), v((3, r, 384), bf16), v((3, r, 384), bf16),
            v((rows, width), bf16), v((rows, width), bf16), v((rows, width), f32), v((2, 40, width // 2), f32),
            v((5, 40, width // 2), f32), v((6, 40, width // 2), f32), v((4, r, 384), f32),
            pltpu.SemaphoreType.DMA((16,)), pltpu.SemaphoreType.DMA((16,)), pltpu.SemaphoreType.DMA((9,)),
        ],
        compiler_params=pltpu.CompilerParams(vmem_limit_bytes=VMEM_MAX, collective_id=2, has_side_effects=True),
        cost_estimate=pl.CostEstimate(flops=2 * rows * width * 384 * 8, bytes_accessed=20_000_000, transcendentals=0),
        name="leave",
    )(x_all, *d, w_qkv, third, first, came, dr1, place, sums, up_sums)


def layer_norm(values, norm_gain, norm_shift):
    centre = values - jnp.mean(values, axis=-1, keepdims=True)
    spread = jnp.mean(centre * centre, axis=-1, keepdims=True)
    return centre * lax.rsqrt(spread + EPSILON) * norm_gain + norm_shift


def gelu_exact(values):
    return jax.nn.gelu(values, approximate=False)


AXES = ("dp", "tensor")


class Grid:
    def __init__(self, dp, tensor):
        self.dp, self.tensor = dp, tensor
        factors, rest = [2], dp // 2
        while rest > 8:
            factors.insert(0, 4)
            rest //= 4
        if rest > 1:
            factors.insert(0, rest)
        self.factors = factors

    def digit(self, j):
        stride = 1
        for f in self.factors[j + 1:]:
            stride *= f
        return stride, self.factors[j]

    def my_digit(self, j):
        stride, f = self.digit(j)
        return lax.axis_index("dp") // stride % f

    def turn(self, value, j, k):
        stride, f = self.digit(j)
        pairs = []
        for d in range(self.dp):
            g = d // stride % f
            to = d + ((g + k) % f - g) * stride
            for t in range(self.tensor):
                pairs.append((d * self.tensor + t, to * self.tensor + t))
        return lax.ppermute(value, AXES, pairs)

    def swap_dp(self, value, bit):
        pairs = [(d * self.tensor + t, (d ^ bit) * self.tensor + t) for d in range(self.dp) for t in range(self.tensor)]
        return lax.ppermute(value, AXES, pairs)

    def swap(self, value, bit):
        pairs = [(d * self.tensor + t, d * self.tensor + (t ^ bit)) for d in range(self.dp) for t in range(self.tensor)]
        return lax.ppermute(value, AXES, pairs)

    def gather_stage(self, value, j, axis):
        _, f = self.digit(j)
        g = self.my_digit(j)
        got = [value] + [self.turn(value, j, k) for k in range(1, f)]
        if f == 2:
            lower = jnp.where(g == 0, got[0], got[1])
            upper = jnp.where(g == 0, got[1], got[0])
            return jnp.stack([lower, upper], axis=axis)
        ring = got[::-1]
        return lax.dynamic_slice_in_dim(jnp.stack(ring + ring[:-1], axis=axis), f - 1 - g, f, axis)

    def gather(self, shard, outer_first=False):
        count = len(self.factors)
        value = shard
        for j in range(count - 1):
            value = self.gather_stage(value, j, j)
        if outer_first:
            value = jnp.stack([value, self.swap(value, 2)])
            value = self.gather_stage(value, count - 1, count)
            return value.reshape(2, -1, shard.shape[-1])
        value = self.gather_stage(value, count - 1, count - 1)
        value = value.reshape(-1, shard.shape[-1])
        return jnp.stack([value, self.swap(value, 2)])

    def reduce_stage(self, value, j, axis):
        _, f = self.digit(j)
        g = self.my_digit(j)
        total = lax.dynamic_index_in_dim(value, g, axis, keepdims=False).astype(jnp.float32)
        for k in range(1, f):
            part = lax.dynamic_index_in_dim(value, (g + k) % f, axis, keepdims=False)
            total = total + self.turn(part.astype(jnp.bfloat16), j, k).astype(jnp.float32)
        return total

    def reduce(self, parts, outer_first=True):
        count = len(self.factors)
        columns = parts.shape[-1]
        value = parts
        if outer_first:
            value = value[0].astype(jnp.float32) + self.swap(value[1].astype(jnp.bfloat16), 2).astype(jnp.float32)
            value = value.reshape(*self.factors, -1, columns)
            value = self.reduce_stage(value, count - 1, count - 1)
        else:
            value = value.reshape(2, *self.factors, -1, columns)
            value = self.reduce_stage(value, count - 1, count)
            value = value[0] + self.swap(value[1].astype(jnp.bfloat16), 2).astype(jnp.float32)
        for j in reversed(range(count - 1)):
            value = self.reduce_stage(value, j, j)
        return value

    @property
    def stages(self):
        return len(self.factors) + 1

    def open(self, parts, outer_first):
        columns = parts.shape[-1]
        return parts if outer_first else parts.reshape(2, *self.factors, -1, columns)

    def stage(self, value, outer_first, n):
        count = len(self.factors)
        if n == (0 if outer_first else 1):
            value = value[0].astype(jnp.float32) + self.swap(value[1].astype(jnp.bfloat16), 2).astype(jnp.float32)
            return value.reshape(*self.factors, -1, value.shape[-1]) if outer_first else value
        if n == 0:
            return self.reduce_stage(value, count - 1, count)
        return self.reduce_stage(value, count - n, count - n)

    def total(self, vector):
        for bit in (1, 2):
            vector = vector + self.swap(vector, bit)
        bit = 1
        while bit < self.dp:
            vector = vector + self.swap_dp(vector, bit)
            bit *= 2
        return vector


def shards(grid, tokens, segment_ids, memory_positions, memory_rows, qkv_weight, qv_bias, out_weight, out_bias,
           norm1_gain, norm1_bias, up_weight, up_bias, down_weight, down_bias, norm2_gain, norm2_bias, out_cotangent):
    f32, bf16 = jnp.float32, jnp.bfloat16
    rows, width = tokens.shape
    group_len = segment_ids.shape[1]
    tensor = lax.axis_index("tensor")
    inner, outer = tensor % 2, tensor // 2
    slice_rows = qkv_weight.shape[0]
    heads = qkv_weight.shape[1]
    hd = 64
    hw = heads * hd
    units = up_weight.shape[1]

    segments = lax.dynamic_index_in_dim(segment_ids, outer, 0, keepdims=False)
    positions = lax.dynamic_index_in_dim(memory_positions, outer, 0, keepdims=False)
    row_place = inner * rows + jnp.arange(rows, dtype=jnp.int32)
    picks = (row_place[:, None] == positions[None, :])
    joined = lambda w: w.transpose(1, 0, 2).reshape(width, -1)

    parts = qkv_weight.reshape(slice_rows, heads, 3, hd)
    order_columns = lambda p: jnp.concatenate([p[..., :2, n, :].reshape(*p.shape[:-3], 2 * hd) for n in range(3)]
                                              + [p[..., 2, n, :] for n in range(3)], axis=-1)
    shard_qkv = order_columns(parts)
    shard_out = jnp.pad(out_weight.reshape(slice_rows, hw), ((0, 0), (0, 256 - hw)))
    bias_parts = qv_bias.reshape(heads, 2, hd)
    bias_qkv = order_columns(jnp.stack([bias_parts[:, 0], jnp.zeros_like(bias_parts[:, 0]), bias_parts[:, 1]], 1))
    bias_qkv = jnp.pad(bias_qkv[None], ((0, 15), (0, 64)))
    own_up_bias = jnp.broadcast_to(up_bias[None], (16, units))
    fused = grid.dp == 8 and grid.tensor == 4
    if fused:
        memory = memory_positions.shape[1]
        place = jnp.pad(positions[None], ((0, 7), (0, 32 - memory)), constant_values=-1)
        table = jnp.pad(memory_rows, ((0, 32 - memory), (0, 0)))
        x0, x_all, q, k, v, w_qkv, up_g, down_g, out_g, b_up = entry(tokens, place, table, shard_qkv, bias_qkv, own_up_bias, up_weight, down_weight, shard_out)
        column = jnp.pad(jnp.broadcast_to(positions[:, None], (memory, 128)), ((0, 32 - memory), (0, 0)), constant_values=-1)
        w_qkv = w_qkv.reshape(2, width, 9 * hd)
        third = jnp.concatenate([w_qkv[o][:, (6 + n) * hd:(7 + n) * hd] for n in range(3) for o in range(2)], 1)
        up_all = up_g.reshape(width, units)
        ups = (up_all, grid.swap(up_all, 2))
        downs = (down_g, grid.turn(down_g, 1, 1))
        outs = (out_g, grid.turn(out_g, 1, 1))
    else:
        x0 = tokens.astype(f32) + jnp.dot(picks.astype(bf16), memory_rows, preferred_element_type=f32)
        xl = x0.astype(bf16)
        w_qkv = grid.gather(shard_qkv)
        other = grid.swap(xl, 1)
        x_all = jnp.concatenate([jnp.where(inner == 0, xl, other), jnp.where(inner == 0, other, xl)])
        b_two = jnp.stack([bias_qkv[0], grid.swap(bias_qkv[0], 2)]).astype(f32)
        y = [(mm(x_all, w_qkv[o]) + b_two[o, :9 * hd]).astype(bf16) for o in range(2)]
        third = lambda n: [one[:, (6 + n) * hd:(7 + n) * hd] for one in y]
        q, k, v = [jnp.concatenate([y[0][:, 2 * n * hd:2 * (n + 1) * hd], y[1][:, 2 * n * hd:2 * (n + 1) * hd]] + third(n), 1)
                   for n in range(3)]
        q = q * jnp.asarray(0.125, bf16)
        b_up = jnp.stack([own_up_bias, grid.swap(own_up_bias, 2)])
        b_up = jnp.concatenate([b_up, grid.swap(b_up, 1)])
        outs, ups, downs = (grid.gather(shard_out, True),), (grid.gather(up_weight),), (grid.gather(down_weight, True),)
    mixed, lse = attend_forward(q, k, v, segments)
    vec = jnp.stack([out_bias, norm1_gain, norm1_bias, down_bias, norm2_gain, norm2_bias, norm2_bias, norm2_bias]).astype(f32)
    (block_out, dr1, do_all, *grads, sums, up_sums) = middle(
        mixed, x0, outs, ups, downs, out_cotangent, vec, b_up)
    if fused:
        return finish_small(grid, tensor, x_all, q, k, v, do_all, mixed, lse, segments, w_qkv, third, dr1, column, sums, up_sums, block_out,
                            grads, hw)
    g_down, g_up, g_out = grads

    TN = (((0,), (0,)), ((), ()))
    tie = lax.optimization_barrier
    kinds = (True, False, True)
    state = [grid.open(parts, kind) for parts, kind in zip((g_down, g_up, g_out), kinds)]
    step = lambda n, state: [grid.stage(value, kind, n) for value, kind in zip(state, kinds)]
    late = [(1, 0, 2)[n] for n in range(3)]
    d = [None] * 3
    state, d[1] = step(0, state), attend_backward(1, q, k, v, do_all, mixed, lse, segments)
    state, d[1], q = tie((state, d[1], q))
    g_one = mm(x_all, d[1], TN).astype(bf16)
    state, d[0] = step(1, state), attend_backward(0, q, k, v, do_all, mixed, lse, segments)
    state, d[0], q, g_one = tie((state, d[0], q, g_one))
    g_zero = mm(x_all, d[0], TN)
    first = g_zero + grid.swap(g_one, 2).astype(f32)
    state, d[2] = step(2, state), attend_backward(2, q, k, v, do_all, mixed, lse, segments)
    state, d[2], first = tie((state, d[2], first))
    for n in range(3, grid.stages):
        state = step(n, state)
    grad_down, grad_up, grad_out = state
    grad_out = grad_out[:, :hw]

    g_two = mm(x_all, d[2], TN)
    side = lambda m, o: jnp.concatenate([m[:, (2 * n + o) * hd:(2 * n + o + 1) * hd] for n in range(3)], 1)
    second = side(g_two, 0) + grid.swap(side(g_two, 1).astype(bf16), 2).astype(f32)
    both = jnp.concatenate([first, second], 1).reshape(*grid.factors, slice_rows, 9 * hd)
    for j in reversed(range(len(grid.factors))):
        both = grid.reduce_stage(both, j, j)
    restore = lambda p: jnp.stack([jnp.concatenate([p[..., 2 * n * hd:2 * (n + 1) * hd].reshape(*p.shape[:-1], 2, hd),
                                                    p[..., None, (6 + n) * hd:(7 + n) * hd]], -2) for n in range(3)], -2)
    grad_qkv = restore(both).reshape(slice_rows, heads, 3 * hd)
    third = jnp.concatenate([w_qkv[o][:, (6 + n) * hd:(7 + n) * hd] for n in range(3) for o in range(2)], 1)
    part = (mm(d[0], w_qkv[0][:, :6 * hd], NT) + mm(d[1], w_qkv[1][:, :6 * hd], NT) + mm(d[2], third, NT)).reshape(2, rows, width)
    mine = lax.dynamic_index_in_dim(part, inner, 0, keepdims=False)
    theirs = lax.dynamic_index_in_dim(part, 1 - inner, 0, keepdims=False).astype(bf16)
    grad_tokens = mine + grid.swap(theirs, 1).astype(f32) + dr1
    d_sum = [jnp.sum(one.astype(f32), axis=0) for one in d]
    d_bias = [jnp.concatenate([d_sum[o]] + [d_sum[2][(2 * n + o) * hd:(2 * n + o + 1) * hd] for n in range(3)]) for o in range(2)]
    dg2, ds2, d_down_bias, dg1, ds1, d_out_bias = jnp.sum(sums, axis=1)
    d_up_bias = jnp.sum(up_sums, axis=1).reshape(2, 2 * units)
    grad_memory = jnp.dot(picks.astype(f32).T, grad_tokens, precision=lax.Precision.HIGHEST)

    order = jnp.arange(4, dtype=jnp.int32) ^ tensor
    up_parts = d_up_bias.reshape(2, 2, units)
    up_parts = jnp.stack([up_parts[0, 0], up_parts[1, 0], up_parts[0, 1], up_parts[1, 1]])[order]
    take = lambda o: restore(d_bias[o])[:, 0::2].reshape(-1)
    blank = jnp.zeros((2 * hw,), f32)
    qv_parts = jnp.stack([take(0), blank, take(1), blank])[order]
    pieces = [grad_memory.reshape(-1), d_out_bias, dg1, ds1, d_down_bias, dg2, ds2, up_parts.reshape(-1), qv_parts.reshape(-1)]
    summed = grid.total(jnp.concatenate(pieces))
    outs, at = [], 0
    for piece in pieces:
        outs.append(lax.slice_in_dim(summed, at, at + piece.size))
        at += piece.size
    t_memory, t_out_bias, t_g1, t_s1, t_down_bias, t_g2, t_s2, t_up, t_qv = outs
    grad_up_bias = lax.dynamic_index_in_dim(t_up.reshape(4, units), tensor, 0, keepdims=False)
    grad_qv = lax.dynamic_index_in_dim(t_qv.reshape(4, heads, 2 * hd), tensor, 0, keepdims=False)
    return (block_out, grad_tokens, t_memory.reshape(-1, width), grad_qkv, grad_qv,
            grad_out.reshape(slice_rows, heads, hd), t_out_bias, t_g1, t_s1, grad_up, grad_up_bias, grad_down,
            t_down_bias, t_g2, t_s2)


def blend_one_kernel(x_ref, down, down_in, up, up_in, out, out_in, kept_down, kept_up, kept_out, send_x, send_y):
    f32, bf16 = jnp.float32, jnp.bfloat16
    x = x_ref[0]
    width = down.shape[-1]
    add = lambda a, b: a.astype(f32) + b.astype(f32)
    kept_down[0] = add(down[0, x], down_in[0, x])
    kept_out[0] = add(out[0, x], out_in[0, x])
    send_x[0, :, 0:width] = add(down[0, 1 - x], down_in[0, 1 - x]).astype(bf16)
    send_x[0, :, width:] = add(out[0, 1 - x], out_in[0, 1 - x]).astype(bf16)
    kept_up[0] = add(up[0, 0], up_in[0, 0])
    send_y[0] = add(up[1, 0], up_in[1, 0]).astype(bf16)


def blend_one(x, down, down_in, up, up_in, out, out_in):
    f32, bf16 = jnp.float32, jnp.bfloat16
    _, zs, r, width = up.shape
    ow = out.shape[-1]
    shape = jax.ShapeDtypeStruct
    by_x = lambda columns: pl.BlockSpec((1, 2, r, columns), lambda j, *_: (j, 0, 0, 0))
    by_y = pl.BlockSpec((2, 1, r, width), lambda j, *_: (0, j, 0, 0))
    one = lambda columns: pl.BlockSpec((1, r, columns), lambda j, *_: (j, 0, 0))
    fold = lambda a: a.reshape(zs, 2, r, a.shape[-1])
    return pl.pallas_call(
        blend_one_kernel,
        out_shape=(shape((zs, r, width), f32), shape((zs, r, width), f32), shape((zs, r, ow), f32),
                   shape((zs, r, width + ow), bf16), shape((zs, r, width), bf16)),
        grid_spec=pltpu.PrefetchScalarGridSpec(
            num_scalar_prefetch=1, grid=(zs,),
            in_specs=[by_x(width), by_x(width), by_y, by_y, by_x(ow), by_x(ow)],
            out_specs=[one(width), one(width), one(ow), one(width + ow), one(width)]),
        compiler_params=pltpu.CompilerParams(dimension_semantics=("arbitrary",), vmem_limit_bytes=VMEM_MAX),
        cost_estimate=pl.CostEstimate(flops=8 * zs * r * width, bytes_accessed=10_000_000, transcendentals=0),
        name="blend_one",
    )(x.reshape(1), fold(down), fold(down_in), up, up_in, fold(out), fold(out_in))


def blend_two_kernel(at_ref, kept_down, kept_up, kept_out, came_x, came_y, first, kept_z, kept_first, *sends):
    f32, bf16 = jnp.float32, jnp.bfloat16
    x, z = at_ref[0], at_ref[1]
    zs, r, width = kept_down.shape
    for k in range(zs):
        n = (z + k) % zs
        parts = (kept_down[n] + came_x[n, :, 0:width].astype(f32), kept_up[n] + came_y[n].astype(f32),
                 kept_out[n] + came_x[n, :, width:].astype(f32))
        start = 0
        for part in parts:
            stop = start + part.shape[1]
            if k == 0:
                kept_z[:, start:stop] = part
            else:
                sends[k - 1][:, start:stop] = part.astype(bf16)
            start = stop
        kept_first[k] = first[k, x]
        sends[zs - 1][k] = first[k, 1 - x].astype(bf16)


def blend_two(x, z, kept_down, kept_up, kept_out, came_x, came_y, first):
    f32, bf16 = jnp.float32, jnp.bfloat16
    zs, r, width = kept_down.shape
    columns = 2 * width + kept_out.shape[-1]
    shape = jax.ShapeDtypeStruct
    vmem = pl.BlockSpec(memory_space=pltpu.VMEM)
    return pl.pallas_call(
        blend_two_kernel,
        out_shape=(shape((r, columns), f32), shape((zs, r, first.shape[-1]), f32), *[shape((r, columns), bf16)] * (zs - 1),
                   shape((zs, r, first.shape[-1]), bf16)),
        in_specs=[pl.BlockSpec(memory_space=pltpu.SMEM)] + [vmem] * 6,
        out_specs=[vmem] * (zs + 2),
        compiler_params=pltpu.CompilerParams(vmem_limit_bytes=VMEM_MAX),
        cost_estimate=pl.CostEstimate(flops=4 * zs * r * columns, bytes_accessed=10_000_000, transcendentals=0),
        name="blend_two",
    )(jnp.stack([x, z]), kept_down, kept_up, kept_out, came_x, came_y, first.reshape(zs, 2, r, first.shape[-1]))


def spread_kernel(t_ref, kept, came_one, came_two, came_three, small, down, up, out, memory, vec, up_bias, qv):
    f32 = jnp.float32
    width = down.shape[1]
    for ref, start in ((down, 0), (up, width), (out, 2 * width)):
        cols = slice(start, start + ref.shape[1])
        ref[...] = (kept[:, cols] + came_one[:, cols].astype(f32)) + (came_two[:, cols].astype(f32) + came_three[:, cols].astype(f32))
    half = width // 2
    t = t_ref[0]
    for h in range(2):
        cols = slice(half * h, half * h + half)
        memory[:, cols] = small[h, 0:memory.shape[0], :]
        vec[:, cols] = small[h, 24:32, :]
        up_bias[:, cols] = small[h, pl.ds(30 + t, 1), :]
        qv[h:h + 1, :] = small[h, pl.ds(34 + t, 1), :]


def spread(tensor, kept, came, small, memory, ow):
    f32 = jnp.float32
    r, columns = kept.shape
    width = 2 * small.shape[2]
    shape = jax.ShapeDtypeStruct
    vmem = pl.BlockSpec(memory_space=pltpu.VMEM)
    return pl.pallas_call(
        spread_kernel,
        out_shape=(shape((r, width), f32), shape((r, width), f32), shape((r, ow), f32), shape((memory, width), f32),
                   shape((8, width), f32), shape((1, width), f32), shape((2, width // 2), f32)),
        in_specs=[pl.BlockSpec(memory_space=pltpu.SMEM)] + [vmem] * 5,
        out_specs=[vmem] * 7,
        compiler_params=pltpu.CompilerParams(vmem_limit_bytes=VMEM_MAX),
        cost_estimate=pl.CostEstimate(flops=3 * r * columns, bytes_accessed=3_000_000, transcendentals=0),
        name="spread",
    )(tensor.reshape(1), kept, *came, small)


def finish_small(grid, tensor, x_all, q, k, v, do_all, mixed, lse, segments, w_qkv, third, dr1, column, sums, up_sums, block_out,
                 grads, hw):
    f32, bf16 = jnp.float32, jnp.bfloat16
    tie = lax.optimization_barrier
    TN = (((0,), (0,)), ((), ()))
    width = dr1.shape[1]
    x, z = lax.axis_index("dp") % 2, lax.axis_index("dp") // 2
    down, down_far, up, up_far, out, out_far = grads

    def beside(pair, q, sends):
        arrays, q = tie(([a for a, _ in sends], q))
        came = [move(a) for a, (_, move) in zip(arrays, sends)]
        d = attend_backward(pair, q, k, v, do_all, mixed, lse, segments)
        return tie((came, d, q))

    over_y = lambda a: grid.swap(a, 2)
    over_x = lambda a: grid.turn(a, 1, 1)
    (down_in, out_in, up_in), d_one, q = beside(1, q, [(down_far, over_y), (out_far, over_y), (up_far, over_x)])
    g_one = mm(x_all, d_one, TN).astype(bf16)
    kept_down, kept_up, kept_out, send_x, send_y = blend_one(x, down, down_in, up, up_in, out, out_in)
    (came_x, came_y, came_one), d_zero, q = beside(0, q, [(send_x, over_x), (send_y, over_y), (g_one, over_y)])
    first = mm(x_all, d_zero, TN) + came_one.astype(f32)
    kept, kept_first, *sends = blend_two(x, z, kept_down, kept_up, kept_out, came_x, came_y, first)
    over_z = [lambda a, n=n: grid.turn(a, 0, n) for n in range(1, 4)]
    came, d_two, q = beside(2, q, list(zip(sends, over_z + [over_x])))
    grad_tokens, one, two, small = leave(x_all, (d_zero, d_one, d_two), w_qkv, third, kept_first, came[3], dr1, column, sums, up_sums)
    grad_down, grad_up, grad_out, grad_memory, vec, up_bias, qv = spread(tensor, kept, came[:3], small, 20, out.shape[-1])
    hd = 64
    slice_rows = one.shape[0]
    two = two.reshape(3, slice_rows // 2, 2, hd).transpose(2, 1, 0, 3).reshape(slice_rows, 1, 3, hd)
    grad_qkv = jnp.concatenate([one.reshape(slice_rows, 3, 2, hd).transpose(0, 2, 1, 3), two], 1).reshape(slice_rows, 3, 3 * hd)
    part = lambda n: jnp.concatenate([qv[0, 128 * n:128 * n + 128].reshape(2, hd), qv[1:2, 128 * n:128 * n + hd]])
    grad_qv = jnp.concatenate([part(0), part(2)], 1)
    t_out_bias, t_g1, t_s1, t_down_bias, t_g2, t_s2 = [vec[n] for n in (5, 3, 4, 2, 0, 1)]
    return (block_out, grad_tokens, grad_memory, grad_qkv, grad_qv,
            grad_out[:, :hw].reshape(slice_rows, 3, hd), t_out_bias, t_g1, t_s1, grad_up, up_bias.reshape(width), grad_down,
            t_down_bias, t_g2, t_s2)


def solution(mesh):
    grid = Grid(mesh.shape["dp"], mesh.shape["tensor"])
    tokens, dp, none = P(AXES, None), P("dp", None), P()
    heads, matrix = P("dp", "tensor", None), P("dp", "tensor")
    in_specs = (tokens, dp, dp, none, heads, P("tensor", None), heads, none, none, none, matrix, P("tensor"), matrix,
                none, none, none, tokens)
    out_specs = (tokens, tokens, none, heads, P("tensor", None), heads, none, none, none, matrix, P("tensor"), matrix,
                 none, none, none)

    def run(*args):
        return shards(grid, *args)

    return jax.shard_map(run, mesh=mesh, in_specs=in_specs, out_specs=out_specs, check_vma=False)
```

```python
import functools

import jax
import jax.numpy as jnp
from jax import lax
from jax.experimental import pallas as pl
from jax.experimental.pallas import tpu as pltpu
from jax.sharding import PartitionSpec as P

EPSILON = 1e-12
TILE = 256
MASKED = -1e30
VMEM_MAX = 64 * 1024 * 1024 - 128 * 1024
NT = (((1,), (1,)), ((), ()))
NN = (((1,), (0,)), ((), ()))


def mm(a, b, dims=NN):
    return lax.dot_general(a, b, dims, preferred_element_type=jnp.float32)


def fold8(x):
    r = x.shape[0]
    return x.reshape(r // 8, 8, x.shape[1])


def head_masks(block):
    lane = lax.broadcasted_iota(jnp.int32, block.shape, 1)
    zero = jnp.zeros_like(block)
    return jnp.where(lane < 64, block, zero), jnp.where(lane < 64, zero, block)


def tile_visible(first_ref, last_ref, i, t):
    return (first_ref[t] == 0) | ((first_ref[t] <= last_ref[i]) & (last_ref[t] >= first_ref[i]))


def forward_kernel(first_ref, last_ref, q_ref, k_ref, v_ref, kseg_ref, qseg_ref, o_ref, lse_ref,
                   vt_ref, qm_ref, s_ref, m_ref, l_ref, acc_ref):
    i = pl.program_id(0)
    tiles = pl.num_programs(0)
    pairs = q_ref.shape[1] // 128
    heads = 2 * pairs

    @pl.when(i == 0)
    def _():
        def turn(t, c):
            rows = pl.ds(pl.multiple_of(t * TILE, TILE), TILE)
            vt_ref[t] = v_ref[rows, :].T
            return c
        lax.fori_loop(0, tiles, turn, 0)

    for g in range(pairs):
        a, b = head_masks(q_ref[:, 128 * g:128 * g + 128])
        qm_ref[2 * g] = a
        qm_ref[2 * g + 1] = b
    m_ref[...] = jnp.full_like(m_ref, MASKED)
    l_ref[...] = jnp.zeros_like(l_ref)
    acc_ref[...] = jnp.zeros_like(acc_ref)
    qseg = qseg_ref[0:1, :]

    def scores(t, c):
        @pl.when(tile_visible(first_ref, last_ref, i, t))
        def _():
            rows = pl.ds(pl.multiple_of(t * TILE, TILE), TILE)
            kseg = kseg_ref[rows, :]
            kseg = jnp.concatenate([kseg, kseg], axis=1)
            seen = (kseg == 0) | (kseg == qseg)
            for h in range(heads):
                kp = k_ref[rows, 128 * (h // 2):128 * (h // 2) + 128]
                s = mm(kp, qm_ref[h], NT)
                s = jnp.where(seen, s, MASKED)
                s_ref[h, t] = s
                m_ref[h] = jnp.maximum(m_ref[h], jnp.max(fold8(s), axis=0))
        return c
    lax.fori_loop(0, tiles, scores, 0)
    for h in range(heads):
        m_ref[h] = jnp.broadcast_to(jnp.max(m_ref[h], axis=0, keepdims=True), (8, TILE))

    def mix(t, c):
        @pl.when(tile_visible(first_ref, last_ref, i, t))
        def _():
            for h in range(heads):
                p = jnp.exp(s_ref[h, t] - m_ref[h, 0:1, :])
                l_ref[h] = l_ref[h] + jnp.sum(fold8(p), axis=0)
                acc_ref[h] = acc_ref[h] + mm(vt_ref[t, 64 * h:64 * h + 64, :], p.astype(jnp.bfloat16))
        return c
    lax.fori_loop(0, tiles, mix, 0)
    for h in range(heads):
        total = jnp.sum(l_ref[h], axis=0, keepdims=True)
        lse_ref[h:h + 1, :] = m_ref[h, 0:1, :] + jnp.log(total)
        acc_ref[h] = acc_ref[h] / total
    for g in range(pairs):
        pair = jnp.concatenate([acc_ref[2 * g], acc_ref[2 * g + 1]], axis=0)
        o_ref[:, 128 * g:128 * g + 128] = pair.T.astype(jnp.bfloat16)


def attend_forward(q, k, v, seg):
    n, width = q.shape
    tiles = n // TILE
    heads = width // 64
    first = seg[::TILE]
    last = seg[TILE - 1::TILE]
    kseg = jnp.broadcast_to(seg[:, None], (n, 128))
    qseg = jnp.broadcast_to(seg[None, :], (8, n))
    whole = lambda shape: pl.BlockSpec(shape, lambda i, *_: (0,) * len(shape))
    return pl.pallas_call(
        forward_kernel,
        out_shape=(jax.ShapeDtypeStruct((n, width), jnp.bfloat16), jax.ShapeDtypeStruct((8, n), jnp.float32)),
        grid_spec=pltpu.PrefetchScalarGridSpec(
            num_scalar_prefetch=2, grid=(tiles,),
            in_specs=[pl.BlockSpec((TILE, width), lambda i, *_: (i, 0)), whole((n, width)), whole((n, width)),
                      whole((n, 128)), pl.BlockSpec((8, TILE), lambda i, *_: (0, i))],
            out_specs=[pl.BlockSpec((TILE, width), lambda i, *_: (i, 0)), pl.BlockSpec((8, TILE), lambda i, *_: (0, i))],
            scratch_shapes=[
                pltpu.VMEM((tiles, width, TILE), jnp.bfloat16),
                pltpu.VMEM((heads, TILE, 128), jnp.bfloat16),
                pltpu.VMEM((heads, tiles, TILE, TILE), jnp.float32),
                pltpu.VMEM((heads, 8, TILE), jnp.float32),
                pltpu.VMEM((heads, 8, TILE), jnp.float32),
                pltpu.VMEM((heads, 64, TILE), jnp.float32),
            ]),
        compiler_params=pltpu.CompilerParams(dimension_semantics=("arbitrary",), vmem_limit_bytes=VMEM_MAX),
        cost_estimate=pl.CostEstimate(flops=4 * n * n * width, bytes_accessed=8 * n * width, transcendentals=n * n * heads),
        name="attend_forward",
    )(first, last, q, k, v, kseg, qseg)


def backward_kernel(base, first_ref, last_ref, q_ref, do_ref, o_ref, k_ref, v_ref, kseg_ref, qseg_ref, lse_ref,
                    d_ref, kt_ref, qm_ref, dom_ref, delta_ref, dqt_ref, dka_ref, dva_ref):
    i = pl.program_id(0)
    tiles = pl.num_programs(0)

    @pl.when(i == 0)
    def _():
        def turn(t, c):
            rows = pl.ds(pl.multiple_of(t * TILE, TILE), TILE)
            kt_ref[t] = k_ref[rows, :].T
            dka_ref[rows, :] = jnp.zeros((TILE, 128), jnp.float32)
            dva_ref[rows, :] = jnp.zeros((TILE, 128), jnp.float32)
            return c
        lax.fori_loop(0, tiles, turn, 0)

    for ref, masked in ((q_ref, qm_ref), (do_ref, dom_ref)):
        masked[0], masked[1] = head_masks(ref[...])
    inner = (do_ref[...].astype(jnp.float32) * o_ref[...].astype(jnp.float32)).T
    for h in range(2):
        delta_ref[h] = jnp.broadcast_to(jnp.sum(inner[64 * h:64 * h + 64], axis=0, keepdims=True), (8, TILE))
    dqt_ref[...] = jnp.zeros_like(dqt_ref)
    qseg = qseg_ref[0:1, :]

    def count(t, c):
        prompt, before, upto = c
        return (prompt + (first_ref[t] == 0).astype(jnp.int32), before + (last_ref[t] < first_ref[i]).astype(jnp.int32),
                upto + (first_ref[t] <= last_ref[i]).astype(jnp.int32))
    zero = jnp.int32(0)
    prompt, before, upto = lax.fori_loop(0, tiles, count, (zero, zero, zero))
    start = jnp.maximum(prompt, before)
    visible = prompt + jnp.maximum(upto - start, 0)

    def one_tile(n):
        t = jnp.where(n < prompt, n, start + n - prompt)
        rows = pl.ds(pl.multiple_of(t * TILE, TILE), TILE)
        kseg = kseg_ref[rows, :]
        kseg = jnp.concatenate([kseg, kseg], axis=1)
        seen = (kseg == 0) | (kseg == qseg)
        kp = k_ref[rows, :]
        vp = v_ref[rows, :]
        s = [mm(kp, qm_ref[h], NT) for h in range(2)]
        d = [mm(vp, dom_ref[h], NT) for h in range(2)]
        p = [jnp.where(seen, jnp.exp(s[h] - lse_ref[base + h:base + h + 1, :]), 0.0) for h in range(2)]
        ds = [(p[h] * (d[h] - delta_ref[h, 0:1, :])).astype(jnp.bfloat16) for h in range(2)]
        p = [value.astype(jnp.bfloat16) for value in p]
        dva_ref[rows, :] = dva_ref[rows, :] + (mm(p[0], dom_ref[0]) + mm(p[1], dom_ref[1]))
        dka_ref[rows, :] = dka_ref[rows, :] + (mm(ds[0], qm_ref[0]) + mm(ds[1], qm_ref[1]))
        return [mm(kt_ref[t, 64 * h:64 * h + 64, :], ds[h]) for h in range(2)]

    def two_tiles(n, c):
        one, two = one_tile(2 * n), one_tile(2 * n + 1)
        for h in range(2):
            dqt_ref[h] = dqt_ref[h] + (one[h] + two[h])
        return c
    lax.fori_loop(0, visible // 2, two_tiles, 0)

    @pl.when(visible % 2 == 1)
    def _():
        for h, value in enumerate(one_tile(visible - 1)):
            dqt_ref[h] = dqt_ref[h] + value
    pair = jnp.concatenate([dqt_ref[0], dqt_ref[1]], axis=0)
    own = pl.ds(pl.multiple_of(i * TILE, TILE), TILE)
    d_ref[own, 0:128] = (pair.T * 0.125).astype(jnp.bfloat16)

    @pl.when(i == tiles - 1)
    def _():
        d_ref[:, 128:256] = dka_ref[...].astype(jnp.bfloat16)
        d_ref[:, 256:384] = dva_ref[...].astype(jnp.bfloat16)


def attend_backward(g, q, k, v, do, o, lse, seg):
    n, width = q.shape[0], 128
    tiles = n // TILE
    heads = width // 64
    first = seg[::TILE]
    last = seg[TILE - 1::TILE]
    kseg = jnp.broadcast_to(seg[:, None], (n, 128))
    qseg = jnp.broadcast_to(seg[None, :], (8, n))
    whole = lambda shape: pl.BlockSpec(shape, lambda i, *_: (0,) * len(shape))
    rows = pl.BlockSpec((TILE, width), lambda i, *_: (i, g))
    column = pl.BlockSpec((n, width), lambda i, *_: (0, g))
    stat = pl.BlockSpec((8, TILE), lambda i, *_: (0, i))
    return pl.pallas_call(
        functools.partial(backward_kernel, 2 * g),
        out_shape=jax.ShapeDtypeStruct((n, 3 * width), jnp.bfloat16),
        grid_spec=pltpu.PrefetchScalarGridSpec(
            num_scalar_prefetch=2, grid=(tiles,),
            in_specs=[rows, rows, rows, column, column, whole((n, 128)), stat, stat],
            out_specs=whole((n, 3 * width)),
            scratch_shapes=[
                pltpu.VMEM((tiles, width, TILE), jnp.bfloat16),
                pltpu.VMEM((heads, TILE, 128), jnp.bfloat16),
                pltpu.VMEM((heads, TILE, 128), jnp.bfloat16),
                pltpu.VMEM((heads, 8, TILE), jnp.float32),
                pltpu.VMEM((heads, 64, TILE), jnp.float32),
                pltpu.VMEM((n, width), jnp.float32),
                pltpu.VMEM((n, width), jnp.float32),
            ]),
        compiler_params=pltpu.CompilerParams(dimension_semantics=("arbitrary",), vmem_limit_bytes=VMEM_MAX),
        cost_estimate=pl.CostEstimate(flops=10 * n * n * width, bytes_accessed=14 * n * width, transcendentals=n * n * heads),
        name="attend_backward",
    )(first, last, q, do, o, k, v, kseg, qseg, lse)


BLOCK = 256
STRIP = 64


def normal_cdf_parts(u):
    v = u * 0.7071067811865476
    c = jnp.clip(v, -3.832506856900711, 3.832506856900711)
    c2 = c * c
    top = 0.00022905065861350646
    for a in (0.0034082910107109506, 0.050955695062380861, 0.18520832239976145, 1.128379143519084):
        top = top * c2 + a
    low = -1.1791602954361697e-7
    for b in (0.000023547966471313185, 0.0010179625278914885, 0.014070470171167667, 0.11098505178285362,
              0.49746925110067538, 1.0):
        low = low * c2 + b
    cdf = 0.5 + 0.5 * (c * top / low)
    slope = jnp.exp(-(v * v)) * (u * 0.3989422804014327)
    return u * cdf, cdf + slope


def middle_kernel(pieces, o_all, x0, outs, ups, downs, cot, vec_ref, bup_ref,
                  block_out, dr1, do_all, g_down, g_up, g_out, sums_ref, upsum_ref,
                  o_ref, raw_ref, wo_ref, wu_ref, wd_ref, hat_ref, inv_ref, acc_ref, hl_ref, hlt_ref, gp_ref, z_ref, c_ref,
                  df_ref, dft_ref, y_ref, st_ref, su_ref, ru_ref, rd_ref, go_ref, rgo_ref, u0_ref, u1_ref,
                  sem, osem, send, recv):
    f32, bf16 = jnp.float32, jnp.bfloat16
    rows, width = hat_ref.shape
    blocks = rows // BLOCK
    part = wu_ref.shape[2]
    bf = lambda a: a.astype(bf16)
    dp, tensor = lax.axis_index("dp"), lax.axis_index("tensor")
    inner = tensor % 2
    partner = (dp, tensor + 1 - 2 * inner)
    z, x = dp // 2, dp % 2
    to_x, to_y = (2 * z + 1 - x, tensor), (dp, (tensor + 2) % 4)
    mine = pl.multiple_of(inner * rows, 1024)
    theirs = pl.multiple_of((1 - inner) * rows, 1024)
    greet([partner, to_x, to_y] if pieces else [partner])

    def remote(n, src, dst, device=partner):
        return pltpu.make_async_remote_copy(src, dst, send.at[n], recv.at[n], device_id=device,
                                            device_id_type=pl.DeviceIdType.MESH)

    swap_o = remote(0, o_all.at[pl.ds(theirs, rows), :], o_ref.at[1])
    swap_o.start()
    count = [0]

    def load(src, dst):
        copy = pltpu.make_async_copy(src, dst, sem.at[count[0]])
        count[0] += 1
        copy.start()
        return copy

    def weight(sources, dst):
        if not pieces:
            return [load(sources[0].at[o], dst.at[o]) for o in range(2)]
        digit = dp % 2
        made = []
        for o in range(2):
            for zi in range(sources[0].shape[1]):
                for n in range(2):
                    place = 2 * zi + (digit if n == 0 else 1 - digit)
                    r = sources[n].shape[2]
                    made.append(load(sources[n].at[o, zi], dst.at[o, pl.ds(pl.multiple_of(place * r, r), r), :]))
        return made

    if pieces:
        r = downs[0].shape[0]
        block = lambda o, zi, xi: wd_ref.at[o, pl.ds(pl.multiple_of((2 * zi + xi) * r, r), r), :]
        zs = [(z + 4 - k) % 4 for k in range(4)]
        held = [load(downs[k], block(0, zs[k], x)) for k in range(4)]
        by_x, by_y = [], []
        for k in range(4):
            held[k].wait()
            by_x.append(remote(12 + k, block(0, zs[k], x), block(0, zs[k], x), to_x))
            by_y.append(remote(16 + k, block(0, zs[k], x), block(1, zs[k], x), to_y))
            by_x[k].start()
            by_y[k].start()

    def relay(k):
        if k < 2:
            by_x[k].wait_recv()
            by_y.append(remote(20 + k, block(0, zs[k], 1 - x), block(1, zs[k], 1 - x), to_y))
            by_y[-1].start()
        else:
            by_y[k].wait_recv()
            by_x.append(remote(20 + k, block(1, zs[k], x), block(1, zs[k], x), to_x))
            by_x[-1].start()
    first = [load(o_all.at[pl.ds(mine, rows), :], o_ref.at[0]), load(x0, hat_ref)] + weight(outs, raw_ref.at[0])
    if pieces:
        second = [load(ups[o], wu_ref.at[o]) for o in range(2)]
    else:
        second = [load(ups[0].at[o], wu_ref.at[o]) for o in range(2)]
    if not pieces:
        second = second + weight(downs, wd_ref)
    late = load(cot, c_ref)
    vec = lambda n: vec_ref[n:n + 1, :]
    sums_ref[...] = jnp.zeros_like(sums_ref)
    upsum_ref[...] = jnp.zeros_like(upsum_ref)
    for copy in first:
        copy.wait()
    swaps = [remote(1, raw_ref.at[0], raw_ref.at[1])]
    swaps[0].start()
    for copy in second:
        copy.wait()
    for o in range(2):
        swaps.append(remote(2 + 2 * o, wu_ref.at[o], wu_ref.at[2 + o]))
        swaps.append(remote(3 + 2 * o, wd_ref.at[o], wd_ref.at[2 + o]))
    for copy in (swaps[1], swaps[3]) if pieces else swaps[1:]:
        copy.start()
    lane = lax.broadcasted_iota(jnp.int32, (width, 128), 1)

    def order_heads(side):
        wo_ref[side, :, 0:128] = raw_ref[side, 0, :, 0:128]
        wo_ref[side, :, 128:256] = raw_ref[side, 1, :, 0:128]
        upper = pltpu.roll(raw_ref[side, 1, :, 128:256].astype(f32), 64, 1)
        wo_ref[side, :, 256:384] = bf(jnp.where(lane < 64, raw_ref[side, 0, :, 128:256].astype(f32), upper))
    order_heads(0)
    swaps[0].wait()
    order_heads(1)
    swap_o.wait()

    def strips(body):
        def run(s, carry):
            body(pl.ds(pl.multiple_of(s * STRIP, STRIP), STRIP))
            return carry
        lax.fori_loop(0, rows // STRIP, run, 0)

    def add_sum(n, value):
        sums_ref[n] = sums_ref[n] + jnp.sum(fold(value), axis=0)

    def fold(value):
        return value.reshape(value.shape[0] // 8, 8, value.shape[1])

    def mean(value):
        return jnp.sum(value, axis=-1, keepdims=True) * (1.0 / width)

    def project(b, carry):
        r = pl.ds(pl.multiple_of(b * BLOCK, BLOCK), BLOCK)
        acc_ref[r, :] = mm(o_ref[0, r, :], wo_ref[0], NT) + mm(o_ref[1, r, :], wo_ref[1], NT)
        return carry
    lax.fori_loop(0, blocks, project, 0)
    if pieces:
        relay(0)
        relay(1)

    def first_norm(r):
        r1 = hat_ref[r, :] + (acc_ref[r, :] + vec(0))
        centre = r1 - mean(r1)
        inv = lax.rsqrt(mean(centre * centre) + EPSILON)
        hat = centre * inv
        hat_ref[r, :] = hat
        inv_ref[r, :] = inv
        hl_ref[r, :] = bf(hat * vec(1) + vec(2))
    strips(first_norm)
    if pieces:
        relay(2)
        relay(3)
        for copy in by_x[2:4]:
            copy.wait_recv()
        swaps[2].start()
    for b in range(blocks):
        hlt_ref[:, BLOCK * b:BLOCK * b + BLOCK] = hl_ref[BLOCK * b:BLOCK * b + BLOCK, :].T
    acc_ref[...] = jnp.zeros_like(acc_ref)

    bufs = (u0_ref, u1_ref)

    def forward(n, carry):
        j = n % 2 * 2 + n // 2
        for o in range(2):
            @pl.when(j == 2 + o)
            def _(o=o):
                swaps[1 + 2 * o].wait()
                swaps[2 + 2 * o].wait()
        if pieces:
            @pl.when(j == 1)
            def _():
                for copy in by_y[:2] + by_y[4:] + by_x[4:]:
                    copy.wait_recv()
                for copy in by_x + by_y:
                    copy.wait_send()
                swaps[4].start()

        def lift(b):
            bufs[b % 2][...] = mm(hl_ref[BLOCK * b:BLOCK * b + BLOCK, :], wu_ref[j]) + bup_ref[j, 0:1, :].astype(f32)
        lift(0)
        for b in range(blocks):
            if b + 1 < blocks:
                lift(b + 1)
            r = slice(BLOCK * b, BLOCK * b + BLOCK)
            for i in range(0, BLOCK, 32):
                for w in range(0, part, 256):
                    z, gp = normal_cdf_parts(bufs[b % 2][i:i + 32, w:w + 256])
                    z_ref[j, BLOCK * b + i:BLOCK * b + i + 32, w:w + 256] = bf(z)
                    gp_ref[j, BLOCK * b + i:BLOCK * b + i + 32, w:w + 256] = gp
            acc_ref[r, :] = acc_ref[r, :] + mm(z_ref[j, r, :], wd_ref[j], NT)
        return carry
    lax.fori_loop(0, 4, forward, 0)
    late.wait()

    def second_norm(r):
        h1 = hat_ref[r, :] * vec(1) + vec(2)
        r2 = h1 + (acc_ref[r, :] + vec(3))
        centre = r2 - mean(r2)
        inv = lax.rsqrt(mean(centre * centre) + EPSILON)
        hat = centre * inv
        y_ref[r, :] = bf(hat * vec(4) + vec(5))
        c = c_ref[r, :].astype(f32)
        add_sum(0, c * hat)
        add_sum(1, c)
        w = c * vec(4)
        dr2 = (w - mean(w) - hat * mean(w * hat)) * inv
        acc_ref[r, :] = dr2
        low = bf(dr2)
        df_ref[r, :] = low
        add_sum(2, low.astype(f32))
    strips(second_norm)
    stores = [pltpu.make_async_copy(y_ref, block_out, osem.at[0])]
    stores[0].start()
    for b in range(blocks):
        dft_ref[:, BLOCK * b:BLOCK * b + BLOCK] = df_ref[BLOCK * b:BLOCK * b + BLOCK, :].T

    def backward(n, carry):
        j = 3 - n

        def lower(b):
            bufs[b % 2][...] = mm(df_ref[BLOCK * b:BLOCK * b + BLOCK, :], wd_ref[j])
        slot = n % 2
        away = [remote(6 + slot, st_ref.at[slot], rd_ref.at[slot]), remote(8 + slot, su_ref.at[slot], ru_ref.at[slot])]
        lower(0)
        for b in range(blocks):
            if b + 1 < blocks:
                lower(b + 1)
            r = slice(BLOCK * b, BLOCK * b + BLOCK)
            for i in range(0, BLOCK, 64):
                q = slice(BLOCK * b + i, BLOCK * b + i + 64)
                dul = bf(bufs[b % 2][i:i + 64, :] * gp_ref[j, q, :])
                upsum_ref[j] = upsum_ref[j] + jnp.sum(fold(dul.astype(f32)), axis=0)
                hat2_ref[q, :] = dul
            acc_ref[r, :] = acc_ref[r, :] + mm(hat2_ref[r, :], wu_ref[j], NT)

        @pl.when(n < 2)
        def _():
            for m in range(0, width, BLOCK):
                st_ref[slot, m:m + BLOCK, :] = bf(mm(dft_ref[m:m + BLOCK, :], z_ref[j]))
            away[0].start()
            for m in range(0, width, BLOCK):
                su_ref[slot, m:m + BLOCK, :] = bf(mm(hlt_ref[m:m + BLOCK, :], hat2_ref[...]))
            away[1].start()

        @pl.when(n >= 2)
        def _():
            away[0].wait()
            for m in range(0, width, BLOCK):
                got = rd_ref[slot, m:m + BLOCK, :].astype(f32)
                st_ref[slot, m:m + BLOCK, :] = bf(mm(dft_ref[m:m + BLOCK, :], z_ref[j]) + got)
            if pieces:
                for o in range(2):
                    @pl.when(j == o)
                    def _(o=o):
                        pltpu.make_async_copy(st_ref.at[slot], g_down[o], osem.at[1 + slot]).start()
            else:
                pltpu.make_async_copy(st_ref.at[slot], g_down.at[j], osem.at[1 + slot]).start()
            away[1].wait()
            for m in range(0, width, BLOCK):
                got = ru_ref[slot, m:m + BLOCK, :].astype(f32)
                su_ref[slot, m:m + BLOCK, :] = bf(mm(hlt_ref[m:m + BLOCK, :], hat2_ref[...]) + got)
            if pieces:
                r = g_up[0].shape[2]
                for zi in range(g_up[0].shape[1]):
                    for o in range(2):
                        at = pl.multiple_of((2 * zi + (dp + o) % 2) * r, r)
                        pltpu.make_async_copy(su_ref.at[slot, pl.ds(at, r), :], g_up[o].at[j, zi], osem.at[3 + slot]).start()
            else:
                pltpu.make_async_copy(su_ref.at[slot], g_up.at[j], osem.at[3 + slot]).start()
        return carry
    hat2_ref = y_ref
    stores[0].wait()
    lax.fori_loop(0, 4, backward, 0)

    def first_back(r):
        dh1 = acc_ref[r, :]
        hat = hat_ref[r, :]
        add_sum(3, dh1 * hat)
        add_sum(4, dh1)
        w = dh1 * vec(1)
        grad = (w - mean(w) - hat * mean(w * hat)) * inv_ref[r, :]
        acc_ref[r, :] = grad
        low = bf(grad)
        df_ref[r, :] = low
        add_sum(5, low.astype(f32))
    strips(first_back)
    out = pltpu.make_async_copy(acc_ref, dr1, osem.at[0])
    out.start()
    stores = [out]
    for b in range(blocks):
        dft_ref[:, BLOCK * b:BLOCK * b + BLOCK] = df_ref[BLOCK * b:BLOCK * b + BLOCK, :].T
    lane = lax.broadcasted_iota(jnp.int32, (BLOCK, 128), 1)

    def out_grad(side, m):
        tiles = [mm(dft_ref[m:m + BLOCK, :], o_ref[side, :, 128 * g:128 * g + 128]) for g in range(3)]
        third = [jnp.where(lane < 64, tiles[2], 0.0), jnp.where(lane < 64, pltpu.roll(tiles[2], 64, 1), 0.0)]
        return [jnp.concatenate([tiles[o], third[o]], axis=1) for o in range(2)]
    for m in range(0, width, BLOCK):
        for o, value in enumerate(out_grad(1, m)):
            go_ref[o, m:m + BLOCK, :] = bf(value)
    swap_go = remote(10, go_ref, rgo_ref)
    swap_go.start()
    ow = wo_ref.shape[2]
    for side in (1, 0):
        def push(b, carry):
            r = pl.ds(pl.multiple_of(b * BLOCK, BLOCK), BLOCK)
            y_ref[r, ow * side:ow * side + ow] = bf(mm(df_ref[r, :], wo_ref[side]))
            return carry
        lax.fori_loop(0, blocks, push, 0)
        if side == 1:
            swap_do = remote(11, y_ref.at[:, pl.ds(ow, ow)], do_all.at[pl.ds(mine, rows), :])
            swap_do.start()
        else:
            copy = pltpu.make_async_copy(y_ref.at[:, pl.ds(0, ow)], do_all.at[pl.ds(mine, rows), :], osem.at[5])
            copy.start()
            stores.append(copy)
    swap_go.wait()
    for m in range(0, width, BLOCK):
        for o, value in enumerate(out_grad(0, m)):
            go_ref[o, m:m + BLOCK, :] = bf(value + rgo_ref[o, m:m + BLOCK, :].astype(f32))
    for o in range(2 if pieces else 1):
        copy = pltpu.make_async_copy(go_ref.at[o] if pieces else go_ref, g_out[o] if pieces else g_out, osem.at[6 + o])
        copy.start()
        stores.append(copy)
    whole = g_down[0] if pieces else g_down.at[0]
    for slot in range(2):
        pltpu.make_async_copy(st_ref.at[slot], whole, osem.at[1 + slot]).wait()
        pltpu.make_async_copy(su_ref.at[slot], whole, osem.at[3 + slot]).wait()
    swap_do.wait()
    for copy in stores:
        copy.wait()


def middle(o_all, x0, outs, ups, downs, cot, vec, bup):
    f32, bf16 = jnp.float32, jnp.bfloat16
    rows, width = x0.shape
    ow = o_all.shape[1]
    part = bup.shape[-1]
    pieces = len(ups) == 2
    shape = jax.ShapeDtypeStruct
    hbm = pl.BlockSpec(memory_space=pl.ANY)
    vmem = pl.BlockSpec(memory_space=pltpu.VMEM)
    v = pltpu.VMEM
    n = len(ups)
    m = 2 * n + len(downs)

    def kernel(o_all, x0, *refs):
        weights, rest = refs[:m], refs[m:]
        if pieces:
            rest = rest[:6] + (rest[6:8], rest[8:10], rest[10:12]) + rest[12:]
        middle_kernel(pieces, o_all, x0, weights[:n], weights[n:2 * n], weights[2 * n:], *rest)

    if pieces:
        parts = (2, len(downs), downs[0].shape[0], part)
        grads = [shape((width, part), bf16)] * 2 + [shape(parts, bf16)] * 2 + [shape((width, 256), bf16)] * 2
    else:
        grads = [shape((2, width, part), bf16), shape((2, width, part), bf16), shape((2, width, 256), bf16)]
    return pl.pallas_call(
        kernel,
        out_shape=(shape((rows, width), bf16), shape((rows, width), f32), shape((2 * rows, ow), bf16),
                   *grads, shape((6, 8, width), f32), shape((4, 8, part), f32)),
        in_specs=[hbm] * (3 + m) + [vmem] * 2,
        out_specs=[hbm] * (3 + len(grads)) + [vmem] * 2,
        scratch_shapes=[
            v((2, rows, ow), bf16), v((2, 2, width, 256), bf16), v((2, width, ow), bf16), v((4, width, part), bf16),
            v((4, width, part), bf16),
            v((rows, width), f32), v((rows, 1), f32), v((rows, width), f32), v((rows, width), bf16), v((width, rows), bf16),
            v((4, rows, part), f32), v((4, rows, part), bf16), v((rows, width), bf16), v((rows, width), bf16),
            v((width, rows), bf16), v((rows, width), bf16), v((2, width, part), bf16),
            v((2, width, part), bf16), v((2, width, part), bf16), v((2, width, part), bf16), v((2, width, 256), bf16),
            v((2, width, 256), bf16), v((BLOCK, part), f32), v((BLOCK, part), f32),
            pltpu.SemaphoreType.DMA((40,)), pltpu.SemaphoreType.DMA((8,)),
            pltpu.SemaphoreType.DMA((24,)), pltpu.SemaphoreType.DMA((24,)),
        ],
        compiler_params=pltpu.CompilerParams(vmem_limit_bytes=VMEM_MAX, collective_id=1, has_side_effects=True),
        cost_estimate=pl.CostEstimate(flops=6 * rows * width * 9 * width, bytes_accessed=60_000_000, transcendentals=2 * rows * 4 * part),
        name="middle",
    )(o_all, x0, *outs, *ups, *downs, cot, vec, bup)


class Exchange:
    def __init__(self, send, recv):
        self.send, self.recv, self.used = send, recv, 0

    def copy(self, src, dst, device):
        n = self.used
        self.used += 1
        return pltpu.make_async_remote_copy(src, dst, self.send.at[n], self.recv.at[n], device_id=device,
                                            device_id_type=pl.DeviceIdType.MESH)


def greet(devices):
    barrier = pltpu.get_barrier_semaphore()
    for device in devices:
        pl.semaphore_signal(barrier, inc=1, device_id=device, device_id_type=pl.DeviceIdType.MESH)
    pl.semaphore_wait(barrier, len(devices))


def entry_kernel(tokens, pos_ref, mem_ref, wq_ref, bq_ref, bu_ref, wu_ref, wo_ref,
                 x0_out, x_out, q_out, k_out, v_out, w_out, up_g, out_g, bu_out,
                 x0_ref, x_ref, g_ref, b_ref, y_ref, q_ref, k_ref, v_ref, ub_ref, send, recv, sem):
    f32, bf16 = jnp.float32, jnp.bfloat16
    rows, width = x0_ref.shape
    dp, tensor = lax.axis_index("dp"), lax.axis_index("tensor")
    z, x = dp // 2, dp % 2
    inner = tensor % 2
    zs = [(z + 4 - k) % 4 for k in range(4)]
    at = [2 * zs[k] + x for k in range(4)]
    far = [2 * zs[k] + 1 - x for k in range(4)]
    to_z = [None] + [(2 * ((z + k) % 4) + x, tensor) for k in range(1, 4)]
    to_x = (2 * z + 1 - x, tensor)
    to_y = (dp, (tensor + 2) % 4)
    to_core = (dp, tensor + 1 - 2 * inner)
    to_both = (dp, 3 - tensor)
    greet(to_z[1:] + [to_x, to_y, to_core, to_both])
    ex = Exchange(send, recv)
    started = []

    def go(src, dst, device):
        copy = ex.copy(src, dst, device)
        copy.start()
        started.append(copy)
        return copy

    local = []

    def keep(src, dst):
        copy = pltpu.make_async_copy(src, dst, sem.at[len(local)])
        copy.start()
        local.append(copy)
        return copy

    own = keep(wq_ref, g_ref.at[0, at[0]])
    own_bias = keep(bq_ref, b_ref.at[0])
    z_q = [None] + [go(wq_ref, g_ref.at[0, at[0]], to_z[k]) for k in range(1, 4)]
    x_q = [go(wq_ref, g_ref.at[0, at[0]], to_x)]
    y_q = [go(wq_ref, g_ref.at[1, at[0]], to_y)]
    bias = go(bq_ref, b_ref.at[1], to_y)
    up_bias = [go(bu_ref, ub_ref.at[n - 1], to) for n, to in ((1, to_y), (2, to_core), (3, to_both))]

    mine = pl.multiple_of(inner * rows, 1024)
    positions = pos_ref[0:1, :]
    strip = 128

    def start(s, carry):
        r = pl.multiple_of(s * strip, strip)
        place = lax.broadcasted_iota(jnp.int32, (strip, positions.shape[1]), 0) + (inner * rows + r)
        picks = jnp.where(place == positions, 1.0, 0.0).astype(bf16)
        value = tokens[pl.ds(r, strip), :].astype(f32) + mm(picks, mem_ref[...])
        x0_ref[pl.ds(r, strip), :] = value
        x_ref[pl.ds(mine + r, strip), :] = value.astype(bf16)
        return carry
    lax.fori_loop(0, rows // strip, start, 0)
    keep(x0_ref, x0_out)
    core = go(x_ref.at[pl.ds(mine, rows), :], x_ref.at[pl.ds(mine, rows), :], to_core)

    for k in range(1, 4):
        z_q[k].wait_recv()
        x_q.append(go(g_ref.at[0, at[k]], g_ref.at[0, at[k]], to_x))
        y_q.append(go(g_ref.at[0, at[k]], g_ref.at[1, at[k]], to_y))
    z_u = [None] + [go(wu_ref, up_g.at[at[0]], to_z[k]) for k in range(1, 4)]
    z_o = [None] + [go(wo_ref, out_g.at[0, z], to_z[k]) for k in range(1, 4)]
    keep(wu_ref, up_g.at[at[0]])
    keep(wo_ref, out_g.at[0, z])
    last = []
    for k in range(2):
        x_q[k].wait_recv()
        last.append(go(g_ref.at[0, far[k]], g_ref.at[1, far[k]], to_y))
    for k in range(2, 4):
        y_q[k].wait_recv()
        last.append(go(g_ref.at[1, at[k]], g_ref.at[1, at[k]], to_x))
    rest = [go(wu_ref, up_g.at[at[0]], to_x), go(wo_ref, out_g.at[1, z], to_y)]
    for copy in x_q[2:] + y_q[:2] + last + [bias, core]:
        copy.wait_recv()
    own.wait()
    own_bias.wait()
    keep(g_ref, w_out)
    keep(x_ref, x_out)

    lane = lax.broadcasted_iota(jnp.int32, (BLOCK, 128), 1)
    y_ref[...] = jnp.zeros_like(y_ref)

    def project(b, carry):
        r = pl.ds(pl.multiple_of(b * BLOCK, BLOCK), BLOCK)
        for o in range(2):
            y_ref[o, :, 0:576] = mm(x_ref[r, :], g_ref[o].reshape(width, 576)) + b_ref[o, 0:1, 0:576].astype(f32)
        tile = lambda o, n: y_ref[o, :, 128 * n:128 * n + 128]
        turn = lambda value: pltpu.roll(value, 64, 1)
        third = (jnp.where(lane < 64, tile(0, 3), turn(tile(1, 3))), jnp.where(lane < 64, turn(tile(0, 3)), tile(1, 3)),
                 jnp.where(lane < 64, tile(0, 4), turn(tile(1, 4))))
        for n, ref in enumerate((q_ref, k_ref, v_ref)):
            for g, value in enumerate((tile(0, n), tile(1, n), third[n])):
                value = value.astype(bf16)
                if n == 0:
                    value = value * jnp.asarray(0.125, bf16)
                ref[r, 128 * g:128 * g + 128] = value
        return carry
    blocks = 2 * rows // BLOCK
    for k in range(1, 4):
        lax.fori_loop(blocks * (k - 1) // 4, blocks * k // 4, project, 0)
        z_u[k].wait_recv()
        rest.append(go(up_g.at[at[k]], up_g.at[at[k]], to_x))
    lax.fori_loop(blocks * 3 // 4, blocks, project, 0)
    for src, dst in ((q_ref, q_out), (k_ref, k_out), (v_ref, v_out)):
        keep(src, dst)
    for k in range(1, 4):
        z_o[k].wait_recv()
        rest.append(go(out_g.at[0, zs[k]], out_g.at[1, zs[k]], to_y))
    for copy in rest + up_bias:
        copy.wait_recv()
    bu_out[0] = bu_ref[...]
    for n in range(3):
        bu_out[n + 1] = ub_ref[n]
    for copy in started:
        copy.wait_send()
    for copy in local[2:]:
        copy.wait()


def entry(tokens, positions, memory_rows, shard_qkv, biases, up_bias, up, out):
    f32, bf16 = jnp.float32, jnp.bfloat16
    rows, width = tokens.shape
    r = up.shape[0]
    shape, v = jax.ShapeDtypeStruct, pltpu.VMEM
    hbm, vmem = pl.BlockSpec(memory_space=pl.ANY), pl.BlockSpec(memory_space=pltpu.VMEM)
    qkv = shape((2 * rows, 384), bf16)
    return pl.pallas_call(
        entry_kernel,
        out_shape=(shape((rows, width), f32), shape((2 * rows, width), bf16), qkv, qkv, qkv,
                   shape((2, 8, r, 576), bf16), shape((8, r, up.shape[1]), bf16),
                   shape((2, 4, r, out.shape[1]), bf16), shape((4, 16, up.shape[1]), bf16)),
        in_specs=[vmem] * 8,
        out_specs=[hbm] * 8 + [vmem],
        scratch_shapes=[
            v((rows, width), f32), v((2 * rows, width), bf16), v((2, 8, r, 576), bf16), v((2, 16, 640), bf16),
            v((2, BLOCK, 640), f32), v((2 * rows, 384), bf16), v((2 * rows, 384), bf16), v((2 * rows, 384), bf16),
            v((3, 16, up.shape[1]), bf16),
            pltpu.SemaphoreType.DMA((48,)), pltpu.SemaphoreType.DMA((48,)), pltpu.SemaphoreType.DMA((16,)),
        ],
        compiler_params=pltpu.CompilerParams(vmem_limit_bytes=VMEM_MAX, collective_id=0, has_side_effects=True),
        cost_estimate=pl.CostEstimate(flops=4 * rows * width * 1152, bytes_accessed=20_000_000, transcendentals=0),
        name="entry",
    )(tokens, positions, memory_rows, shard_qkv, biases, up_bias, up, out)


def exit_kernel(x_all, d0, d1, d2, w_all, third, kept_ref, came_ref, dr1, pos_ref, sums_in, up_in,
                tok_out, first_out, second_out, small_out,
                x_ref, xt_ref, d_ref, w_ref, dr_ref, g_ref, own_ref, oth_ref, yb_ref, xs_ref, xb_ref, zt_ref, zs_ref, zb_ref,
                fs_ref, fb_ref, their_ref, got_ref, tok_ref, s_ref, t_ref, r_ref, first_ref, send, recv, sem):
    f32, bf16 = jnp.float32, jnp.bfloat16
    rows, width = dr_ref.shape
    dp, tensor = lax.axis_index("dp"), lax.axis_index("tensor")
    z, x = dp // 2, dp % 2
    inner, outer = tensor % 2, tensor // 2
    up_z = [None] + [(z + k) % 4 for k in range(1, 4)]
    to_z = [None] + [(2 * up_z[k] + x, tensor) for k in range(1, 4)]
    to_x = (2 * z + 1 - x, tensor)
    to_y = (dp, (tensor + 2) % 4)
    to_core = (dp, tensor + 1 - 2 * inner)
    near_z = (2 * (z + 1 - 2 * (z % 2)) + x, tensor)
    far_z = to_z[2]
    loads = []
    for src, dst in ((d2, d_ref.at[2]), (x_all, x_ref), (d0, d_ref.at[0]), (d1, d_ref.at[1]),
                     (w_all.at[0, :, pl.ds(0, 384)], w_ref.at[0]), (w_all.at[1, :, pl.ds(0, 384)], w_ref.at[1]),
                     (third, w_ref.at[2]), (dr1, dr_ref)):
        copy = pltpu.make_async_copy(src, dst, sem.at[len(loads)])
        copy.start()
        loads.append(copy)
    greet(to_z[1:] + [to_x, to_y, to_core])
    ex = Exchange(send, recv)
    started = []

    def go(src, dst, device):
        copy = ex.copy(src, dst, device)
        copy.start()
        started.append(copy)
        return copy

    for k in range(4):
        first_ref[k] = kept_ref[k] + came_ref[k].astype(f32)
    for k in range(1, 4):
        fs_ref[k - 1] = first_ref[up_z[k]].astype(bf16)
    z_first = [go(fs_ref.at[k - 1], fb_ref.at[k - 1], to_z[k]) for k in range(1, 4)]

    loads[0].wait()
    loads[1].wait()
    for b in range(2 * rows // BLOCK):
        xt_ref[:, BLOCK * b:BLOCK * b + BLOCK] = x_ref[BLOCK * b:BLOCK * b + BLOCK, :].T
    for m in range(0, width, BLOCK):
        g_ref[m:m + BLOCK, :] = mm(xt_ref[m:m + BLOCK, :], d_ref[2])
    half = own_ref.shape[3]
    lane = lax.broadcasted_iota(jnp.int32, (half, 128), 1)
    for p in range(8):
        for n in range(3):
            low = g_ref[2 * half * p:2 * half * p + half, 128 * n:128 * n + 128]
            high = g_ref[2 * half * p + half:2 * half * (p + 1), 128 * n:128 * n + 128]
            own_ref[p % 2, p // 2, n] = jnp.where(lane < 64, low, pltpu.roll(high, 64, 1))
            oth_ref[p % 2, p // 2, n] = jnp.where(lane < 64, pltpu.roll(low, 64, 1), high).astype(bf16)
    y_far = go(oth_ref.at[1 - x], yb_ref.at[0], to_y)
    y_near = go(oth_ref.at[x], yb_ref.at[1], to_y)

    for copy in loads[2:]:
        copy.wait()
    place = lax.broadcasted_iota(jnp.int32, (32, 2 * rows), 1)
    which = lax.broadcasted_iota(jnp.int32, (32, 2 * rows), 0)
    picks = jnp.where((place == pos_ref[:, 0:1]) | (which == 24), 1.0, 0.0).astype(bf16)
    picked = [mm(picks, d_ref[n]) for n in range(3)]
    own_place = lax.broadcasted_iota(jnp.int32, (32, rows), 1) + inner * rows
    own_picks = jnp.where(own_place == pos_ref[:, 0:1], 1.0, 0.0)
    memory = lax.dot_general(own_picks, dr_ref[...], NN, precision=lax.Precision.HIGHEST, preferred_element_type=f32)
    for n in range(3):
        memory = memory + mm(picked[n].astype(bf16), w_ref[n], NT)
    hw = s_ref.shape[2]

    def put(row, value):
        for h in range(2):
            s_ref[h, row:row + 1, :] = value[:, hw * h:hw * h + hw]
    for h in range(2):
        s_ref[h, 0:24, :] = memory[0:24, hw * h:hw * h + hw]
        s_ref[h, 38:40, :] = jnp.zeros((2, hw), f32)
    for n in range(6):
        put(24 + n, jnp.sum(sums_in[n], axis=0, keepdims=True))
    ups = [jnp.sum(up_in[n], axis=0, keepdims=True) for n in (0, 2, 1, 3)]
    total = [value[24:25, :] for value in picked]
    turned = jnp.concatenate([pltpu.roll(picked[2][24:32, 128 * n:128 * n + 128], 64, 1) for n in range(3)], axis=1)[0:1, :]
    for t in range(4):
        n = (t % 2 + inner) % 2 + 2 * ((t // 2 + outer) % 2)
        value = jnp.zeros_like(ups[0])
        for other in range(4):
            value = value + jnp.where(n == other, ups[other], 0.0)
        put(30 + t, value)
        s_ref[0, 34 + t:35 + t, :] = jnp.where(n == 0, total[0], 0.0) + jnp.where(n == 2, total[1], 0.0)
        s_ref[1, 34 + t:35 + t, :] = jnp.where(n == 0, total[2], 0.0) + jnp.where(n == 2, turned, 0.0)
    small = [go(s_ref.at[1 - inner], r_ref.at[0], to_core)]
    hops = [to_y, to_x, near_z, far_z]

    def hop(n):
        small[n].wait_recv()
        t_ref[n] = (s_ref[inner] if n == 0 else t_ref[n - 1]) + r_ref[n]
        if n < 4:
            small.append(go(t_ref.at[n], r_ref.at[n + 1], hops[n]))
        else:
            small.append(go(t_ref.at[n], r_ref.at[5], to_core))
            small_out[inner] = t_ref[n]

    mine = pl.multiple_of(inner * rows, 1024)
    theirs = pl.multiple_of((1 - inner) * rows, 1024)

    def block(start):
        r = pl.ds(pl.multiple_of(start, BLOCK), BLOCK)
        return mm(d_ref[0, r, :], w_ref[0], NT) + mm(d_ref[1, r, :], w_ref[1], NT) + mm(d_ref[2, r, :], w_ref[2], NT)

    def away(b, carry):
        their_ref[pl.ds(pl.multiple_of(b * BLOCK, BLOCK), BLOCK), :] = block(theirs + b * BLOCK).astype(bf16)
        return carry
    lax.fori_loop(0, rows // BLOCK, away, 0)
    tokens = go(their_ref, got_ref, to_core)
    hop(0)
    y_far.wait_recv()
    for k in range(4):
        xs_ref[k] = (own_ref[1 - x, k] + yb_ref[0, k].astype(f32)).astype(bf16)
    x_sum = go(xs_ref, xb_ref, to_x)

    def stay(b, carry):
        tok_ref[pl.ds(pl.multiple_of(b * BLOCK, BLOCK), BLOCK), :] = block(mine + b * BLOCK)
        return carry
    lax.fori_loop(0, rows // BLOCK, stay, 0)
    hop(1)
    y_near.wait_recv()
    x_sum.wait_recv()
    for k in range(4):
        zt_ref[k] = own_ref[x, k] + yb_ref[1, k].astype(f32) + xb_ref[k].astype(f32)
    for k in range(1, 4):
        zs_ref[k - 1] = zt_ref[up_z[k]].astype(bf16)
    z_second = [go(zs_ref.at[k - 1], zb_ref.at[k - 1], to_z[k]) for k in range(1, 4)]
    hop(2)
    tokens.wait_recv()

    def finish(s, carry):
        r = pl.ds(pl.multiple_of(s * STRIP, STRIP), STRIP)
        tok_ref[r, :] = tok_ref[r, :] + got_ref[r, :].astype(f32) + dr_ref[r, :]
        return carry
    lax.fori_loop(0, rows // STRIP, finish, 0)
    out = pltpu.make_async_copy(tok_ref, tok_out, sem.at[8])
    out.start()
    hop(3)
    for copy in z_first:
        copy.wait_recv()
    first_out[...] = first_ref[z] + fb_ref[0].astype(f32) + fb_ref[1].astype(f32) + fb_ref[2].astype(f32)
    for copy in z_second:
        copy.wait_recv()
    second_out[...] = zt_ref[z] + zb_ref[0].astype(f32) + zb_ref[1].astype(f32) + zb_ref[2].astype(f32)
    hop(4)
    small[5].wait_recv()
    small_out[1 - inner] = r_ref[5]
    for copy in started:
        copy.wait_send()
    out.wait()


def leave(x_all, d, w_qkv, third, first, came, dr1, place, sums, up_sums):
    f32, bf16 = jnp.float32, jnp.bfloat16
    rows, width = dr1.shape
    r, half = first.shape[1], first.shape[1] // 2
    shape, v = jax.ShapeDtypeStruct, pltpu.VMEM
    hbm, vmem = pl.BlockSpec(memory_space=pl.ANY), pl.BlockSpec(memory_space=pltpu.VMEM)
    return pl.pallas_call(
        exit_kernel,
        out_shape=(shape((rows, width), f32), shape((r, 384), f32), shape((3, half, 128), f32), shape((2, 40, width // 2), f32)),
        in_specs=[hbm] * 6 + [vmem] * 2 + [hbm] + [vmem] * 3,
        out_specs=[hbm] + [vmem] * 3,
        scratch_shapes=[
            v((2 * rows, width), bf16), v((width, 2 * rows), bf16), v((3, 2 * rows, 384), bf16), v((3, width, 384), bf16),
            v((rows, width), f32), v((width, 384), f32), v((2, 4, 3, half, 128), f32), v((2, 4, 3, half, 128), bf16),
            v((2, 4, 3, half, 128), bf16), v((4, 3, half, 128), bf16), v((4, 3, half, 128), bf16), v((4, 3, half, 128), f32),
            v((3, 3, half, 128), bf16), v((3, 3, half, 128), bf16), v((3, r, 384), bf16), v((3, r, 384), bf16),
            v((rows, width), bf16), v((rows, width), bf16), v((rows, width), f32), v((2, 40, width // 2), f32),
            v((5, 40, width // 2), f32), v((6, 40, width // 2), f32), v((4, r, 384), f32),
            pltpu.SemaphoreType.DMA((16,)), pltpu.SemaphoreType.DMA((16,)), pltpu.SemaphoreType.DMA((9,)),
        ],
        compiler_params=pltpu.CompilerParams(vmem_limit_bytes=VMEM_MAX, collective_id=2, has_side_effects=True),
        cost_estimate=pl.CostEstimate(flops=2 * rows * width * 384 * 8, bytes_accessed=20_000_000, transcendentals=0),
        name="leave",
    )(x_all, *d, w_qkv, third, first, came, dr1, place, sums, up_sums)


def layer_norm(values, norm_gain, norm_shift):
    centre = values - jnp.mean(values, axis=-1, keepdims=True)
    spread = jnp.mean(centre * centre, axis=-1, keepdims=True)
    return centre * lax.rsqrt(spread + EPSILON) * norm_gain + norm_shift


def gelu_exact(values):
    return jax.nn.gelu(values, approximate=False)


AXES = ("dp", "tensor")


class Grid:
    def __init__(self, dp, tensor):
        self.dp, self.tensor = dp, tensor
        factors, rest = [2], dp // 2
        while rest > 8:
            factors.insert(0, 4)
            rest //= 4
        if rest > 1:
            factors.insert(0, rest)
        self.factors = factors

    def digit(self, j):
        stride = 1
        for f in self.factors[j + 1:]:
            stride *= f
        return stride, self.factors[j]

    def my_digit(self, j):
        stride, f = self.digit(j)
        return lax.axis_index("dp") // stride % f

    def turn(self, value, j, k):
        stride, f = self.digit(j)
        pairs = []
        for d in range(self.dp):
            g = d // stride % f
            to = d + ((g + k) % f - g) * stride
            for t in range(self.tensor):
                pairs.append((d * self.tensor + t, to * self.tensor + t))
        return lax.ppermute(value, AXES, pairs)

    def swap_dp(self, value, bit):
        pairs = [(d * self.tensor + t, (d ^ bit) * self.tensor + t) for d in range(self.dp) for t in range(self.tensor)]
        return lax.ppermute(value, AXES, pairs)

    def swap(self, value, bit):
        pairs = [(d * self.tensor + t, d * self.tensor + (t ^ bit)) for d in range(self.dp) for t in range(self.tensor)]
        return lax.ppermute(value, AXES, pairs)

    def gather_stage(self, value, j, axis):
        _, f = self.digit(j)
        g = self.my_digit(j)
        got = [value] + [self.turn(value, j, k) for k in range(1, f)]
        if f == 2:
            lower = jnp.where(g == 0, got[0], got[1])
            upper = jnp.where(g == 0, got[1], got[0])
            return jnp.stack([lower, upper], axis=axis)
        ring = got[::-1]
        return lax.dynamic_slice_in_dim(jnp.stack(ring + ring[:-1], axis=axis), f - 1 - g, f, axis)

    def gather(self, shard, outer_first=False):
        count = len(self.factors)
        value = shard
        for j in range(count - 1):
            value = self.gather_stage(value, j, j)
        if outer_first:
            value = jnp.stack([value, self.swap(value, 2)])
            value = self.gather_stage(value, count - 1, count)
            return value.reshape(2, -1, shard.shape[-1])
        value = self.gather_stage(value, count - 1, count - 1)
        value = value.reshape(-1, shard.shape[-1])
        return jnp.stack([value, self.swap(value, 2)])

    def reduce_stage(self, value, j, axis):
        _, f = self.digit(j)
        g = self.my_digit(j)
        total = lax.dynamic_index_in_dim(value, g, axis, keepdims=False).astype(jnp.float32)
        for k in range(1, f):
            part = lax.dynamic_index_in_dim(value, (g + k) % f, axis, keepdims=False)
            total = total + self.turn(part.astype(jnp.bfloat16), j, k).astype(jnp.float32)
        return total

    def reduce(self, parts, outer_first=True):
        count = len(self.factors)
        columns = parts.shape[-1]
        value = parts
        if outer_first:
            value = value[0].astype(jnp.float32) + self.swap(value[1].astype(jnp.bfloat16), 2).astype(jnp.float32)
            value = value.reshape(*self.factors, -1, columns)
            value = self.reduce_stage(value, count - 1, count - 1)
        else:
            value = value.reshape(2, *self.factors, -1, columns)
            value = self.reduce_stage(value, count - 1, count)
            value = value[0] + self.swap(value[1].astype(jnp.bfloat16), 2).astype(jnp.float32)
        for j in reversed(range(count - 1)):
            value = self.reduce_stage(value, j, j)
        return value

    @property
    def stages(self):
        return len(self.factors) + 1

    def open(self, parts, outer_first):
        columns = parts.shape[-1]
        return parts if outer_first else parts.reshape(2, *self.factors, -1, columns)

    def stage(self, value, outer_first, n):
        count = len(self.factors)
        if n == (0 if outer_first else 1):
            value = value[0].astype(jnp.float32) + self.swap(value[1].astype(jnp.bfloat16), 2).astype(jnp.float32)
            return value.reshape(*self.factors, -1, value.shape[-1]) if outer_first else value
        if n == 0:
            return self.reduce_stage(value, count - 1, count)
        return self.reduce_stage(value, count - n, count - n)

    def total(self, vector):
        for bit in (1, 2):
            vector = vector + self.swap(vector, bit)
        bit = 1
        while bit < self.dp:
            vector = vector + self.swap_dp(vector, bit)
            bit *= 2
        return vector


def shards(grid, tokens, segment_ids, memory_positions, memory_rows, qkv_weight, qv_bias, out_weight, out_bias,
           norm1_gain, norm1_bias, up_weight, up_bias, down_weight, down_bias, norm2_gain, norm2_bias, out_cotangent):
    f32, bf16 = jnp.float32, jnp.bfloat16
    rows, width = tokens.shape
    group_len = segment_ids.shape[1]
    tensor = lax.axis_index("tensor")
    inner, outer = tensor % 2, tensor // 2
    slice_rows = qkv_weight.shape[0]
    heads = qkv_weight.shape[1]
    hd = 64
    hw = heads * hd
    units = up_weight.shape[1]

    segments = lax.dynamic_index_in_dim(segment_ids, outer, 0, keepdims=False)
    positions = lax.dynamic_index_in_dim(memory_positions, outer, 0, keepdims=False)
    row_place = inner * rows + jnp.arange(rows, dtype=jnp.int32)
    picks = (row_place[:, None] == positions[None, :])
    joined = lambda w: w.transpose(1, 0, 2).reshape(width, -1)

    parts = qkv_weight.reshape(slice_rows, heads, 3, hd)
    order_columns = lambda p: jnp.concatenate([p[..., :2, n, :].reshape(*p.shape[:-3], 2 * hd) for n in range(3)]
                                              + [p[..., 2, n, :] for n in range(3)], axis=-1)
    shard_qkv = order_columns(parts)
    shard_out = jnp.pad(out_weight.reshape(slice_rows, hw), ((0, 0), (0, 256 - hw)))
    bias_parts = qv_bias.reshape(heads, 2, hd)
    bias_qkv = order_columns(jnp.stack([bias_parts[:, 0], jnp.zeros_like(bias_parts[:, 0]), bias_parts[:, 1]], 1))
    bias_qkv = jnp.pad(bias_qkv[None], ((0, 15), (0, 64)))
    own_up_bias = jnp.broadcast_to(up_bias[None], (16, units))
    fused = grid.dp == 8 and grid.tensor == 4
    if fused:
        memory = memory_positions.shape[1]
        place = jnp.pad(positions[None], ((0, 7), (0, 32 - memory)), constant_values=-1)
        table = jnp.pad(memory_rows, ((0, 32 - memory), (0, 0)))
        x0, x_all, q, k, v, w_qkv, up_g, out_g, b_up = entry(tokens, place, table, shard_qkv, bias_qkv, own_up_bias, up_weight, shard_out)
        column = jnp.pad(jnp.broadcast_to(positions[:, None], (memory, 128)), ((0, 32 - memory), (0, 0)), constant_values=-1)
        w_qkv = w_qkv.reshape(2, width, 9 * hd)
        third = jnp.concatenate([w_qkv[o][:, (6 + n) * hd:(7 + n) * hd] for n in range(3) for o in range(2)], 1)
        up_all = up_g.reshape(width, units)
        ups = (up_all, grid.swap(up_all, 2))
        own_down, q = lax.optimization_barrier((down_weight, q))
        downs = (own_down, *[grid.turn(own_down, 0, k) for k in range(1, 4)])
        outs = (out_g, grid.turn(out_g, 1, 1))
    else:
        x0 = tokens.astype(f32) + jnp.dot(picks.astype(bf16), memory_rows, preferred_element_type=f32)
        xl = x0.astype(bf16)
        w_qkv = grid.gather(shard_qkv)
        other = grid.swap(xl, 1)
        x_all = jnp.concatenate([jnp.where(inner == 0, xl, other), jnp.where(inner == 0, other, xl)])
        b_two = jnp.stack([bias_qkv[0], grid.swap(bias_qkv[0], 2)]).astype(f32)
        y = [(mm(x_all, w_qkv[o]) + b_two[o, :9 * hd]).astype(bf16) for o in range(2)]
        third = lambda n: [one[:, (6 + n) * hd:(7 + n) * hd] for one in y]
        q, k, v = [jnp.concatenate([y[0][:, 2 * n * hd:2 * (n + 1) * hd], y[1][:, 2 * n * hd:2 * (n + 1) * hd]] + third(n), 1)
                   for n in range(3)]
        q = q * jnp.asarray(0.125, bf16)
        b_up = jnp.stack([own_up_bias, grid.swap(own_up_bias, 2)])
        b_up = jnp.concatenate([b_up, grid.swap(b_up, 1)])
        outs, ups, downs = (grid.gather(shard_out, True),), (grid.gather(up_weight),), (grid.gather(down_weight, True),)
    mixed, lse = attend_forward(q, k, v, segments)
    vec = jnp.stack([out_bias, norm1_gain, norm1_bias, down_bias, norm2_gain, norm2_bias, norm2_bias, norm2_bias]).astype(f32)
    (block_out, dr1, do_all, *grads, sums, up_sums) = middle(
        mixed, x0, outs, ups, downs, out_cotangent, vec, b_up)
    if fused:
        return finish_small(grid, tensor, x_all, q, k, v, do_all, mixed, lse, segments, w_qkv, third, dr1, column, sums, up_sums, block_out,
                            grads, hw)
    g_down, g_up, g_out = grads

    TN = (((0,), (0,)), ((), ()))
    tie = lax.optimization_barrier
    kinds = (True, False, True)
    state = [grid.open(parts, kind) for parts, kind in zip((g_down, g_up, g_out), kinds)]
    step = lambda n, state: [grid.stage(value, kind, n) for value, kind in zip(state, kinds)]
    late = [(1, 0, 2)[n] for n in range(3)]
    d = [None] * 3
    state, d[1] = step(0, state), attend_backward(1, q, k, v, do_all, mixed, lse, segments)
    state, d[1], q = tie((state, d[1], q))
    g_one = mm(x_all, d[1], TN).astype(bf16)
    state, d[0] = step(1, state), attend_backward(0, q, k, v, do_all, mixed, lse, segments)
    state, d[0], q, g_one = tie((state, d[0], q, g_one))
    g_zero = mm(x_all, d[0], TN)
    first = g_zero + grid.swap(g_one, 2).astype(f32)
    state, d[2] = step(2, state), attend_backward(2, q, k, v, do_all, mixed, lse, segments)
    state, d[2], first = tie((state, d[2], first))
    for n in range(3, grid.stages):
        state = step(n, state)
    grad_down, grad_up, grad_out = state
    grad_out = grad_out[:, :hw]

    g_two = mm(x_all, d[2], TN)
    side = lambda m, o: jnp.concatenate([m[:, (2 * n + o) * hd:(2 * n + o + 1) * hd] for n in range(3)], 1)
    second = side(g_two, 0) + grid.swap(side(g_two, 1).astype(bf16), 2).astype(f32)
    both = jnp.concatenate([first, second], 1).reshape(*grid.factors, slice_rows, 9 * hd)
    for j in reversed(range(len(grid.factors))):
        both = grid.reduce_stage(both, j, j)
    restore = lambda p: jnp.stack([jnp.concatenate([p[..., 2 * n * hd:2 * (n + 1) * hd].reshape(*p.shape[:-1], 2, hd),
                                                    p[..., None, (6 + n) * hd:(7 + n) * hd]], -2) for n in range(3)], -2)
    grad_qkv = restore(both).reshape(slice_rows, heads, 3 * hd)
    third = jnp.concatenate([w_qkv[o][:, (6 + n) * hd:(7 + n) * hd] for n in range(3) for o in range(2)], 1)
    part = (mm(d[0], w_qkv[0][:, :6 * hd], NT) + mm(d[1], w_qkv[1][:, :6 * hd], NT) + mm(d[2], third, NT)).reshape(2, rows, width)
    mine = lax.dynamic_index_in_dim(part, inner, 0, keepdims=False)
    theirs = lax.dynamic_index_in_dim(part, 1 - inner, 0, keepdims=False).astype(bf16)
    grad_tokens = mine + grid.swap(theirs, 1).astype(f32) + dr1
    d_sum = [jnp.sum(one.astype(f32), axis=0) for one in d]
    d_bias = [jnp.concatenate([d_sum[o]] + [d_sum[2][(2 * n + o) * hd:(2 * n + o + 1) * hd] for n in range(3)]) for o in range(2)]
    dg2, ds2, d_down_bias, dg1, ds1, d_out_bias = jnp.sum(sums, axis=1)
    d_up_bias = jnp.sum(up_sums, axis=1).reshape(2, 2 * units)
    grad_memory = jnp.dot(picks.astype(f32).T, grad_tokens, precision=lax.Precision.HIGHEST)

    order = jnp.arange(4, dtype=jnp.int32) ^ tensor
    up_parts = d_up_bias.reshape(2, 2, units)
    up_parts = jnp.stack([up_parts[0, 0], up_parts[1, 0], up_parts[0, 1], up_parts[1, 1]])[order]
    take = lambda o: restore(d_bias[o])[:, 0::2].reshape(-1)
    blank = jnp.zeros((2 * hw,), f32)
    qv_parts = jnp.stack([take(0), blank, take(1), blank])[order]
    pieces = [grad_memory.reshape(-1), d_out_bias, dg1, ds1, d_down_bias, dg2, ds2, up_parts.reshape(-1), qv_parts.reshape(-1)]
    summed = grid.total(jnp.concatenate(pieces))
    outs, at = [], 0
    for piece in pieces:
        outs.append(lax.slice_in_dim(summed, at, at + piece.size))
        at += piece.size
    t_memory, t_out_bias, t_g1, t_s1, t_down_bias, t_g2, t_s2, t_up, t_qv = outs
    grad_up_bias = lax.dynamic_index_in_dim(t_up.reshape(4, units), tensor, 0, keepdims=False)
    grad_qv = lax.dynamic_index_in_dim(t_qv.reshape(4, heads, 2 * hd), tensor, 0, keepdims=False)
    return (block_out, grad_tokens, t_memory.reshape(-1, width), grad_qkv, grad_qv,
            grad_out.reshape(slice_rows, heads, hd), t_out_bias, t_g1, t_s1, grad_up, grad_up_bias, grad_down,
            t_down_bias, t_g2, t_s2)


def blend_one_kernel(x_ref, down, down_in, up, up_in, out, out_in, kept_down, kept_up, kept_out, send_x, send_y):
    f32, bf16 = jnp.float32, jnp.bfloat16
    x = x_ref[0]
    width = down.shape[-1]
    add = lambda a, b: a.astype(f32) + b.astype(f32)
    kept_down[0] = add(down[0, x], down_in[0, x])
    kept_out[0] = add(out[0, x], out_in[0, x])
    send_x[0, :, 0:width] = add(down[0, 1 - x], down_in[0, 1 - x]).astype(bf16)
    send_x[0, :, width:] = add(out[0, 1 - x], out_in[0, 1 - x]).astype(bf16)
    kept_up[0] = add(up[0, 0], up_in[0, 0])
    send_y[0] = add(up[1, 0], up_in[1, 0]).astype(bf16)


def blend_one(x, down, down_in, up, up_in, out, out_in):
    f32, bf16 = jnp.float32, jnp.bfloat16
    _, zs, r, width = up.shape
    ow = out.shape[-1]
    shape = jax.ShapeDtypeStruct
    by_x = lambda columns: pl.BlockSpec((1, 2, r, columns), lambda j, *_: (j, 0, 0, 0))
    by_y = pl.BlockSpec((2, 1, r, width), lambda j, *_: (0, j, 0, 0))
    one = lambda columns: pl.BlockSpec((1, r, columns), lambda j, *_: (j, 0, 0))
    fold = lambda a: a.reshape(zs, 2, r, a.shape[-1])
    return pl.pallas_call(
        blend_one_kernel,
        out_shape=(shape((zs, r, width), f32), shape((zs, r, width), f32), shape((zs, r, ow), f32),
                   shape((zs, r, width + ow), bf16), shape((zs, r, width), bf16)),
        grid_spec=pltpu.PrefetchScalarGridSpec(
            num_scalar_prefetch=1, grid=(zs,),
            in_specs=[by_x(width), by_x(width), by_y, by_y, by_x(ow), by_x(ow)],
            out_specs=[one(width), one(width), one(ow), one(width + ow), one(width)]),
        compiler_params=pltpu.CompilerParams(dimension_semantics=("arbitrary",), vmem_limit_bytes=VMEM_MAX),
        cost_estimate=pl.CostEstimate(flops=8 * zs * r * width, bytes_accessed=10_000_000, transcendentals=0),
        name="blend_one",
    )(x.reshape(1), fold(down), fold(down_in), up, up_in, fold(out), fold(out_in))


def blend_two_kernel(at_ref, kept_down, kept_up, kept_out, came_x, came_y, first, kept_z, kept_first, *sends):
    f32, bf16 = jnp.float32, jnp.bfloat16
    x, z = at_ref[0], at_ref[1]
    zs, r, width = kept_down.shape
    for k in range(zs):
        n = (z + k) % zs
        parts = (kept_down[n] + came_x[n, :, 0:width].astype(f32), kept_up[n] + came_y[n].astype(f32),
                 kept_out[n] + came_x[n, :, width:].astype(f32))
        start = 0
        for part in parts:
            stop = start + part.shape[1]
            if k == 0:
                kept_z[:, start:stop] = part
            else:
                sends[k - 1][:, start:stop] = part.astype(bf16)
            start = stop
        kept_first[k] = first[k, x]
        sends[zs - 1][k] = first[k, 1 - x].astype(bf16)


def blend_two(x, z, kept_down, kept_up, kept_out, came_x, came_y, first):
    f32, bf16 = jnp.float32, jnp.bfloat16
    zs, r, width = kept_down.shape
    columns = 2 * width + kept_out.shape[-1]
    shape = jax.ShapeDtypeStruct
    vmem = pl.BlockSpec(memory_space=pltpu.VMEM)
    return pl.pallas_call(
        blend_two_kernel,
        out_shape=(shape((r, columns), f32), shape((zs, r, first.shape[-1]), f32), *[shape((r, columns), bf16)] * (zs - 1),
                   shape((zs, r, first.shape[-1]), bf16)),
        in_specs=[pl.BlockSpec(memory_space=pltpu.SMEM)] + [vmem] * 6,
        out_specs=[vmem] * (zs + 2),
        compiler_params=pltpu.CompilerParams(vmem_limit_bytes=VMEM_MAX),
        cost_estimate=pl.CostEstimate(flops=4 * zs * r * columns, bytes_accessed=10_000_000, transcendentals=0),
        name="blend_two",
    )(jnp.stack([x, z]), kept_down, kept_up, kept_out, came_x, came_y, first.reshape(zs, 2, r, first.shape[-1]))


def spread_kernel(t_ref, kept, came_one, came_two, came_three, small, down, up, out, memory, vec, up_bias, qv):
    f32 = jnp.float32
    width = down.shape[1]
    for ref, start in ((down, 0), (up, width), (out, 2 * width)):
        cols = slice(start, start + ref.shape[1])
        ref[...] = (kept[:, cols] + came_one[:, cols].astype(f32)) + (came_two[:, cols].astype(f32) + came_three[:, cols].astype(f32))
    half = width // 2
    t = t_ref[0]
    for h in range(2):
        cols = slice(half * h, half * h + half)
        memory[:, cols] = small[h, 0:memory.shape[0], :]
        vec[:, cols] = small[h, 24:32, :]
        up_bias[:, cols] = small[h, pl.ds(30 + t, 1), :]
        qv[h:h + 1, :] = small[h, pl.ds(34 + t, 1), :]


def spread(tensor, kept, came, small, memory, ow):
    f32 = jnp.float32
    r, columns = kept.shape
    width = 2 * small.shape[2]
    shape = jax.ShapeDtypeStruct
    vmem = pl.BlockSpec(memory_space=pltpu.VMEM)
    return pl.pallas_call(
        spread_kernel,
        out_shape=(shape((r, width), f32), shape((r, width), f32), shape((r, ow), f32), shape((memory, width), f32),
                   shape((8, width), f32), shape((1, width), f32), shape((2, width // 2), f32)),
        in_specs=[pl.BlockSpec(memory_space=pltpu.SMEM)] + [vmem] * 5,
        out_specs=[vmem] * 7,
        compiler_params=pltpu.CompilerParams(vmem_limit_bytes=VMEM_MAX),
        cost_estimate=pl.CostEstimate(flops=3 * r * columns, bytes_accessed=3_000_000, transcendentals=0),
        name="spread",
    )(tensor.reshape(1), kept, *came, small)


def finish_small(grid, tensor, x_all, q, k, v, do_all, mixed, lse, segments, w_qkv, third, dr1, column, sums, up_sums, block_out,
                 grads, hw):
    f32, bf16 = jnp.float32, jnp.bfloat16
    tie = lax.optimization_barrier
    TN = (((0,), (0,)), ((), ()))
    width = dr1.shape[1]
    x, z = lax.axis_index("dp") % 2, lax.axis_index("dp") // 2
    down, down_far, up, up_far, out, out_far = grads

    def beside(pair, q, sends):
        arrays, q = tie(([a for a, _ in sends], q))
        came = [move(a) for a, (_, move) in zip(arrays, sends)]
        d = attend_backward(pair, q, k, v, do_all, mixed, lse, segments)
        return tie((came, d, q))

    over_y = lambda a: grid.swap(a, 2)
    over_x = lambda a: grid.turn(a, 1, 1)
    (down_in, out_in, up_in), d_one, q = beside(1, q, [(down_far, over_y), (out_far, over_y), (up_far, over_x)])
    g_one = mm(x_all, d_one, TN).astype(bf16)
    kept_down, kept_up, kept_out, send_x, send_y = blend_one(x, down, down_in, up, up_in, out, out_in)
    (came_x, came_y, came_one), d_zero, q = beside(0, q, [(send_x, over_x), (send_y, over_y), (g_one, over_y)])
    first = mm(x_all, d_zero, TN) + came_one.astype(f32)
    kept, kept_first, *sends = blend_two(x, z, kept_down, kept_up, kept_out, came_x, came_y, first)
    over_z = [lambda a, n=n: grid.turn(a, 0, n) for n in range(1, 4)]
    came, d_two, q = beside(2, q, list(zip(sends, over_z + [over_x])))
    grad_tokens, one, two, small = leave(x_all, (d_zero, d_one, d_two), w_qkv, third, kept_first, came[3], dr1, column, sums, up_sums)
    grad_down, grad_up, grad_out, grad_memory, vec, up_bias, qv = spread(tensor, kept, came[:3], small, 20, out.shape[-1])
    hd = 64
    slice_rows = one.shape[0]
    two = two.reshape(3, slice_rows // 2, 2, hd).transpose(2, 1, 0, 3).reshape(slice_rows, 1, 3, hd)
    grad_qkv = jnp.concatenate([one.reshape(slice_rows, 3, 2, hd).transpose(0, 2, 1, 3), two], 1).reshape(slice_rows, 3, 3 * hd)
    part = lambda n: jnp.concatenate([qv[0, 128 * n:128 * n + 128].reshape(2, hd), qv[1:2, 128 * n:128 * n + hd]])
    grad_qv = jnp.concatenate([part(0), part(2)], 1)
    t_out_bias, t_g1, t_s1, t_down_bias, t_g2, t_s2 = [vec[n] for n in (5, 3, 4, 2, 0, 1)]
    return (block_out, grad_tokens, grad_memory, grad_qkv, grad_qv,
            grad_out[:, :hw].reshape(slice_rows, 3, hd), t_out_bias, t_g1, t_s1, grad_up, up_bias.reshape(width), grad_down,
            t_down_bias, t_g2, t_s2)


def solution(mesh):
    grid = Grid(mesh.shape["dp"], mesh.shape["tensor"])
    tokens, dp, none = P(AXES, None), P("dp", None), P()
    heads, matrix = P("dp", "tensor", None), P("dp", "tensor")
    in_specs = (tokens, dp, dp, none, heads, P("tensor", None), heads, none, none, none, matrix, P("tensor"), matrix,
                none, none, none, tokens)
    out_specs = (tokens, tokens, none, heads, P("tensor", None), heads, none, none, none, matrix, P("tensor"), matrix,
                 none, none, none)

    def run(*args):
        return shards(grid, *args)

    return jax.shard_map(run, mesh=mesh, in_specs=in_specs, out_specs=out_specs, check_vma=False)
```

```python
import functools

import jax
import jax.numpy as jnp
from jax import lax
from jax.experimental import pallas as pl
from jax.experimental.pallas import tpu as pltpu
from jax.sharding import PartitionSpec as P

EPSILON = 1e-12
TILE = 256
MASKED = -1e30
VMEM_MAX = 64 * 1024 * 1024 - 128 * 1024
NT = (((1,), (1,)), ((), ()))
NN = (((1,), (0,)), ((), ()))


def mm(a, b, dims=NN):
    return lax.dot_general(a, b, dims, preferred_element_type=jnp.float32)


def fold8(x):
    r = x.shape[0]
    return x.reshape(r // 8, 8, x.shape[1])


def head_masks(block):
    lane = lax.broadcasted_iota(jnp.int32, block.shape, 1)
    zero = jnp.zeros_like(block)
    return jnp.where(lane < 64, block, zero), jnp.where(lane < 64, zero, block)


def tile_visible(first_ref, last_ref, i, t):
    return (first_ref[t] == 0) | ((first_ref[t] <= last_ref[i]) & (last_ref[t] >= first_ref[i]))


def forward_kernel(first_ref, last_ref, q_ref, k_ref, v_ref, kseg_ref, qseg_ref, o_ref, lse_ref,
                   vt_ref, qm_ref, s_ref, m_ref, l_ref, acc_ref):
    i = pl.program_id(0)
    tiles = pl.num_programs(0)
    pairs = q_ref.shape[1] // 128
    heads = 2 * pairs

    @pl.when(i == 0)
    def _():
        def turn(t, c):
            rows = pl.ds(pl.multiple_of(t * TILE, TILE), TILE)
            vt_ref[t] = v_ref[rows, :].T
            return c
        lax.fori_loop(0, tiles, turn, 0)

    for g in range(pairs):
        a, b = head_masks(q_ref[:, 128 * g:128 * g + 128])
        qm_ref[2 * g] = a
        qm_ref[2 * g + 1] = b
    m_ref[...] = jnp.full_like(m_ref, MASKED)
    l_ref[...] = jnp.zeros_like(l_ref)
    acc_ref[...] = jnp.zeros_like(acc_ref)
    qseg = qseg_ref[0:1, :]

    def scores(t, c):
        @pl.when(tile_visible(first_ref, last_ref, i, t))
        def _():
            rows = pl.ds(pl.multiple_of(t * TILE, TILE), TILE)
            kseg = kseg_ref[rows, :]
            kseg = jnp.concatenate([kseg, kseg], axis=1)
            seen = (kseg == 0) | (kseg == qseg)
            for h in range(heads):
                kp = k_ref[rows, 128 * (h // 2):128 * (h // 2) + 128]
                s = mm(kp, qm_ref[h], NT)
                s = jnp.where(seen, s, MASKED)
                s_ref[h, t] = s
                m_ref[h] = jnp.maximum(m_ref[h], jnp.max(fold8(s), axis=0))
        return c
    lax.fori_loop(0, tiles, scores, 0)
    for h in range(heads):
        m_ref[h] = jnp.broadcast_to(jnp.max(m_ref[h], axis=0, keepdims=True), (8, TILE))

    def mix(t, c):
        @pl.when(tile_visible(first_ref, last_ref, i, t))
        def _():
            for h in range(heads):
                p = jnp.exp(s_ref[h, t] - m_ref[h, 0:1, :])
                l_ref[h] = l_ref[h] + jnp.sum(fold8(p), axis=0)
                acc_ref[h] = acc_ref[h] + mm(vt_ref[t, 64 * h:64 * h + 64, :], p.astype(jnp.bfloat16))
        return c
    lax.fori_loop(0, tiles, mix, 0)
    for h in range(heads):
        total = jnp.sum(l_ref[h], axis=0, keepdims=True)
        lse_ref[h:h + 1, :] = m_ref[h, 0:1, :] + jnp.log(total)
        acc_ref[h] = acc_ref[h] / total
    for g in range(pairs):
        pair = jnp.concatenate([acc_ref[2 * g], acc_ref[2 * g + 1]], axis=0)
        o_ref[:, 128 * g:128 * g + 128] = pair.T.astype(jnp.bfloat16)


def attend_forward(q, k, v, seg):
    n, width = q.shape
    tiles = n // TILE
    heads = width // 64
    first = seg[::TILE]
    last = seg[TILE - 1::TILE]
    kseg = jnp.broadcast_to(seg[:, None], (n, 128))
    qseg = jnp.broadcast_to(seg[None, :], (8, n))
    whole = lambda shape: pl.BlockSpec(shape, lambda i, *_: (0,) * len(shape))
    return pl.pallas_call(
        forward_kernel,
        out_shape=(jax.ShapeDtypeStruct((n, width), jnp.bfloat16), jax.ShapeDtypeStruct((8, n), jnp.float32)),
        grid_spec=pltpu.PrefetchScalarGridSpec(
            num_scalar_prefetch=2, grid=(tiles,),
            in_specs=[pl.BlockSpec((TILE, width), lambda i, *_: (i, 0)), whole((n, width)), whole((n, width)),
                      whole((n, 128)), pl.BlockSpec((8, TILE), lambda i, *_: (0, i))],
            out_specs=[pl.BlockSpec((TILE, width), lambda i, *_: (i, 0)), pl.BlockSpec((8, TILE), lambda i, *_: (0, i))],
            scratch_shapes=[
                pltpu.VMEM((tiles, width, TILE), jnp.bfloat16),
                pltpu.VMEM((heads, TILE, 128), jnp.bfloat16),
                pltpu.VMEM((heads, tiles, TILE, TILE), jnp.float32),
                pltpu.VMEM((heads, 8, TILE), jnp.float32),
                pltpu.VMEM((heads, 8, TILE), jnp.float32),
                pltpu.VMEM((heads, 64, TILE), jnp.float32),
            ]),
        compiler_params=pltpu.CompilerParams(dimension_semantics=("arbitrary",), vmem_limit_bytes=VMEM_MAX),
        cost_estimate=pl.CostEstimate(flops=4 * n * n * width, bytes_accessed=8 * n * width, transcendentals=n * n * heads),
        name="attend_forward",
    )(first, last, q, k, v, kseg, qseg)


def backward_kernel(base, first_ref, last_ref, q_ref, do_ref, o_ref, k_ref, v_ref, kseg_ref, qseg_ref, lse_ref,
                    d_ref, kt_ref, qm_ref, dom_ref, delta_ref, dqt_ref, dka_ref, dva_ref):
    i = pl.program_id(0)
    tiles = pl.num_programs(0)

    @pl.when(i == 0)
    def _():
        def turn(t, c):
            rows = pl.ds(pl.multiple_of(t * TILE, TILE), TILE)
            kt_ref[t] = k_ref[rows, :].T
            dka_ref[rows, :] = jnp.zeros((TILE, 128), jnp.float32)
            dva_ref[rows, :] = jnp.zeros((TILE, 128), jnp.float32)
            return c
        lax.fori_loop(0, tiles, turn, 0)

    for ref, masked in ((q_ref, qm_ref), (do_ref, dom_ref)):
        masked[0], masked[1] = head_masks(ref[...])
    inner = (do_ref[...].astype(jnp.float32) * o_ref[...].astype(jnp.float32)).T
    for h in range(2):
        delta_ref[h] = jnp.broadcast_to(jnp.sum(inner[64 * h:64 * h + 64], axis=0, keepdims=True), (8, TILE))
    dqt_ref[...] = jnp.zeros_like(dqt_ref)
    qseg = qseg_ref[0:1, :]

    def count(t, c):
        prompt, before, upto = c
        return (prompt + (first_ref[t] == 0).astype(jnp.int32), before + (last_ref[t] < first_ref[i]).astype(jnp.int32),
                upto + (first_ref[t] <= last_ref[i]).astype(jnp.int32))
    zero = jnp.int32(0)
    prompt, before, upto = lax.fori_loop(0, tiles, count, (zero, zero, zero))
    start = jnp.maximum(prompt, before)
    visible = prompt + jnp.maximum(upto - start, 0)

    def one_tile(n):
        t = jnp.where(n < prompt, n, start + n - prompt)
        rows = pl.ds(pl.multiple_of(t * TILE, TILE), TILE)
        kseg = kseg_ref[rows, :]
        kseg = jnp.concatenate([kseg, kseg], axis=1)
        seen = (kseg == 0) | (kseg == qseg)
        kp = k_ref[rows, :]
        vp = v_ref[rows, :]
        s = [mm(kp, qm_ref[h], NT) for h in range(2)]
        d = [mm(vp, dom_ref[h], NT) for h in range(2)]
        p = [jnp.where(seen, jnp.exp(s[h] - lse_ref[base + h:base + h + 1, :]), 0.0) for h in range(2)]
        ds = [(p[h] * (d[h] - delta_ref[h, 0:1, :])).astype(jnp.bfloat16) for h in range(2)]
        p = [value.astype(jnp.bfloat16) for value in p]
        dva_ref[rows, :] = dva_ref[rows, :] + (mm(p[0], dom_ref[0]) + mm(p[1], dom_ref[1]))
        dka_ref[rows, :] = dka_ref[rows, :] + (mm(ds[0], qm_ref[0]) + mm(ds[1], qm_ref[1]))
        return [mm(kt_ref[t, 64 * h:64 * h + 64, :], ds[h]) for h in range(2)]

    def two_tiles(n, c):
        one, two = one_tile(2 * n), one_tile(2 * n + 1)
        for h in range(2):
            dqt_ref[h] = dqt_ref[h] + (one[h] + two[h])
        return c
    lax.fori_loop(0, visible // 2, two_tiles, 0)

    @pl.when(visible % 2 == 1)
    def _():
        for h, value in enumerate(one_tile(visible - 1)):
            dqt_ref[h] = dqt_ref[h] + value
    pair = jnp.concatenate([dqt_ref[0], dqt_ref[1]], axis=0)
    own = pl.ds(pl.multiple_of(i * TILE, TILE), TILE)
    d_ref[own, 0:128] = (pair.T * 0.125).astype(jnp.bfloat16)

    @pl.when(i == tiles - 1)
    def _():
        d_ref[:, 128:256] = dka_ref[...].astype(jnp.bfloat16)
        d_ref[:, 256:384] = dva_ref[...].astype(jnp.bfloat16)


def attend_backward(g, q, k, v, do, o, lse, seg):
    n, width = q.shape[0], 128
    tiles = n // TILE
    heads = width // 64
    first = seg[::TILE]
    last = seg[TILE - 1::TILE]
    kseg = jnp.broadcast_to(seg[:, None], (n, 128))
    qseg = jnp.broadcast_to(seg[None, :], (8, n))
    whole = lambda shape: pl.BlockSpec(shape, lambda i, *_: (0,) * len(shape))
    rows = pl.BlockSpec((TILE, width), lambda i, *_: (i, g))
    column = pl.BlockSpec((n, width), lambda i, *_: (0, g))
    stat = pl.BlockSpec((8, TILE), lambda i, *_: (0, i))
    return pl.pallas_call(
        functools.partial(backward_kernel, 2 * g),
        out_shape=jax.ShapeDtypeStruct((n, 3 * width), jnp.bfloat16),
        grid_spec=pltpu.PrefetchScalarGridSpec(
            num_scalar_prefetch=2, grid=(tiles,),
            in_specs=[rows, rows, rows, column, column, whole((n, 128)), stat, stat],
            out_specs=whole((n, 3 * width)),
            scratch_shapes=[
                pltpu.VMEM((tiles, width, TILE), jnp.bfloat16),
                pltpu.VMEM((heads, TILE, 128), jnp.bfloat16),
                pltpu.VMEM((heads, TILE, 128), jnp.bfloat16),
                pltpu.VMEM((heads, 8, TILE), jnp.float32),
                pltpu.VMEM((heads, 64, TILE), jnp.float32),
                pltpu.VMEM((n, width), jnp.float32),
                pltpu.VMEM((n, width), jnp.float32),
            ]),
        compiler_params=pltpu.CompilerParams(dimension_semantics=("arbitrary",), vmem_limit_bytes=VMEM_MAX),
        cost_estimate=pl.CostEstimate(flops=10 * n * n * width, bytes_accessed=14 * n * width, transcendentals=n * n * heads),
        name="attend_backward",
    )(first, last, q, do, o, k, v, kseg, qseg, lse)


BLOCK = 256
STRIP = 64


def normal_cdf_parts(u):
    v = u * 0.7071067811865476
    c = jnp.clip(v, -3.832506856900711, 3.832506856900711)
    c2 = c * c
    top = 0.00022905065861350646
    for a in (0.0034082910107109506, 0.050955695062380861, 0.18520832239976145, 1.128379143519084):
        top = top * c2 + a
    low = -1.1791602954361697e-7
    for b in (0.000023547966471313185, 0.0010179625278914885, 0.014070470171167667, 0.11098505178285362,
              0.49746925110067538, 1.0):
        low = low * c2 + b
    cdf = 0.5 + 0.5 * (c * top / low)
    slope = jnp.exp(-(v * v)) * (u * 0.3989422804014327)
    return u * cdf, cdf + slope


def middle_kernel(pieces, o_all, x0, outs, ups, downs, cot, vec_ref, bup_ref,
                  block_out, dr1, do_all, g_down, g_up, g_out, sums_ref, upsum_ref,
                  o_ref, raw_ref, wo_ref, wu_ref, wd_ref, hat_ref, inv_ref, acc_ref, hl_ref, hlt_ref, gp_ref, z_ref, c_ref,
                  df_ref, dft_ref, y_ref, st_ref, su_ref, ru_ref, rd_ref, go_ref, rgo_ref, u0_ref, u1_ref,
                  sem, osem, send, recv):
    f32, bf16 = jnp.float32, jnp.bfloat16
    rows, width = hat_ref.shape
    blocks = rows // BLOCK
    part = wu_ref.shape[2]
    bf = lambda a: a.astype(bf16)
    dp, tensor = lax.axis_index("dp"), lax.axis_index("tensor")
    inner = tensor % 2
    partner = (dp, tensor + 1 - 2 * inner)
    z = dp // 2
    to_y = (dp, (tensor + 2) % 4)
    mine = pl.multiple_of(inner * rows, 1024)
    theirs = pl.multiple_of((1 - inner) * rows, 1024)
    greet([partner, to_y] if pieces else [partner])

    def remote(n, src, dst, device=partner):
        return pltpu.make_async_remote_copy(src, dst, send.at[n], recv.at[n], device_id=device,
                                            device_id_type=pl.DeviceIdType.MESH)

    swap_o = remote(0, o_all.at[pl.ds(theirs, rows), :], o_ref.at[1])
    swap_o.start()
    count = [0]

    def load(src, dst):
        copy = pltpu.make_async_copy(src, dst, sem.at[count[0]])
        count[0] += 1
        copy.start()
        return copy

    def weight(sources, dst):
        if not pieces:
            return [load(sources[0].at[o], dst.at[o]) for o in range(2)]
        digit = dp % 2
        made = []
        for o in range(2):
            for zi in range(sources[0].shape[1]):
                for n in range(2):
                    place = 2 * zi + (digit if n == 0 else 1 - digit)
                    r = sources[n].shape[2]
                    made.append(load(sources[n].at[o, zi], dst.at[o, pl.ds(pl.multiple_of(place * r, r), r), :]))
        return made

    if pieces:
        r = downs[0].shape[0]
        block = lambda o, zi: wd_ref.at[o, pl.ds(pl.multiple_of(zi * r, r), r), :]
        zs = [(z + 4 - k) % 4 for k in range(4)]
        held = [load(downs[k], block(0, zs[k])) for k in range(4)]
    first = [load(o_all.at[pl.ds(mine, rows), :], o_ref.at[0]), load(x0, hat_ref)] + weight(outs, raw_ref.at[0])
    if pieces:
        second = [load(ups[o], wu_ref.at[o]) for o in range(2)]
    else:
        second = [load(ups[0].at[o], wu_ref.at[o]) for o in range(2)]
    if not pieces:
        second = second + weight(downs, wd_ref)
    late = load(cot, c_ref)
    if pieces:
        by_y = []
        for k in range(4):
            held[k].wait()
            by_y.append(remote(12 + k, block(0, zs[k]), block(1, zs[k]), to_y))
            by_y[k].start()
    vec = lambda n: vec_ref[n:n + 1, :]
    sums_ref[...] = jnp.zeros_like(sums_ref)
    upsum_ref[...] = jnp.zeros_like(upsum_ref)
    for copy in first:
        copy.wait()
    swaps = [remote(1, raw_ref.at[0], raw_ref.at[1])]
    swaps[0].start()
    for copy in second:
        copy.wait()
    for o in range(2):
        swaps.append(remote(2 + 2 * o, wu_ref.at[o], wu_ref.at[2 + o]))
        swaps.append(remote(3 + 2 * o, wd_ref.at[o], wd_ref.at[2 + o]))
    for copy in swaps[1:4] if pieces else swaps[1:]:
        copy.start()
    lane = lax.broadcasted_iota(jnp.int32, (width, 128), 1)

    def order_heads(side):
        wo_ref[side, :, 0:128] = raw_ref[side, 0, :, 0:128]
        wo_ref[side, :, 128:256] = raw_ref[side, 1, :, 0:128]
        upper = pltpu.roll(raw_ref[side, 1, :, 128:256].astype(f32), 64, 1)
        wo_ref[side, :, 256:384] = bf(jnp.where(lane < 64, raw_ref[side, 0, :, 128:256].astype(f32), upper))
    order_heads(0)
    swaps[0].wait()
    order_heads(1)
    swap_o.wait()

    def strips(body):
        def run(s, carry):
            body(pl.ds(pl.multiple_of(s * STRIP, STRIP), STRIP))
            return carry
        lax.fori_loop(0, rows // STRIP, run, 0)

    def add_sum(n, value):
        sums_ref[n] = sums_ref[n] + jnp.sum(fold(value), axis=0)

    def fold(value):
        return value.reshape(value.shape[0] // 8, 8, value.shape[1])

    def mean(value):
        return jnp.sum(value, axis=-1, keepdims=True) * (1.0 / width)

    def project(b, carry):
        r = pl.ds(pl.multiple_of(b * BLOCK, BLOCK), BLOCK)
        acc_ref[r, :] = mm(o_ref[0, r, :], wo_ref[0], NT) + mm(o_ref[1, r, :], wo_ref[1], NT)
        return carry
    lax.fori_loop(0, blocks, project, 0)

    def first_norm(r):
        r1 = hat_ref[r, :] + (acc_ref[r, :] + vec(0))
        centre = r1 - mean(r1)
        inv = lax.rsqrt(mean(centre * centre) + EPSILON)
        hat = centre * inv
        hat_ref[r, :] = hat
        inv_ref[r, :] = inv
        hl_ref[r, :] = bf(hat * vec(1) + vec(2))
    strips(first_norm)
    for b in range(blocks):
        hlt_ref[:, BLOCK * b:BLOCK * b + BLOCK] = hl_ref[BLOCK * b:BLOCK * b + BLOCK, :].T
    acc_ref[...] = jnp.zeros_like(acc_ref)

    bufs = (u0_ref, u1_ref)

    def forward(n, carry):
        j = n % 2 * 2 + n // 2
        for o in range(2):
            @pl.when(j == 2 + o)
            def _(o=o):
                swaps[1 + 2 * o].wait()
                swaps[2 + 2 * o].wait()
        if pieces:
            @pl.when(j == 1)
            def _():
                for copy in by_y:
                    copy.wait()
                swaps[4].start()

        def lift(b):
            bufs[b % 2][...] = mm(hl_ref[BLOCK * b:BLOCK * b + BLOCK, :], wu_ref[j]) + bup_ref[j, 0:1, :].astype(f32)
        lift(0)
        for b in range(blocks):
            if b + 1 < blocks:
                lift(b + 1)
            r = slice(BLOCK * b, BLOCK * b + BLOCK)
            for i in range(0, BLOCK, 32):
                for w in range(0, part, 256):
                    z, gp = normal_cdf_parts(bufs[b % 2][i:i + 32, w:w + 256])
                    z_ref[j, BLOCK * b + i:BLOCK * b + i + 32, w:w + 256] = bf(z)
                    gp_ref[j, BLOCK * b + i:BLOCK * b + i + 32, w:w + 256] = gp
            acc_ref[r, :] = acc_ref[r, :] + mm(z_ref[j, r, :], wd_ref[j], NT)
        return carry
    lax.fori_loop(0, 4, forward, 0)
    late.wait()

    def second_norm(r):
        h1 = hat_ref[r, :] * vec(1) + vec(2)
        r2 = h1 + (acc_ref[r, :] + vec(3))
        centre = r2 - mean(r2)
        inv = lax.rsqrt(mean(centre * centre) + EPSILON)
        hat = centre * inv
        y_ref[r, :] = bf(hat * vec(4) + vec(5))
        c = c_ref[r, :].astype(f32)
        add_sum(0, c * hat)
        add_sum(1, c)
        w = c * vec(4)
        dr2 = (w - mean(w) - hat * mean(w * hat)) * inv
        acc_ref[r, :] = dr2
        low = bf(dr2)
        df_ref[r, :] = low
        add_sum(2, low.astype(f32))
    strips(second_norm)
    stores = [pltpu.make_async_copy(y_ref, block_out, osem.at[0])]
    stores[0].start()
    for b in range(blocks):
        dft_ref[:, BLOCK * b:BLOCK * b + BLOCK] = df_ref[BLOCK * b:BLOCK * b + BLOCK, :].T

    def backward(n, carry):
        j = 3 - n

        def lower(b):
            bufs[b % 2][...] = mm(df_ref[BLOCK * b:BLOCK * b + BLOCK, :], wd_ref[j])
        slot = n % 2
        away = [remote(6 + slot, st_ref.at[slot], rd_ref.at[slot]), remote(8 + slot, su_ref.at[slot], ru_ref.at[slot])]
        lower(0)
        for b in range(blocks):
            if b + 1 < blocks:
                lower(b + 1)
            r = slice(BLOCK * b, BLOCK * b + BLOCK)
            for i in range(0, BLOCK, 64):
                q = slice(BLOCK * b + i, BLOCK * b + i + 64)
                dul = bf(bufs[b % 2][i:i + 64, :] * gp_ref[j, q, :])
                upsum_ref[j] = upsum_ref[j] + jnp.sum(fold(dul.astype(f32)), axis=0)
                hat2_ref[q, :] = dul
            acc_ref[r, :] = acc_ref[r, :] + mm(hat2_ref[r, :], wu_ref[j], NT)

        @pl.when(n < 2)
        def _():
            for m in range(0, width, BLOCK):
                st_ref[slot, m:m + BLOCK, :] = bf(mm(dft_ref[m:m + BLOCK, :], z_ref[j]))
            away[0].start()
            for m in range(0, width, BLOCK):
                su_ref[slot, m:m + BLOCK, :] = bf(mm(hlt_ref[m:m + BLOCK, :], hat2_ref[...]))
            away[1].start()

        @pl.when(n >= 2)
        def _():
            away[0].wait()
            for m in range(0, width, BLOCK):
                got = rd_ref[slot, m:m + BLOCK, :].astype(f32)
                st_ref[slot, m:m + BLOCK, :] = bf(mm(dft_ref[m:m + BLOCK, :], z_ref[j]) + got)
            if pieces:
                @pl.when(j == 0)
                def _():
                    pltpu.make_async_copy(st_ref.at[1], g_down[0], osem.at[2]).start()

                @pl.when(j == 1)
                def _():
                    early.start()
                    pltpu.make_async_copy(st_ref.at[0, width // 2:, :], g_down[1], osem.at[1]).start()
            else:
                pltpu.make_async_copy(st_ref.at[slot], g_down.at[j], osem.at[1 + slot]).start()
            away[1].wait()
            for m in range(0, width, BLOCK):
                got = ru_ref[slot, m:m + BLOCK, :].astype(f32)
                su_ref[slot, m:m + BLOCK, :] = bf(mm(hlt_ref[m:m + BLOCK, :], hat2_ref[...]) + got)
            if pieces:
                r = g_up[0].shape[2]
                for zi in range(g_up[0].shape[1]):
                    for o in range(2):
                        at = pl.multiple_of((2 * zi + (dp + o) % 2) * r, r)
                        pltpu.make_async_copy(su_ref.at[slot, pl.ds(at, r), :], g_up[o].at[j, zi], osem.at[3 + slot]).start()
            else:
                pltpu.make_async_copy(su_ref.at[slot], g_up.at[j], osem.at[3 + slot]).start()
        return carry
    hat2_ref = y_ref
    stores[0].wait()
    if pieces:
        early = remote(16, st_ref.at[0, 0:width // 2, :], g_down[2], to_y)
    lax.fori_loop(0, 4, backward, 0)

    def first_back(r):
        dh1 = acc_ref[r, :]
        hat = hat_ref[r, :]
        add_sum(3, dh1 * hat)
        add_sum(4, dh1)
        w = dh1 * vec(1)
        grad = (w - mean(w) - hat * mean(w * hat)) * inv_ref[r, :]
        acc_ref[r, :] = grad
        low = bf(grad)
        df_ref[r, :] = low
        add_sum(5, low.astype(f32))
    strips(first_back)
    out = pltpu.make_async_copy(acc_ref, dr1, osem.at[0])
    out.start()
    stores = [out]
    for b in range(blocks):
        dft_ref[:, BLOCK * b:BLOCK * b + BLOCK] = df_ref[BLOCK * b:BLOCK * b + BLOCK, :].T
    lane = lax.broadcasted_iota(jnp.int32, (BLOCK, 128), 1)

    def out_grad(side, m):
        tiles = [mm(dft_ref[m:m + BLOCK, :], o_ref[side, :, 128 * g:128 * g + 128]) for g in range(3)]
        third = [jnp.where(lane < 64, tiles[2], 0.0), jnp.where(lane < 64, pltpu.roll(tiles[2], 64, 1), 0.0)]
        return [jnp.concatenate([tiles[o], third[o]], axis=1) for o in range(2)]
    for m in range(0, width, BLOCK):
        for o, value in enumerate(out_grad(1, m)):
            go_ref[o, m:m + BLOCK, :] = bf(value)
    swap_go = remote(10, go_ref, rgo_ref)
    swap_go.start()
    ow = wo_ref.shape[2]
    for side in (1, 0):
        def push(b, carry):
            r = pl.ds(pl.multiple_of(b * BLOCK, BLOCK), BLOCK)
            y_ref[r, ow * side:ow * side + ow] = bf(mm(df_ref[r, :], wo_ref[side]))
            return carry
        lax.fori_loop(0, blocks, push, 0)
        if side == 1:
            swap_do = remote(11, y_ref.at[:, pl.ds(ow, ow)], do_all.at[pl.ds(mine, rows), :])
            swap_do.start()
        else:
            copy = pltpu.make_async_copy(y_ref.at[:, pl.ds(0, ow)], do_all.at[pl.ds(mine, rows), :], osem.at[5])
            copy.start()
            stores.append(copy)
    swap_go.wait()
    for m in range(0, width, BLOCK):
        for o, value in enumerate(out_grad(0, m)):
            go_ref[o, m:m + BLOCK, :] = bf(value + rgo_ref[o, m:m + BLOCK, :].astype(f32))
    for o in range(2 if pieces else 1):
        copy = pltpu.make_async_copy(go_ref.at[o] if pieces else go_ref, g_out[o] if pieces else g_out, osem.at[6 + o])
        copy.start()
        stores.append(copy)
    whole = g_down[0] if pieces else g_down.at[0]
    for slot in range(2):
        if pieces and slot == 0:
            pltpu.make_async_copy(st_ref.at[0, width // 2:, :], g_down[1], osem.at[1]).wait()
        else:
            pltpu.make_async_copy(st_ref.at[slot], whole, osem.at[1 + slot]).wait()
        pltpu.make_async_copy(su_ref.at[slot], whole, osem.at[3 + slot]).wait()
    if pieces:
        early.wait()
    swap_do.wait()
    for copy in stores:
        copy.wait()


def middle(o_all, x0, outs, ups, downs, cot, vec, bup):
    f32, bf16 = jnp.float32, jnp.bfloat16
    rows, width = x0.shape
    ow = o_all.shape[1]
    part = bup.shape[-1]
    pieces = len(ups) == 2
    shape = jax.ShapeDtypeStruct
    hbm = pl.BlockSpec(memory_space=pl.ANY)
    vmem = pl.BlockSpec(memory_space=pltpu.VMEM)
    v = pltpu.VMEM
    n = len(ups)
    m = 2 * n + len(downs)

    def kernel(o_all, x0, *refs):
        weights, rest = refs[:m], refs[m:]
        if pieces:
            rest = rest[:6] + (rest[6:9], rest[9:11], rest[11:13]) + rest[13:]
        middle_kernel(pieces, o_all, x0, weights[:n], weights[n:2 * n], weights[2 * n:], *rest)

    if pieces:
        parts = (2, len(downs), downs[0].shape[0] // 2, part)
        grads = [shape((width, part), bf16)] + [shape((width // 2, part), bf16)] * 2 + [shape(parts, bf16)] * 2 + [shape((width, 256), bf16)] * 2
    else:
        grads = [shape((2, width, part), bf16), shape((2, width, part), bf16), shape((2, width, 256), bf16)]
    return pl.pallas_call(
        kernel,
        out_shape=(shape((rows, width), bf16), shape((rows, width), f32), shape((2 * rows, ow), bf16),
                   *grads, shape((6, 8, width), f32), shape((4, 8, part), f32)),
        in_specs=[hbm] * (3 + m) + [vmem] * 2,
        out_specs=[hbm] * (3 + len(grads)) + [vmem] * 2,
        scratch_shapes=[
            v((2, rows, ow), bf16), v((2, 2, width, 256), bf16), v((2, width, ow), bf16), v((4, width, part), bf16),
            v((4, width, part), bf16),
            v((rows, width), f32), v((rows, 1), f32), v((rows, width), f32), v((rows, width), bf16), v((width, rows), bf16),
            v((4, rows, part), f32), v((4, rows, part), bf16), v((rows, width), bf16), v((rows, width), bf16),
            v((width, rows), bf16), v((rows, width), bf16), v((2, width, part), bf16),
            v((2, width, part), bf16), v((2, width, part), bf16), v((2, width, part), bf16), v((2, width, 256), bf16),
            v((2, width, 256), bf16), v((BLOCK, part), f32), v((BLOCK, part), f32),
            pltpu.SemaphoreType.DMA((40,)), pltpu.SemaphoreType.DMA((8,)),
            pltpu.SemaphoreType.DMA((24,)), pltpu.SemaphoreType.DMA((24,)),
        ],
        compiler_params=pltpu.CompilerParams(vmem_limit_bytes=VMEM_MAX, collective_id=1, has_side_effects=True),
        cost_estimate=pl.CostEstimate(flops=6 * rows * width * 9 * width, bytes_accessed=60_000_000, transcendentals=2 * rows * 4 * part),
        name="middle",
    )(o_all, x0, *outs, *ups, *downs, cot, vec, bup)


class Exchange:
    def __init__(self, send, recv):
        self.send, self.recv, self.used = send, recv, 0

    def copy(self, src, dst, device):
        n = self.used
        self.used += 1
        return pltpu.make_async_remote_copy(src, dst, self.send.at[n], self.recv.at[n], device_id=device,
                                            device_id_type=pl.DeviceIdType.MESH)


def greet(devices):
    barrier = pltpu.get_barrier_semaphore()
    for device in devices:
        pl.semaphore_signal(barrier, inc=1, device_id=device, device_id_type=pl.DeviceIdType.MESH)
    pl.semaphore_wait(barrier, len(devices))


def entry_kernel(tokens, pos_ref, mem_ref, wq_ref, bq_ref, bu_ref, wu_ref, wd_ref, wo_ref,
                 x0_out, x_out, q_out, k_out, v_out, w_out, up_g, down_g, out_g, bu_out,
                 x0_ref, x_ref, g_ref, b_ref, y_ref, third_ref, q_ref, k_ref, v_ref, ub_ref, send, recv, sem):
    f32, bf16 = jnp.float32, jnp.bfloat16
    rows, width = x0_ref.shape
    dp, tensor = lax.axis_index("dp"), lax.axis_index("tensor")
    z, x = dp // 2, dp % 2
    inner = tensor % 2
    zs = [(z + 4 - k) % 4 for k in range(4)]
    at = [2 * zs[k] + x for k in range(4)]
    far = [2 * zs[k] + 1 - x for k in range(4)]
    to_z = [None] + [(2 * ((z + k) % 4) + x, tensor) for k in range(1, 4)]
    to_x = (2 * z + 1 - x, tensor)
    to_y = (dp, (tensor + 2) % 4)
    to_core = (dp, tensor + 1 - 2 * inner)
    to_both = (dp, 3 - tensor)
    greet(to_z[1:] + [to_x, to_y, to_core, to_both])
    ex = Exchange(send, recv)
    started = []

    def go(src, dst, device):
        copy = ex.copy(src, dst, device)
        copy.start()
        started.append(copy)
        return copy

    local = []

    def keep(src, dst):
        copy = pltpu.make_async_copy(src, dst, sem.at[len(local)])
        copy.start()
        local.append(copy)
        return copy

    own = keep(wq_ref, g_ref.at[0, at[0]])
    own_bias = keep(bq_ref, b_ref.at[0])
    z_q = [None] + [go(wq_ref, g_ref.at[0, at[0]], to_z[k]) for k in range(1, 4)]
    x_q = [go(wq_ref, g_ref.at[0, at[0]], to_x)]
    y_q = [go(wq_ref, g_ref.at[1, at[0]], to_y)]
    bias = go(bq_ref, b_ref.at[1], to_y)
    up_bias = [go(bu_ref, ub_ref.at[n - 1], to) for n, to in ((1, to_y), (2, to_core), (3, to_both))]

    mine = pl.multiple_of(inner * rows, 1024)
    positions = pos_ref[0:1, :]
    strip = 128

    def start(s, carry):
        r = pl.multiple_of(s * strip, strip)
        place = lax.broadcasted_iota(jnp.int32, (strip, positions.shape[1]), 0) + (inner * rows + r)
        picks = jnp.where(place == positions, 1.0, 0.0).astype(bf16)
        value = tokens[pl.ds(r, strip), :].astype(f32) + mm(picks, mem_ref[...])
        x0_ref[pl.ds(r, strip), :] = value
        x_ref[pl.ds(mine + r, strip), :] = value.astype(bf16)
        return carry
    lax.fori_loop(0, rows // strip, start, 0)
    keep(x0_ref, x0_out)
    core = go(x_ref.at[pl.ds(mine, rows), :], x_ref.at[pl.ds(mine, rows), :], to_core)

    for k in range(1, 4):
        z_q[k].wait_recv()
        x_q.append(go(g_ref.at[0, at[k]], g_ref.at[0, at[k]], to_x))
        y_q.append(go(g_ref.at[0, at[k]], g_ref.at[1, at[k]], to_y))
    z_u = [None] + [go(wu_ref, up_g.at[at[0]], to_z[k]) for k in range(1, 4)]
    z_o = [None] + [go(wo_ref, out_g.at[0, z], to_z[k]) for k in range(1, 4)]
    keep(wu_ref, up_g.at[at[0]])
    keep(wd_ref, down_g.at[x])
    keep(wo_ref, out_g.at[0, z])
    last = []
    for k in range(2):
        x_q[k].wait_recv()
        last.append(go(g_ref.at[0, far[k]], g_ref.at[1, far[k]], to_y))
    for k in range(2, 4):
        y_q[k].wait_recv()
        last.append(go(g_ref.at[1, at[k]], g_ref.at[1, at[k]], to_x))
    rest = [go(wd_ref, down_g.at[x], to_x), go(wu_ref, up_g.at[at[0]], to_x), go(wo_ref, out_g.at[1, z], to_y)]
    own.wait()
    own_bias.wait()
    for copy in x_q[2:] + [core]:
        copy.wait_recv()
    keep(x_ref, x_out)
    lane = lax.broadcasted_iota(jnp.int32, (BLOCK, 128), 1)
    blocks = 2 * rows // BLOCK
    heads = (q_ref, k_ref, v_ref)

    def write(n, g, r, value):
        value = value.astype(bf16)
        if n == 0:
            value = value * jnp.asarray(0.125, bf16)
        heads[n][r, 128 * g:128 * g + 128] = value

    def project(o, b):
        r = pl.ds(pl.multiple_of(b * BLOCK, BLOCK), BLOCK)
        y_ref[:, 0:576] = mm(x_ref[r, :], g_ref[o].reshape(width, 576)) + b_ref[o, 0:1, 0:576].astype(f32)
        for n in range(3):
            write(n, o, r, y_ref[:, 128 * n:128 * n + 128])
        return r

    def project_own(b, carry):
        r = project(0, b)
        third_ref[r, :] = y_ref[:, 384:640]
        return carry

    def project_other(b, carry):
        r = project(1, b)
        turn = lambda value: pltpu.roll(value, 64, 1)
        left, right = third_ref[r, 0:128], y_ref[:, 384:512]
        write(0, 2, r, jnp.where(lane < 64, left, turn(right)))
        write(1, 2, r, jnp.where(lane < 64, turn(left), right))
        write(2, 2, r, jnp.where(lane < 64, third_ref[r, 128:256], turn(y_ref[:, 512:640])))
        return carry
    y_ref[...] = jnp.zeros_like(y_ref)
    lax.fori_loop(0, blocks, project_own, 0)
    for copy in y_q[:2] + last + [bias]:
        copy.wait_recv()
    keep(g_ref, w_out)
    for k in range(1, 4):
        z_u[k].wait_recv()
        rest.append(go(up_g.at[at[k]], up_g.at[at[k]], to_x))
        lax.fori_loop(blocks * (k - 1) // 4, blocks * k // 4, project_other, 0)
    lax.fori_loop(blocks * 3 // 4, blocks, project_other, 0)
    for src, dst in ((q_ref, q_out), (k_ref, k_out), (v_ref, v_out)):
        keep(src, dst)
    for k in range(1, 4):
        z_o[k].wait_recv()
        rest.append(go(out_g.at[0, zs[k]], out_g.at[1, zs[k]], to_y))
    for copy in rest + up_bias:
        copy.wait_recv()
    bu_out[0] = bu_ref[...]
    for n in range(3):
        bu_out[n + 1] = ub_ref[n]
    for copy in started:
        copy.wait_send()
    for copy in local[2:]:
        copy.wait()


def entry(tokens, positions, memory_rows, shard_qkv, biases, up_bias, up, down, out):
    f32, bf16 = jnp.float32, jnp.bfloat16
    rows, width = tokens.shape
    r = up.shape[0]
    shape, v = jax.ShapeDtypeStruct, pltpu.VMEM
    hbm, vmem = pl.BlockSpec(memory_space=pl.ANY), pl.BlockSpec(memory_space=pltpu.VMEM)
    qkv = shape((2 * rows, 384), bf16)
    return pl.pallas_call(
        entry_kernel,
        out_shape=(shape((rows, width), f32), shape((2 * rows, width), bf16), qkv, qkv, qkv,
                   shape((2, 8, r, 576), bf16), shape((8, r, up.shape[1]), bf16), shape((2, r, down.shape[1]), bf16),
                   shape((2, 4, r, out.shape[1]), bf16), shape((4, 16, up.shape[1]), bf16)),
        in_specs=[vmem] * 9,
        out_specs=[hbm] * 9 + [vmem],
        scratch_shapes=[
            v((rows, width), f32), v((2 * rows, width), bf16), v((2, 8, r, 576), bf16), v((2, 16, 640), bf16),
            v((BLOCK, 640), f32), v((2 * rows, 256), f32), v((2 * rows, 384), bf16), v((2 * rows, 384), bf16), v((2 * rows, 384), bf16),
            v((3, 16, up.shape[1]), bf16),
            pltpu.SemaphoreType.DMA((48,)), pltpu.SemaphoreType.DMA((48,)), pltpu.SemaphoreType.DMA((16,)),
        ],
        compiler_params=pltpu.CompilerParams(vmem_limit_bytes=VMEM_MAX, collective_id=0, has_side_effects=True),
        cost_estimate=pl.CostEstimate(flops=4 * rows * width * 1152, bytes_accessed=20_000_000, transcendentals=0),
        name="entry",
    )(tokens, positions, memory_rows, shard_qkv, biases, up_bias, up, down, out)


def exit_kernel(x_all, d0, d1, d2, w_all, third, kept_ref, came_ref, dr1, pos_ref, sums_in, up_in,
                tok_out, first_out, second_out, small_out,
                x_ref, xt_ref, d_ref, w_ref, dr_ref, g_ref, own_ref, oth_ref, yb_ref, xs_ref, xb_ref, zt_ref, zs_ref, zb_ref,
                fs_ref, fb_ref, their_ref, got_ref, tok_ref, s_ref, t_ref, r_ref, first_ref, send, recv, sem):
    f32, bf16 = jnp.float32, jnp.bfloat16
    rows, width = dr_ref.shape
    dp, tensor = lax.axis_index("dp"), lax.axis_index("tensor")
    z, x = dp // 2, dp % 2
    inner, outer = tensor % 2, tensor // 2
    up_z = [None] + [(z + k) % 4 for k in range(1, 4)]
    to_z = [None] + [(2 * up_z[k] + x, tensor) for k in range(1, 4)]
    to_x = (2 * z + 1 - x, tensor)
    to_y = (dp, (tensor + 2) % 4)
    to_core = (dp, tensor + 1 - 2 * inner)
    near_z = (2 * (z + 1 - 2 * (z % 2)) + x, tensor)
    far_z = to_z[2]
    loads = []
    for src, dst in ((d2, d_ref.at[2]), (x_all, x_ref), (d0, d_ref.at[0]), (d1, d_ref.at[1]),
                     (w_all.at[0, :, pl.ds(0, 384)], w_ref.at[0]), (w_all.at[1, :, pl.ds(0, 384)], w_ref.at[1]),
                     (third, w_ref.at[2]), (dr1, dr_ref)):
        copy = pltpu.make_async_copy(src, dst, sem.at[len(loads)])
        copy.start()
        loads.append(copy)
    greet(to_z[1:] + [to_x, to_y, to_core])
    ex = Exchange(send, recv)
    started = []

    def go(src, dst, device):
        copy = ex.copy(src, dst, device)
        copy.start()
        started.append(copy)
        return copy

    for k in range(4):
        first_ref[k] = kept_ref[k] + came_ref[k].astype(f32)
    for k in range(1, 4):
        fs_ref[k - 1] = first_ref[up_z[k]].astype(bf16)
    z_first = [go(fs_ref.at[k - 1], fb_ref.at[k - 1], to_z[k]) for k in range(1, 4)]

    loads[0].wait()
    loads[1].wait()
    for b in range(2 * rows // BLOCK):
        xt_ref[:, BLOCK * b:BLOCK * b + BLOCK] = x_ref[BLOCK * b:BLOCK * b + BLOCK, :].T
    for m in range(0, width, BLOCK):
        g_ref[m:m + BLOCK, :] = mm(xt_ref[m:m + BLOCK, :], d_ref[2])
    half = own_ref.shape[3]
    lane = lax.broadcasted_iota(jnp.int32, (half, 128), 1)
    for p in range(8):
        for n in range(3):
            low = g_ref[2 * half * p:2 * half * p + half, 128 * n:128 * n + 128]
            high = g_ref[2 * half * p + half:2 * half * (p + 1), 128 * n:128 * n + 128]
            own_ref[p % 2, p // 2, n] = jnp.where(lane < 64, low, pltpu.roll(high, 64, 1))
            oth_ref[p % 2, p // 2, n] = jnp.where(lane < 64, pltpu.roll(low, 64, 1), high).astype(bf16)
    y_far = go(oth_ref.at[1 - x], yb_ref.at[0], to_y)
    y_near = go(oth_ref.at[x], yb_ref.at[1], to_y)

    for copy in loads[2:]:
        copy.wait()
    place = lax.broadcasted_iota(jnp.int32, (32, 2 * rows), 1)
    which = lax.broadcasted_iota(jnp.int32, (32, 2 * rows), 0)
    picks = jnp.where((place == pos_ref[:, 0:1]) | (which == 24), 1.0, 0.0).astype(bf16)
    picked = [mm(picks, d_ref[n]) for n in range(3)]
    own_place = lax.broadcasted_iota(jnp.int32, (32, rows), 1) + inner * rows
    own_picks = jnp.where(own_place == pos_ref[:, 0:1], 1.0, 0.0)
    memory = lax.dot_general(own_picks, dr_ref[...], NN, precision=lax.Precision.HIGHEST, preferred_element_type=f32)
    for n in range(3):
        memory = memory + mm(picked[n].astype(bf16), w_ref[n], NT)
    hw = s_ref.shape[2]

    def put(row, value):
        for h in range(2):
            s_ref[h, row:row + 1, :] = value[:, hw * h:hw * h + hw]
    for h in range(2):
        s_ref[h, 0:24, :] = memory[0:24, hw * h:hw * h + hw]
        s_ref[h, 38:40, :] = jnp.zeros((2, hw), f32)
    for n in range(6):
        put(24 + n, jnp.sum(sums_in[n], axis=0, keepdims=True))
    ups = [jnp.sum(up_in[n], axis=0, keepdims=True) for n in (0, 2, 1, 3)]
    total = [value[24:25, :] for value in picked]
    turned = jnp.concatenate([pltpu.roll(picked[2][24:32, 128 * n:128 * n + 128], 64, 1) for n in range(3)], axis=1)[0:1, :]
    for t in range(4):
        n = (t % 2 + inner) % 2 + 2 * ((t // 2 + outer) % 2)
        value = jnp.zeros_like(ups[0])
        for other in range(4):
            value = value + jnp.where(n == other, ups[other], 0.0)
        put(30 + t, value)
        s_ref[0, 34 + t:35 + t, :] = jnp.where(n == 0, total[0], 0.0) + jnp.where(n == 2, total[1], 0.0)
        s_ref[1, 34 + t:35 + t, :] = jnp.where(n == 0, total[2], 0.0) + jnp.where(n == 2, turned, 0.0)
    small = [go(s_ref.at[1 - inner], r_ref.at[0], to_core)]
    hops = [to_y, to_x, near_z, far_z]

    def hop(n):
        small[n].wait_recv()
        t_ref[n] = (s_ref[inner] if n == 0 else t_ref[n - 1]) + r_ref[n]
        if n < 4:
            small.append(go(t_ref.at[n], r_ref.at[n + 1], hops[n]))
        else:
            small.append(go(t_ref.at[n], r_ref.at[5], to_core))
            small_out[inner] = t_ref[n]

    mine = pl.multiple_of(inner * rows, 1024)
    theirs = pl.multiple_of((1 - inner) * rows, 1024)

    def block(start):
        r = pl.ds(pl.multiple_of(start, BLOCK), BLOCK)
        return mm(d_ref[0, r, :], w_ref[0], NT) + mm(d_ref[1, r, :], w_ref[1], NT) + mm(d_ref[2, r, :], w_ref[2], NT)

    def away(b, carry):
        their_ref[pl.ds(pl.multiple_of(b * BLOCK, BLOCK), BLOCK), :] = block(theirs + b * BLOCK).astype(bf16)
        return carry
    lax.fori_loop(0, rows // BLOCK, away, 0)
    tokens = go(their_ref, got_ref, to_core)
    hop(0)
    y_far.wait_recv()
    for k in range(4):
        xs_ref[k] = (own_ref[1 - x, k] + yb_ref[0, k].astype(f32)).astype(bf16)
    x_sum = go(xs_ref, xb_ref, to_x)

    def stay(b, carry):
        tok_ref[pl.ds(pl.multiple_of(b * BLOCK, BLOCK), BLOCK), :] = block(mine + b * BLOCK)
        return carry
    lax.fori_loop(0, rows // BLOCK, stay, 0)
    hop(1)
    y_near.wait_recv()
    x_sum.wait_recv()
    for k in range(4):
        zt_ref[k] = own_ref[x, k] + yb_ref[1, k].astype(f32) + xb_ref[k].astype(f32)
    for k in range(1, 4):
        zs_ref[k - 1] = zt_ref[up_z[k]].astype(bf16)
    z_second = [go(zs_ref.at[k - 1], zb_ref.at[k - 1], to_z[k]) for k in range(1, 4)]
    hop(2)
    tokens.wait_recv()

    def finish(s, carry):
        r = pl.ds(pl.multiple_of(s * STRIP, STRIP), STRIP)
        tok_ref[r, :] = tok_ref[r, :] + got_ref[r, :].astype(f32) + dr_ref[r, :]
        return carry
    lax.fori_loop(0, rows // STRIP, finish, 0)
    out = pltpu.make_async_copy(tok_ref, tok_out, sem.at[8])
    out.start()
    hop(3)
    for copy in z_first:
        copy.wait_recv()
    first_out[...] = first_ref[z] + fb_ref[0].astype(f32) + fb_ref[1].astype(f32) + fb_ref[2].astype(f32)
    for copy in z_second:
        copy.wait_recv()
    second_out[...] = zt_ref[z] + zb_ref[0].astype(f32) + zb_ref[1].astype(f32) + zb_ref[2].astype(f32)
    hop(4)
    small[5].wait_recv()
    small_out[1 - inner] = r_ref[5]
    for copy in started:
        copy.wait_send()
    out.wait()


def leave(x_all, d, w_qkv, third, first, came, dr1, place, sums, up_sums):
    f32, bf16 = jnp.float32, jnp.bfloat16
    rows, width = dr1.shape
    r, half = first.shape[1], first.shape[1] // 2
    shape, v = jax.ShapeDtypeStruct, pltpu.VMEM
    hbm, vmem = pl.BlockSpec(memory_space=pl.ANY), pl.BlockSpec(memory_space=pltpu.VMEM)
    return pl.pallas_call(
        exit_kernel,
        out_shape=(shape((rows, width), f32), shape((r, 384), f32), shape((3, half, 128), f32), shape((2, 40, width // 2), f32)),
        in_specs=[hbm] * 6 + [vmem] * 2 + [hbm] + [vmem] * 3,
        out_specs=[hbm] + [vmem] * 3,
        scratch_shapes=[
            v((2 * rows, width), bf16), v((width, 2 * rows), bf16), v((3, 2 * rows, 384), bf16), v((3, width, 384), bf16),
            v((rows, width), f32), v((width, 384), f32), v((2, 4, 3, half, 128), f32), v((2, 4, 3, half, 128), bf16),
            v((2, 4, 3, half, 128), bf16), v((4, 3, half, 128), bf16), v((4, 3, half, 128), bf16), v((4, 3, half, 128), f32),
            v((3, 3, half, 128), bf16), v((3, 3, half, 128), bf16), v((3, r, 384), bf16), v((3, r, 384), bf16),
            v((rows, width), bf16), v((rows, width), bf16), v((rows, width), f32), v((2, 40, width // 2), f32),
            v((5, 40, width // 2), f32), v((6, 40, width // 2), f32), v((4, r, 384), f32),
            pltpu.SemaphoreType.DMA((16,)), pltpu.SemaphoreType.DMA((16,)), pltpu.SemaphoreType.DMA((9,)),
        ],
        compiler_params=pltpu.CompilerParams(vmem_limit_bytes=VMEM_MAX, collective_id=2, has_side_effects=True),
        cost_estimate=pl.CostEstimate(flops=2 * rows * width * 384 * 8, bytes_accessed=20_000_000, transcendentals=0),
        name="leave",
    )(x_all, *d, w_qkv, third, first, came, dr1, place, sums, up_sums)


def layer_norm(values, norm_gain, norm_shift):
    centre = values - jnp.mean(values, axis=-1, keepdims=True)
    spread = jnp.mean(centre * centre, axis=-1, keepdims=True)
    return centre * lax.rsqrt(spread + EPSILON) * norm_gain + norm_shift


def gelu_exact(values):
    return jax.nn.gelu(values, approximate=False)


AXES = ("dp", "tensor")


class Grid:
    def __init__(self, dp, tensor):
        self.dp, self.tensor = dp, tensor
        factors, rest = [2], dp // 2
        while rest > 8:
            factors.insert(0, 4)
            rest //= 4
        if rest > 1:
            factors.insert(0, rest)
        self.factors = factors

    def digit(self, j):
        stride = 1
        for f in self.factors[j + 1:]:
            stride *= f
        return stride, self.factors[j]

    def my_digit(self, j):
        stride, f = self.digit(j)
        return lax.axis_index("dp") // stride % f

    def turn(self, value, j, k):
        stride, f = self.digit(j)
        pairs = []
        for d in range(self.dp):
            g = d // stride % f
            to = d + ((g + k) % f - g) * stride
            for t in range(self.tensor):
                pairs.append((d * self.tensor + t, to * self.tensor + t))
        return lax.ppermute(value, AXES, pairs)

    def swap_dp(self, value, bit):
        pairs = [(d * self.tensor + t, (d ^ bit) * self.tensor + t) for d in range(self.dp) for t in range(self.tensor)]
        return lax.ppermute(value, AXES, pairs)

    def swap(self, value, bit):
        pairs = [(d * self.tensor + t, d * self.tensor + (t ^ bit)) for d in range(self.dp) for t in range(self.tensor)]
        return lax.ppermute(value, AXES, pairs)

    def gather_stage(self, value, j, axis):
        _, f = self.digit(j)
        g = self.my_digit(j)
        got = [value] + [self.turn(value, j, k) for k in range(1, f)]
        if f == 2:
            lower = jnp.where(g == 0, got[0], got[1])
            upper = jnp.where(g == 0, got[1], got[0])
            return jnp.stack([lower, upper], axis=axis)
        ring = got[::-1]
        return lax.dynamic_slice_in_dim(jnp.stack(ring + ring[:-1], axis=axis), f - 1 - g, f, axis)

    def gather(self, shard, outer_first=False):
        count = len(self.factors)
        value = shard
        for j in range(count - 1):
            value = self.gather_stage(value, j, j)
        if outer_first:
            value = jnp.stack([value, self.swap(value, 2)])
            value = self.gather_stage(value, count - 1, count)
            return value.reshape(2, -1, shard.shape[-1])
        value = self.gather_stage(value, count - 1, count - 1)
        value = value.reshape(-1, shard.shape[-1])
        return jnp.stack([value, self.swap(value, 2)])

    def reduce_stage(self, value, j, axis):
        _, f = self.digit(j)
        g = self.my_digit(j)
        total = lax.dynamic_index_in_dim(value, g, axis, keepdims=False).astype(jnp.float32)
        for k in range(1, f):
            part = lax.dynamic_index_in_dim(value, (g + k) % f, axis, keepdims=False)
            total = total + self.turn(part.astype(jnp.bfloat16), j, k).astype(jnp.float32)
        return total

    def reduce(self, parts, outer_first=True):
        count = len(self.factors)
        columns = parts.shape[-1]
        value = parts
        if outer_first:
            value = value[0].astype(jnp.float32) + self.swap(value[1].astype(jnp.bfloat16), 2).astype(jnp.float32)
            value = value.reshape(*self.factors, -1, columns)
            value = self.reduce_stage(value, count - 1, count - 1)
        else:
            value = value.reshape(2, *self.factors, -1, columns)
            value = self.reduce_stage(value, count - 1, count)
            value = value[0] + self.swap(value[1].astype(jnp.bfloat16), 2).astype(jnp.float32)
        for j in reversed(range(count - 1)):
            value = self.reduce_stage(value, j, j)
        return value

    @property
    def stages(self):
        return len(self.factors) + 1

    def open(self, parts, outer_first):
        columns = parts.shape[-1]
        return parts if outer_first else parts.reshape(2, *self.factors, -1, columns)

    def stage(self, value, outer_first, n):
        count = len(self.factors)
        if n == (0 if outer_first else 1):
            value = value[0].astype(jnp.float32) + self.swap(value[1].astype(jnp.bfloat16), 2).astype(jnp.float32)
            return value.reshape(*self.factors, -1, value.shape[-1]) if outer_first else value
        if n == 0:
            return self.reduce_stage(value, count - 1, count)
        return self.reduce_stage(value, count - n, count - n)

    def total(self, vector):
        for bit in (1, 2):
            vector = vector + self.swap(vector, bit)
        bit = 1
        while bit < self.dp:
            vector = vector + self.swap_dp(vector, bit)
            bit *= 2
        return vector


def shards(grid, tokens, segment_ids, memory_positions, memory_rows, qkv_weight, qv_bias, out_weight, out_bias,
           norm1_gain, norm1_bias, up_weight, up_bias, down_weight, down_bias, norm2_gain, norm2_bias, out_cotangent):
    f32, bf16 = jnp.float32, jnp.bfloat16
    rows, width = tokens.shape
    group_len = segment_ids.shape[1]
    tensor = lax.axis_index("tensor")
    inner, outer = tensor % 2, tensor // 2
    slice_rows = qkv_weight.shape[0]
    heads = qkv_weight.shape[1]
    hd = 64
    hw = heads * hd
    units = up_weight.shape[1]

    segments = lax.dynamic_index_in_dim(segment_ids, outer, 0, keepdims=False)
    positions = lax.dynamic_index_in_dim(memory_positions, outer, 0, keepdims=False)
    row_place = inner * rows + jnp.arange(rows, dtype=jnp.int32)
    picks = (row_place[:, None] == positions[None, :])
    joined = lambda w: w.transpose(1, 0, 2).reshape(width, -1)

    parts = qkv_weight.reshape(slice_rows, heads, 3, hd)
    order_columns = lambda p: jnp.concatenate([p[..., :2, n, :].reshape(*p.shape[:-3], 2 * hd) for n in range(3)]
                                              + [p[..., 2, n, :] for n in range(3)], axis=-1)
    shard_qkv = order_columns(parts)
    shard_out = jnp.pad(out_weight.reshape(slice_rows, hw), ((0, 0), (0, 256 - hw)))
    bias_parts = qv_bias.reshape(heads, 2, hd)
    bias_qkv = order_columns(jnp.stack([bias_parts[:, 0], jnp.zeros_like(bias_parts[:, 0]), bias_parts[:, 1]], 1))
    bias_qkv = jnp.pad(bias_qkv[None], ((0, 15), (0, 64)))
    own_up_bias = jnp.broadcast_to(up_bias[None], (16, units))
    fused = grid.dp == 8 and grid.tensor == 4
    if fused:
        memory = memory_positions.shape[1]
        place = jnp.pad(positions[None], ((0, 7), (0, 32 - memory)), constant_values=-1)
        table = jnp.pad(memory_rows, ((0, 32 - memory), (0, 0)))
        x0, x_all, q, k, v, w_qkv, up_g, down_g, out_g, b_up = entry(tokens, place, table, shard_qkv, bias_qkv, own_up_bias, up_weight, down_weight, shard_out)
        column = jnp.pad(jnp.broadcast_to(positions[:, None], (memory, 128)), ((0, 32 - memory), (0, 0)), constant_values=-1)
        w_qkv = w_qkv.reshape(2, width, 9 * hd)
        third = jnp.concatenate([w_qkv[o][:, (6 + n) * hd:(7 + n) * hd] for n in range(3) for o in range(2)], 1)
        up_all = up_g.reshape(width, units)
        ups = (up_all, grid.swap(up_all, 2))
        down_pair = down_g.reshape(-1, units)
        downs = (down_pair, *[grid.turn(down_pair, 0, k) for k in range(1, 4)])
        outs = (out_g, grid.turn(out_g, 1, 1))
    else:
        x0 = tokens.astype(f32) + jnp.dot(picks.astype(bf16), memory_rows, preferred_element_type=f32)
        xl = x0.astype(bf16)
        w_qkv = grid.gather(shard_qkv)
        other = grid.swap(xl, 1)
        x_all = jnp.concatenate([jnp.where(inner == 0, xl, other), jnp.where(inner == 0, other, xl)])
        b_two = jnp.stack([bias_qkv[0], grid.swap(bias_qkv[0], 2)]).astype(f32)
        y = [(mm(x_all, w_qkv[o]) + b_two[o, :9 * hd]).astype(bf16) for o in range(2)]
        third = lambda n: [one[:, (6 + n) * hd:(7 + n) * hd] for one in y]
        q, k, v = [jnp.concatenate([y[0][:, 2 * n * hd:2 * (n + 1) * hd], y[1][:, 2 * n * hd:2 * (n + 1) * hd]] + third(n), 1)
                   for n in range(3)]
        q = q * jnp.asarray(0.125, bf16)
        b_up = jnp.stack([own_up_bias, grid.swap(own_up_bias, 2)])
        b_up = jnp.concatenate([b_up, grid.swap(b_up, 1)])
        outs, ups, downs = (grid.gather(shard_out, True),), (grid.gather(up_weight),), (grid.gather(down_weight, True),)
    mixed, lse = attend_forward(q, k, v, segments)
    vec = jnp.stack([out_bias, norm1_gain, norm1_bias, down_bias, norm2_gain, norm2_bias, norm2_bias, norm2_bias]).astype(f32)
    (block_out, dr1, do_all, *grads, sums, up_sums) = middle(
        mixed, x0, outs, ups, downs, out_cotangent, vec, b_up)
    if fused:
        return finish_small(grid, tensor, x_all, q, k, v, do_all, mixed, lse, segments, w_qkv, third, dr1, column, sums, up_sums, block_out,
                            grads, hw)
    g_down, g_up, g_out = grads

    TN = (((0,), (0,)), ((), ()))
    tie = lax.optimization_barrier
    kinds = (True, False, True)
    state = [grid.open(parts, kind) for parts, kind in zip((g_down, g_up, g_out), kinds)]
    step = lambda n, state: [grid.stage(value, kind, n) for value, kind in zip(state, kinds)]
    late = [(1, 0, 2)[n] for n in range(3)]
    d = [None] * 3
    state, d[1] = step(0, state), attend_backward(1, q, k, v, do_all, mixed, lse, segments)
    state, d[1], q = tie((state, d[1], q))
    g_one = mm(x_all, d[1], TN).astype(bf16)
    state, d[0] = step(1, state), attend_backward(0, q, k, v, do_all, mixed, lse, segments)
    state, d[0], q, g_one = tie((state, d[0], q, g_one))
    g_zero = mm(x_all, d[0], TN)
    first = g_zero + grid.swap(g_one, 2).astype(f32)
    state, d[2] = step(2, state), attend_backward(2, q, k, v, do_all, mixed, lse, segments)
    state, d[2], first = tie((state, d[2], first))
    for n in range(3, grid.stages):
        state = step(n, state)
    grad_down, grad_up, grad_out = state
    grad_out = grad_out[:, :hw]

    g_two = mm(x_all, d[2], TN)
    side = lambda m, o: jnp.concatenate([m[:, (2 * n + o) * hd:(2 * n + o + 1) * hd] for n in range(3)], 1)
    second = side(g_two, 0) + grid.swap(side(g_two, 1).astype(bf16), 2).astype(f32)
    both = jnp.concatenate([first, second], 1).reshape(*grid.factors, slice_rows, 9 * hd)
    for j in reversed(range(len(grid.factors))):
        both = grid.reduce_stage(both, j, j)
    restore = lambda p: jnp.stack([jnp.concatenate([p[..., 2 * n * hd:2 * (n + 1) * hd].reshape(*p.shape[:-1], 2, hd),
                                                    p[..., None, (6 + n) * hd:(7 + n) * hd]], -2) for n in range(3)], -2)
    grad_qkv = restore(both).reshape(slice_rows, heads, 3 * hd)
    third = jnp.concatenate([w_qkv[o][:, (6 + n) * hd:(7 + n) * hd] for n in range(3) for o in range(2)], 1)
    part = (mm(d[0], w_qkv[0][:, :6 * hd], NT) + mm(d[1], w_qkv[1][:, :6 * hd], NT) + mm(d[2], third, NT)).reshape(2, rows, width)
    mine = lax.dynamic_index_in_dim(part, inner, 0, keepdims=False)
    theirs = lax.dynamic_index_in_dim(part, 1 - inner, 0, keepdims=False).astype(bf16)
    grad_tokens = mine + grid.swap(theirs, 1).astype(f32) + dr1
    d_sum = [jnp.sum(one.astype(f32), axis=0) for one in d]
    d_bias = [jnp.concatenate([d_sum[o]] + [d_sum[2][(2 * n + o) * hd:(2 * n + o + 1) * hd] for n in range(3)]) for o in range(2)]
    dg2, ds2, d_down_bias, dg1, ds1, d_out_bias = jnp.sum(sums, axis=1)
    d_up_bias = jnp.sum(up_sums, axis=1).reshape(2, 2 * units)
    grad_memory = jnp.dot(picks.astype(f32).T, grad_tokens, precision=lax.Precision.HIGHEST)

    order = jnp.arange(4, dtype=jnp.int32) ^ tensor
    up_parts = d_up_bias.reshape(2, 2, units)
    up_parts = jnp.stack([up_parts[0, 0], up_parts[1, 0], up_parts[0, 1], up_parts[1, 1]])[order]
    take = lambda o: restore(d_bias[o])[:, 0::2].reshape(-1)
    blank = jnp.zeros((2 * hw,), f32)
    qv_parts = jnp.stack([take(0), blank, take(1), blank])[order]
    pieces = [grad_memory.reshape(-1), d_out_bias, dg1, ds1, d_down_bias, dg2, ds2, up_parts.reshape(-1), qv_parts.reshape(-1)]
    summed = grid.total(jnp.concatenate(pieces))
    outs, at = [], 0
    for piece in pieces:
        outs.append(lax.slice_in_dim(summed, at, at + piece.size))
        at += piece.size
    t_memory, t_out_bias, t_g1, t_s1, t_down_bias, t_g2, t_s2, t_up, t_qv = outs
    grad_up_bias = lax.dynamic_index_in_dim(t_up.reshape(4, units), tensor, 0, keepdims=False)
    grad_qv = lax.dynamic_index_in_dim(t_qv.reshape(4, heads, 2 * hd), tensor, 0, keepdims=False)
    return (block_out, grad_tokens, t_memory.reshape(-1, width), grad_qkv, grad_qv,
            grad_out.reshape(slice_rows, heads, hd), t_out_bias, t_g1, t_s1, grad_up, grad_up_bias, grad_down,
            t_down_bias, t_g2, t_s2)


def blend_one_kernel(x_ref, down, down_early, down_late, up, up_in, out, out_in, kept_down, kept_up, kept_out, send_x, send_y):
    f32, bf16 = jnp.float32, jnp.bfloat16
    x = x_ref[0]
    width = down.shape[-1]
    add = lambda a, b: a.astype(f32) + b.astype(f32)
    early = pl.program_id(0) < pl.num_programs(0) // 2
    down_in = lambda n: jnp.where(early, down_early[0, n], down_late[0, n])
    kept_down[0] = add(down[0, x], down_in(x))
    kept_out[0] = add(out[0, x], out_in[0, x])
    send_x[0, :, 0:width] = add(down[0, 1 - x], down_in(1 - x)).astype(bf16)
    send_x[0, :, width:] = add(out[0, 1 - x], out_in[0, 1 - x]).astype(bf16)
    kept_up[0] = add(up[0, 0], up_in[0, 0])
    send_y[0] = add(up[1, 0], up_in[1, 0]).astype(bf16)


def blend_one(x, down, down_early, down_late, up, up_in, out, out_in):
    f32, bf16 = jnp.float32, jnp.bfloat16
    _, zs, r, width = up.shape
    ow = out.shape[-1]
    shape = jax.ShapeDtypeStruct
    by_x = lambda columns: pl.BlockSpec((1, 2, r, columns), lambda j, *_: (j, 0, 0, 0))
    by_y = pl.BlockSpec((2, 1, r, width), lambda j, *_: (0, j, 0, 0))
    one = lambda columns: pl.BlockSpec((1, r, columns), lambda j, *_: (j, 0, 0))
    lower = pl.BlockSpec((1, 2, r, width), lambda j, *_: (jnp.minimum(j, zs // 2 - 1), 0, 0, 0))
    upper = pl.BlockSpec((1, 2, r, width), lambda j, *_: (jnp.maximum(j - zs // 2, 0), 0, 0, 0))
    fold = lambda a: a.reshape(-1, 2, r, a.shape[-1])
    return pl.pallas_call(
        blend_one_kernel,
        out_shape=(shape((zs, r, width), f32), shape((zs, r, width), f32), shape((zs, r, ow), f32),
                   shape((zs, r, width + ow), bf16), shape((zs, r, width), bf16)),
        grid_spec=pltpu.PrefetchScalarGridSpec(
            num_scalar_prefetch=1, grid=(zs,),
            in_specs=[by_x(width), lower, upper, by_y, by_y, by_x(ow), by_x(ow)],
            out_specs=[one(width), one(width), one(ow), one(width + ow), one(width)]),
        compiler_params=pltpu.CompilerParams(dimension_semantics=("arbitrary",), vmem_limit_bytes=VMEM_MAX),
        cost_estimate=pl.CostEstimate(flops=8 * zs * r * width, bytes_accessed=10_000_000, transcendentals=0),
        name="blend_one",
    )(x.reshape(1), fold(down), fold(down_early), fold(down_late), up, up_in, fold(out), fold(out_in))


def blend_two_kernel(at_ref, kept_down, kept_up, kept_out, came_x, came_y, first, kept_z, kept_first, *sends):
    f32, bf16 = jnp.float32, jnp.bfloat16
    x, z = at_ref[0], at_ref[1]
    zs, r, width = kept_down.shape
    for k in range(zs):
        n = (z + k) % zs
        parts = (kept_down[n] + came_x[n, :, 0:width].astype(f32), kept_up[n] + came_y[n].astype(f32),
                 kept_out[n] + came_x[n, :, width:].astype(f32))
        start = 0
        for part in parts:
            stop = start + part.shape[1]
            if k == 0:
                kept_z[:, start:stop] = part
            else:
                sends[k - 1][:, start:stop] = part.astype(bf16)
            start = stop
        kept_first[k] = first[k, x]
        sends[zs - 1][k] = first[k, 1 - x].astype(bf16)


def blend_two(x, z, kept_down, kept_up, kept_out, came_x, came_y, first):
    f32, bf16 = jnp.float32, jnp.bfloat16
    zs, r, width = kept_down.shape
    columns = 2 * width + kept_out.shape[-1]
    shape = jax.ShapeDtypeStruct
    vmem = pl.BlockSpec(memory_space=pltpu.VMEM)
    return pl.pallas_call(
        blend_two_kernel,
        out_shape=(shape((r, columns), f32), shape((zs, r, first.shape[-1]), f32), *[shape((r, columns), bf16)] * (zs - 1),
                   shape((zs, r, first.shape[-1]), bf16)),
        in_specs=[pl.BlockSpec(memory_space=pltpu.SMEM)] + [vmem] * 6,
        out_specs=[vmem] * (zs + 2),
        compiler_params=pltpu.CompilerParams(vmem_limit_bytes=VMEM_MAX),
        cost_estimate=pl.CostEstimate(flops=4 * zs * r * columns, bytes_accessed=10_000_000, transcendentals=0),
        name="blend_two",
    )(jnp.stack([x, z]), kept_down, kept_up, kept_out, came_x, came_y, first.reshape(zs, 2, r, first.shape[-1]))


def spread_kernel(t_ref, kept, came_one, came_two, came_three, small, down, up, out, memory, vec, up_bias, qv):
    f32 = jnp.float32
    width = down.shape[1]
    for ref, start in ((down, 0), (up, width), (out, 2 * width)):
        cols = slice(start, start + ref.shape[1])
        ref[...] = (kept[:, cols] + came_one[:, cols].astype(f32)) + (came_two[:, cols].astype(f32) + came_three[:, cols].astype(f32))
    half = width // 2
    t = t_ref[0]
    for h in range(2):
        cols = slice(half * h, half * h + half)
        memory[:, cols] = small[h, 0:memory.shape[0], :]
        vec[:, cols] = small[h, 24:32, :]
        up_bias[:, cols] = small[h, pl.ds(30 + t, 1), :]
        qv[h:h + 1, :] = small[h, pl.ds(34 + t, 1), :]


def spread(tensor, kept, came, small, memory, ow):
    f32 = jnp.float32
    r, columns = kept.shape
    width = 2 * small.shape[2]
    shape = jax.ShapeDtypeStruct
    vmem = pl.BlockSpec(memory_space=pltpu.VMEM)
    return pl.pallas_call(
        spread_kernel,
        out_shape=(shape((r, width), f32), shape((r, width), f32), shape((r, ow), f32), shape((memory, width), f32),
                   shape((8, width), f32), shape((1, width), f32), shape((2, width // 2), f32)),
        in_specs=[pl.BlockSpec(memory_space=pltpu.SMEM)] + [vmem] * 5,
        out_specs=[vmem] * 7,
        compiler_params=pltpu.CompilerParams(vmem_limit_bytes=VMEM_MAX),
        cost_estimate=pl.CostEstimate(flops=3 * r * columns, bytes_accessed=3_000_000, transcendentals=0),
        name="spread",
    )(tensor.reshape(1), kept, *came, small)


def finish_small(grid, tensor, x_all, q, k, v, do_all, mixed, lse, segments, w_qkv, third, dr1, column, sums, up_sums, block_out,
                 grads, hw):
    f32, bf16 = jnp.float32, jnp.bfloat16
    tie = lax.optimization_barrier
    TN = (((0,), (0,)), ((), ()))
    width = dr1.shape[1]
    x, z = lax.axis_index("dp") % 2, lax.axis_index("dp") // 2
    down, down_far, down_early, up, up_far, out, out_far = grads

    def beside(pair, q, sends):
        arrays, q = tie(([a for a, _ in sends], q))
        came = [move(a) for a, (_, move) in zip(arrays, sends)]
        d = attend_backward(pair, q, k, v, do_all, mixed, lse, segments)
        return tie((came, d, q))

    over_y = lambda a: grid.swap(a, 2)
    over_x = lambda a: grid.turn(a, 1, 1)
    (down_in, out_in, up_in), d_one, q = beside(1, q, [(down_far, over_y), (out_far, over_y), (up_far, over_x)])
    g_one = mm(x_all, d_one, TN).astype(bf16)
    kept_down, kept_up, kept_out, send_x, send_y = blend_one(x, down, down_early, down_in, up, up_in, out, out_in)
    (came_x, came_y, came_one), d_zero, q = beside(0, q, [(send_x, over_x), (send_y, over_y), (g_one, over_y)])
    first = mm(x_all, d_zero, TN) + came_one.astype(f32)
    kept, kept_first, *sends = blend_two(x, z, kept_down, kept_up, kept_out, came_x, came_y, first)
    over_z = [lambda a, n=n: grid.turn(a, 0, n) for n in range(1, 4)]
    came, d_two, q = beside(2, q, list(zip(sends, over_z + [over_x])))
    grad_tokens, one, two, small = leave(x_all, (d_zero, d_one, d_two), w_qkv, third, kept_first, came[3], dr1, column, sums, up_sums)
    grad_down, grad_up, grad_out, grad_memory, vec, up_bias, qv = spread(tensor, kept, came[:3], small, 20, out.shape[-1])
    hd = 64
    slice_rows = one.shape[0]
    two = two.reshape(3, slice_rows // 2, 2, hd).transpose(2, 1, 0, 3).reshape(slice_rows, 1, 3, hd)
    grad_qkv = jnp.concatenate([one.reshape(slice_rows, 3, 2, hd).transpose(0, 2, 1, 3), two], 1).reshape(slice_rows, 3, 3 * hd)
    part = lambda n: jnp.concatenate([qv[0, 128 * n:128 * n + 128].reshape(2, hd), qv[1:2, 128 * n:128 * n + hd]])
    grad_qv = jnp.concatenate([part(0), part(2)], 1)
    t_out_bias, t_g1, t_s1, t_down_bias, t_g2, t_s2 = [vec[n] for n in (5, 3, 4, 2, 0, 1)]
    return (block_out, grad_tokens, grad_memory, grad_qkv, grad_qv,
            grad_out[:, :hw].reshape(slice_rows, 3, hd), t_out_bias, t_g1, t_s1, grad_up, up_bias.reshape(width), grad_down,
            t_down_bias, t_g2, t_s2)


def solution(mesh):
    grid = Grid(mesh.shape["dp"], mesh.shape["tensor"])
    tokens, dp, none = P(AXES, None), P("dp", None), P()
    heads, matrix = P("dp", "tensor", None), P("dp", "tensor")
    in_specs = (tokens, dp, dp, none, heads, P("tensor", None), heads, none, none, none, matrix, P("tensor"), matrix,
                none, none, none, tokens)
    out_specs = (tokens, tokens, none, heads, P("tensor", None), heads, none, none, none, matrix, P("tensor"), matrix,
                 none, none, none)

    def run(*args):
        return shards(grid, *args)

    return jax.shard_map(run, mesh=mesh, in_specs=in_specs, out_specs=out_specs, check_vma=False)
```

```python
import functools

import jax
import jax.numpy as jnp
from jax import lax
from jax.experimental import pallas as pl
from jax.experimental.pallas import tpu as pltpu
from jax.sharding import PartitionSpec as P

EPSILON = 1e-12
TILE = 256
MASKED = -1e30
VMEM_MAX = 64 * 1024 * 1024 - 128 * 1024
NT = (((1,), (1,)), ((), ()))
NN = (((1,), (0,)), ((), ()))


def mm(a, b, dims=NN):
    return lax.dot_general(a, b, dims, preferred_element_type=jnp.float32)


def fold8(x):
    r = x.shape[0]
    return x.reshape(r // 8, 8, x.shape[1])


def head_masks(block):
    lane = lax.broadcasted_iota(jnp.int32, block.shape, 1)
    zero = jnp.zeros_like(block)
    return jnp.where(lane < 64, block, zero), jnp.where(lane < 64, zero, block)


def tile_visible(first_ref, last_ref, i, t):
    return (first_ref[t] == 0) | ((first_ref[t] <= last_ref[i]) & (last_ref[t] >= first_ref[i]))


def forward_kernel(first_ref, last_ref, q_ref, k_ref, v_ref, kseg_ref, qseg_ref, o_ref, lse_ref,
                   vt_ref, qm_ref, s_ref, m_ref, l_ref, acc_ref):
    i = pl.program_id(0)
    tiles = pl.num_programs(0)
    pairs = q_ref.shape[1] // 128
    heads = 2 * pairs

    @pl.when(i == 0)
    def _():
        def turn(t, c):
            rows = pl.ds(pl.multiple_of(t * TILE, TILE), TILE)
            vt_ref[t] = v_ref[rows, :].T
            return c
        lax.fori_loop(0, tiles, turn, 0)

    for g in range(pairs):
        a, b = head_masks(q_ref[:, 128 * g:128 * g + 128])
        qm_ref[2 * g] = a
        qm_ref[2 * g + 1] = b
    m_ref[...] = jnp.full_like(m_ref, MASKED)
    l_ref[...] = jnp.zeros_like(l_ref)
    acc_ref[...] = jnp.zeros_like(acc_ref)
    qseg = qseg_ref[0:1, :]

    def scores(t, c):
        @pl.when(tile_visible(first_ref, last_ref, i, t))
        def _():
            rows = pl.ds(pl.multiple_of(t * TILE, TILE), TILE)
            kseg = kseg_ref[rows, :]
            kseg = jnp.concatenate([kseg, kseg], axis=1)
            seen = (kseg == 0) | (kseg == qseg)
            for h in range(heads):
                kp = k_ref[rows, 128 * (h // 2):128 * (h // 2) + 128]
                s = mm(kp, qm_ref[h], NT)
                s = jnp.where(seen, s, MASKED)
                s_ref[h, t] = s
                m_ref[h] = jnp.maximum(m_ref[h], jnp.max(fold8(s), axis=0))
        return c
    lax.fori_loop(0, tiles, scores, 0)
    for h in range(heads):
        m_ref[h] = jnp.broadcast_to(jnp.max(m_ref[h], axis=0, keepdims=True), (8, TILE))

    def mix(t, c):
        @pl.when(tile_visible(first_ref, last_ref, i, t))
        def _():
            for h in range(heads):
                p = jnp.exp(s_ref[h, t] - m_ref[h, 0:1, :])
                l_ref[h] = l_ref[h] + jnp.sum(fold8(p), axis=0)
                acc_ref[h] = acc_ref[h] + mm(vt_ref[t, 64 * h:64 * h + 64, :], p.astype(jnp.bfloat16))
        return c
    lax.fori_loop(0, tiles, mix, 0)
    for h in range(heads):
        total = jnp.sum(l_ref[h], axis=0, keepdims=True)
        lse_ref[h:h + 1, :] = m_ref[h, 0:1, :] + jnp.log(total)
        acc_ref[h] = acc_ref[h] / total
    for g in range(pairs):
        pair = jnp.concatenate([acc_ref[2 * g], acc_ref[2 * g + 1]], axis=0)
        o_ref[:, 128 * g:128 * g + 128] = pair.T.astype(jnp.bfloat16)


def attend_forward(q, k, v, seg):
    n, width = q.shape
    tiles = n // TILE
    heads = width // 64
    first = seg[::TILE]
    last = seg[TILE - 1::TILE]
    kseg = jnp.broadcast_to(seg[:, None], (n, 128))
    qseg = jnp.broadcast_to(seg[None, :], (8, n))
    whole = lambda shape: pl.BlockSpec(shape, lambda i, *_: (0,) * len(shape))
    return pl.pallas_call(
        forward_kernel,
        out_shape=(jax.ShapeDtypeStruct((n, width), jnp.bfloat16), jax.ShapeDtypeStruct((8, n), jnp.float32)),
        grid_spec=pltpu.PrefetchScalarGridSpec(
            num_scalar_prefetch=2, grid=(tiles,),
            in_specs=[pl.BlockSpec((TILE, width), lambda i, *_: (i, 0)), whole((n, width)), whole((n, width)),
                      whole((n, 128)), pl.BlockSpec((8, TILE), lambda i, *_: (0, i))],
            out_specs=[pl.BlockSpec((TILE, width), lambda i, *_: (i, 0)), pl.BlockSpec((8, TILE), lambda i, *_: (0, i))],
            scratch_shapes=[
                pltpu.VMEM((tiles, width, TILE), jnp.bfloat16),
                pltpu.VMEM((heads, TILE, 128), jnp.bfloat16),
                pltpu.VMEM((heads, tiles, TILE, TILE), jnp.float32),
                pltpu.VMEM((heads, 8, TILE), jnp.float32),
                pltpu.VMEM((heads, 8, TILE), jnp.float32),
                pltpu.VMEM((heads, 64, TILE), jnp.float32),
            ]),
        compiler_params=pltpu.CompilerParams(dimension_semantics=("arbitrary",), vmem_limit_bytes=VMEM_MAX),
        cost_estimate=pl.CostEstimate(flops=4 * n * n * width, bytes_accessed=8 * n * width, transcendentals=n * n * heads),
        name="attend_forward",
    )(first, last, q, k, v, kseg, qseg)


def backward_kernel(base, first_ref, last_ref, q_ref, do_ref, o_ref, k_ref, v_ref, kseg_ref, qseg_ref, lse_ref,
                    d_ref, kt_ref, qm_ref, dom_ref, delta_ref, dqt_ref, dka_ref, dva_ref):
    i = pl.program_id(0)
    tiles = pl.num_programs(0)

    @pl.when(i == 0)
    def _():
        def turn(t, c):
            rows = pl.ds(pl.multiple_of(t * TILE, TILE), TILE)
            kt_ref[t] = k_ref[rows, :].T
            dka_ref[rows, :] = jnp.zeros((TILE, 128), jnp.float32)
            dva_ref[rows, :] = jnp.zeros((TILE, 128), jnp.float32)
            return c
        lax.fori_loop(0, tiles, turn, 0)

    for ref, masked in ((q_ref, qm_ref), (do_ref, dom_ref)):
        masked[0], masked[1] = head_masks(ref[...])
    inner = (do_ref[...].astype(jnp.float32) * o_ref[...].astype(jnp.float32)).T
    for h in range(2):
        delta_ref[h] = jnp.broadcast_to(jnp.sum(inner[64 * h:64 * h + 64], axis=0, keepdims=True), (8, TILE))
    dqt_ref[...] = jnp.zeros_like(dqt_ref)
    qseg = qseg_ref[0:1, :]

    def count(t, c):
        prompt, before, upto = c
        return (prompt + (first_ref[t] == 0).astype(jnp.int32), before + (last_ref[t] < first_ref[i]).astype(jnp.int32),
                upto + (first_ref[t] <= last_ref[i]).astype(jnp.int32))
    zero = jnp.int32(0)
    prompt, before, upto = lax.fori_loop(0, tiles, count, (zero, zero, zero))
    start = jnp.maximum(prompt, before)
    visible = prompt + jnp.maximum(upto - start, 0)

    def one_tile(n):
        t = jnp.where(n < prompt, n, start + n - prompt)
        rows = pl.ds(pl.multiple_of(t * TILE, TILE), TILE)
        kseg = kseg_ref[rows, :]
        kseg = jnp.concatenate([kseg, kseg], axis=1)
        seen = (kseg == 0) | (kseg == qseg)
        kp = k_ref[rows, :]
        vp = v_ref[rows, :]
        s = [mm(kp, qm_ref[h], NT) for h in range(2)]
        d = [mm(vp, dom_ref[h], NT) for h in range(2)]
        p = [jnp.where(seen, jnp.exp(s[h] - lse_ref[base + h:base + h + 1, :]), 0.0) for h in range(2)]
        ds = [(p[h] * (d[h] - delta_ref[h, 0:1, :])).astype(jnp.bfloat16) for h in range(2)]
        p = [value.astype(jnp.bfloat16) for value in p]
        dva_ref[rows, :] = dva_ref[rows, :] + (mm(p[0], dom_ref[0]) + mm(p[1], dom_ref[1]))
        dka_ref[rows, :] = dka_ref[rows, :] + (mm(ds[0], qm_ref[0]) + mm(ds[1], qm_ref[1]))
        return [mm(kt_ref[t, 64 * h:64 * h + 64, :], ds[h]) for h in range(2)]

    def two_tiles(n, c):
        one, two = one_tile(2 * n), one_tile(2 * n + 1)
        for h in range(2):
            dqt_ref[h] = dqt_ref[h] + (one[h] + two[h])
        return c
    lax.fori_loop(0, visible // 2, two_tiles, 0)

    @pl.when(visible % 2 == 1)
    def _():
        for h, value in enumerate(one_tile(visible - 1)):
            dqt_ref[h] = dqt_ref[h] + value
    pair = jnp.concatenate([dqt_ref[0], dqt_ref[1]], axis=0)
    own = pl.ds(pl.multiple_of(i * TILE, TILE), TILE)
    d_ref[own, 0:128] = (pair.T * 0.125).astype(jnp.bfloat16)

    @pl.when(i == tiles - 1)
    def _():
        d_ref[:, 128:256] = dka_ref[...].astype(jnp.bfloat16)
        d_ref[:, 256:384] = dva_ref[...].astype(jnp.bfloat16)


def attend_backward(g, q, k, v, do, o, lse, seg):
    n, width = q.shape[0], 128
    tiles = n // TILE
    heads = width // 64
    first = seg[::TILE]
    last = seg[TILE - 1::TILE]
    kseg = jnp.broadcast_to(seg[:, None], (n, 128))
    qseg = jnp.broadcast_to(seg[None, :], (8, n))
    whole = lambda shape: pl.BlockSpec(shape, lambda i, *_: (0,) * len(shape))
    rows = pl.BlockSpec((TILE, width), lambda i, *_: (i, g))
    column = pl.BlockSpec((n, width), lambda i, *_: (0, g))
    stat = pl.BlockSpec((8, TILE), lambda i, *_: (0, i))
    return pl.pallas_call(
        functools.partial(backward_kernel, 2 * g),
        out_shape=jax.ShapeDtypeStruct((n, 3 * width), jnp.bfloat16),
        grid_spec=pltpu.PrefetchScalarGridSpec(
            num_scalar_prefetch=2, grid=(tiles,),
            in_specs=[rows, rows, rows, column, column, whole((n, 128)), stat, stat],
            out_specs=whole((n, 3 * width)),
            scratch_shapes=[
                pltpu.VMEM((tiles, width, TILE), jnp.bfloat16),
                pltpu.VMEM((heads, TILE, 128), jnp.bfloat16),
                pltpu.VMEM((heads, TILE, 128), jnp.bfloat16),
                pltpu.VMEM((heads, 8, TILE), jnp.float32),
                pltpu.VMEM((heads, 64, TILE), jnp.float32),
                pltpu.VMEM((n, width), jnp.float32),
                pltpu.VMEM((n, width), jnp.float32),
            ]),
        compiler_params=pltpu.CompilerParams(dimension_semantics=("arbitrary",), vmem_limit_bytes=VMEM_MAX),
        cost_estimate=pl.CostEstimate(flops=10 * n * n * width, bytes_accessed=14 * n * width, transcendentals=n * n * heads),
        name="attend_backward",
    )(first, last, q, do, o, k, v, kseg, qseg, lse)


BLOCK = 256
STRIP = 64


def normal_cdf_parts(u):
    v = u * 0.7071067811865476
    c = jnp.clip(v, -3.832506856900711, 3.832506856900711)
    c2 = c * c
    top = 0.00022905065861350646
    for a in (0.0034082910107109506, 0.050955695062380861, 0.18520832239976145, 1.128379143519084):
        top = top * c2 + a
    low = -1.1791602954361697e-7
    for b in (0.000023547966471313185, 0.0010179625278914885, 0.014070470171167667, 0.11098505178285362,
              0.49746925110067538, 1.0):
        low = low * c2 + b
    cdf = 0.5 + 0.5 * (c * top / low)
    slope = jnp.exp(-(v * v)) * (u * 0.3989422804014327)
    return u * cdf, cdf + slope


def middle_kernel(pieces, o_all, x0, outs, ups, downs, cot, vec_ref, bup_ref,
                  block_out, dr1, do_all, g_down, g_up, g_out, sums_ref, upsum_ref,
                  o_ref, raw_ref, wo_ref, wu_ref, wd_ref, hat_ref, inv_ref, acc_ref, hl_ref, hlt_ref, gp_ref, z_ref, c_ref,
                  df_ref, dft_ref, y_ref, st_ref, su_ref, ru_ref, rd_ref, go_ref, rgo_ref, u0_ref, u1_ref,
                  sem, osem, send, recv):
    f32, bf16 = jnp.float32, jnp.bfloat16
    rows, width = hat_ref.shape
    blocks = rows // BLOCK
    part = wu_ref.shape[2]
    bf = lambda a: a.astype(bf16)
    dp, tensor = lax.axis_index("dp"), lax.axis_index("tensor")
    inner = tensor % 2
    partner = (dp, tensor + 1 - 2 * inner)
    z, x = dp // 2, dp % 2
    to_x = (2 * z + 1 - x, tensor)
    to_y = (dp, (tensor + 2) % 4)
    mine = pl.multiple_of(inner * rows, 1024)
    theirs = pl.multiple_of((1 - inner) * rows, 1024)
    greet([partner, to_x, to_y] if pieces else [partner])

    def remote(n, src, dst, device=partner):
        return pltpu.make_async_remote_copy(src, dst, send.at[n], recv.at[n], device_id=device,
                                            device_id_type=pl.DeviceIdType.MESH)

    swap_o = remote(0, o_all.at[pl.ds(theirs, rows), :], o_ref.at[1])
    swap_o.start()
    count = [0]

    def load(src, dst):
        copy = pltpu.make_async_copy(src, dst, sem.at[count[0]])
        count[0] += 1
        copy.start()
        return copy

    def weight(sources, dst):
        if not pieces:
            return [load(sources[0].at[o], dst.at[o]) for o in range(2)]
        digit = dp % 2
        made = []
        for o in range(2):
            for zi in range(sources[0].shape[1]):
                for n in range(2):
                    place = 2 * zi + (digit if n == 0 else 1 - digit)
                    r = sources[n].shape[2]
                    made.append(load(sources[n].at[o, zi], dst.at[o, pl.ds(pl.multiple_of(place * r, r), r), :]))
        return made

    if pieces:
        r = downs[0].shape[0]
        block = lambda o, zi: wd_ref.at[o, pl.ds(pl.multiple_of(zi * r, r), r), :]
        zs = [(z + 4 - k) % 4 for k in range(4)]
        held = [load(downs[k], block(0, zs[k])) for k in range(4)]
    first = [load(o_all.at[pl.ds(mine, rows), :], o_ref.at[0]), load(x0, hat_ref)] + weight(outs, raw_ref.at[0])
    if pieces:
        second = [load(ups[o], wu_ref.at[o]) for o in range(2)]
    else:
        second = [load(ups[0].at[o], wu_ref.at[o]) for o in range(2)]
    if not pieces:
        second = second + weight(downs, wd_ref)
    late = load(cot, c_ref)
    if pieces:
        for copy in held:
            copy.wait()
        by_y = [remote(12 + m, block(0, 2 * x + m), block(1, 2 * x + m), to_y) for m in range(2)]
        by_x = [remote(14 + m, block(1, 2 * x + m), block(1, 2 * x + m), to_x) for m in range(2)]
        for copy in by_y:
            copy.start()
    vec = lambda n: vec_ref[n:n + 1, :]
    sums_ref[...] = jnp.zeros_like(sums_ref)
    upsum_ref[...] = jnp.zeros_like(upsum_ref)
    for copy in first:
        copy.wait()
    swaps = [remote(1, raw_ref.at[0], raw_ref.at[1])]
    swaps[0].start()
    for copy in second:
        copy.wait()
    for o in range(2):
        swaps.append(remote(2 + 2 * o, wu_ref.at[o], wu_ref.at[2 + o]))
        swaps.append(remote(3 + 2 * o, wd_ref.at[o], wd_ref.at[2 + o]))
    for copy in swaps[1:4] if pieces else swaps[1:]:
        copy.start()
    lane = lax.broadcasted_iota(jnp.int32, (width, 128), 1)

    def order_heads(side):
        wo_ref[side, :, 0:128] = raw_ref[side, 0, :, 0:128]
        wo_ref[side, :, 128:256] = raw_ref[side, 1, :, 0:128]
        upper = pltpu.roll(raw_ref[side, 1, :, 128:256].astype(f32), 64, 1)
        wo_ref[side, :, 256:384] = bf(jnp.where(lane < 64, raw_ref[side, 0, :, 128:256].astype(f32), upper))
    order_heads(0)
    swaps[0].wait()
    order_heads(1)
    swap_o.wait()

    def strips(body):
        def run(s, carry):
            body(pl.ds(pl.multiple_of(s * STRIP, STRIP), STRIP))
            return carry
        lax.fori_loop(0, rows // STRIP, run, 0)

    def add_sum(n, value):
        sums_ref[n] = sums_ref[n] + jnp.sum(fold(value), axis=0)

    def fold(value):
        return value.reshape(value.shape[0] // 8, 8, value.shape[1])

    def mean(value):
        return jnp.sum(value, axis=-1, keepdims=True) * (1.0 / width)

    def project(b, carry):
        r = pl.ds(pl.multiple_of(b * BLOCK, BLOCK), BLOCK)
        acc_ref[r, :] = mm(o_ref[0, r, :], wo_ref[0], NT) + mm(o_ref[1, r, :], wo_ref[1], NT)
        return carry
    lax.fori_loop(0, blocks, project, 0)

    def first_norm(r):
        r1 = hat_ref[r, :] + (acc_ref[r, :] + vec(0))
        centre = r1 - mean(r1)
        inv = lax.rsqrt(mean(centre * centre) + EPSILON)
        hat = centre * inv
        hat_ref[r, :] = hat
        inv_ref[r, :] = inv
        hl_ref[r, :] = bf(hat * vec(1) + vec(2))
    strips(first_norm)
    if pieces:
        by_y[0].wait_recv()
        by_x[0].start()
    for b in range(blocks):
        hlt_ref[:, BLOCK * b:BLOCK * b + BLOCK] = hl_ref[BLOCK * b:BLOCK * b + BLOCK, :].T
    acc_ref[...] = jnp.zeros_like(acc_ref)

    bufs = (u0_ref, u1_ref)

    def forward(n, carry):
        j = n % 2 * 2 + n // 2
        for o in range(2):
            @pl.when(j == 2 + o)
            def _(o=o):
                swaps[1 + 2 * o].wait()
                swaps[2 + 2 * o].wait()
        if pieces:
            @pl.when(j == 2)
            def _():
                by_y[1].wait_recv()
                by_x[1].start()

            @pl.when(j == 1)
            def _():
                for copy in by_x:
                    copy.wait()
                for copy in by_y:
                    copy.wait_send()
                swaps[4].start()

        def lift(b):
            bufs[b % 2][...] = mm(hl_ref[BLOCK * b:BLOCK * b + BLOCK, :], wu_ref[j]) + bup_ref[j, 0:1, :].astype(f32)
        lift(0)
        for b in range(blocks):
            if b + 1 < blocks:
                lift(b + 1)
            r = slice(BLOCK * b, BLOCK * b + BLOCK)
            for i in range(0, BLOCK, 32):
                for w in range(0, part, 256):
                    z, gp = normal_cdf_parts(bufs[b % 2][i:i + 32, w:w + 256])
                    z_ref[j, BLOCK * b + i:BLOCK * b + i + 32, w:w + 256] = bf(z)
                    gp_ref[j, BLOCK * b + i:BLOCK * b + i + 32, w:w + 256] = gp
            acc_ref[r, :] = acc_ref[r, :] + mm(z_ref[j, r, :], wd_ref[j], NT)
        return carry
    lax.fori_loop(0, 4, forward, 0)
    late.wait()

    def second_norm(r):
        h1 = hat_ref[r, :] * vec(1) + vec(2)
        r2 = h1 + (acc_ref[r, :] + vec(3))
        centre = r2 - mean(r2)
        inv = lax.rsqrt(mean(centre * centre) + EPSILON)
        hat = centre * inv
        y_ref[r, :] = bf(hat * vec(4) + vec(5))
        c = c_ref[r, :].astype(f32)
        add_sum(0, c * hat)
        add_sum(1, c)
        w = c * vec(4)
        dr2 = (w - mean(w) - hat * mean(w * hat)) * inv
        acc_ref[r, :] = dr2
        low = bf(dr2)
        df_ref[r, :] = low
        add_sum(2, low.astype(f32))
    strips(second_norm)
    stores = [pltpu.make_async_copy(y_ref, block_out, osem.at[0])]
    stores[0].start()
    for b in range(blocks):
        dft_ref[:, BLOCK * b:BLOCK * b + BLOCK] = df_ref[BLOCK * b:BLOCK * b + BLOCK, :].T

    def backward(n, carry):
        j = 3 - n

        def lower(b):
            bufs[b % 2][...] = mm(df_ref[BLOCK * b:BLOCK * b + BLOCK, :], wd_ref[j])
        slot = n % 2
        away = [remote(6 + slot, st_ref.at[slot], rd_ref.at[slot]), remote(8 + slot, su_ref.at[slot], ru_ref.at[slot])]
        lower(0)
        for b in range(blocks):
            if b + 1 < blocks:
                lower(b + 1)
            r = slice(BLOCK * b, BLOCK * b + BLOCK)
            for i in range(0, BLOCK, 64):
                q = slice(BLOCK * b + i, BLOCK * b + i + 64)
                dul = bf(bufs[b % 2][i:i + 64, :] * gp_ref[j, q, :])
                upsum_ref[j] = upsum_ref[j] + jnp.sum(fold(dul.astype(f32)), axis=0)
                hat2_ref[q, :] = dul
            acc_ref[r, :] = acc_ref[r, :] + mm(hat2_ref[r, :], wu_ref[j], NT)

        @pl.when(n < 2)
        def _():
            for m in range(0, width, BLOCK):
                st_ref[slot, m:m + BLOCK, :] = bf(mm(dft_ref[m:m + BLOCK, :], z_ref[j]))
            away[0].start()
            for m in range(0, width, BLOCK):
                su_ref[slot, m:m + BLOCK, :] = bf(mm(hlt_ref[m:m + BLOCK, :], hat2_ref[...]))
            away[1].start()

        @pl.when(n >= 2)
        def _():
            away[0].wait()
            for m in range(0, width, BLOCK):
                got = rd_ref[slot, m:m + BLOCK, :].astype(f32)
                st_ref[slot, m:m + BLOCK, :] = bf(mm(dft_ref[m:m + BLOCK, :], z_ref[j]) + got)
            if pieces:
                @pl.when(j == 0)
                def _():
                    pltpu.make_async_copy(st_ref.at[1], g_down[0], osem.at[2]).start()

                @pl.when(j == 1)
                def _():
                    early.start()
                    pltpu.make_async_copy(st_ref.at[0, width // 2:, :], g_down[1], osem.at[1]).start()
            else:
                pltpu.make_async_copy(st_ref.at[slot], g_down.at[j], osem.at[1 + slot]).start()
            away[1].wait()
            for m in range(0, width, BLOCK):
                got = ru_ref[slot, m:m + BLOCK, :].astype(f32)
                su_ref[slot, m:m + BLOCK, :] = bf(mm(hlt_ref[m:m + BLOCK, :], hat2_ref[...]) + got)
            if pieces:
                r = g_up[0].shape[2]
                for zi in range(g_up[0].shape[1]):
                    for o in range(2):
                        at = pl.multiple_of((2 * zi + (dp + o) % 2) * r, r)
                        pltpu.make_async_copy(su_ref.at[slot, pl.ds(at, r), :], g_up[o].at[j, zi], osem.at[3 + slot]).start()
            else:
                pltpu.make_async_copy(su_ref.at[slot], g_up.at[j], osem.at[3 + slot]).start()
        return carry
    hat2_ref = y_ref
    stores[0].wait()
    if pieces:
        early = remote(16, st_ref.at[0, 0:width // 2, :], g_down[2], to_y)
    lax.fori_loop(0, 4, backward, 0)

    def first_back(r):
        dh1 = acc_ref[r, :]
        hat = hat_ref[r, :]
        add_sum(3, dh1 * hat)
        add_sum(4, dh1)
        w = dh1 * vec(1)
        grad = (w - mean(w) - hat * mean(w * hat)) * inv_ref[r, :]
        acc_ref[r, :] = grad
        low = bf(grad)
        df_ref[r, :] = low
        add_sum(5, low.astype(f32))
    strips(first_back)
    out = pltpu.make_async_copy(acc_ref, dr1, osem.at[0])
    out.start()
    stores = [out]
    for b in range(blocks):
        dft_ref[:, BLOCK * b:BLOCK * b + BLOCK] = df_ref[BLOCK * b:BLOCK * b + BLOCK, :].T
    lane = lax.broadcasted_iota(jnp.int32, (BLOCK, 128), 1)

    def out_grad(side, m):
        tiles = [mm(dft_ref[m:m + BLOCK, :], o_ref[side, :, 128 * g:128 * g + 128]) for g in range(3)]
        third = [jnp.where(lane < 64, tiles[2], 0.0), jnp.where(lane < 64, pltpu.roll(tiles[2], 64, 1), 0.0)]
        return [jnp.concatenate([tiles[o], third[o]], axis=1) for o in range(2)]
    for m in range(0, width, BLOCK):
        for o, value in enumerate(out_grad(1, m)):
            go_ref[o, m:m + BLOCK, :] = bf(value)
    swap_go = remote(10, go_ref, rgo_ref)
    swap_go.start()
    ow = wo_ref.shape[2]
    for side in (1, 0):
        def push(b, carry):
            r = pl.ds(pl.multiple_of(b * BLOCK, BLOCK), BLOCK)
            y_ref[r, ow * side:ow * side + ow] = bf(mm(df_ref[r, :], wo_ref[side]))
            return carry
        lax.fori_loop(0, blocks, push, 0)
        if side == 1:
            swap_do = remote(11, y_ref.at[:, pl.ds(ow, ow)], do_all.at[pl.ds(mine, rows), :])
            swap_do.start()
        else:
            copy = pltpu.make_async_copy(y_ref.at[:, pl.ds(0, ow)], do_all.at[pl.ds(mine, rows), :], osem.at[5])
            copy.start()
            stores.append(copy)
    swap_go.wait()
    for m in range(0, width, BLOCK):
        for o, value in enumerate(out_grad(0, m)):
            go_ref[o, m:m + BLOCK, :] = bf(value + rgo_ref[o, m:m + BLOCK, :].astype(f32))
    for o in range(2 if pieces else 1):
        copy = pltpu.make_async_copy(go_ref.at[o] if pieces else go_ref, g_out[o] if pieces else g_out, osem.at[6 + o])
        copy.start()
        stores.append(copy)
    whole = g_down[0] if pieces else g_down.at[0]
    for slot in range(2):
        if pieces and slot == 0:
            pltpu.make_async_copy(st_ref.at[0, width // 2:, :], g_down[1], osem.at[1]).wait()
        else:
            pltpu.make_async_copy(st_ref.at[slot], whole, osem.at[1 + slot]).wait()
        pltpu.make_async_copy(su_ref.at[slot], whole, osem.at[3 + slot]).wait()
    if pieces:
        early.wait()
    swap_do.wait()
    for copy in stores:
        copy.wait()


def middle(o_all, x0, outs, ups, downs, cot, vec, bup):
    f32, bf16 = jnp.float32, jnp.bfloat16
    rows, width = x0.shape
    ow = o_all.shape[1]
    part = bup.shape[-1]
    pieces = len(ups) == 2
    shape = jax.ShapeDtypeStruct
    hbm = pl.BlockSpec(memory_space=pl.ANY)
    vmem = pl.BlockSpec(memory_space=pltpu.VMEM)
    v = pltpu.VMEM
    n = len(ups)
    m = 2 * n + len(downs)

    def kernel(o_all, x0, *refs):
        weights, rest = refs[:m], refs[m:]
        if pieces:
            rest = rest[:6] + (rest[6:9], rest[9:11], rest[11:13]) + rest[13:]
        middle_kernel(pieces, o_all, x0, weights[:n], weights[n:2 * n], weights[2 * n:], *rest)

    if pieces:
        parts = (2, len(downs), downs[0].shape[0] // 2, part)
        grads = [shape((width, part), bf16)] + [shape((width // 2, part), bf16)] * 2 + [shape(parts, bf16)] * 2 + [shape((width, 256), bf16)] * 2
    else:
        grads = [shape((2, width, part), bf16), shape((2, width, part), bf16), shape((2, width, 256), bf16)]
    return pl.pallas_call(
        kernel,
        out_shape=(shape((rows, width), bf16), shape((rows, width), f32), shape((2 * rows, ow), bf16),
                   *grads, shape((6, 8, width), f32), shape((4, 8, part), f32)),
        in_specs=[hbm] * (3 + m) + [vmem] * 2,
        out_specs=[hbm] * (3 + len(grads)) + [vmem] * 2,
        scratch_shapes=[
            v((2, rows, ow), bf16), v((2, 2, width, 256), bf16), v((2, width, ow), bf16), v((4, width, part), bf16),
            v((4, width, part), bf16),
            v((rows, width), f32), v((rows, 1), f32), v((rows, width), f32), v((rows, width), bf16), v((width, rows), bf16),
            v((4, rows, part), f32), v((4, rows, part), bf16), v((rows, width), bf16), v((rows, width), bf16),
            v((width, rows), bf16), v((rows, width), bf16), v((2, width, part), bf16),
            v((2, width, part), bf16), v((2, width, part), bf16), v((2, width, part), bf16), v((2, width, 256), bf16),
            v((2, width, 256), bf16), v((BLOCK, part), f32), v((BLOCK, part), f32),
            pltpu.SemaphoreType.DMA((40,)), pltpu.SemaphoreType.DMA((8,)),
            pltpu.SemaphoreType.DMA((24,)), pltpu.SemaphoreType.DMA((24,)),
        ],
        compiler_params=pltpu.CompilerParams(vmem_limit_bytes=VMEM_MAX, collective_id=1, has_side_effects=True),
        cost_estimate=pl.CostEstimate(flops=6 * rows * width * 9 * width, bytes_accessed=60_000_000, transcendentals=2 * rows * 4 * part),
        name="middle",
    )(o_all, x0, *outs, *ups, *downs, cot, vec, bup)


class Exchange:
    def __init__(self, send, recv):
        self.send, self.recv, self.used = send, recv, 0

    def copy(self, src, dst, device):
        n = self.used
        self.used += 1
        return pltpu.make_async_remote_copy(src, dst, self.send.at[n], self.recv.at[n], device_id=device,
                                            device_id_type=pl.DeviceIdType.MESH)


def greet(devices):
    barrier = pltpu.get_barrier_semaphore()
    for device in devices:
        pl.semaphore_signal(barrier, inc=1, device_id=device, device_id_type=pl.DeviceIdType.MESH)
    pl.semaphore_wait(barrier, len(devices))


def entry_kernel(tokens, pos_ref, mem_in, wq_in, bq_ref, bu_in, wu_ref, wd_ref, wo_ref,
                 x0_out, x_out, q_out, k_out, v_out, w_out, up_g, down_g, out_g, bu_out,
                 x0_ref, x_ref, g_ref, b_ref, y_ref, third_ref, q_ref, k_ref, v_ref, ub_ref, wq_ref, bu_ref, mem_ref, send, recv, sem):
    f32, bf16 = jnp.float32, jnp.bfloat16
    rows, width = x0_ref.shape
    dp, tensor = lax.axis_index("dp"), lax.axis_index("tensor")
    z, x = dp // 2, dp % 2
    inner = tensor % 2
    zs = [(z + 4 - k) % 4 for k in range(4)]
    at = [2 * zs[k] + x for k in range(4)]
    far = [2 * zs[k] + 1 - x for k in range(4)]
    to_z = [None] + [(2 * ((z + k) % 4) + x, tensor) for k in range(1, 4)]
    to_x = (2 * z + 1 - x, tensor)
    to_y = (dp, (tensor + 2) % 4)
    to_core = (dp, tensor + 1 - 2 * inner)
    to_both = (dp, 3 - tensor)
    heads = [wq_in[n, :, 0:128].astype(f32) for n in range(3)]
    values = [wq_in[n, :, 128:192].astype(f32) for n in range(3)]
    lane = lax.broadcasted_iota(jnp.int32, heads[0].shape, 1)
    wq_ref[:, 0:128] = jnp.where(lane < 64, heads[0], pltpu.roll(heads[1], 64, 1)).astype(bf16)
    wq_ref[:, 128:256] = jnp.where(lane < 64, pltpu.roll(heads[0], 64, 1), heads[1]).astype(bf16)
    wq_ref[:, 256:384] = jnp.concatenate(values[0:2], axis=1).astype(bf16)
    wq_ref[:, 384:512] = wq_in[2, :, 0:128]
    wq_ref[:, 512:576] = wq_in[2, :, 128:192]
    bu_ref[...] = jnp.broadcast_to(bu_in[...].astype(f32), bu_ref.shape).astype(bf16)
    mem_ref[...] = jnp.zeros_like(mem_ref)
    mem_ref[0:mem_in.shape[0], :] = mem_in[...]
    greet(to_z[1:] + [to_x, to_y, to_core, to_both])
    ex = Exchange(send, recv)
    started = []

    def go(src, dst, device):
        copy = ex.copy(src, dst, device)
        copy.start()
        started.append(copy)
        return copy

    local = []

    def keep(src, dst):
        copy = pltpu.make_async_copy(src, dst, sem.at[len(local)])
        copy.start()
        local.append(copy)
        return copy

    own = keep(wq_ref, g_ref.at[0, at[0]])
    own_bias = keep(bq_ref, b_ref.at[0])
    z_q = [None] + [go(wq_ref, g_ref.at[0, at[0]], to_z[k]) for k in range(1, 4)]
    x_q = [go(wq_ref, g_ref.at[0, at[0]], to_x)]
    y_q = [go(wq_ref, g_ref.at[1, at[0]], to_y)]
    bias = go(bq_ref, b_ref.at[1], to_y)
    up_bias = [go(bu_ref, ub_ref.at[n - 1], to) for n, to in ((1, to_y), (2, to_core), (3, to_both))]

    mine = pl.multiple_of(inner * rows, 1024)
    positions = pos_ref[0:1, :]
    strip = 128

    def start(s, carry):
        r = pl.multiple_of(s * strip, strip)
        place = lax.broadcasted_iota(jnp.int32, (strip, positions.shape[1]), 0) + (inner * rows + r)
        picks = jnp.where(place == positions, 1.0, 0.0).astype(bf16)
        value = tokens[pl.ds(r, strip), :].astype(f32) + mm(picks, mem_ref[...])
        x0_ref[pl.ds(r, strip), :] = value
        x_ref[pl.ds(mine + r, strip), :] = value.astype(bf16)
        return carry
    lax.fori_loop(0, rows // strip, start, 0)
    keep(x0_ref, x0_out)
    core = go(x_ref.at[pl.ds(mine, rows), :], x_ref.at[pl.ds(mine, rows), :], to_core)

    for k in range(1, 4):
        z_q[k].wait_recv()
        x_q.append(go(g_ref.at[0, at[k]], g_ref.at[0, at[k]], to_x))
        y_q.append(go(g_ref.at[0, at[k]], g_ref.at[1, at[k]], to_y))
    z_u = [None] + [go(wu_ref, up_g.at[at[0]], to_z[k]) for k in range(1, 4)]
    z_o = [None] + [go(wo_ref, out_g.at[0, z], to_z[k]) for k in range(1, 4)]
    keep(wu_ref, up_g.at[at[0]])
    keep(wd_ref, down_g.at[x])
    keep(wo_ref, out_g.at[0, z])
    last = []
    for k in range(2):
        x_q[k].wait_recv()
        last.append(go(g_ref.at[0, far[k]], g_ref.at[1, far[k]], to_y))
    for k in range(2, 4):
        y_q[k].wait_recv()
        last.append(go(g_ref.at[1, at[k]], g_ref.at[1, at[k]], to_x))
    rest = [go(wd_ref, down_g.at[x], to_x), go(wu_ref, up_g.at[at[0]], to_x), go(wo_ref, out_g.at[1, z], to_y)]
    own.wait()
    own_bias.wait()
    for copy in x_q[2:] + [core]:
        copy.wait_recv()
    keep(x_ref, x_out)
    lane = lax.broadcasted_iota(jnp.int32, (BLOCK, 128), 1)
    blocks = 2 * rows // BLOCK
    heads = (q_ref, k_ref, v_ref)

    def write(n, g, r, value):
        value = value.astype(bf16)
        if n == 0:
            value = value * jnp.asarray(0.125, bf16)
        heads[n][r, 128 * g:128 * g + 128] = value

    def project(o, b):
        r = pl.ds(pl.multiple_of(b * BLOCK, BLOCK), BLOCK)
        y_ref[:, 0:576] = mm(x_ref[r, :], g_ref[o].reshape(width, 576)) + b_ref[o, 0:1, 0:576].astype(f32)
        for n in range(3):
            write(n, o, r, y_ref[:, 128 * n:128 * n + 128])
        return r

    def project_own(b, carry):
        r = project(0, b)
        third_ref[r, :] = y_ref[:, 384:640]
        return carry

    def project_other(b, carry):
        r = project(1, b)
        turn = lambda value: pltpu.roll(value, 64, 1)
        left, right = third_ref[r, 0:128], y_ref[:, 384:512]
        write(0, 2, r, jnp.where(lane < 64, left, turn(right)))
        write(1, 2, r, jnp.where(lane < 64, turn(left), right))
        write(2, 2, r, jnp.where(lane < 64, third_ref[r, 128:256], turn(y_ref[:, 512:640])))
        return carry
    y_ref[...] = jnp.zeros_like(y_ref)
    lax.fori_loop(0, blocks, project_own, 0)
    for copy in y_q[:2] + last + [bias]:
        copy.wait_recv()
    keep(g_ref, w_out)
    for k in range(1, 4):
        z_u[k].wait_recv()
        rest.append(go(up_g.at[at[k]], up_g.at[at[k]], to_x))
        lax.fori_loop(blocks * (k - 1) // 4, blocks * k // 4, project_other, 0)
    lax.fori_loop(blocks * 3 // 4, blocks, project_other, 0)
    for src, dst in ((q_ref, q_out), (k_ref, k_out), (v_ref, v_out)):
        keep(src, dst)
    for k in range(1, 4):
        z_o[k].wait_recv()
        rest.append(go(out_g.at[0, zs[k]], out_g.at[1, zs[k]], to_y))
    for copy in rest + up_bias:
        copy.wait_recv()
    bu_out[0] = bu_ref[...]
    for n in range(3):
        bu_out[n + 1] = ub_ref[n]
    for copy in started:
        copy.wait_send()
    for copy in local[2:]:
        copy.wait()


def entry(tokens, positions, memory_rows, qkv_heads, biases, up_bias, up, down, out):
    f32, bf16 = jnp.float32, jnp.bfloat16
    rows, width = tokens.shape
    r = up.shape[0]
    shape, v = jax.ShapeDtypeStruct, pltpu.VMEM
    hbm, vmem = pl.BlockSpec(memory_space=pl.ANY), pl.BlockSpec(memory_space=pltpu.VMEM)
    qkv = shape((2 * rows, 384), bf16)
    return pl.pallas_call(
        entry_kernel,
        out_shape=(shape((rows, width), f32), shape((2 * rows, width), bf16), qkv, qkv, qkv,
                   shape((2, 8, r, 576), bf16), shape((8, r, up.shape[1]), bf16), shape((2, r, down.shape[1]), bf16),
                   shape((2, 4, r, out.shape[1]), bf16), shape((4, 16, up.shape[1]), bf16)),
        in_specs=[vmem] * 9,
        out_specs=[hbm] * 9 + [vmem],
        scratch_shapes=[
            v((rows, width), f32), v((2 * rows, width), bf16), v((2, 8, r, 576), bf16), v((2, 16, 640), bf16),
            v((BLOCK, 640), f32), v((2 * rows, 256), f32), v((2 * rows, 384), bf16), v((2 * rows, 384), bf16), v((2 * rows, 384), bf16),
            v((3, 16, up.shape[1]), bf16), v((r, 576), bf16), v((16, up.shape[1]), bf16), v((32, width), bf16),
            pltpu.SemaphoreType.DMA((48,)), pltpu.SemaphoreType.DMA((48,)), pltpu.SemaphoreType.DMA((16,)),
        ],
        compiler_params=pltpu.CompilerParams(vmem_limit_bytes=VMEM_MAX, collective_id=0, has_side_effects=True),
        cost_estimate=pl.CostEstimate(flops=4 * rows * width * 1152, bytes_accessed=20_000_000, transcendentals=0),
        name="entry",
    )(tokens, positions, memory_rows, qkv_heads, biases, up_bias, up, down, out)


def exit_kernel(x_all, d0, d1, d2, w_all, third, kept_ref, came_ref, dr1, pos_ref, sums_in, up_in,
                tok_out, first_out, second_out, small_out,
                x_ref, xt_ref, d_ref, w_ref, dr_ref, g_ref, own_ref, oth_ref, yb_ref, xs_ref, xb_ref, zt_ref, zs_ref, zb_ref,
                fs_ref, fb_ref, their_ref, got_ref, tok_ref, s_ref, t_ref, r_ref, first_ref, send, recv, sem):
    f32, bf16 = jnp.float32, jnp.bfloat16
    rows, width = dr_ref.shape
    dp, tensor = lax.axis_index("dp"), lax.axis_index("tensor")
    z, x = dp // 2, dp % 2
    inner, outer = tensor % 2, tensor // 2
    up_z = [None] + [(z + k) % 4 for k in range(1, 4)]
    to_z = [None] + [(2 * up_z[k] + x, tensor) for k in range(1, 4)]
    to_x = (2 * z + 1 - x, tensor)
    to_y = (dp, (tensor + 2) % 4)
    to_core = (dp, tensor + 1 - 2 * inner)
    near_z = (2 * (z + 1 - 2 * (z % 2)) + x, tensor)
    far_z = to_z[2]
    loads = []
    for src, dst in ((d2, d_ref.at[2]), (x_all, x_ref), (d0, d_ref.at[0]), (d1, d_ref.at[1]),
                     (w_all.at[0, :, pl.ds(0, 384)], w_ref.at[0]), (w_all.at[1, :, pl.ds(0, 384)], w_ref.at[1]),
                     (third, w_ref.at[2]), (dr1, dr_ref)):
        copy = pltpu.make_async_copy(src, dst, sem.at[len(loads)])
        copy.start()
        loads.append(copy)
    greet(to_z[1:] + [to_x, to_y, to_core])
    ex = Exchange(send, recv)
    started = []

    def go(src, dst, device):
        copy = ex.copy(src, dst, device)
        copy.start()
        started.append(copy)
        return copy

    for k in range(4):
        first_ref[k] = kept_ref[k] + came_ref[k].astype(f32)
    for k in range(1, 4):
        fs_ref[k - 1] = first_ref[up_z[k]].astype(bf16)
    z_first = [go(fs_ref.at[k - 1], fb_ref.at[k - 1], to_z[k]) for k in range(1, 4)]

    loads[0].wait()
    loads[1].wait()
    for b in range(2 * rows // BLOCK):
        xt_ref[:, BLOCK * b:BLOCK * b + BLOCK] = x_ref[BLOCK * b:BLOCK * b + BLOCK, :].T
    for m in range(0, width, BLOCK):
        g_ref[m:m + BLOCK, :] = mm(xt_ref[m:m + BLOCK, :], d_ref[2])
    half = own_ref.shape[3]
    lane = lax.broadcasted_iota(jnp.int32, (half, 128), 1)
    for p in range(8):
        for n in range(3):
            low = g_ref[2 * half * p:2 * half * p + half, 128 * n:128 * n + 128]
            high = g_ref[2 * half * p + half:2 * half * (p + 1), 128 * n:128 * n + 128]
            own_ref[p % 2, p // 2, n] = jnp.where(lane < 64, low, pltpu.roll(high, 64, 1))
            oth_ref[p % 2, p // 2, n] = jnp.where(lane < 64, pltpu.roll(low, 64, 1), high).astype(bf16)
    y_far = go(oth_ref.at[1 - x], yb_ref.at[0], to_y)
    y_near = go(oth_ref.at[x], yb_ref.at[1], to_y)

    for copy in loads[2:]:
        copy.wait()
    place = lax.broadcasted_iota(jnp.int32, (32, 2 * rows), 1)
    which = lax.broadcasted_iota(jnp.int32, (32, 2 * rows), 0)
    picks = jnp.where((place == pos_ref[:, 0:1]) | (which == 24), 1.0, 0.0).astype(bf16)
    picked = [mm(picks, d_ref[n]) for n in range(3)]
    own_place = lax.broadcasted_iota(jnp.int32, (32, rows), 1) + inner * rows
    own_picks = jnp.where(own_place == pos_ref[:, 0:1], 1.0, 0.0)
    memory = lax.dot_general(own_picks, dr_ref[...], NN, precision=lax.Precision.HIGHEST, preferred_element_type=f32)
    for n in range(3):
        memory = memory + mm(picked[n].astype(bf16), w_ref[n], NT)
    hw = s_ref.shape[2]

    def put(row, value):
        for h in range(2):
            s_ref[h, row:row + 1, :] = value[:, hw * h:hw * h + hw]
    for h in range(2):
        s_ref[h, 0:24, :] = memory[0:24, hw * h:hw * h + hw]
        s_ref[h, 38:40, :] = jnp.zeros((2, hw), f32)
    for n in range(6):
        put(24 + n, jnp.sum(sums_in[n], axis=0, keepdims=True))
    ups = [jnp.sum(up_in[n], axis=0, keepdims=True) for n in (0, 2, 1, 3)]
    total = [value[24:25, :] for value in picked]
    turned = jnp.concatenate([pltpu.roll(picked[2][24:32, 128 * n:128 * n + 128], 64, 1) for n in range(3)], axis=1)[0:1, :]
    for t in range(4):
        n = (t % 2 + inner) % 2 + 2 * ((t // 2 + outer) % 2)
        value = jnp.zeros_like(ups[0])
        for other in range(4):
            value = value + jnp.where(n == other, ups[other], 0.0)
        put(30 + t, value)
        s_ref[0, 34 + t:35 + t, :] = jnp.where(n == 0, total[0], 0.0) + jnp.where(n == 2, total[1], 0.0)
        s_ref[1, 34 + t:35 + t, :] = jnp.where(n == 0, total[2], 0.0) + jnp.where(n == 2, turned, 0.0)
    small = [go(s_ref.at[1 - inner], r_ref.at[0], to_core)]
    hops = [to_y, to_x, near_z, far_z]

    def hop(n):
        small[n].wait_recv()
        t_ref[n] = (s_ref[inner] if n == 0 else t_ref[n - 1]) + r_ref[n]
        if n < 4:
            small.append(go(t_ref.at[n], r_ref.at[n + 1], hops[n]))
        else:
            small.append(go(t_ref.at[n], r_ref.at[5], to_core))
            small_out[inner] = t_ref[n]

    mine = pl.multiple_of(inner * rows, 1024)
    theirs = pl.multiple_of((1 - inner) * rows, 1024)

    def block(start):
        r = pl.ds(pl.multiple_of(start, BLOCK), BLOCK)
        return mm(d_ref[0, r, :], w_ref[0], NT) + mm(d_ref[1, r, :], w_ref[1], NT) + mm(d_ref[2, r, :], w_ref[2], NT)

    def away(b, carry):
        their_ref[pl.ds(pl.multiple_of(b * BLOCK, BLOCK), BLOCK), :] = block(theirs + b * BLOCK).astype(bf16)
        return carry
    lax.fori_loop(0, rows // BLOCK, away, 0)
    tokens = go(their_ref, got_ref, to_core)
    hop(0)
    y_far.wait_recv()
    for k in range(4):
        xs_ref[k] = (own_ref[1 - x, k] + yb_ref[0, k].astype(f32)).astype(bf16)
    x_sum = go(xs_ref, xb_ref, to_x)

    def stay(b, carry):
        tok_ref[pl.ds(pl.multiple_of(b * BLOCK, BLOCK), BLOCK), :] = block(mine + b * BLOCK)
        return carry
    lax.fori_loop(0, rows // BLOCK, stay, 0)
    hop(1)
    y_near.wait_recv()
    x_sum.wait_recv()
    for k in range(4):
        zt_ref[k] = own_ref[x, k] + yb_ref[1, k].astype(f32) + xb_ref[k].astype(f32)
    for k in range(1, 4):
        zs_ref[k - 1] = zt_ref[up_z[k]].astype(bf16)
    z_second = [go(zs_ref.at[k - 1], zb_ref.at[k - 1], to_z[k]) for k in range(1, 4)]
    hop(2)
    tokens.wait_recv()

    def finish(s, carry):
        r = pl.ds(pl.multiple_of(s * STRIP, STRIP), STRIP)
        tok_ref[r, :] = tok_ref[r, :] + got_ref[r, :].astype(f32) + dr_ref[r, :]
        return carry
    lax.fori_loop(0, rows // STRIP, finish, 0)
    out = pltpu.make_async_copy(tok_ref, tok_out, sem.at[8])
    out.start()
    hop(3)
    for copy in z_first:
        copy.wait_recv()
    first_out[...] = first_ref[z] + fb_ref[0].astype(f32) + fb_ref[1].astype(f32) + fb_ref[2].astype(f32)
    for copy in z_second:
        copy.wait_recv()
    second_out[...] = zt_ref[z] + zb_ref[0].astype(f32) + zb_ref[1].astype(f32) + zb_ref[2].astype(f32)
    hop(4)
    small[5].wait_recv()
    small_out[1 - inner] = r_ref[5]
    for copy in started:
        copy.wait_send()
    out.wait()


def leave(x_all, d, w_qkv, third, first, came, dr1, place, sums, up_sums):
    f32, bf16 = jnp.float32, jnp.bfloat16
    rows, width = dr1.shape
    r, half = first.shape[1], first.shape[1] // 2
    shape, v = jax.ShapeDtypeStruct, pltpu.VMEM
    hbm, vmem = pl.BlockSpec(memory_space=pl.ANY), pl.BlockSpec(memory_space=pltpu.VMEM)
    return pl.pallas_call(
        exit_kernel,
        out_shape=(shape((rows, width), f32), shape((r, 384), f32), shape((3, half, 128), f32), shape((2, 40, width // 2), f32)),
        in_specs=[hbm] * 6 + [vmem] * 2 + [hbm] + [vmem] * 3,
        out_specs=[hbm] + [vmem] * 3,
        scratch_shapes=[
            v((2 * rows, width), bf16), v((width, 2 * rows), bf16), v((3, 2 * rows, 384), bf16), v((3, width, 384), bf16),
            v((rows, width), f32), v((width, 384), f32), v((2, 4, 3, half, 128), f32), v((2, 4, 3, half, 128), bf16),
            v((2, 4, 3, half, 128), bf16), v((4, 3, half, 128), bf16), v((4, 3, half, 128), bf16), v((4, 3, half, 128), f32),
            v((3, 3, half, 128), bf16), v((3, 3, half, 128), bf16), v((3, r, 384), bf16), v((3, r, 384), bf16),
            v((rows, width), bf16), v((rows, width), bf16), v((rows, width), f32), v((2, 40, width // 2), f32),
            v((5, 40, width // 2), f32), v((6, 40, width // 2), f32), v((4, r, 384), f32),
            pltpu.SemaphoreType.DMA((16,)), pltpu.SemaphoreType.DMA((16,)), pltpu.SemaphoreType.DMA((9,)),
        ],
        compiler_params=pltpu.CompilerParams(vmem_limit_bytes=VMEM_MAX, collective_id=2, has_side_effects=True),
        cost_estimate=pl.CostEstimate(flops=2 * rows * width * 384 * 8, bytes_accessed=20_000_000, transcendentals=0),
        name="leave",
    )(x_all, *d, w_qkv, third, first, came, dr1, place, sums, up_sums)


def layer_norm(values, norm_gain, norm_shift):
    centre = values - jnp.mean(values, axis=-1, keepdims=True)
    spread = jnp.mean(centre * centre, axis=-1, keepdims=True)
    return centre * lax.rsqrt(spread + EPSILON) * norm_gain + norm_shift


def gelu_exact(values):
    return jax.nn.gelu(values, approximate=False)


AXES = ("dp", "tensor")


class Grid:
    def __init__(self, dp, tensor):
        self.dp, self.tensor = dp, tensor
        factors, rest = [2], dp // 2
        while rest > 8:
            factors.insert(0, 4)
            rest //= 4
        if rest > 1:
            factors.insert(0, rest)
        self.factors = factors

    def digit(self, j):
        stride = 1
        for f in self.factors[j + 1:]:
            stride *= f
        return stride, self.factors[j]

    def my_digit(self, j):
        stride, f = self.digit(j)
        return lax.axis_index("dp") // stride % f

    def turn(self, value, j, k):
        stride, f = self.digit(j)
        pairs = []
        for d in range(self.dp):
            g = d // stride % f
            to = d + ((g + k) % f - g) * stride
            for t in range(self.tensor):
                pairs.append((d * self.tensor + t, to * self.tensor + t))
        return lax.ppermute(value, AXES, pairs)

    def swap_dp(self, value, bit):
        pairs = [(d * self.tensor + t, (d ^ bit) * self.tensor + t) for d in range(self.dp) for t in range(self.tensor)]
        return lax.ppermute(value, AXES, pairs)

    def swap(self, value, bit):
        pairs = [(d * self.tensor + t, d * self.tensor + (t ^ bit)) for d in range(self.dp) for t in range(self.tensor)]
        return lax.ppermute(value, AXES, pairs)

    def gather_stage(self, value, j, axis):
        _, f = self.digit(j)
        g = self.my_digit(j)
        got = [value] + [self.turn(value, j, k) for k in range(1, f)]
        if f == 2:
            lower = jnp.where(g == 0, got[0], got[1])
            upper = jnp.where(g == 0, got[1], got[0])
            return jnp.stack([lower, upper], axis=axis)
        ring = got[::-1]
        return lax.dynamic_slice_in_dim(jnp.stack(ring + ring[:-1], axis=axis), f - 1 - g, f, axis)

    def gather(self, shard, outer_first=False):
        count = len(self.factors)
        value = shard
        for j in range(count - 1):
            value = self.gather_stage(value, j, j)
        if outer_first:
            value = jnp.stack([value, self.swap(value, 2)])
            value = self.gather_stage(value, count - 1, count)
            return value.reshape(2, -1, shard.shape[-1])
        value = self.gather_stage(value, count - 1, count - 1)
        value = value.reshape(-1, shard.shape[-1])
        return jnp.stack([value, self.swap(value, 2)])

    def reduce_stage(self, value, j, axis):
        _, f = self.digit(j)
        g = self.my_digit(j)
        total = lax.dynamic_index_in_dim(value, g, axis, keepdims=False).astype(jnp.float32)
        for k in range(1, f):
            part = lax.dynamic_index_in_dim(value, (g + k) % f, axis, keepdims=False)
            total = total + self.turn(part.astype(jnp.bfloat16), j, k).astype(jnp.float32)
        return total

    def reduce(self, parts, outer_first=True):
        count = len(self.factors)
        columns = parts.shape[-1]
        value = parts
        if outer_first:
            value = value[0].astype(jnp.float32) + self.swap(value[1].astype(jnp.bfloat16), 2).astype(jnp.float32)
            value = value.reshape(*self.factors, -1, columns)
            value = self.reduce_stage(value, count - 1, count - 1)
        else:
            value = value.reshape(2, *self.factors, -1, columns)
            value = self.reduce_stage(value, count - 1, count)
            value = value[0] + self.swap(value[1].astype(jnp.bfloat16), 2).astype(jnp.float32)
        for j in reversed(range(count - 1)):
            value = self.reduce_stage(value, j, j)
        return value

    @property
    def stages(self):
        return len(self.factors) + 1

    def open(self, parts, outer_first):
        columns = parts.shape[-1]
        return parts if outer_first else parts.reshape(2, *self.factors, -1, columns)

    def stage(self, value, outer_first, n):
        count = len(self.factors)
        if n == (0 if outer_first else 1):
            value = value[0].astype(jnp.float32) + self.swap(value[1].astype(jnp.bfloat16), 2).astype(jnp.float32)
            return value.reshape(*self.factors, -1, value.shape[-1]) if outer_first else value
        if n == 0:
            return self.reduce_stage(value, count - 1, count)
        return self.reduce_stage(value, count - n, count - n)

    def total(self, vector):
        for bit in (1, 2):
            vector = vector + self.swap(vector, bit)
        bit = 1
        while bit < self.dp:
            vector = vector + self.swap_dp(vector, bit)
            bit *= 2
        return vector


def shards(grid, tokens, segment_ids, memory_positions, memory_rows, qkv_weight, qv_bias, out_weight, out_bias,
           norm1_gain, norm1_bias, up_weight, up_bias, down_weight, down_bias, norm2_gain, norm2_bias, out_cotangent):
    f32, bf16 = jnp.float32, jnp.bfloat16
    rows, width = tokens.shape
    group_len = segment_ids.shape[1]
    tensor = lax.axis_index("tensor")
    inner, outer = tensor % 2, tensor // 2
    slice_rows = qkv_weight.shape[0]
    heads = qkv_weight.shape[1]
    hd = 64
    hw = heads * hd
    units = up_weight.shape[1]

    segments = lax.dynamic_index_in_dim(segment_ids, outer, 0, keepdims=False)
    positions = lax.dynamic_index_in_dim(memory_positions, outer, 0, keepdims=False)
    row_place = inner * rows + jnp.arange(rows, dtype=jnp.int32)
    picks = (row_place[:, None] == positions[None, :])
    joined = lambda w: w.transpose(1, 0, 2).reshape(width, -1)

    parts = qkv_weight.reshape(slice_rows, heads, 3, hd)
    order_columns = lambda p: jnp.concatenate([p[..., :2, n, :].reshape(*p.shape[:-3], 2 * hd) for n in range(3)]
                                              + [p[..., 2, n, :] for n in range(3)], axis=-1)
    shard_qkv = order_columns(parts)
    shard_out = jnp.pad(out_weight.reshape(slice_rows, hw), ((0, 0), (0, 256 - hw)))
    bias_parts = qv_bias.reshape(heads, 2, hd)
    bias_qkv = order_columns(jnp.stack([bias_parts[:, 0], jnp.zeros_like(bias_parts[:, 0]), bias_parts[:, 1]], 1))
    bias_qkv = jnp.pad(bias_qkv[None], ((0, 15), (0, 64)))
    own_up_bias = jnp.broadcast_to(up_bias[None], (16, units))
    fused = grid.dp == 8 and grid.tensor == 4
    if fused:
        memory = memory_positions.shape[1]
        place = jnp.pad(positions[None], ((0, 7), (0, 32 - memory)), constant_values=-1)
        x0, x_all, q, k, v, w_qkv, up_g, down_g, out_g, b_up = entry(tokens, place, memory_rows, qkv_weight.transpose(1, 0, 2), bias_qkv, up_bias[None], up_weight, down_weight, shard_out)
        column = jnp.pad(jnp.broadcast_to(positions[:, None], (memory, 128)), ((0, 32 - memory), (0, 0)), constant_values=-1)
        w_qkv = w_qkv.reshape(2, width, 9 * hd)
        third = jnp.concatenate([w_qkv[o][:, (6 + n) * hd:(7 + n) * hd] for n in range(3) for o in range(2)], 1)
        up_all = up_g.reshape(width, units)
        ups = (up_all, grid.swap(up_all, 2))
        down_pair = down_g.reshape(-1, units)
        downs = (down_pair, *[grid.turn(down_pair, 0, k) for k in range(1, 4)])
        outs = (out_g, grid.turn(out_g, 1, 1))
    else:
        x0 = tokens.astype(f32) + jnp.dot(picks.astype(bf16), memory_rows, preferred_element_type=f32)
        xl = x0.astype(bf16)
        w_qkv = grid.gather(shard_qkv)
        other = grid.swap(xl, 1)
        x_all = jnp.concatenate([jnp.where(inner == 0, xl, other), jnp.where(inner == 0, other, xl)])
        b_two = jnp.stack([bias_qkv[0], grid.swap(bias_qkv[0], 2)]).astype(f32)
        y = [(mm(x_all, w_qkv[o]) + b_two[o, :9 * hd]).astype(bf16) for o in range(2)]
        third = lambda n: [one[:, (6 + n) * hd:(7 + n) * hd] for one in y]
        q, k, v = [jnp.concatenate([y[0][:, 2 * n * hd:2 * (n + 1) * hd], y[1][:, 2 * n * hd:2 * (n + 1) * hd]] + third(n), 1)
                   for n in range(3)]
        q = q * jnp.asarray(0.125, bf16)
        b_up = jnp.stack([own_up_bias, grid.swap(own_up_bias, 2)])
        b_up = jnp.concatenate([b_up, grid.swap(b_up, 1)])
        outs, ups, downs = (grid.gather(shard_out, True),), (grid.gather(up_weight),), (grid.gather(down_weight, True),)
    mixed, lse = attend_forward(q, k, v, segments)
    vec = jnp.stack([out_bias, norm1_gain, norm1_bias, down_bias, norm2_gain, norm2_bias, norm2_bias, norm2_bias]).astype(f32)
    (block_out, dr1, do_all, *grads, sums, up_sums) = middle(
        mixed, x0, outs, ups, downs, out_cotangent, vec, b_up)
    if fused:
        return finish_small(grid, tensor, x_all, q, k, v, do_all, mixed, lse, segments, w_qkv, third, dr1, column, sums, up_sums, block_out,
                            grads, hw)
    g_down, g_up, g_out = grads

    TN = (((0,), (0,)), ((), ()))
    tie = lax.optimization_barrier
    kinds = (True, False, True)
    state = [grid.open(parts, kind) for parts, kind in zip((g_down, g_up, g_out), kinds)]
    step = lambda n, state: [grid.stage(value, kind, n) for value, kind in zip(state, kinds)]
    late = [(1, 0, 2)[n] for n in range(3)]
    d = [None] * 3
    state, d[1] = step(0, state), attend_backward(1, q, k, v, do_all, mixed, lse, segments)
    state, d[1], q = tie((state, d[1], q))
    g_one = mm(x_all, d[1], TN).astype(bf16)
    state, d[0] = step(1, state), attend_backward(0, q, k, v, do_all, mixed, lse, segments)
    state, d[0], q, g_one = tie((state, d[0], q, g_one))
    g_zero = mm(x_all, d[0], TN)
    first = g_zero + grid.swap(g_one, 2).astype(f32)
    state, d[2] = step(2, state), attend_backward(2, q, k, v, do_all, mixed, lse, segments)
    state, d[2], first = tie((state, d[2], first))
    for n in range(3, grid.stages):
        state = step(n, state)
    grad_down, grad_up, grad_out = state
    grad_out = grad_out[:, :hw]

    g_two = mm(x_all, d[2], TN)
    side = lambda m, o: jnp.concatenate([m[:, (2 * n + o) * hd:(2 * n + o + 1) * hd] for n in range(3)], 1)
    second = side(g_two, 0) + grid.swap(side(g_two, 1).astype(bf16), 2).astype(f32)
    both = jnp.concatenate([first, second], 1).reshape(*grid.factors, slice_rows, 9 * hd)
    for j in reversed(range(len(grid.factors))):
        both = grid.reduce_stage(both, j, j)
    restore = lambda p: jnp.stack([jnp.concatenate([p[..., 2 * n * hd:2 * (n + 1) * hd].reshape(*p.shape[:-1], 2, hd),
                                                    p[..., None, (6 + n) * hd:(7 + n) * hd]], -2) for n in range(3)], -2)
    grad_qkv = restore(both).reshape(slice_rows, heads, 3 * hd)
    third = jnp.concatenate([w_qkv[o][:, (6 + n) * hd:(7 + n) * hd] for n in range(3) for o in range(2)], 1)
    part = (mm(d[0], w_qkv[0][:, :6 * hd], NT) + mm(d[1], w_qkv[1][:, :6 * hd], NT) + mm(d[2], third, NT)).reshape(2, rows, width)
    mine = lax.dynamic_index_in_dim(part, inner, 0, keepdims=False)
    theirs = lax.dynamic_index_in_dim(part, 1 - inner, 0, keepdims=False).astype(bf16)
    grad_tokens = mine + grid.swap(theirs, 1).astype(f32) + dr1
    d_sum = [jnp.sum(one.astype(f32), axis=0) for one in d]
    d_bias = [jnp.concatenate([d_sum[o]] + [d_sum[2][(2 * n + o) * hd:(2 * n + o + 1) * hd] for n in range(3)]) for o in range(2)]
    dg2, ds2, d_down_bias, dg1, ds1, d_out_bias = jnp.sum(sums, axis=1)
    d_up_bias = jnp.sum(up_sums, axis=1).reshape(2, 2 * units)
    grad_memory = jnp.dot(picks.astype(f32).T, grad_tokens, precision=lax.Precision.HIGHEST)

    order = jnp.arange(4, dtype=jnp.int32) ^ tensor
    up_parts = d_up_bias.reshape(2, 2, units)
    up_parts = jnp.stack([up_parts[0, 0], up_parts[1, 0], up_parts[0, 1], up_parts[1, 1]])[order]
    take = lambda o: restore(d_bias[o])[:, 0::2].reshape(-1)
    blank = jnp.zeros((2 * hw,), f32)
    qv_parts = jnp.stack([take(0), blank, take(1), blank])[order]
    pieces = [grad_memory.reshape(-1), d_out_bias, dg1, ds1, d_down_bias, dg2, ds2, up_parts.reshape(-1), qv_parts.reshape(-1)]
    summed = grid.total(jnp.concatenate(pieces))
    outs, at = [], 0
    for piece in pieces:
        outs.append(lax.slice_in_dim(summed, at, at + piece.size))
        at += piece.size
    t_memory, t_out_bias, t_g1, t_s1, t_down_bias, t_g2, t_s2, t_up, t_qv = outs
    grad_up_bias = lax.dynamic_index_in_dim(t_up.reshape(4, units), tensor, 0, keepdims=False)
    grad_qv = lax.dynamic_index_in_dim(t_qv.reshape(4, heads, 2 * hd), tensor, 0, keepdims=False)
    return (block_out, grad_tokens, t_memory.reshape(-1, width), grad_qkv, grad_qv,
            grad_out.reshape(slice_rows, heads, hd), t_out_bias, t_g1, t_s1, grad_up, grad_up_bias, grad_down,
            t_down_bias, t_g2, t_s2)


def blend_one_kernel(x_ref, down, down_early, down_late, up, up_in, out, out_in, kept_down, kept_up, kept_out, send_x, send_y):
    f32, bf16 = jnp.float32, jnp.bfloat16
    x = x_ref[0]
    width = down.shape[-1]
    add = lambda a, b: a.astype(f32) + b.astype(f32)
    early = pl.program_id(0) < pl.num_programs(0) // 2
    down_in = lambda n: jnp.where(early, down_early[0, n], down_late[0, n])
    kept_down[0] = add(down[0, x], down_in(x))
    kept_out[0] = add(out[0, x], out_in[0, x])
    send_x[0, :, 0:width] = add(down[0, 1 - x], down_in(1 - x)).astype(bf16)
    send_x[0, :, width:] = add(out[0, 1 - x], out_in[0, 1 - x]).astype(bf16)
    kept_up[0] = add(up[0, 0], up_in[0, 0])
    send_y[0] = add(up[1, 0], up_in[1, 0]).astype(bf16)


def blend_one(x, down, down_early, down_late, up, up_in, out, out_in):
    f32, bf16 = jnp.float32, jnp.bfloat16
    _, zs, r, width = up.shape
    ow = out.shape[-1]
    shape = jax.ShapeDtypeStruct
    by_x = lambda columns: pl.BlockSpec((1, 2, r, columns), lambda j, *_: (j, 0, 0, 0))
    by_y = pl.BlockSpec((2, 1, r, width), lambda j, *_: (0, j, 0, 0))
    one = lambda columns: pl.BlockSpec((1, r, columns), lambda j, *_: (j, 0, 0))
    lower = pl.BlockSpec((1, 2, r, width), lambda j, *_: (jnp.minimum(j, zs // 2 - 1), 0, 0, 0))
    upper = pl.BlockSpec((1, 2, r, width), lambda j, *_: (jnp.maximum(j - zs // 2, 0), 0, 0, 0))
    fold = lambda a: a.reshape(-1, 2, r, a.shape[-1])
    return pl.pallas_call(
        blend_one_kernel,
        out_shape=(shape((zs, r, width), f32), shape((zs, r, width), f32), shape((zs, r, ow), f32),
                   shape((zs, r, width + ow), bf16), shape((zs, r, width), bf16)),
        grid_spec=pltpu.PrefetchScalarGridSpec(
            num_scalar_prefetch=1, grid=(zs,),
            in_specs=[by_x(width), lower, upper, by_y, by_y, by_x(ow), by_x(ow)],
            out_specs=[one(width), one(width), one(ow), one(width + ow), one(width)]),
        compiler_params=pltpu.CompilerParams(dimension_semantics=("arbitrary",), vmem_limit_bytes=VMEM_MAX),
        cost_estimate=pl.CostEstimate(flops=8 * zs * r * width, bytes_accessed=10_000_000, transcendentals=0),
        name="blend_one",
    )(x.reshape(1), fold(down), fold(down_early), fold(down_late), up, up_in, fold(out), fold(out_in))


def blend_two_kernel(at_ref, kept_down, kept_up, kept_out, came_x, came_y, first, kept_z, kept_first, *sends):
    f32, bf16 = jnp.float32, jnp.bfloat16
    x, z = at_ref[0], at_ref[1]
    zs, r, width = kept_down.shape
    for k in range(zs):
        n = (z + k) % zs
        parts = (kept_down[n] + came_x[n, :, 0:width].astype(f32), kept_up[n] + came_y[n].astype(f32),
                 kept_out[n] + came_x[n, :, width:].astype(f32))
        start = 0
        for part in parts:
            stop = start + part.shape[1]
            if k == 0:
                kept_z[:, start:stop] = part
            else:
                sends[k - 1][:, start:stop] = part.astype(bf16)
            start = stop
        kept_first[k] = first[k, x]
        sends[zs - 1][k] = first[k, 1 - x].astype(bf16)


def blend_two(x, z, kept_down, kept_up, kept_out, came_x, came_y, first):
    f32, bf16 = jnp.float32, jnp.bfloat16
    zs, r, width = kept_down.shape
    columns = 2 * width + kept_out.shape[-1]
    shape = jax.ShapeDtypeStruct
    vmem = pl.BlockSpec(memory_space=pltpu.VMEM)
    return pl.pallas_call(
        blend_two_kernel,
        out_shape=(shape((r, columns), f32), shape((zs, r, first.shape[-1]), f32), *[shape((r, columns), bf16)] * (zs - 1),
                   shape((zs, r, first.shape[-1]), bf16)),
        in_specs=[pl.BlockSpec(memory_space=pltpu.SMEM)] + [vmem] * 6,
        out_specs=[vmem] * (zs + 2),
        compiler_params=pltpu.CompilerParams(vmem_limit_bytes=VMEM_MAX),
        cost_estimate=pl.CostEstimate(flops=4 * zs * r * columns, bytes_accessed=10_000_000, transcendentals=0),
        name="blend_two",
    )(jnp.stack([x, z]), kept_down, kept_up, kept_out, came_x, came_y, first.reshape(zs, 2, r, first.shape[-1]))


def spread_kernel(t_ref, kept, came_one, came_two, came_three, small, one, two,
                  down, up, out, memory, up_bias, qkv, qv, *vectors):
    f32 = jnp.float32
    width = down.shape[1]
    total = lambda cols: ((kept[:, cols] + came_one[:, cols].astype(f32))
                          + (came_two[:, cols].astype(f32) + came_three[:, cols].astype(f32)))
    down[...] = total(slice(0, width))
    up[...] = total(slice(width, 2 * width))
    out[...] = total(slice(2 * width, 2 * width + 256)).T[0:192, :]
    half = width // 2
    t = t_ref[0]
    for h in range(2):
        cols = slice(half * h, half * h + half)
        memory[:, cols] = small[h, 0:memory.shape[0], :]
        qv[h:h + 1, :] = small[h, pl.ds(34 + t, 1), :]
        for n, ref in enumerate(vectors):
            ref[cols] = small[h, 24 + n, :]
        up_bias[cols] = small[h, pl.ds(30 + t, 1), :].reshape(half)
    turn = lambda value: pltpu.roll(value, 64, 1)
    q, k, v = [one[:, 128 * n:128 * n + 128] for n in range(3)]
    lane = lax.broadcasted_iota(jnp.int32, q.shape, 1)
    qkv[0, :, 0:128] = jnp.where(lane < 64, q, turn(k))
    qkv[0, :, 128:192] = v[:, 0:64]
    qkv[1, :, 0:128] = jnp.where(lane < 64, turn(q), k)
    qkv[1, :, 128:192] = turn(v)[:, 0:64]
    n = two.shape[1]
    lane = lax.broadcasted_iota(jnp.int32, two.shape[1:], 1)
    qkv[2, 0:n, 0:128] = jnp.where(lane < 64, two[0], turn(two[1]))
    qkv[2, n:2 * n, 0:128] = jnp.where(lane < 64, turn(two[0]), two[1])
    qkv[2, 0:n, 128:192] = two[2][:, 0:64]
    qkv[2, n:2 * n, 128:192] = turn(two[2])[:, 0:64]


def spread(tensor, kept, came, small, one, two, memory):
    f32 = jnp.float32
    r, columns = kept.shape
    width = 2 * small.shape[2]
    shape = jax.ShapeDtypeStruct
    vmem = pl.BlockSpec(memory_space=pltpu.VMEM)
    return pl.pallas_call(
        spread_kernel,
        out_shape=(shape((r, width), f32), shape((r, width), f32), shape((192, r), f32), shape((memory, width), f32),
                   shape((width,), f32), shape((3, r, 192), f32), shape((2, width // 2), f32), *[shape((width,), f32)] * 6),
        in_specs=[pl.BlockSpec(memory_space=pltpu.SMEM)] + [vmem] * 7,
        out_specs=[vmem] * 13,
        compiler_params=pltpu.CompilerParams(vmem_limit_bytes=VMEM_MAX),
        cost_estimate=pl.CostEstimate(flops=3 * r * columns, bytes_accessed=3_000_000, transcendentals=0),
        name="spread",
    )(tensor.reshape(1), kept, *came, small, one, two)


def finish_small(grid, tensor, x_all, q, k, v, do_all, mixed, lse, segments, w_qkv, third, dr1, column, sums, up_sums, block_out,
                 grads, hw):
    f32, bf16 = jnp.float32, jnp.bfloat16
    tie = lax.optimization_barrier
    TN = (((0,), (0,)), ((), ()))
    width = dr1.shape[1]
    x, z = lax.axis_index("dp") % 2, lax.axis_index("dp") // 2
    down, down_far, down_early, up, up_far, out, out_far = grads

    def beside(pair, q, sends):
        arrays, q = tie(([a for a, _ in sends], q))
        came = [move(a) for a, (_, move) in zip(arrays, sends)]
        d = attend_backward(pair, q, k, v, do_all, mixed, lse, segments)
        return tie((came, d, q))

    over_y = lambda a: grid.swap(a, 2)
    over_x = lambda a: grid.turn(a, 1, 1)
    (down_in, out_in, up_in), d_one, q = beside(1, q, [(down_far, over_y), (out_far, over_y), (up_far, over_x)])
    g_one = mm(x_all, d_one, TN).astype(bf16)
    kept_down, kept_up, kept_out, send_x, send_y = blend_one(x, down, down_early, down_in, up, up_in, out, out_in)
    (came_x, came_y, came_one), d_zero, q = beside(0, q, [(send_x, over_x), (send_y, over_y), (g_one, over_y)])
    first = mm(x_all, d_zero, TN) + came_one.astype(f32)
    kept, kept_first, *sends = blend_two(x, z, kept_down, kept_up, kept_out, came_x, came_y, first)
    over_z = [lambda a, n=n: grid.turn(a, 0, n) for n in range(1, 4)]
    came, d_two, q = beside(2, q, list(zip(sends, over_z + [over_x])))
    grad_tokens, one, two, small = leave(x_all, (d_zero, d_one, d_two), w_qkv, third, kept_first, came[3], dr1, column, sums, up_sums)
    grad_down, grad_up, grad_out, grad_memory, up_bias, grad_qkv, qv, *vec = spread(tensor, kept, came[:3], small, one, two, 20)
    hd = 64
    part = lambda n: jnp.concatenate([qv[0, 128 * n:128 * n + 128].reshape(2, hd), qv[1:2, 128 * n:128 * n + hd]])
    grad_qv = jnp.concatenate([part(0), part(2)], 1)
    t_out_bias, t_g1, t_s1, t_down_bias, t_g2, t_s2 = [vec[n] for n in (5, 3, 4, 2, 0, 1)]
    return (block_out, grad_tokens, grad_memory, grad_qkv.transpose(1, 0, 2), grad_qv,
            grad_out.reshape(3, hd, -1).transpose(2, 0, 1), t_out_bias, t_g1, t_s1, grad_up, up_bias, grad_down,
            t_down_bias, t_g2, t_s2)


def solution(mesh):
    grid = Grid(mesh.shape["dp"], mesh.shape["tensor"])
    tokens, dp, none = P(AXES, None), P("dp", None), P()
    heads, matrix = P("dp", "tensor", None), P("dp", "tensor")
    in_specs = (tokens, dp, dp, none, heads, P("tensor", None), heads, none, none, none, matrix, P("tensor"), matrix,
                none, none, none, tokens)
    out_specs = (tokens, tokens, none, heads, P("tensor", None), heads, none, none, none, matrix, P("tensor"), matrix,
                 none, none, none)

    def run(*args):
        return shards(grid, *args)

    return jax.shard_map(run, mesh=mesh, in_specs=in_specs, out_specs=out_specs, check_vma=False)
```

```python
import functools

import jax
import jax.numpy as jnp
from jax import lax
from jax.experimental import pallas as pl
from jax.experimental.pallas import tpu as pltpu
from jax.sharding import PartitionSpec as P

EPSILON = 1e-12
TILE = 256
MASKED = -1e30
VMEM_MAX = 64 * 1024 * 1024 - 128 * 1024
NT = (((1,), (1,)), ((), ()))
NN = (((1,), (0,)), ((), ()))


def mm(a, b, dims=NN):
    return lax.dot_general(a, b, dims, preferred_element_type=jnp.float32)


def fold8(x):
    r = x.shape[0]
    return x.reshape(r // 8, 8, x.shape[1])


def head_masks(block):
    lane = lax.broadcasted_iota(jnp.int32, block.shape, 1)
    zero = jnp.zeros_like(block)
    return jnp.where(lane < 64, block, zero), jnp.where(lane < 64, zero, block)


def tile_visible(first_ref, last_ref, i, t):
    return (first_ref[t] == 0) | ((first_ref[t] <= last_ref[i]) & (last_ref[t] >= first_ref[i]))


def forward_kernel(first_ref, last_ref, q_ref, k_ref, v_ref, kseg_ref, qseg_ref, o_ref, lse_ref,
                   vt_ref, qm_ref, s_ref, m_ref, l_ref, acc_ref):
    i = pl.program_id(0)
    tiles = pl.num_programs(0)
    pairs = q_ref.shape[1] // 128
    heads = 2 * pairs

    @pl.when(i == 0)
    def _():
        def turn(t, c):
            rows = pl.ds(pl.multiple_of(t * TILE, TILE), TILE)
            vt_ref[t] = v_ref[rows, :].T
            return c
        lax.fori_loop(0, tiles, turn, 0)

    for g in range(pairs):
        a, b = head_masks(q_ref[:, 128 * g:128 * g + 128])
        qm_ref[2 * g] = a
        qm_ref[2 * g + 1] = b
    m_ref[...] = jnp.full_like(m_ref, MASKED)
    l_ref[...] = jnp.zeros_like(l_ref)
    acc_ref[...] = jnp.zeros_like(acc_ref)
    qseg = qseg_ref[0:1, :]

    def scores(t, c):
        @pl.when(tile_visible(first_ref, last_ref, i, t))
        def _():
            rows = pl.ds(pl.multiple_of(t * TILE, TILE), TILE)
            kseg = kseg_ref[rows, :]
            kseg = jnp.concatenate([kseg, kseg], axis=1)
            seen = (kseg == 0) | (kseg == qseg)
            for h in range(heads):
                kp = k_ref[rows, 128 * (h // 2):128 * (h // 2) + 128]
                s = mm(kp, qm_ref[h], NT)
                s = jnp.where(seen, s, MASKED)
                s_ref[h, t] = s
                m_ref[h] = jnp.maximum(m_ref[h], jnp.max(fold8(s), axis=0))
        return c
    lax.fori_loop(0, tiles, scores, 0)
    for h in range(heads):
        m_ref[h] = jnp.broadcast_to(jnp.max(m_ref[h], axis=0, keepdims=True), (8, TILE))

    def mix(t, c):
        @pl.when(tile_visible(first_ref, last_ref, i, t))
        def _():
            for h in range(heads):
                p = jnp.exp(s_ref[h, t] - m_ref[h, 0:1, :])
                l_ref[h] = l_ref[h] + jnp.sum(fold8(p), axis=0)
                acc_ref[h] = acc_ref[h] + mm(vt_ref[t, 64 * h:64 * h + 64, :], p.astype(jnp.bfloat16))
        return c
    lax.fori_loop(0, tiles, mix, 0)
    for h in range(heads):
        total = jnp.sum(l_ref[h], axis=0, keepdims=True)
        lse_ref[h:h + 1, :] = m_ref[h, 0:1, :] + jnp.log(total)
        acc_ref[h] = acc_ref[h] / total
    for g in range(pairs):
        pair = jnp.concatenate([acc_ref[2 * g], acc_ref[2 * g + 1]], axis=0)
        o_ref[:, 128 * g:128 * g + 128] = pair.T.astype(jnp.bfloat16)


def attend_forward(q, k, v, seg):
    n, width = q.shape
    tiles = n // TILE
    heads = width // 64
    first = seg[::TILE]
    last = seg[TILE - 1::TILE]
    kseg = jnp.broadcast_to(seg[:, None], (n, 128))
    qseg = jnp.broadcast_to(seg[None, :], (8, n))
    whole = lambda shape: pl.BlockSpec(shape, lambda i, *_: (0,) * len(shape))
    return pl.pallas_call(
        forward_kernel,
        out_shape=(jax.ShapeDtypeStruct((n, width), jnp.bfloat16), jax.ShapeDtypeStruct((8, n), jnp.float32)),
        grid_spec=pltpu.PrefetchScalarGridSpec(
            num_scalar_prefetch=2, grid=(tiles,),
            in_specs=[pl.BlockSpec((TILE, width), lambda i, *_: (i, 0)), whole((n, width)), whole((n, width)),
                      whole((n, 128)), pl.BlockSpec((8, TILE), lambda i, *_: (0, i))],
            out_specs=[pl.BlockSpec((TILE, width), lambda i, *_: (i, 0)), pl.BlockSpec((8, TILE), lambda i, *_: (0, i))],
            scratch_shapes=[
                pltpu.VMEM((tiles, width, TILE), jnp.bfloat16),
                pltpu.VMEM((heads, TILE, 128), jnp.bfloat16),
                pltpu.VMEM((heads, tiles, TILE, TILE), jnp.float32),
                pltpu.VMEM((heads, 8, TILE), jnp.float32),
                pltpu.VMEM((heads, 8, TILE), jnp.float32),
                pltpu.VMEM((heads, 64, TILE), jnp.float32),
            ]),
        compiler_params=pltpu.CompilerParams(dimension_semantics=("arbitrary",), vmem_limit_bytes=VMEM_MAX),
        cost_estimate=pl.CostEstimate(flops=4 * n * n * width, bytes_accessed=8 * n * width, transcendentals=n * n * heads),
        name="attend_forward",
    )(first, last, q, k, v, kseg, qseg)


def backward_kernel(base, first_ref, last_ref, q_ref, do_ref, o_ref, k_ref, v_ref, kseg_ref, qseg_ref, lse_ref,
                    d_ref, kt_ref, qm_ref, dom_ref, delta_ref, dqt_ref, dka_ref, dva_ref):
    i = pl.program_id(0)
    tiles = pl.num_programs(0)

    @pl.when(i == 0)
    def _():
        def turn(t, c):
            rows = pl.ds(pl.multiple_of(t * TILE, TILE), TILE)
            kt_ref[t] = k_ref[rows, :].T
            dka_ref[rows, :] = jnp.zeros((TILE, 128), jnp.float32)
            dva_ref[rows, :] = jnp.zeros((TILE, 128), jnp.float32)
            return c
        lax.fori_loop(0, tiles, turn, 0)

    for ref, masked in ((q_ref, qm_ref), (do_ref, dom_ref)):
        masked[0], masked[1] = head_masks(ref[...])
    inner = (do_ref[...].astype(jnp.float32) * o_ref[...].astype(jnp.float32)).T
    for h in range(2):
        delta_ref[h] = jnp.broadcast_to(jnp.sum(inner[64 * h:64 * h + 64], axis=0, keepdims=True), (8, TILE))
    dqt_ref[...] = jnp.zeros_like(dqt_ref)
    qseg = qseg_ref[0:1, :]

    def count(t, c):
        prompt, before, upto = c
        return (prompt + (first_ref[t] == 0).astype(jnp.int32), before + (last_ref[t] < first_ref[i]).astype(jnp.int32),
                upto + (first_ref[t] <= last_ref[i]).astype(jnp.int32))
    zero = jnp.int32(0)
    prompt, before, upto = lax.fori_loop(0, tiles, count, (zero, zero, zero))
    start = jnp.maximum(prompt, before)
    visible = prompt + jnp.maximum(upto - start, 0)

    def one_tile(n):
        t = jnp.where(n < prompt, n, start + n - prompt)
        rows = pl.ds(pl.multiple_of(t * TILE, TILE), TILE)
        kseg = kseg_ref[rows, :]
        kseg = jnp.concatenate([kseg, kseg], axis=1)
        seen = (kseg == 0) | (kseg == qseg)
        kp = k_ref[rows, :]
        vp = v_ref[rows, :]
        s = [mm(kp, qm_ref[h], NT) for h in range(2)]
        d = [mm(vp, dom_ref[h], NT) for h in range(2)]
        p = [jnp.where(seen, jnp.exp(s[h] - lse_ref[base + h:base + h + 1, :]), 0.0) for h in range(2)]
        ds = [(p[h] * (d[h] - delta_ref[h, 0:1, :])).astype(jnp.bfloat16) for h in range(2)]
        p = [value.astype(jnp.bfloat16) for value in p]
        dva_ref[rows, :] = dva_ref[rows, :] + (mm(p[0], dom_ref[0]) + mm(p[1], dom_ref[1]))
        dka_ref[rows, :] = dka_ref[rows, :] + (mm(ds[0], qm_ref[0]) + mm(ds[1], qm_ref[1]))
        return [mm(kt_ref[t, 64 * h:64 * h + 64, :], ds[h]) for h in range(2)]

    def two_tiles(n, c):
        one, two = one_tile(2 * n), one_tile(2 * n + 1)
        for h in range(2):
            dqt_ref[h] = dqt_ref[h] + (one[h] + two[h])
        return c
    lax.fori_loop(0, visible // 2, two_tiles, 0)

    @pl.when(visible % 2 == 1)
    def _():
        for h, value in enumerate(one_tile(visible - 1)):
            dqt_ref[h] = dqt_ref[h] + value
    pair = jnp.concatenate([dqt_ref[0], dqt_ref[1]], axis=0)
    own = pl.ds(pl.multiple_of(i * TILE, TILE), TILE)
    d_ref[own, 0:128] = (pair.T * 0.125).astype(jnp.bfloat16)

    @pl.when(i == tiles - 1)
    def _():
        d_ref[:, 128:256] = dka_ref[...].astype(jnp.bfloat16)
        d_ref[:, 256:384] = dva_ref[...].astype(jnp.bfloat16)


def attend_backward(g, q, k, v, do, o, lse, seg):
    n, width = q.shape[0], 128
    tiles = n // TILE
    heads = width // 64
    first = seg[::TILE]
    last = seg[TILE - 1::TILE]
    kseg = jnp.broadcast_to(seg[:, None], (n, 128))
    qseg = jnp.broadcast_to(seg[None, :], (8, n))
    whole = lambda shape: pl.BlockSpec(shape, lambda i, *_: (0,) * len(shape))
    rows = pl.BlockSpec((TILE, width), lambda i, *_: (i, g))
    column = pl.BlockSpec((n, width), lambda i, *_: (0, g))
    stat = pl.BlockSpec((8, TILE), lambda i, *_: (0, i))
    return pl.pallas_call(
        functools.partial(backward_kernel, 2 * g),
        out_shape=jax.ShapeDtypeStruct((n, 3 * width), jnp.bfloat16),
        grid_spec=pltpu.PrefetchScalarGridSpec(
            num_scalar_prefetch=2, grid=(tiles,),
            in_specs=[rows, rows, rows, column, column, whole((n, 128)), stat, stat],
            out_specs=whole((n, 3 * width)),
            scratch_shapes=[
                pltpu.VMEM((tiles, width, TILE), jnp.bfloat16),
                pltpu.VMEM((heads, TILE, 128), jnp.bfloat16),
                pltpu.VMEM((heads, TILE, 128), jnp.bfloat16),
                pltpu.VMEM((heads, 8, TILE), jnp.float32),
                pltpu.VMEM((heads, 64, TILE), jnp.float32),
                pltpu.VMEM((n, width), jnp.float32),
                pltpu.VMEM((n, width), jnp.float32),
            ]),
        compiler_params=pltpu.CompilerParams(dimension_semantics=("arbitrary",), vmem_limit_bytes=VMEM_MAX),
        cost_estimate=pl.CostEstimate(flops=10 * n * n * width, bytes_accessed=14 * n * width, transcendentals=n * n * heads),
        name="attend_backward",
    )(first, last, q, do, o, k, v, kseg, qseg, lse)


BLOCK = 256
STRIP = 64


def normal_cdf_parts(u):
    v = u * 0.7071067811865476
    c = jnp.clip(v, -3.832506856900711, 3.832506856900711)
    c2 = c * c
    top = 0.00022905065861350646
    for a in (0.0034082910107109506, 0.050955695062380861, 0.18520832239976145, 1.128379143519084):
        top = top * c2 + a
    low = -1.1791602954361697e-7
    for b in (0.000023547966471313185, 0.0010179625278914885, 0.014070470171167667, 0.11098505178285362,
              0.49746925110067538, 1.0):
        low = low * c2 + b
    cdf = 0.5 + 0.5 * (c * top / low)
    slope = jnp.exp(-(v * v)) * (u * 0.3989422804014327)
    return u * cdf, cdf + slope


def middle_kernel(pieces, o_all, x0, outs, ups, downs, cot, vec_ref, bup_ref,
                  block_out, dr1, do_all, g_down, g_up, g_out, sums_ref, upsum_ref,
                  o_ref, raw_ref, wo_ref, wu_ref, wd_ref, hat_ref, inv_ref, acc_ref, hl_ref, hlt_ref, gp_ref, z_ref, c_ref,
                  df_ref, dft_ref, y_ref, st_ref, su_ref, ru_ref, rd_ref, go_ref, rgo_ref, u0_ref, u1_ref,
                  sem, osem, send, recv):
    f32, bf16 = jnp.float32, jnp.bfloat16
    rows, width = hat_ref.shape
    blocks = rows // BLOCK
    part = wu_ref.shape[2]
    bf = lambda a: a.astype(bf16)
    dp, tensor = lax.axis_index("dp"), lax.axis_index("tensor")
    inner = tensor % 2
    partner = (dp, tensor + 1 - 2 * inner)
    z, x = dp // 2, dp % 2
    to_x = (2 * z + 1 - x, tensor)
    to_y = (dp, (tensor + 2) % 4)
    mine = pl.multiple_of(inner * rows, 1024)
    theirs = pl.multiple_of((1 - inner) * rows, 1024)
    greet([partner, to_x, to_y] if pieces else [partner])

    def remote(n, src, dst, device=partner):
        return pltpu.make_async_remote_copy(src, dst, send.at[n], recv.at[n], device_id=device,
                                            device_id_type=pl.DeviceIdType.MESH)

    swap_o = remote(0, o_all.at[pl.ds(theirs, rows), :], o_ref.at[1])
    swap_o.start()
    count = [0]

    def load(src, dst):
        copy = pltpu.make_async_copy(src, dst, sem.at[count[0]])
        count[0] += 1
        copy.start()
        return copy

    def weight(sources, dst):
        if not pieces:
            return [load(sources[0].at[o], dst.at[o]) for o in range(2)]
        digit = dp % 2
        made = []
        for o in range(2):
            for zi in range(sources[0].shape[1]):
                for n in range(2):
                    place = 2 * zi + (digit if n == 0 else 1 - digit)
                    r = sources[n].shape[2]
                    made.append(load(sources[n].at[o, zi], dst.at[o, pl.ds(pl.multiple_of(place * r, r), r), :]))
        return made

    if pieces:
        r = downs[0].shape[0]
        block = lambda o, zi: wd_ref.at[o, pl.ds(pl.multiple_of(zi * r, r), r), :]
        zs = [(z + 4 - k) % 4 for k in range(4)]
        held = [load(downs[k], block(0, zs[k])) for k in range(4)]
    first = [load(o_all.at[pl.ds(mine, rows), :], o_ref.at[0]), load(x0, hat_ref)] + weight(outs, raw_ref.at[0])
    if pieces:
        second = [load(ups[o], wu_ref.at[o]) for o in range(2)]
    else:
        second = [load(ups[0].at[o], wu_ref.at[o]) for o in range(2)]
    if not pieces:
        second = second + weight(downs, wd_ref)
    late = load(cot, c_ref)
    if pieces:
        for copy in held:
            copy.wait()
        by_y = [remote(12 + m, block(0, 2 * x + m), block(1, 2 * x + m), to_y) for m in range(2)]
        by_x = [remote(14 + m, block(1, 2 * x + m), block(1, 2 * x + m), to_x) for m in range(2)]
        for copy in by_y:
            copy.start()
    vec = lambda n: vec_ref[n:n + 1, :]
    sums_ref[...] = jnp.zeros_like(sums_ref)
    upsum_ref[...] = jnp.zeros_like(upsum_ref)
    for copy in first:
        copy.wait()
    swaps = [remote(1, raw_ref.at[0], raw_ref.at[1])]
    swaps[0].start()
    for copy in second:
        copy.wait()
    for o in range(2):
        swaps.append(remote(2 + 2 * o, wu_ref.at[o], wu_ref.at[2 + o]))
        swaps.append(remote(3 + 2 * o, wd_ref.at[o], wd_ref.at[2 + o]))
    for copy in swaps[1:4] if pieces else swaps[1:]:
        copy.start()
    lane = lax.broadcasted_iota(jnp.int32, (width, 128), 1)

    def order_heads(side):
        wo_ref[side, :, 0:128] = raw_ref[side, 0, :, 0:128]
        wo_ref[side, :, 128:256] = raw_ref[side, 1, :, 0:128]
        upper = pltpu.roll(raw_ref[side, 1, :, 128:256].astype(f32), 64, 1)
        wo_ref[side, :, 256:384] = bf(jnp.where(lane < 64, raw_ref[side, 0, :, 128:256].astype(f32), upper))
    order_heads(0)
    swaps[0].wait()
    order_heads(1)
    swap_o.wait()

    def strips(body):
        def run(s, carry):
            body(pl.ds(pl.multiple_of(s * STRIP, STRIP), STRIP))
            return carry
        lax.fori_loop(0, rows // STRIP, run, 0)

    def add_sum(n, value):
        sums_ref[n] = sums_ref[n] + jnp.sum(fold(value), axis=0)

    def fold(value):
        return value.reshape(value.shape[0] // 8, 8, value.shape[1])

    def mean(value):
        return jnp.sum(value, axis=-1, keepdims=True) * (1.0 / width)

    def project(b, carry):
        r = pl.ds(pl.multiple_of(b * BLOCK, BLOCK), BLOCK)
        acc_ref[r, :] = mm(o_ref[0, r, :], wo_ref[0], NT) + mm(o_ref[1, r, :], wo_ref[1], NT)
        return carry
    lax.fori_loop(0, blocks, project, 0)

    def first_norm(r):
        r1 = hat_ref[r, :] + (acc_ref[r, :] + vec(0))
        centre = r1 - mean(r1)
        inv = lax.rsqrt(mean(centre * centre) + EPSILON)
        hat = centre * inv
        hat_ref[r, :] = hat
        inv_ref[r, :] = inv
        hl_ref[r, :] = bf(hat * vec(1) + vec(2))
    strips(first_norm)
    if pieces:
        by_y[0].wait_recv()
        by_x[0].start()
    for b in range(blocks):
        hlt_ref[:, BLOCK * b:BLOCK * b + BLOCK] = hl_ref[BLOCK * b:BLOCK * b + BLOCK, :].T
    acc_ref[...] = jnp.zeros_like(acc_ref)

    bufs = (u0_ref, u1_ref)

    def forward(n, carry):
        j = n % 2 * 2 + n // 2
        for o in range(2):
            @pl.when(j == 2 + o)
            def _(o=o):
                swaps[1 + 2 * o].wait()
                swaps[2 + 2 * o].wait()
        if pieces:
            def relay():
                by_y[1].wait_recv()
                by_x[1].start()

            def arrive():
                for copy in by_x:
                    copy.wait()
                for copy in by_y:
                    copy.wait_send()
                swaps[4].start()

        def lift(b):
            bufs[b % 2][...] = mm(hl_ref[BLOCK * b:BLOCK * b + BLOCK, :], wu_ref[j]) + bup_ref[j, 0:1, :].astype(f32)
        lift(0)
        for b in range(blocks):
            if b + 1 < blocks:
                lift(b + 1)
            if pieces and b == blocks // 2:
                pl.when(j == 2)(relay)
            r = slice(BLOCK * b, BLOCK * b + BLOCK)
            for i in range(0, BLOCK, 32):
                for w in range(0, part, 256):
                    z, gp = normal_cdf_parts(bufs[b % 2][i:i + 32, w:w + 256])
                    z_ref[j, BLOCK * b + i:BLOCK * b + i + 32, w:w + 256] = bf(z)
                    gp_ref[j, BLOCK * b + i:BLOCK * b + i + 32, w:w + 256] = gp
            if pieces and b == 0:
                pl.when(j == 1)(arrive)
            acc_ref[r, :] = acc_ref[r, :] + mm(z_ref[j, r, :], wd_ref[j], NT)
        return carry
    lax.fori_loop(0, 4, forward, 0)
    late.wait()

    def second_norm(r):
        h1 = hat_ref[r, :] * vec(1) + vec(2)
        r2 = h1 + (acc_ref[r, :] + vec(3))
        centre = r2 - mean(r2)
        inv = lax.rsqrt(mean(centre * centre) + EPSILON)
        hat = centre * inv
        y_ref[r, :] = bf(hat * vec(4) + vec(5))
        c = c_ref[r, :].astype(f32)
        add_sum(0, c * hat)
        add_sum(1, c)
        w = c * vec(4)
        dr2 = (w - mean(w) - hat * mean(w * hat)) * inv
        acc_ref[r, :] = dr2
        low = bf(dr2)
        df_ref[r, :] = low
        add_sum(2, low.astype(f32))
    strips(second_norm)
    stores = [pltpu.make_async_copy(y_ref, block_out, osem.at[0])]
    stores[0].start()
    for b in range(blocks):
        dft_ref[:, BLOCK * b:BLOCK * b + BLOCK] = df_ref[BLOCK * b:BLOCK * b + BLOCK, :].T

    def backward(n, carry):
        j = 3 - n

        def lower(b):
            bufs[b % 2][...] = mm(df_ref[BLOCK * b:BLOCK * b + BLOCK, :], wd_ref[j])
        slot = n % 2
        away = [remote(6 + slot, st_ref.at[slot], rd_ref.at[slot]), remote(8 + slot, su_ref.at[slot], ru_ref.at[slot])]
        lower(0)
        for b in range(blocks):
            if b + 1 < blocks:
                lower(b + 1)
            r = slice(BLOCK * b, BLOCK * b + BLOCK)
            for i in range(0, BLOCK, 64):
                q = slice(BLOCK * b + i, BLOCK * b + i + 64)
                dul = bf(bufs[b % 2][i:i + 64, :] * gp_ref[j, q, :])
                upsum_ref[j] = upsum_ref[j] + jnp.sum(fold(dul.astype(f32)), axis=0)
                hat2_ref[q, :] = dul
            acc_ref[r, :] = acc_ref[r, :] + mm(hat2_ref[r, :], wu_ref[j], NT)

        @pl.when(n < 2)
        def _():
            for m in range(0, width, BLOCK):
                st_ref[slot, m:m + BLOCK, :] = bf(mm(dft_ref[m:m + BLOCK, :], z_ref[j]))
            away[0].start()
            for m in range(0, width, BLOCK):
                su_ref[slot, m:m + BLOCK, :] = bf(mm(hlt_ref[m:m + BLOCK, :], hat2_ref[...]))
            away[1].start()

        @pl.when(n >= 2)
        def _():
            away[0].wait()
            for m in range(0, width, BLOCK):
                got = rd_ref[slot, m:m + BLOCK, :].astype(f32)
                st_ref[slot, m:m + BLOCK, :] = bf(mm(dft_ref[m:m + BLOCK, :], z_ref[j]) + got)
            if pieces:
                @pl.when(j == 0)
                def _():
                    pltpu.make_async_copy(st_ref.at[1], g_down[0], osem.at[2]).start()

                @pl.when(j == 1)
                def _():
                    early.start()
                    pltpu.make_async_copy(st_ref.at[0, width // 2:, :], g_down[1], osem.at[1]).start()
            else:
                pltpu.make_async_copy(st_ref.at[slot], g_down.at[j], osem.at[1 + slot]).start()
            away[1].wait()
            for m in range(0, width, BLOCK):
                got = ru_ref[slot, m:m + BLOCK, :].astype(f32)
                su_ref[slot, m:m + BLOCK, :] = bf(mm(hlt_ref[m:m + BLOCK, :], hat2_ref[...]) + got)
            if pieces:
                r = g_up[0].shape[2]
                for zi in range(g_up[0].shape[1]):
                    for o in range(2):
                        at = pl.multiple_of((2 * zi + (dp + o) % 2) * r, r)
                        pltpu.make_async_copy(su_ref.at[slot, pl.ds(at, r), :], g_up[o].at[j, zi], osem.at[3 + slot]).start()
            else:
                pltpu.make_async_copy(su_ref.at[slot], g_up.at[j], osem.at[3 + slot]).start()
        return carry
    hat2_ref = y_ref
    stores[0].wait()
    if pieces:
        early = remote(16, st_ref.at[0, 0:width // 2, :], g_down[2], to_y)
    lax.fori_loop(0, 4, backward, 0)

    def first_back(r):
        dh1 = acc_ref[r, :]
        hat = hat_ref[r, :]
        add_sum(3, dh1 * hat)
        add_sum(4, dh1)
        w = dh1 * vec(1)
        grad = (w - mean(w) - hat * mean(w * hat)) * inv_ref[r, :]
        acc_ref[r, :] = grad
        low = bf(grad)
        df_ref[r, :] = low
        add_sum(5, low.astype(f32))
    strips(first_back)
    out = pltpu.make_async_copy(acc_ref, dr1, osem.at[0])
    out.start()
    stores = [out]
    for b in range(blocks):
        dft_ref[:, BLOCK * b:BLOCK * b + BLOCK] = df_ref[BLOCK * b:BLOCK * b + BLOCK, :].T
    lane = lax.broadcasted_iota(jnp.int32, (BLOCK, 128), 1)

    def out_grad(side, m):
        tiles = [mm(dft_ref[m:m + BLOCK, :], o_ref[side, :, 128 * g:128 * g + 128]) for g in range(3)]
        third = [jnp.where(lane < 64, tiles[2], 0.0), jnp.where(lane < 64, pltpu.roll(tiles[2], 64, 1), 0.0)]
        return [jnp.concatenate([tiles[o], third[o]], axis=1) for o in range(2)]
    for m in range(0, width, BLOCK):
        for o, value in enumerate(out_grad(1, m)):
            go_ref[o, m:m + BLOCK, :] = bf(value)
    swap_go = remote(10, go_ref, rgo_ref)
    swap_go.start()
    ow = wo_ref.shape[2]
    for side in (1, 0):
        def push(b, carry):
            r = pl.ds(pl.multiple_of(b * BLOCK, BLOCK), BLOCK)
            y_ref[r, ow * side:ow * side + ow] = bf(mm(df_ref[r, :], wo_ref[side]))
            return carry
        lax.fori_loop(0, blocks, push, 0)
        if side == 1:
            swap_do = remote(11, y_ref.at[:, pl.ds(ow, ow)], do_all.at[pl.ds(mine, rows), :])
            swap_do.start()
        else:
            copy = pltpu.make_async_copy(y_ref.at[:, pl.ds(0, ow)], do_all.at[pl.ds(mine, rows), :], osem.at[5])
            copy.start()
            stores.append(copy)
    swap_go.wait()
    for m in range(0, width, BLOCK):
        for o, value in enumerate(out_grad(0, m)):
            go_ref[o, m:m + BLOCK, :] = bf(value + rgo_ref[o, m:m + BLOCK, :].astype(f32))
    for o in range(2 if pieces else 1):
        copy = pltpu.make_async_copy(go_ref.at[o] if pieces else go_ref, g_out[o] if pieces else g_out, osem.at[6 + o])
        copy.start()
        stores.append(copy)
    whole = g_down[0] if pieces else g_down.at[0]
    for slot in range(2):
        if pieces and slot == 0:
            pltpu.make_async_copy(st_ref.at[0, width // 2:, :], g_down[1], osem.at[1]).wait()
        else:
            pltpu.make_async_copy(st_ref.at[slot], whole, osem.at[1 + slot]).wait()
        pltpu.make_async_copy(su_ref.at[slot], whole, osem.at[3 + slot]).wait()
    if pieces:
        early.wait()
    swap_do.wait()
    for copy in stores:
        copy.wait()


def middle(o_all, x0, outs, ups, downs, cot, vec, bup):
    f32, bf16 = jnp.float32, jnp.bfloat16
    rows, width = x0.shape
    ow = o_all.shape[1]
    part = bup.shape[-1]
    pieces = len(ups) == 2
    shape = jax.ShapeDtypeStruct
    hbm = pl.BlockSpec(memory_space=pl.ANY)
    vmem = pl.BlockSpec(memory_space=pltpu.VMEM)
    v = pltpu.VMEM
    n = len(ups)
    m = 2 * n + len(downs)

    def kernel(o_all, x0, *refs):
        weights, rest = refs[:m], refs[m:]
        if pieces:
            rest = rest[:6] + (rest[6:9], rest[9:11], rest[11:13]) + rest[13:]
        middle_kernel(pieces, o_all, x0, weights[:n], weights[n:2 * n], weights[2 * n:], *rest)

    if pieces:
        parts = (2, len(downs), downs[0].shape[0] // 2, part)
        grads = [shape((width, part), bf16)] + [shape((width // 2, part), bf16)] * 2 + [shape(parts, bf16)] * 2 + [shape((width, 256), bf16)] * 2
    else:
        grads = [shape((2, width, part), bf16), shape((2, width, part), bf16), shape((2, width, 256), bf16)]
    return pl.pallas_call(
        kernel,
        out_shape=(shape((rows, width), bf16), shape((rows, width), f32), shape((2 * rows, ow), bf16),
                   *grads, shape((6, 8, width), f32), shape((4, 8, part), f32)),
        in_specs=[hbm] * (3 + m) + [vmem] * 2,
        out_specs=[hbm] * (3 + len(grads)) + [vmem] * 2,
        scratch_shapes=[
            v((2, rows, ow), bf16), v((2, 2, width, 256), bf16), v((2, width, ow), bf16), v((4, width, part), bf16),
            v((4, width, part), bf16),
            v((rows, width), f32), v((rows, 1), f32), v((rows, width), f32), v((rows, width), bf16), v((width, rows), bf16),
            v((4, rows, part), f32), v((4, rows, part), bf16), v((rows, width), bf16), v((rows, width), bf16),
            v((width, rows), bf16), v((rows, width), bf16), v((2, width, part), bf16),
            v((2, width, part), bf16), v((2, width, part), bf16), v((2, width, part), bf16), v((2, width, 256), bf16),
            v((2, width, 256), bf16), v((BLOCK, part), f32), v((BLOCK, part), f32),
            pltpu.SemaphoreType.DMA((40,)), pltpu.SemaphoreType.DMA((8,)),
            pltpu.SemaphoreType.DMA((24,)), pltpu.SemaphoreType.DMA((24,)),
        ],
        compiler_params=pltpu.CompilerParams(vmem_limit_bytes=VMEM_MAX, collective_id=1, has_side_effects=True),
        cost_estimate=pl.CostEstimate(flops=6 * rows * width * 9 * width, bytes_accessed=60_000_000, transcendentals=2 * rows * 4 * part),
        name="middle",
    )(o_all, x0, *outs, *ups, *downs, cot, vec, bup)


class Exchange:
    def __init__(self, send, recv):
        self.send, self.recv, self.used = send, recv, 0

    def copy(self, src, dst, device):
        n = self.used
        self.used += 1
        return pltpu.make_async_remote_copy(src, dst, self.send.at[n], self.recv.at[n], device_id=device,
                                            device_id_type=pl.DeviceIdType.MESH)


def greet(devices):
    barrier = pltpu.get_barrier_semaphore()
    for device in devices:
        pl.semaphore_signal(barrier, inc=1, device_id=device, device_id_type=pl.DeviceIdType.MESH)
    pl.semaphore_wait(barrier, len(devices))


def entry_kernel(tokens, pos_ref, mem_in, wq_in, bq_ref, bu_in, wu_ref, wd_ref, wo_ref,
                 x0_out, x_out, q_out, k_out, v_out, w_out, up_g, down_g, out_g, bu_out,
                 x0_ref, x_ref, g_ref, b_ref, y_ref, third_ref, q_ref, k_ref, v_ref, ub_ref, wq_ref, bu_ref, mem_ref, send, recv, sem):
    f32, bf16 = jnp.float32, jnp.bfloat16
    rows, width = x0_ref.shape
    dp, tensor = lax.axis_index("dp"), lax.axis_index("tensor")
    z, x = dp // 2, dp % 2
    inner = tensor % 2
    zs = [(z + 4 - k) % 4 for k in range(4)]
    at = [2 * zs[k] + x for k in range(4)]
    far = [2 * zs[k] + 1 - x for k in range(4)]
    to_z = [None] + [(2 * ((z + k) % 4) + x, tensor) for k in range(1, 4)]
    to_x = (2 * z + 1 - x, tensor)
    to_y = (dp, (tensor + 2) % 4)
    to_core = (dp, tensor + 1 - 2 * inner)
    to_both = (dp, 3 - tensor)
    heads = [wq_in[n, :, 0:128].astype(f32) for n in range(3)]
    values = [wq_in[n, :, 128:192].astype(f32) for n in range(3)]
    lane = lax.broadcasted_iota(jnp.int32, heads[0].shape, 1)
    wq_ref[:, 0:128] = jnp.where(lane < 64, heads[0], pltpu.roll(heads[1], 64, 1)).astype(bf16)
    wq_ref[:, 128:256] = jnp.where(lane < 64, pltpu.roll(heads[0], 64, 1), heads[1]).astype(bf16)
    wq_ref[:, 256:384] = jnp.concatenate(values[0:2], axis=1).astype(bf16)
    wq_ref[:, 384:512] = wq_in[2, :, 0:128]
    wq_ref[:, 512:576] = wq_in[2, :, 128:192]
    bu_ref[...] = jnp.broadcast_to(bu_in[...].astype(f32), bu_ref.shape).astype(bf16)
    mem_ref[...] = jnp.zeros_like(mem_ref)
    mem_ref[0:mem_in.shape[0], :] = mem_in[...]
    greet(to_z[1:] + [to_x, to_y, to_core, to_both])
    ex = Exchange(send, recv)
    started = []

    def go(src, dst, device):
        copy = ex.copy(src, dst, device)
        copy.start()
        started.append(copy)
        return copy

    local = []

    def keep(src, dst):
        copy = pltpu.make_async_copy(src, dst, sem.at[len(local)])
        copy.start()
        local.append(copy)
        return copy

    own = keep(wq_ref, g_ref.at[0, at[0]])
    own_bias = keep(bq_ref, b_ref.at[0])
    z_q = [None] + [go(wq_ref, g_ref.at[0, at[0]], to_z[k]) for k in range(1, 4)]
    x_q = [go(wq_ref, g_ref.at[0, at[0]], to_x)]
    y_q = [go(wq_ref, g_ref.at[1, at[0]], to_y)]
    bias = go(bq_ref, b_ref.at[1], to_y)
    up_bias = [go(bu_ref, ub_ref.at[n - 1], to) for n, to in ((1, to_y), (2, to_core), (3, to_both))]

    mine = pl.multiple_of(inner * rows, 1024)
    positions = pos_ref[0:1, :]
    strip = 128

    def start(s, carry):
        r = pl.multiple_of(s * strip, strip)
        place = lax.broadcasted_iota(jnp.int32, (strip, positions.shape[1]), 0) + (inner * rows + r)
        picks = jnp.where(place == positions, 1.0, 0.0).astype(bf16)
        value = tokens[pl.ds(r, strip), :].astype(f32) + mm(picks, mem_ref[...])
        x0_ref[pl.ds(r, strip), :] = value
        x_ref[pl.ds(mine + r, strip), :] = value.astype(bf16)
        return carry
    lax.fori_loop(0, rows // strip, start, 0)
    keep(x0_ref, x0_out)
    core = go(x_ref.at[pl.ds(mine, rows), :], x_ref.at[pl.ds(mine, rows), :], to_core)

    for k in range(1, 4):
        z_q[k].wait_recv()
        x_q.append(go(g_ref.at[0, at[k]], g_ref.at[0, at[k]], to_x))
        y_q.append(go(g_ref.at[0, at[k]], g_ref.at[1, at[k]], to_y))
    z_u = [None] + [go(wu_ref, up_g.at[at[0]], to_z[k]) for k in range(1, 4)]
    z_o = [None] + [go(wo_ref, out_g.at[0, z], to_z[k]) for k in range(1, 4)]
    keep(wu_ref, up_g.at[at[0]])
    keep(wd_ref, down_g.at[x])
    keep(wo_ref, out_g.at[0, z])
    last = []
    for k in range(2):
        x_q[k].wait_recv()
        last.append(go(g_ref.at[0, far[k]], g_ref.at[1, far[k]], to_y))
    for k in range(2, 4):
        y_q[k].wait_recv()
        last.append(go(g_ref.at[1, at[k]], g_ref.at[1, at[k]], to_x))
    rest = [go(wd_ref, down_g.at[x], to_x), go(wu_ref, up_g.at[at[0]], to_x), go(wo_ref, out_g.at[1, z], to_y)]
    own.wait()
    own_bias.wait()
    for copy in x_q[2:] + [core]:
        copy.wait_recv()
    keep(x_ref, x_out)
    lane = lax.broadcasted_iota(jnp.int32, (BLOCK, 128), 1)
    blocks = 2 * rows // BLOCK
    heads = (q_ref, k_ref, v_ref)

    def write(n, g, r, value):
        value = value.astype(bf16)
        if n == 0:
            value = value * jnp.asarray(0.125, bf16)
        heads[n][r, 128 * g:128 * g + 128] = value

    def project(o, b):
        r = pl.ds(pl.multiple_of(b * BLOCK, BLOCK), BLOCK)
        y_ref[:, 0:576] = mm(x_ref[r, :], g_ref[o].reshape(width, 576)) + b_ref[o, 0:1, 0:576].astype(f32)
        for n in range(3):
            write(n, o, r, y_ref[:, 128 * n:128 * n + 128])
        return r

    def project_own(b, carry):
        r = project(0, b)
        third_ref[r, :] = y_ref[:, 384:640]
        return carry

    def project_other(b, carry):
        r = project(1, b)
        turn = lambda value: pltpu.roll(value, 64, 1)
        left, right = third_ref[r, 0:128], y_ref[:, 384:512]
        write(0, 2, r, jnp.where(lane < 64, left, turn(right)))
        write(1, 2, r, jnp.where(lane < 64, turn(left), right))
        write(2, 2, r, jnp.where(lane < 64, third_ref[r, 128:256], turn(y_ref[:, 512:640])))
        return carry
    y_ref[...] = jnp.zeros_like(y_ref)
    lax.fori_loop(0, blocks, project_own, 0)
    for copy in y_q[:2] + last + [bias]:
        copy.wait_recv()
    keep(g_ref, w_out)
    for k in range(1, 4):
        z_u[k].wait_recv()
        rest.append(go(up_g.at[at[k]], up_g.at[at[k]], to_x))
        lax.fori_loop(blocks * (k - 1) // 4, blocks * k // 4, project_other, 0)
    lax.fori_loop(blocks * 3 // 4, blocks, project_other, 0)
    for src, dst in ((q_ref, q_out), (k_ref, k_out), (v_ref, v_out)):
        keep(src, dst)
    for k in range(1, 4):
        z_o[k].wait_recv()
        rest.append(go(out_g.at[0, zs[k]], out_g.at[1, zs[k]], to_y))
    for copy in rest + up_bias:
        copy.wait_recv()
    bu_out[0] = bu_ref[...]
    for n in range(3):
        bu_out[n + 1] = ub_ref[n]
    for copy in started:
        copy.wait_send()
    for copy in local[2:]:
        copy.wait()


def entry(tokens, positions, memory_rows, qkv_heads, biases, up_bias, up, down, out):
    f32, bf16 = jnp.float32, jnp.bfloat16
    rows, width = tokens.shape
    r = up.shape[0]
    shape, v = jax.ShapeDtypeStruct, pltpu.VMEM
    hbm, vmem = pl.BlockSpec(memory_space=pl.ANY), pl.BlockSpec(memory_space=pltpu.VMEM)
    qkv = shape((2 * rows, 384), bf16)
    return pl.pallas_call(
        entry_kernel,
        out_shape=(shape((rows, width), f32), shape((2 * rows, width), bf16), qkv, qkv, qkv,
                   shape((2, 8, r, 576), bf16), shape((8, r, up.shape[1]), bf16), shape((2, r, down.shape[1]), bf16),
                   shape((2, 4, r, out.shape[1]), bf16), shape((4, 16, up.shape[1]), bf16)),
        in_specs=[vmem] * 9,
        out_specs=[hbm] * 9 + [vmem],
        scratch_shapes=[
            v((rows, width), f32), v((2 * rows, width), bf16), v((2, 8, r, 576), bf16), v((2, 16, 640), bf16),
            v((BLOCK, 640), f32), v((2 * rows, 256), f32), v((2 * rows, 384), bf16), v((2 * rows, 384), bf16), v((2 * rows, 384), bf16),
            v((3, 16, up.shape[1]), bf16), v((r, 576), bf16), v((16, up.shape[1]), bf16), v((32, width), bf16),
            pltpu.SemaphoreType.DMA((48,)), pltpu.SemaphoreType.DMA((48,)), pltpu.SemaphoreType.DMA((16,)),
        ],
        compiler_params=pltpu.CompilerParams(vmem_limit_bytes=VMEM_MAX, collective_id=0, has_side_effects=True),
        cost_estimate=pl.CostEstimate(flops=4 * rows * width * 1152, bytes_accessed=20_000_000, transcendentals=0),
        name="entry",
    )(tokens, positions, memory_rows, qkv_heads, biases, up_bias, up, down, out)


def exit_kernel(x_all, d0, d1, d2, w_all, kept_ref, came_ref, dr1, pos_ref, sums_in, up_in,
                tok_out, first_out, second_out, small_out,
                x_ref, xt_ref, d_ref, w_ref, third_ref, dr_ref, g_ref, own_ref, oth_ref, yb_ref, xs_ref, xb_ref, zt_ref, zs_ref, zb_ref,
                fs_ref, fb_ref, their_ref, got_ref, tok_ref, s_ref, t_ref, r_ref, first_ref, send, recv, sem):
    f32, bf16 = jnp.float32, jnp.bfloat16
    rows, width = dr_ref.shape
    dp, tensor = lax.axis_index("dp"), lax.axis_index("tensor")
    z, x = dp // 2, dp % 2
    inner, outer = tensor % 2, tensor // 2
    up_z = [None] + [(z + k) % 4 for k in range(1, 4)]
    to_z = [None] + [(2 * up_z[k] + x, tensor) for k in range(1, 4)]
    to_x = (2 * z + 1 - x, tensor)
    to_y = (dp, (tensor + 2) % 4)
    to_core = (dp, tensor + 1 - 2 * inner)
    near_z = (2 * (z + 1 - 2 * (z % 2)) + x, tensor)
    far_z = to_z[2]
    loads = []
    for src, dst in ((d2, d_ref.at[2]), (x_all, x_ref), (d0, d_ref.at[0]), (d1, d_ref.at[1]),
                     (w_all, w_ref), (dr1, dr_ref)):
        copy = pltpu.make_async_copy(src, dst, sem.at[len(loads)])
        copy.start()
        loads.append(copy)
    greet(to_z[1:] + [to_x, to_y, to_core])
    ex = Exchange(send, recv)
    started = []

    def go(src, dst, device):
        copy = ex.copy(src, dst, device)
        copy.start()
        started.append(copy)
        return copy

    for k in range(4):
        first_ref[k] = kept_ref[k] + came_ref[k].astype(f32)
    for k in range(1, 4):
        fs_ref[k - 1] = first_ref[up_z[k]].astype(bf16)
    z_first = [go(fs_ref.at[k - 1], fb_ref.at[k - 1], to_z[k]) for k in range(1, 4)]

    loads[0].wait()
    loads[1].wait()
    for b in range(2 * rows // BLOCK):
        xt_ref[:, BLOCK * b:BLOCK * b + BLOCK] = x_ref[BLOCK * b:BLOCK * b + BLOCK, :].T
    for m in range(0, width, BLOCK):
        g_ref[m:m + BLOCK, :] = mm(xt_ref[m:m + BLOCK, :], d_ref[2])
    half = own_ref.shape[3]
    lane = lax.broadcasted_iota(jnp.int32, (half, 128), 1)
    for p in range(8):
        for n in range(3):
            low = g_ref[2 * half * p:2 * half * p + half, 128 * n:128 * n + 128]
            high = g_ref[2 * half * p + half:2 * half * (p + 1), 128 * n:128 * n + 128]
            own_ref[p % 2, p // 2, n] = jnp.where(lane < 64, low, pltpu.roll(high, 64, 1))
            oth_ref[p % 2, p // 2, n] = jnp.where(lane < 64, pltpu.roll(low, 64, 1), high).astype(bf16)
    y_far = go(oth_ref.at[1 - x], yb_ref.at[0], to_y)
    y_near = go(oth_ref.at[x], yb_ref.at[1], to_y)

    for copy in loads[2:]:
        copy.wait()
    place = lax.broadcasted_iota(jnp.int32, (32, 2 * rows), 1)
    which = lax.broadcasted_iota(jnp.int32, (32, 2 * rows), 0)
    picks = jnp.where((place == pos_ref[:, 0:1]) | (which == 24), 1.0, 0.0).astype(bf16)
    picked = [mm(picks, d_ref[n]) for n in range(3)]
    own_place = lax.broadcasted_iota(jnp.int32, (32, rows), 1) + inner * rows
    own_picks = jnp.where(own_place == pos_ref[:, 0:1], 1.0, 0.0)
    memory = lax.dot_general(own_picks, dr_ref[...], NN, precision=lax.Precision.HIGHEST, preferred_element_type=f32)
    lane = lax.broadcasted_iota(jnp.int32, (BLOCK, 128), 1)
    for m in range(0, width, BLOCK):
        r = slice(m, m + BLOCK)
        own, far = [w_ref[o, r, 384:512].astype(f32) for o in range(2)]
        third_ref[r, 0:128] = jnp.where(lane < 64, own, pltpu.roll(far, 64, 1)).astype(bf16)
        third_ref[r, 128:256] = jnp.where(lane < 64, pltpu.roll(own, 64, 1), far).astype(bf16)
        last = [w_ref[o, r, 512:576].astype(f32) for o in range(2)]
        third_ref[r, 256:384] = jnp.concatenate(last, axis=1).astype(bf16)
    sides = lambda n: third_ref[...] if n == 2 else w_ref[n, :, 0:384]
    for n in range(3):
        memory = memory + mm(picked[n].astype(bf16), sides(n), NT)
    hw = s_ref.shape[2]

    def put(row, value):
        for h in range(2):
            s_ref[h, row:row + 1, :] = value[:, hw * h:hw * h + hw]
    for h in range(2):
        s_ref[h, 0:24, :] = memory[0:24, hw * h:hw * h + hw]
        s_ref[h, 38:40, :] = jnp.zeros((2, hw), f32)
    for n in range(6):
        put(24 + n, jnp.sum(sums_in[n], axis=0, keepdims=True))
    ups = [jnp.sum(up_in[n], axis=0, keepdims=True) for n in (0, 2, 1, 3)]
    total = [value[24:25, :] for value in picked]
    turned = jnp.concatenate([pltpu.roll(picked[2][24:32, 128 * n:128 * n + 128], 64, 1) for n in range(3)], axis=1)[0:1, :]
    for t in range(4):
        n = (t % 2 + inner) % 2 + 2 * ((t // 2 + outer) % 2)
        value = jnp.zeros_like(ups[0])
        for other in range(4):
            value = value + jnp.where(n == other, ups[other], 0.0)
        put(30 + t, value)
        s_ref[0, 34 + t:35 + t, :] = jnp.where(n == 0, total[0], 0.0) + jnp.where(n == 2, total[1], 0.0)
        s_ref[1, 34 + t:35 + t, :] = jnp.where(n == 0, total[2], 0.0) + jnp.where(n == 2, turned, 0.0)
    small = [go(s_ref.at[1 - inner], r_ref.at[0], to_core)]
    hops = [to_y, to_x, near_z, far_z]

    def hop(n):
        small[n].wait_recv()
        t_ref[n] = (s_ref[inner] if n == 0 else t_ref[n - 1]) + r_ref[n]
        if n < 4:
            small.append(go(t_ref.at[n], r_ref.at[n + 1], hops[n]))
        else:
            small.append(go(t_ref.at[n], r_ref.at[5], to_core))
            small_out[inner] = t_ref[n]

    mine = pl.multiple_of(inner * rows, 1024)
    theirs = pl.multiple_of((1 - inner) * rows, 1024)

    def block(start):
        r = pl.ds(pl.multiple_of(start, BLOCK), BLOCK)
        return mm(d_ref[0, r, :], sides(0), NT) + mm(d_ref[1, r, :], sides(1), NT) + mm(d_ref[2, r, :], sides(2), NT)

    def away(b, carry):
        their_ref[pl.ds(pl.multiple_of(b * BLOCK, BLOCK), BLOCK), :] = block(theirs + b * BLOCK).astype(bf16)
        return carry
    lax.fori_loop(0, rows // BLOCK, away, 0)
    tokens = go(their_ref, got_ref, to_core)
    hop(0)
    y_far.wait_recv()
    for k in range(4):
        xs_ref[k] = (own_ref[1 - x, k] + yb_ref[0, k].astype(f32)).astype(bf16)
    x_sum = go(xs_ref, xb_ref, to_x)

    def stay(b, carry):
        tok_ref[pl.ds(pl.multiple_of(b * BLOCK, BLOCK), BLOCK), :] = block(mine + b * BLOCK)
        return carry
    lax.fori_loop(0, rows // BLOCK, stay, 0)
    hop(1)
    y_near.wait_recv()
    x_sum.wait_recv()
    for k in range(4):
        zt_ref[k] = own_ref[x, k] + yb_ref[1, k].astype(f32) + xb_ref[k].astype(f32)
    for k in range(1, 4):
        zs_ref[k - 1] = zt_ref[up_z[k]].astype(bf16)
    z_second = [go(zs_ref.at[k - 1], zb_ref.at[k - 1], to_z[k]) for k in range(1, 4)]
    hop(2)
    tokens.wait_recv()

    def finish(s, carry):
        r = pl.ds(pl.multiple_of(s * STRIP, STRIP), STRIP)
        tok_ref[r, :] = tok_ref[r, :] + got_ref[r, :].astype(f32) + dr_ref[r, :]
        return carry
    lax.fori_loop(0, rows // STRIP, finish, 0)
    out = pltpu.make_async_copy(tok_ref, tok_out, sem.at[6])
    out.start()
    hop(3)
    for copy in z_first:
        copy.wait_recv()
    first_out[...] = first_ref[z] + fb_ref[0].astype(f32) + fb_ref[1].astype(f32) + fb_ref[2].astype(f32)
    for copy in z_second:
        copy.wait_recv()
    second_out[...] = zt_ref[z] + zb_ref[0].astype(f32) + zb_ref[1].astype(f32) + zb_ref[2].astype(f32)
    hop(4)
    small[5].wait_recv()
    small_out[1 - inner] = r_ref[5]
    for copy in started:
        copy.wait_send()
    out.wait()


def leave(x_all, d, w_qkv, first, came, dr1, place, sums, up_sums):
    f32, bf16 = jnp.float32, jnp.bfloat16
    rows, width = dr1.shape
    r, half = first.shape[1], first.shape[1] // 2
    shape, v = jax.ShapeDtypeStruct, pltpu.VMEM
    hbm, vmem = pl.BlockSpec(memory_space=pl.ANY), pl.BlockSpec(memory_space=pltpu.VMEM)
    return pl.pallas_call(
        exit_kernel,
        out_shape=(shape((rows, width), f32), shape((r, 384), f32), shape((3, half, 128), f32), shape((2, 40, width // 2), f32)),
        in_specs=[hbm] * 5 + [vmem] * 2 + [hbm] + [vmem] * 3,
        out_specs=[hbm] + [vmem] * 3,
        scratch_shapes=[
            v((2 * rows, width), bf16), v((width, 2 * rows), bf16), v((3, 2 * rows, 384), bf16), v((2, width, 576), bf16), v((width, 384), bf16),
            v((rows, width), f32), v((width, 384), f32), v((2, 4, 3, half, 128), f32), v((2, 4, 3, half, 128), bf16),
            v((2, 4, 3, half, 128), bf16), v((4, 3, half, 128), bf16), v((4, 3, half, 128), bf16), v((4, 3, half, 128), f32),
            v((3, 3, half, 128), bf16), v((3, 3, half, 128), bf16), v((3, r, 384), bf16), v((3, r, 384), bf16),
            v((rows, width), bf16), v((rows, width), bf16), v((rows, width), f32), v((2, 40, width // 2), f32),
            v((5, 40, width // 2), f32), v((6, 40, width // 2), f32), v((4, r, 384), f32),
            pltpu.SemaphoreType.DMA((16,)), pltpu.SemaphoreType.DMA((16,)), pltpu.SemaphoreType.DMA((9,)),
        ],
        compiler_params=pltpu.CompilerParams(vmem_limit_bytes=VMEM_MAX, collective_id=2, has_side_effects=True),
        cost_estimate=pl.CostEstimate(flops=2 * rows * width * 384 * 8, bytes_accessed=20_000_000, transcendentals=0),
        name="leave",
    )(x_all, *d, w_qkv, first, came, dr1, place, sums, up_sums)


def layer_norm(values, norm_gain, norm_shift):
    centre = values - jnp.mean(values, axis=-1, keepdims=True)
    spread = jnp.mean(centre * centre, axis=-1, keepdims=True)
    return centre * lax.rsqrt(spread + EPSILON) * norm_gain + norm_shift


def gelu_exact(values):
    return jax.nn.gelu(values, approximate=False)


AXES = ("dp", "tensor")


class Grid:
    def __init__(self, dp, tensor):
        self.dp, self.tensor = dp, tensor
        factors, rest = [2], dp // 2
        while rest > 8:
            factors.insert(0, 4)
            rest //= 4
        if rest > 1:
            factors.insert(0, rest)
        self.factors = factors

    def digit(self, j):
        stride = 1
        for f in self.factors[j + 1:]:
            stride *= f
        return stride, self.factors[j]

    def my_digit(self, j):
        stride, f = self.digit(j)
        return lax.axis_index("dp") // stride % f

    def turn(self, value, j, k):
        stride, f = self.digit(j)
        pairs = []
        for d in range(self.dp):
            g = d // stride % f
            to = d + ((g + k) % f - g) * stride
            for t in range(self.tensor):
                pairs.append((d * self.tensor + t, to * self.tensor + t))
        return lax.ppermute(value, AXES, pairs)

    def swap_dp(self, value, bit):
        pairs = [(d * self.tensor + t, (d ^ bit) * self.tensor + t) for d in range(self.dp) for t in range(self.tensor)]
        return lax.ppermute(value, AXES, pairs)

    def swap(self, value, bit):
        pairs = [(d * self.tensor + t, d * self.tensor + (t ^ bit)) for d in range(self.dp) for t in range(self.tensor)]
        return lax.ppermute(value, AXES, pairs)

    def gather_stage(self, value, j, axis):
        _, f = self.digit(j)
        g = self.my_digit(j)
        got = [value] + [self.turn(value, j, k) for k in range(1, f)]
        if f == 2:
            lower = jnp.where(g == 0, got[0], got[1])
            upper = jnp.where(g == 0, got[1], got[0])
            return jnp.stack([lower, upper], axis=axis)
        ring = got[::-1]
        return lax.dynamic_slice_in_dim(jnp.stack(ring + ring[:-1], axis=axis), f - 1 - g, f, axis)

    def gather(self, shard, outer_first=False):
        count = len(self.factors)
        value = shard
        for j in range(count - 1):
            value = self.gather_stage(value, j, j)
        if outer_first:
            value = jnp.stack([value, self.swap(value, 2)])
            value = self.gather_stage(value, count - 1, count)
            return value.reshape(2, -1, shard.shape[-1])
        value = self.gather_stage(value, count - 1, count - 1)
        value = value.reshape(-1, shard.shape[-1])
        return jnp.stack([value, self.swap(value, 2)])

    def reduce_stage(self, value, j, axis):
        _, f = self.digit(j)
        g = self.my_digit(j)
        total = lax.dynamic_index_in_dim(value, g, axis, keepdims=False).astype(jnp.float32)
        for k in range(1, f):
            part = lax.dynamic_index_in_dim(value, (g + k) % f, axis, keepdims=False)
            total = total + self.turn(part.astype(jnp.bfloat16), j, k).astype(jnp.float32)
        return total

    def reduce(self, parts, outer_first=True):
        count = len(self.factors)
        columns = parts.shape[-1]
        value = parts
        if outer_first:
            value = value[0].astype(jnp.float32) + self.swap(value[1].astype(jnp.bfloat16), 2).astype(jnp.float32)
            value = value.reshape(*self.factors, -1, columns)
            value = self.reduce_stage(value, count - 1, count - 1)
        else:
            value = value.reshape(2, *self.factors, -1, columns)
            value = self.reduce_stage(value, count - 1, count)
            value = value[0] + self.swap(value[1].astype(jnp.bfloat16), 2).astype(jnp.float32)
        for j in reversed(range(count - 1)):
            value = self.reduce_stage(value, j, j)
        return value

    @property
    def stages(self):
        return len(self.factors) + 1

    def open(self, parts, outer_first):
        columns = parts.shape[-1]
        return parts if outer_first else parts.reshape(2, *self.factors, -1, columns)

    def stage(self, value, outer_first, n):
        count = len(self.factors)
        if n == (0 if outer_first else 1):
            value = value[0].astype(jnp.float32) + self.swap(value[1].astype(jnp.bfloat16), 2).astype(jnp.float32)
            return value.reshape(*self.factors, -1, value.shape[-1]) if outer_first else value
        if n == 0:
            return self.reduce_stage(value, count - 1, count)
        return self.reduce_stage(value, count - n, count - n)

    def total(self, vector):
        for bit in (1, 2):
            vector = vector + self.swap(vector, bit)
        bit = 1
        while bit < self.dp:
            vector = vector + self.swap_dp(vector, bit)
            bit *= 2
        return vector


def shards(grid, tokens, segment_ids, memory_positions, memory_rows, qkv_weight, qv_bias, out_weight, out_bias,
           norm1_gain, norm1_bias, up_weight, up_bias, down_weight, down_bias, norm2_gain, norm2_bias, out_cotangent):
    f32, bf16 = jnp.float32, jnp.bfloat16
    rows, width = tokens.shape
    group_len = segment_ids.shape[1]
    tensor = lax.axis_index("tensor")
    inner, outer = tensor % 2, tensor // 2
    slice_rows = qkv_weight.shape[0]
    heads = qkv_weight.shape[1]
    hd = 64
    hw = heads * hd
    units = up_weight.shape[1]

    segments = lax.dynamic_index_in_dim(segment_ids, outer, 0, keepdims=False)
    positions = lax.dynamic_index_in_dim(memory_positions, outer, 0, keepdims=False)
    row_place = inner * rows + jnp.arange(rows, dtype=jnp.int32)
    picks = (row_place[:, None] == positions[None, :])
    joined = lambda w: w.transpose(1, 0, 2).reshape(width, -1)

    parts = qkv_weight.reshape(slice_rows, heads, 3, hd)
    order_columns = lambda p: jnp.concatenate([p[..., :2, n, :].reshape(*p.shape[:-3], 2 * hd) for n in range(3)]
                                              + [p[..., 2, n, :] for n in range(3)], axis=-1)
    shard_qkv = order_columns(parts)
    shard_out = jnp.pad(out_weight.reshape(slice_rows, hw), ((0, 0), (0, 256 - hw)))
    bias_parts = qv_bias.reshape(heads, 2, hd)
    bias_qkv = order_columns(jnp.stack([bias_parts[:, 0], jnp.zeros_like(bias_parts[:, 0]), bias_parts[:, 1]], 1))
    bias_qkv = jnp.pad(bias_qkv[None], ((0, 15), (0, 64)))
    own_up_bias = jnp.broadcast_to(up_bias[None], (16, units))
    fused = grid.dp == 8 and grid.tensor == 4
    if fused:
        memory = memory_positions.shape[1]
        place = jnp.pad(positions[None], ((0, 7), (0, 32 - memory)), constant_values=-1)
        x0, x_all, q, k, v, w_qkv, up_g, down_g, out_g, b_up = entry(tokens, place, memory_rows, qkv_weight.transpose(1, 0, 2), bias_qkv, up_bias[None], up_weight, down_weight, shard_out)
        column = jnp.pad(jnp.broadcast_to(positions[:, None], (memory, 128)), ((0, 32 - memory), (0, 0)), constant_values=-1)
        w_qkv = w_qkv.reshape(2, width, 9 * hd)
        up_all = up_g.reshape(width, units)
        ups = (up_all, grid.swap(up_all, 2))
        down_pair = down_g.reshape(-1, units)
        downs = (down_pair, *[grid.turn(down_pair, 0, k) for k in range(1, 4)])
        outs = (out_g, grid.turn(out_g, 1, 1))
    else:
        x0 = tokens.astype(f32) + jnp.dot(picks.astype(bf16), memory_rows, preferred_element_type=f32)
        xl = x0.astype(bf16)
        w_qkv = grid.gather(shard_qkv)
        other = grid.swap(xl, 1)
        x_all = jnp.concatenate([jnp.where(inner == 0, xl, other), jnp.where(inner == 0, other, xl)])
        b_two = jnp.stack([bias_qkv[0], grid.swap(bias_qkv[0], 2)]).astype(f32)
        y = [(mm(x_all, w_qkv[o]) + b_two[o, :9 * hd]).astype(bf16) for o in range(2)]
        third = lambda n: [one[:, (6 + n) * hd:(7 + n) * hd] for one in y]
        q, k, v = [jnp.concatenate([y[0][:, 2 * n * hd:2 * (n + 1) * hd], y[1][:, 2 * n * hd:2 * (n + 1) * hd]] + third(n), 1)
                   for n in range(3)]
        q = q * jnp.asarray(0.125, bf16)
        b_up = jnp.stack([own_up_bias, grid.swap(own_up_bias, 2)])
        b_up = jnp.concatenate([b_up, grid.swap(b_up, 1)])
        outs, ups, downs = (grid.gather(shard_out, True),), (grid.gather(up_weight),), (grid.gather(down_weight, True),)
    mixed, lse = attend_forward(q, k, v, segments)
    vec = jnp.stack([out_bias, norm1_gain, norm1_bias, down_bias, norm2_gain, norm2_bias, norm2_bias, norm2_bias]).astype(f32)
    (block_out, dr1, do_all, *grads, sums, up_sums) = middle(
        mixed, x0, outs, ups, downs, out_cotangent, vec, b_up)
    if fused:
        return finish_small(grid, tensor, x_all, q, k, v, do_all, mixed, lse, segments, w_qkv, dr1, column, sums, up_sums, block_out,
                            grads, hw)
    g_down, g_up, g_out = grads

    TN = (((0,), (0,)), ((), ()))
    tie = lax.optimization_barrier
    kinds = (True, False, True)
    state = [grid.open(parts, kind) for parts, kind in zip((g_down, g_up, g_out), kinds)]
    step = lambda n, state: [grid.stage(value, kind, n) for value, kind in zip(state, kinds)]
    late = [(1, 0, 2)[n] for n in range(3)]
    d = [None] * 3
    state, d[1] = step(0, state), attend_backward(1, q, k, v, do_all, mixed, lse, segments)
    state, d[1], q = tie((state, d[1], q))
    g_one = mm(x_all, d[1], TN).astype(bf16)
    state, d[0] = step(1, state), attend_backward(0, q, k, v, do_all, mixed, lse, segments)
    state, d[0], q, g_one = tie((state, d[0], q, g_one))
    g_zero = mm(x_all, d[0], TN)
    first = g_zero + grid.swap(g_one, 2).astype(f32)
    state, d[2] = step(2, state), attend_backward(2, q, k, v, do_all, mixed, lse, segments)
    state, d[2], first = tie((state, d[2], first))
    for n in range(3, grid.stages):
        state = step(n, state)
    grad_down, grad_up, grad_out = state
    grad_out = grad_out[:, :hw]

    g_two = mm(x_all, d[2], TN)
    side = lambda m, o: jnp.concatenate([m[:, (2 * n + o) * hd:(2 * n + o + 1) * hd] for n in range(3)], 1)
    second = side(g_two, 0) + grid.swap(side(g_two, 1).astype(bf16), 2).astype(f32)
    both = jnp.concatenate([first, second], 1).reshape(*grid.factors, slice_rows, 9 * hd)
    for j in reversed(range(len(grid.factors))):
        both = grid.reduce_stage(both, j, j)
    restore = lambda p: jnp.stack([jnp.concatenate([p[..., 2 * n * hd:2 * (n + 1) * hd].reshape(*p.shape[:-1], 2, hd),
                                                    p[..., None, (6 + n) * hd:(7 + n) * hd]], -2) for n in range(3)], -2)
    grad_qkv = restore(both).reshape(slice_rows, heads, 3 * hd)
    third = jnp.concatenate([w_qkv[o][:, (6 + n) * hd:(7 + n) * hd] for n in range(3) for o in range(2)], 1)
    part = (mm(d[0], w_qkv[0][:, :6 * hd], NT) + mm(d[1], w_qkv[1][:, :6 * hd], NT) + mm(d[2], third, NT)).reshape(2, rows, width)
    mine = lax.dynamic_index_in_dim(part, inner, 0, keepdims=False)
    theirs = lax.dynamic_index_in_dim(part, 1 - inner, 0, keepdims=False).astype(bf16)
    grad_tokens = mine + grid.swap(theirs, 1).astype(f32) + dr1
    d_sum = [jnp.sum(one.astype(f32), axis=0) for one in d]
    d_bias = [jnp.concatenate([d_sum[o]] + [d_sum[2][(2 * n + o) * hd:(2 * n + o + 1) * hd] for n in range(3)]) for o in range(2)]
    dg2, ds2, d_down_bias, dg1, ds1, d_out_bias = jnp.sum(sums, axis=1)
    d_up_bias = jnp.sum(up_sums, axis=1).reshape(2, 2 * units)
    grad_memory = jnp.dot(picks.astype(f32).T, grad_tokens, precision=lax.Precision.HIGHEST)

    order = jnp.arange(4, dtype=jnp.int32) ^ tensor
    up_parts = d_up_bias.reshape(2, 2, units)
    up_parts = jnp.stack([up_parts[0, 0], up_parts[1, 0], up_parts[0, 1], up_parts[1, 1]])[order]
    take = lambda o: restore(d_bias[o])[:, 0::2].reshape(-1)
    blank = jnp.zeros((2 * hw,), f32)
    qv_parts = jnp.stack([take(0), blank, take(1), blank])[order]
    pieces = [grad_memory.reshape(-1), d_out_bias, dg1, ds1, d_down_bias, dg2, ds2, up_parts.reshape(-1), qv_parts.reshape(-1)]
    summed = grid.total(jnp.concatenate(pieces))
    outs, at = [], 0
    for piece in pieces:
        outs.append(lax.slice_in_dim(summed, at, at + piece.size))
        at += piece.size
    t_memory, t_out_bias, t_g1, t_s1, t_down_bias, t_g2, t_s2, t_up, t_qv = outs
    grad_up_bias = lax.dynamic_index_in_dim(t_up.reshape(4, units), tensor, 0, keepdims=False)
    grad_qv = lax.dynamic_index_in_dim(t_qv.reshape(4, heads, 2 * hd), tensor, 0, keepdims=False)
    return (block_out, grad_tokens, t_memory.reshape(-1, width), grad_qkv, grad_qv,
            grad_out.reshape(slice_rows, heads, hd), t_out_bias, t_g1, t_s1, grad_up, grad_up_bias, grad_down,
            t_down_bias, t_g2, t_s2)


def blend_one_kernel(x_ref, down, down_early, down_late, up, up_in, out, out_in, kept_down, kept_up, kept_out, send_x, send_y):
    f32, bf16 = jnp.float32, jnp.bfloat16
    x = x_ref[0]
    width = down.shape[-1]
    add = lambda a, b: a.astype(f32) + b.astype(f32)
    early = pl.program_id(0) < pl.num_programs(0) // 2
    down_in = lambda n: jnp.where(early, down_early[0, n], down_late[0, n])
    kept_down[0] = add(down[0, x], down_in(x))
    kept_out[0] = add(out[0, x], out_in[0, x])
    send_x[0, :, 0:width] = add(down[0, 1 - x], down_in(1 - x)).astype(bf16)
    send_x[0, :, width:] = add(out[0, 1 - x], out_in[0, 1 - x]).astype(bf16)
    kept_up[0] = add(up[0, 0], up_in[0, 0])
    send_y[0] = add(up[1, 0], up_in[1, 0]).astype(bf16)


def blend_one(x, down, down_early, down_late, up, up_in, out, out_in):
    f32, bf16 = jnp.float32, jnp.bfloat16
    _, zs, r, width = up.shape
    ow = out.shape[-1]
    shape = jax.ShapeDtypeStruct
    by_x = lambda columns: pl.BlockSpec((1, 2, r, columns), lambda j, *_: (j, 0, 0, 0))
    by_y = pl.BlockSpec((2, 1, r, width), lambda j, *_: (0, j, 0, 0))
    one = lambda columns: pl.BlockSpec((1, r, columns), lambda j, *_: (j, 0, 0))
    lower = pl.BlockSpec((1, 2, r, width), lambda j, *_: (jnp.minimum(j, zs // 2 - 1), 0, 0, 0))
    upper = pl.BlockSpec((1, 2, r, width), lambda j, *_: (jnp.maximum(j - zs // 2, 0), 0, 0, 0))
    fold = lambda a: a.reshape(-1, 2, r, a.shape[-1])
    return pl.pallas_call(
        blend_one_kernel,
        out_shape=(shape((zs, r, width), f32), shape((zs, r, width), f32), shape((zs, r, ow), f32),
                   shape((zs, r, width + ow), bf16), shape((zs, r, width), bf16)),
        grid_spec=pltpu.PrefetchScalarGridSpec(
            num_scalar_prefetch=1, grid=(zs,),
            in_specs=[by_x(width), lower, upper, by_y, by_y, by_x(ow), by_x(ow)],
            out_specs=[one(width), one(width), one(ow), one(width + ow), one(width)]),
        compiler_params=pltpu.CompilerParams(dimension_semantics=("arbitrary",), vmem_limit_bytes=VMEM_MAX),
        cost_estimate=pl.CostEstimate(flops=8 * zs * r * width, bytes_accessed=10_000_000, transcendentals=0),
        name="blend_one",
    )(x.reshape(1), fold(down), fold(down_early), fold(down_late), up, up_in, fold(out), fold(out_in))


def blend_two_kernel(at_ref, kept_down, kept_up, kept_out, came_x, came_y, first, kept_z, kept_first, *sends):
    f32, bf16 = jnp.float32, jnp.bfloat16
    x, z = at_ref[0], at_ref[1]
    zs, r, width = kept_down.shape
    for k in range(zs):
        n = (z + k) % zs
        parts = (kept_down[n] + came_x[n, :, 0:width].astype(f32), kept_up[n] + came_y[n].astype(f32),
                 kept_out[n] + came_x[n, :, width:].astype(f32))
        start = 0
        for part in parts:
            stop = start + part.shape[1]
            if k == 0:
                kept_z[:, start:stop] = part
            else:
                sends[k - 1][:, start:stop] = part.astype(bf16)
            start = stop
        kept_first[k] = first[k, x]
        sends[zs - 1][k] = first[k, 1 - x].astype(bf16)


def blend_two(x, z, kept_down, kept_up, kept_out, came_x, came_y, first):
    f32, bf16 = jnp.float32, jnp.bfloat16
    zs, r, width = kept_down.shape
    columns = 2 * width + kept_out.shape[-1]
    shape = jax.ShapeDtypeStruct
    vmem = pl.BlockSpec(memory_space=pltpu.VMEM)
    return pl.pallas_call(
        blend_two_kernel,
        out_shape=(shape((r, columns), f32), shape((zs, r, first.shape[-1]), f32), *[shape((r, columns), bf16)] * (zs - 1),
                   shape((zs, r, first.shape[-1]), bf16)),
        in_specs=[pl.BlockSpec(memory_space=pltpu.SMEM)] + [vmem] * 6,
        out_specs=[vmem] * (zs + 2),
        compiler_params=pltpu.CompilerParams(vmem_limit_bytes=VMEM_MAX),
        cost_estimate=pl.CostEstimate(flops=4 * zs * r * columns, bytes_accessed=10_000_000, transcendentals=0),
        name="blend_two",
    )(jnp.stack([x, z]), kept_down, kept_up, kept_out, came_x, came_y, first.reshape(zs, 2, r, first.shape[-1]))


def spread_kernel(t_ref, kept, came_one, came_two, came_three, small, one, two,
                  down, up, out, memory, up_bias, qkv, qv, *vectors):
    f32 = jnp.float32
    width = down.shape[1]
    total = lambda cols: ((kept[:, cols] + came_one[:, cols].astype(f32))
                          + (came_two[:, cols].astype(f32) + came_three[:, cols].astype(f32)))
    down[...] = total(slice(0, width))
    up[...] = total(slice(width, 2 * width))
    out[...] = total(slice(2 * width, 2 * width + 256)).T[0:192, :]
    half = width // 2
    t = t_ref[0]
    for h in range(2):
        cols = slice(half * h, half * h + half)
        memory[:, cols] = small[h, 0:memory.shape[0], :]
        qv[h:h + 1, :] = small[h, pl.ds(34 + t, 1), :]
        for n, ref in enumerate(vectors):
            ref[cols] = small[h, 24 + n, :]
        up_bias[cols] = small[h, pl.ds(30 + t, 1), :].reshape(half)
    turn = lambda value: pltpu.roll(value, 64, 1)
    q, k, v = [one[:, 128 * n:128 * n + 128] for n in range(3)]
    lane = lax.broadcasted_iota(jnp.int32, q.shape, 1)
    qkv[0, :, 0:128] = jnp.where(lane < 64, q, turn(k))
    qkv[0, :, 128:192] = v[:, 0:64]
    qkv[1, :, 0:128] = jnp.where(lane < 64, turn(q), k)
    qkv[1, :, 128:192] = turn(v)[:, 0:64]
    n = two.shape[1]
    lane = lax.broadcasted_iota(jnp.int32, two.shape[1:], 1)
    qkv[2, 0:n, 0:128] = jnp.where(lane < 64, two[0], turn(two[1]))
    qkv[2, n:2 * n, 0:128] = jnp.where(lane < 64, turn(two[0]), two[1])
    qkv[2, 0:n, 128:192] = two[2][:, 0:64]
    qkv[2, n:2 * n, 128:192] = turn(two[2])[:, 0:64]


def spread(tensor, kept, came, small, one, two, memory):
    f32 = jnp.float32
    r, columns = kept.shape
    width = 2 * small.shape[2]
    shape = jax.ShapeDtypeStruct
    vmem = pl.BlockSpec(memory_space=pltpu.VMEM)
    return pl.pallas_call(
        spread_kernel,
        out_shape=(shape((r, width), f32), shape((r, width), f32), shape((192, r), f32), shape((memory, width), f32),
                   shape((width,), f32), shape((3, r, 192), f32), shape((2, width // 2), f32), *[shape((width,), f32)] * 6),
        in_specs=[pl.BlockSpec(memory_space=pltpu.SMEM)] + [vmem] * 7,
        out_specs=[vmem] * 13,
        compiler_params=pltpu.CompilerParams(vmem_limit_bytes=VMEM_MAX),
        cost_estimate=pl.CostEstimate(flops=3 * r * columns, bytes_accessed=3_000_000, transcendentals=0),
        name="spread",
    )(tensor.reshape(1), kept, *came, small, one, two)


def finish_small(grid, tensor, x_all, q, k, v, do_all, mixed, lse, segments, w_qkv, dr1, column, sums, up_sums, block_out,
                 grads, hw):
    f32, bf16 = jnp.float32, jnp.bfloat16
    tie = lax.optimization_barrier
    TN = (((0,), (0,)), ((), ()))
    width = dr1.shape[1]
    x, z = lax.axis_index("dp") % 2, lax.axis_index("dp") // 2
    down, down_far, down_early, up, up_far, out, out_far = grads

    def beside(pair, q, sends):
        arrays, q = tie(([a for a, _ in sends], q))
        came = [move(a) for a, (_, move) in zip(arrays, sends)]
        d = attend_backward(pair, q, k, v, do_all, mixed, lse, segments)
        return tie((came, d, q))

    over_y = lambda a: grid.swap(a, 2)
    over_x = lambda a: grid.turn(a, 1, 1)
    (down_in, out_in, up_in), d_one, q = beside(1, q, [(down_far, over_y), (out_far, over_y), (up_far, over_x)])
    g_one = mm(x_all, d_one, TN).astype(bf16)
    kept_down, kept_up, kept_out, send_x, send_y = blend_one(x, down, down_early, down_in, up, up_in, out, out_in)
    (came_x, came_y, came_one), d_zero, q = beside(0, q, [(send_x, over_x), (send_y, over_y), (g_one, over_y)])
    first = mm(x_all, d_zero, TN) + came_one.astype(f32)
    kept, kept_first, *sends = blend_two(x, z, kept_down, kept_up, kept_out, came_x, came_y, first)
    over_z = [lambda a, n=n: grid.turn(a, 0, n) for n in range(1, 4)]
    came, d_two, q = beside(2, q, list(zip(sends, over_z + [over_x])))
    grad_tokens, one, two, small = leave(x_all, (d_zero, d_one, d_two), w_qkv, kept_first, came[3], dr1, column, sums, up_sums)
    grad_down, grad_up, grad_out, grad_memory, up_bias, grad_qkv, qv, *vec = spread(tensor, kept, came[:3], small, one, two, 20)
    hd = 64
    part = lambda n: jnp.concatenate([qv[0, 128 * n:128 * n + 128].reshape(2, hd), qv[1:2, 128 * n:128 * n + hd]])
    grad_qv = jnp.concatenate([part(0), part(2)], 1)
    t_out_bias, t_g1, t_s1, t_down_bias, t_g2, t_s2 = [vec[n] for n in (5, 3, 4, 2, 0, 1)]
    return (block_out, grad_tokens, grad_memory, grad_qkv.transpose(1, 0, 2), grad_qv,
            grad_out.reshape(3, hd, -1).transpose(2, 0, 1), t_out_bias, t_g1, t_s1, grad_up, up_bias, grad_down,
            t_down_bias, t_g2, t_s2)


def solution(mesh):
    grid = Grid(mesh.shape["dp"], mesh.shape["tensor"])
    tokens, dp, none = P(AXES, None), P("dp", None), P()
    heads, matrix = P("dp", "tensor", None), P("dp", "tensor")
    in_specs = (tokens, dp, dp, none, heads, P("tensor", None), heads, none, none, none, matrix, P("tensor"), matrix,
                none, none, none, tokens)
    out_specs = (tokens, tokens, none, heads, P("tensor", None), heads, none, none, none, matrix, P("tensor"), matrix,
                 none, none, none)

    def run(*args):
        return shards(grid, *args)

    return jax.shard_map(run, mesh=mesh, in_specs=in_specs, out_specs=out_specs, check_vma=False)
```
